32 devices in a mesh: dp: 16 (over z, y, x), tensor: 2 (over core).
Axes of the slice: x: 2, y: 2, z: 4, core: 2. Of those that a mesh axis runs over, the one named last changes fastest.
Arguments:
- inputs: bfloat16 [2, 16, 1024, 1024], P(None, 'dp', 'tensor'), may hold values from -6 to 6
- prefix: int32 [2, 16], P(None, 'dp'), may hold values from 102 to 512, as said below
- ln1_gain: float32 [1024], P(('dp', 'tensor')), may hold values from 0.5 to 1.5
- ln1_bias: float32 [1024], P(('dp', 'tensor')), may hold values from -4 to 4
- query_weight: bfloat16 [1024, 1024], P('dp', 'tensor'), may hold values from -0.1875 to 0.1875
- query_bias: float32 [1024], P(('dp', 'tensor')), may hold values from -4 to 4
- key_weight: bfloat16 [1024, 1024], P('dp', 'tensor'), may hold values from -0.1875 to 0.1875
- value_weight: bfloat16 [1024, 1024], P('dp', 'tensor'), may hold values from -0.1875 to 0.1875
- value_bias: float32 [1024], P(('dp', 'tensor')), may hold values from -4 to 4
- out_weight: bfloat16 [1024, 1024], P('tensor', 'dp'), may hold values from -1.5 to 1.5
- out_bias: float32 [1024], P(('dp', 'tensor')), may hold values from -4 to 4
- ln2_gain: float32 [1024], P(('dp', 'tensor')), may hold values from 0.5 to 1.5
- ln2_bias: float32 [1024], P(('dp', 'tensor')), may hold values from -4 to 4
- up_weight: bfloat16 [1024, 4096], P('dp', 'tensor'), may hold values from -0.1875 to 0.1875
- up_bias: float32 [4096], P(('dp', 'tensor')), may hold values from -4 to 4
- down_weight: bfloat16 [4096, 1024], P('tensor', 'dp'), may hold values from -0.125 to 0.125
- down_bias: float32 [1024], P(('dp', 'tensor')), may hold values from -4 to 4
- cotangent: bfloat16 [2, 16, 1024, 1024], P(None, 'dp', 'tensor'), may hold values from -6 to 6
Outputs:
- layer_out: float32 [2, 16, 1024, 1024], P(None, 'dp', 'tensor')
- input_grad: float32 [2, 16, 1024, 1024], P(None, 'dp', 'tensor')
- ln1_gain_grad: float32 [1024], P(('dp', 'tensor'))
- ln1_bias_grad: float32 [1024], P(('dp', 'tensor'))
- query_weight_grad: float32 [1024, 1024], P('dp', 'tensor')
- query_bias_grad: float32 [1024], P(('dp', 'tensor'))
- key_weight_grad: float32 [1024, 1024], P('dp', 'tensor')
- value_weight_grad: float32 [1024, 1024], P('dp', 'tensor')
- value_bias_grad: float32 [1024], P(('dp', 'tensor'))
- out_weight_grad: float32 [1024, 1024], P('tensor', 'dp')
- out_bias_grad: float32 [1024], P(('dp', 'tensor'))
- ln2_gain_grad: float32 [1024], P(('dp', 'tensor'))
- ln2_bias_grad: float32 [1024], P(('dp', 'tensor'))
- up_weight_grad: float32 [1024, 4096], P('dp', 'tensor')
- up_bias_grad: float32 [4096], P(('dp', 'tensor'))
- down_weight_grad: float32 [4096, 1024], P('tensor', 'dp')
- down_bias_grad: float32 [1024], P(('dp', 'tensor'))
The draws below stay inside these ranges and needn't reach their ends.
Inputs may be any that keep to these rules, and one draw needn't show every extreme that they name: prefix[m, s] tokens at the start of sequence s of micro-batch m see one another both ways; 102 and 512 both occur in every draw.
All inputs are finite; a program needn't handle non-finite values.
Results may differ from the reference program's by a relative error of at most 0.023.
Values may be sent and summed in bfloat16 or wider, within the bound.
A program may use at most 112 MiB of HBM per device.

```python
import math
import jax
import jax.numpy as jnp
from jax import lax

D = 1024
HEADS = 8
HEAD_DIM = 128
FF = 4096
SEQ = 1024
MICRO = 2
BLOCK = 512
SEQS = 16


def draw_prefix(key, part):
    key_one, key_two, key_three = jax.random.split(key, 3)
    lengths = jax.random.randint(key_one, (MICRO, SEQS), SEQ // 10, SEQ // 2 + 1)
    places = jnp.arange(MICRO * SEQS).reshape(MICRO, SEQS)
    longest = jax.random.randint(key_two, (), 0, MICRO * SEQS)
    shortest = (longest + 1 + jax.random.randint(key_three, (), 0, MICRO * SEQS - 1)) % (MICRO * SEQS)
    lengths = jnp.where(places == longest, SEQ // 2, lengths)
    lengths = jnp.where(places == shortest, SEQ // 10, lengths)
    return lengths.astype(jnp.int32)


def steps_of(key, dims, shards, low, high):
    loudness, own = 1.0, jax.random.fold_in(key, 6)
    for dim, blocks in shards:
        steps = jnp.exp(jax.random.uniform(jax.random.fold_in(own, dim), (blocks,), jnp.float32, low / len(shards), high / len(shards)))
        loudness = loudness * jnp.repeat(steps, dims[dim] // blocks).reshape([-1 if axis == dim else 1 for axis in range(len(dims))])
    return loudness


def bell_draw(rng, shape, deviation, bound, cuts=(), held_as=jnp.bfloat16):
    level = steps_of(rng, shape, cuts, -0.22, 0.18) if cuts else 1.0
    values = jax.random.normal(rng, shape, jnp.float32) * deviation * level
    return jnp.minimum(jnp.maximum(values, -bound), bound).astype(held_as)


def setup_inputs(seed: int = 0) -> dict:
    key_of = jax.random.split(jax.random.key(seed), 19)
    inputs = bell_draw(key_of[0], (MICRO, SEQS, SEQ, D), 1.0, 6.0, ((1, 16), (2, 2)))
    prefix = draw_prefix(jax.random.fold_in(key_of[18], 71), 0)
    ln1_gain = jnp.clip(1.0 + 0.1 * jax.random.normal(key_of[2], (D,), jnp.float32), 0.5, 1.5)
    ln1_bias = bell_draw(key_of[3], (D,), 0.3, 4.0, ((0, 32),), jnp.float32)
    query_weight = bell_draw(key_of[4], (D, D), D ** -0.5, 0.1875, ((0, 16), (1, 2)))
    query_bias = bell_draw(key_of[5], (D,), 0.3, 4.0, ((0, 32),), jnp.float32)
    key_weight = bell_draw(key_of[6], (D, D), D ** -0.5, 0.1875, ((0, 16), (1, 2)))
    value_weight = bell_draw(key_of[7], (D, D), D ** -0.5, 0.1875, ((0, 16), (1, 2)))
    value_bias = bell_draw(key_of[8], (D,), 0.3, 4.0, ((0, 32),), jnp.float32)
    out_weight = bell_draw(key_of[9], (D, D), (max(1, 16 * D // SEQ)) ** -0.5, 1.5, ((0, 2), (1, 16)))
    out_bias = bell_draw(key_of[10], (D,), 0.3, 4.0, ((0, 32),), jnp.float32)
    ln2_gain = jnp.clip(1.0 + 0.1 * jax.random.normal(key_of[11], (D,), jnp.float32), 0.5, 1.5)
    ln2_bias = bell_draw(key_of[12], (D,), 0.3, 4.0, ((0, 32),), jnp.float32)
    up_weight = bell_draw(key_of[13], (D, FF), D ** -0.5, 0.1875, ((0, 16), (1, 2)))
    up_bias = bell_draw(key_of[14], (FF,), 0.3, 4.0, ((0, 32),), jnp.float32)
    down_weight = bell_draw(key_of[15], (FF, D), (FF // 2) ** -0.5, 0.125, ((0, 2), (1, 16)))
    down_bias = bell_draw(key_of[16], (D,), 0.3, 4.0, ((0, 32),), jnp.float32)
    cotangent = bell_draw(key_of[17], (MICRO, SEQS, SEQ, D), 1.0, 6.0, ((1, 16), (2, 2)))
    return {"inputs": inputs, "prefix": prefix, "ln1_gain": ln1_gain, "ln1_bias": ln1_bias, "query_weight": query_weight, "query_bias": query_bias, "key_weight": key_weight, "value_weight": value_weight, "value_bias": value_bias, "out_weight": out_weight, "out_bias": out_bias, "ln2_gain": ln2_gain, "ln2_bias": ln2_bias, "up_weight": up_weight, "up_bias": up_bias, "down_weight": down_weight, "down_bias": down_bias, "cotangent": cotangent}


EPSILON = 1e-05
HIGH = lax.Precision.HIGHEST

@jax.custom_vjp
def low(v):
    return lax.optimization_barrier(v.astype(jnp.bfloat16)).astype(jnp.float32)

@jax.custom_vjp
def low_back(v):
    return v

def low_keep(v):
    return (low(v), None)

def low_pass(kept, grad):
    return (grad,)

def back_keep(v):
    return (v, None)

def back_low(kept, grad):
    return (low(grad),)
low.defvjp(low_keep, low_pass)
low_back.defvjp(back_keep, back_low)

def matmul(left, right):
    return jnp.dot(left, right, precision=HIGH, preferred_element_type=jnp.float32)

def layer_norm(values, gain, shift):
    center = values - lax.optimization_barrier(jnp.mean(values, axis=-1, keepdims=True))
    spread = lax.optimization_barrier(jnp.mean(center * center, axis=-1, keepdims=True))
    return center * lax.rsqrt(spread + EPSILON) * gain + shift

def attention(queries, key_rows, value_rows, prefix_len):
    seq_len = queries.shape[0]
    count = seq_len // BLOCK
    scale = 1.0 / math.sqrt(HEAD_DIM)
    columns = jnp.arange(seq_len, dtype=jnp.int32)

    def one_block(items):
        query_block, start = items
        scores = jnp.einsum('qhd,khd->hqk', query_block, key_rows, precision=HIGH) * scale
        scores = low_back(scores)
        places = start + jnp.arange(BLOCK, dtype=jnp.int32)
        allowed = (columns[None, :] <= places[:, None]) | (columns[None, :] < prefix_len)
        scores = jnp.where(allowed[None], scores, -jnp.inf)
        peak = lax.optimization_barrier(jnp.max(scores, axis=-1, keepdims=True))
        raw_weights = jnp.exp(scores - peak)
        probs = raw_weights / lax.optimization_barrier(jnp.sum(raw_weights, axis=-1, keepdims=True))
        probs = low(probs)
        return jnp.einsum('hqk,khd->qhd', probs, value_rows, precision=HIGH)
    starts = jnp.arange(count, dtype=jnp.int32) * BLOCK
    blocks = lax.map(jax.checkpoint(one_block), (queries.reshape(count, BLOCK, HEADS, HEAD_DIM), starts))
    return blocks.reshape(seq_len, HEADS * HEAD_DIM)

def forward(params, seq_rows, prefix_len):
    gain_one, shift_one, query_w, query_b, key_w, value_w, value_b, out_w, out_b, gain_two, shift_two, up_w, up_b, down_w, down_b = params
    seq_len = seq_rows.shape[0]
    normed = low(layer_norm(seq_rows, gain_one, shift_one))
    queries = low_back(low(matmul(normed, query_w) + query_b))
    key_rows = low_back(low(matmul(normed, key_w)))
    value_rows = low_back(low(matmul(normed, value_w) + value_b))
    shaped = (seq_len, HEADS, HEAD_DIM)
    mixed = attention(queries.reshape(shaped), key_rows.reshape(shaped), value_rows.reshape(shaped), prefix_len)
    mixed = low_back(low(mixed))
    branch = low_back(matmul(mixed, out_w))
    residual = seq_rows + branch + out_b
    second = low(layer_norm(residual, gain_two, shift_two))
    hidden_pre = low_back(matmul(second, up_w) + up_b)
    hidden = low(jax.nn.gelu(hidden_pre, approximate=False))
    return residual + matmul(hidden, down_w) + down_b

def reference(inputs, prefix, ln1_gain, ln1_bias, query_weight, query_bias, key_weight, value_weight, value_bias, out_weight, out_bias, ln2_gain, ln2_bias, up_weight, up_bias, down_weight, down_bias, cotangent):
    params = tuple((array.astype(jnp.float32) for array in (ln1_gain, ln1_bias, query_weight, query_bias, key_weight, value_weight, value_bias, out_weight, out_bias, ln2_gain, ln2_bias, up_weight, up_bias, down_weight, down_bias)))
    flat_inputs = inputs.astype(jnp.float32).reshape(MICRO * SEQS, SEQ, D)
    flat_grads = cotangent.astype(jnp.float32).reshape(MICRO * SEQS, SEQ, D)
    flat_prefix = prefix.reshape(MICRO * SEQS).astype(jnp.int32)

    def one_sequence(totals, items):
        seq_rows, grad_rows, prefix_len = items

        def run_layer(weights, values):
            return forward(weights, values, prefix_len)
        result, pullback = jax.vjp(run_layer, params, seq_rows)
        weight_grads, input_part = pullback(grad_rows)
        totals = jax.tree.map(lambda left, right: left + right, totals, weight_grads)
        return (totals, (result, input_part))
    start_totals = jax.tree.map(jnp.zeros_like, params)
    totals, (results, input_parts) = lax.scan(one_sequence, start_totals, (flat_inputs, flat_grads, flat_prefix))
    out_shape = (MICRO, SEQS, SEQ, D)
    return (results.reshape(out_shape), input_parts.reshape(out_shape), totals[0], totals[1], totals[2], totals[3], totals[4], totals[5], totals[6], totals[7], totals[8], totals[9], totals[10], totals[11], totals[12], totals[13], totals[14])
```

```python
import math

import jax
import jax.numpy as jnp
from jax import lax
from jax.experimental import pallas as pl
from jax.experimental.pallas import tpu as pltpu
from jax.sharding import PartitionSpec as P

MESH = pl.DeviceIdType.MESH
LONGEST = 512

HEAD_DIM = 128
BLOCK = 512


EPSILON = 1e-05


def norm_forward(values, gain, shift):
    center = values - jnp.mean(values, axis=-1, keepdims=True)
    inverse = lax.rsqrt(jnp.mean(center * center, axis=-1, keepdims=True) + EPSILON)
    scaled = center * inverse
    return (scaled * gain + shift, scaled, inverse)


def norm_backward(grad_out, scaled, inverse, gain):
    weighted = grad_out * gain
    mean_plain = jnp.mean(weighted, axis=-1, keepdims=True)
    mean_scaled = jnp.mean(weighted * scaled, axis=-1, keepdims=True)
    return inverse * (weighted - mean_plain - scaled * mean_scaled)


def smooth_gate(values):
    return jax.nn.gelu(values, approximate=False)


def smooth_slope(values):
    normal_cdf = 0.5 * (1.0 + jax.scipy.special.erf(values / math.sqrt(2.0)))
    density = jnp.exp(-0.5 * values * values) / math.sqrt(2.0 * math.pi)
    return normal_cdf + values * density


def masked_scores(query_block, key_rows, start, prefix_len):
    scale = 1.0 / math.sqrt(key_rows.shape[2])
    scores = (
        jnp.einsum("qhd,khd->hqk", query_block, key_rows, preferred_element_type=jnp.float32)
        * scale
    )
    places = start + jnp.arange(query_block.shape[0], dtype=jnp.int32)
    columns = jnp.arange(key_rows.shape[0], dtype=jnp.int32)
    allowed = (columns[None, :] <= places[:, None]) | (columns[None, :] < prefix_len)
    return jnp.where(allowed[None], scores, -jnp.inf)


def attend_forward(queries, key_rows, value_rows, prefix_len):
    seq_len, heads_local, head_size = queries.shape
    count = seq_len // BLOCK

    def one_block(items):
        query_block, start = items
        scores = masked_scores(query_block, key_rows, start, prefix_len)
        peak = jnp.max(scores, axis=-1, keepdims=True)
        raw_weights = jnp.exp(scores - peak)
        totals = jnp.sum(raw_weights, axis=-1, keepdims=True)
        probs = (raw_weights / totals).astype(jnp.bfloat16)
        mixed = jnp.einsum("hqk,khd->qhd", probs, value_rows, preferred_element_type=jnp.float32)
        return (mixed.astype(jnp.bfloat16), (peak + jnp.log(totals))[..., 0])

    starts = jnp.arange(count, dtype=jnp.int32) * BLOCK
    mixed, log_totals = lax.map(
        one_block, (queries.reshape(count, BLOCK, heads_local, head_size), starts)
    )
    return (mixed.reshape(seq_len, heads_local * head_size), log_totals)


def attend_backward(queries, key_rows, value_rows, grad_mixed, log_totals, prefix_len):
    seq_len, heads_local, head_size = queries.shape
    count = seq_len // BLOCK
    scale = 1.0 / math.sqrt(head_size)

    def one_block(carry, items):
        key_total, value_total = carry
        query_block, grad_block, log_block, start = items
        scores = masked_scores(query_block, key_rows, start, prefix_len)
        probs = jnp.exp(scores - log_block[..., None])
        grad_probs = jnp.einsum(
            "qhd,khd->hqk", grad_block, value_rows, preferred_element_type=jnp.float32
        )
        inner = jnp.sum(probs * grad_probs, axis=-1, keepdims=True)
        grad_scores = (probs * (grad_probs - inner)).astype(jnp.bfloat16)
        grad_query = (
            jnp.einsum("hqk,khd->qhd", grad_scores, key_rows, preferred_element_type=jnp.float32)
            * scale
        )
        key_total = (
            key_total
            + jnp.einsum(
                "hqk,qhd->khd", grad_scores, query_block, preferred_element_type=jnp.float32
            )
            * scale
        )
        value_total = value_total + jnp.einsum(
            "hqk,qhd->khd",
            probs.astype(jnp.bfloat16),
            grad_block,
            preferred_element_type=jnp.float32,
        )
        return ((key_total, value_total), grad_query.astype(jnp.bfloat16))

    empty_total = jnp.zeros(queries.shape, jnp.float32)
    starts = jnp.arange(count, dtype=jnp.int32) * BLOCK
    blocked = (count, BLOCK, heads_local, head_size)
    (key_total, value_total), grad_queries = lax.scan(
        one_block,
        (empty_total, empty_total),
        (queries.reshape(blocked), grad_mixed.reshape(blocked), log_totals, starts),
    )
    width = heads_local * head_size
    return (
        grad_queries.reshape(seq_len, width),
        key_total.astype(jnp.bfloat16).reshape(seq_len, width),
        value_total.astype(jnp.bfloat16).reshape(seq_len, width),
    )


def body(
    inputs,
    prefix,
    ln1_gain,
    ln1_bias,
    query_weight,
    query_bias,
    key_weight,
    value_weight,
    value_bias,
    out_weight,
    out_bias,
    ln2_gain,
    ln2_bias,
    up_weight,
    up_bias,
    down_weight,
    down_bias,
    cotangent,
):
    local_width = query_weight.shape[1]
    local_hidden = up_weight.shape[1]
    shard_rows = inputs.shape[2]
    micro = inputs.shape[0]
    model_width = inputs.shape[3]
    heads_local = local_width // HEAD_DIM
    offset_width = lax.axis_index("tensor") * local_width
    offset_hidden = lax.axis_index("tensor") * local_hidden
    vectors = (
        lax.all_gather(ln1_gain, ("dp", "tensor"), axis=0, tiled=True),
        lax.all_gather(ln1_bias, ("dp", "tensor"), axis=0, tiled=True),
        lax.all_gather(query_bias, ("dp", "tensor"), axis=0, tiled=True),
        lax.all_gather(value_bias, ("dp", "tensor"), axis=0, tiled=True),
        lax.all_gather(out_bias, ("dp", "tensor"), axis=0, tiled=True),
        lax.all_gather(ln2_gain, ("dp", "tensor"), axis=0, tiled=True),
        lax.all_gather(ln2_bias, ("dp", "tensor"), axis=0, tiled=True),
        lax.all_gather(up_bias, ("dp", "tensor"), axis=0, tiled=True),
        lax.all_gather(down_bias, ("dp", "tensor"), axis=0, tiled=True),
    )
    (
        gain_one,
        shift_one,
        query_full_bias,
        value_full_bias,
        out_shift,
        gain_two,
        shift_two,
        up_full_bias,
        down_shift,
    ) = vectors
    query_shift = lax.dynamic_slice_in_dim(query_full_bias, offset_width, local_width)
    value_shift = lax.dynamic_slice_in_dim(value_full_bias, offset_width, local_width)
    up_shift = lax.dynamic_slice_in_dim(up_full_bias, offset_hidden, local_hidden)
    zero_width = jnp.zeros((model_width,), jnp.float32)
    gain_one_grad = zero_width
    shift_one_grad = zero_width
    query_bias_grad = zero_width
    value_bias_grad = zero_width
    out_bias_grad = zero_width
    gain_two_grad = zero_width
    shift_two_grad = zero_width
    up_bias_grad = jnp.zeros((up_full_bias.shape[0],), jnp.float32)
    down_bias_grad = zero_width
    weight_totals = None
    layer_rows = []
    input_rows = []
    for index in range(micro):
        gathered = (
            lax.all_gather(query_weight, "dp", axis=0, tiled=True),
            lax.all_gather(key_weight, "dp", axis=0, tiled=True),
            lax.all_gather(value_weight, "dp", axis=0, tiled=True),
            lax.all_gather(out_weight, "dp", axis=1, tiled=True),
            lax.all_gather(up_weight, "dp", axis=0, tiled=True),
            lax.all_gather(down_weight, "dp", axis=1, tiled=True),
        )
        full_query, full_key, full_value, full_out, full_up, full_down = gathered
        rows_in = inputs[index, 0].astype(jnp.float32)
        prefix_len = prefix[index, 0]
        normed, scaled_one, inverse_one = norm_forward(rows_in, gain_one, shift_one)
        normed_all = lax.all_gather(normed.astype(jnp.bfloat16), "tensor", axis=0, tiled=True)
        seq_len = normed_all.shape[0]
        queries = (
            jnp.dot(normed_all, full_query, preferred_element_type=jnp.float32) + query_shift
        ).astype(jnp.bfloat16)
        key_rows = jnp.dot(normed_all, full_key, preferred_element_type=jnp.float32).astype(
            jnp.bfloat16
        )
        value_rows = (
            jnp.dot(normed_all, full_value, preferred_element_type=jnp.float32) + value_shift
        ).astype(jnp.bfloat16)
        head_shape = (seq_len, heads_local, HEAD_DIM)
        queries_h = queries.reshape(head_shape)
        keys_h = key_rows.reshape(head_shape)
        values_h = value_rows.reshape(head_shape)
        attended, log_totals = attend_forward(queries_h, keys_h, values_h, prefix_len)
        attention_share = lax.psum_scatter(
            jnp.dot(attended, full_out, preferred_element_type=jnp.float32).astype(jnp.bfloat16),
            "tensor",
            scatter_dimension=0,
            tiled=True,
        ).astype(jnp.float32)
        residual = rows_in + attention_share + out_shift
        second, scaled_two, inverse_two = norm_forward(residual, gain_two, shift_two)
        grad_rows = cotangent[index, 0]
        down_bias_grad = down_bias_grad + jnp.sum(grad_rows.astype(jnp.float32), axis=0)
        second_all = lax.all_gather(second.astype(jnp.bfloat16), "tensor", axis=0, tiled=True)
        hidden_pre = jnp.dot(second_all, full_up, preferred_element_type=jnp.float32) + up_shift
        hidden_act = smooth_gate(hidden_pre).astype(jnp.bfloat16)
        feed_share = lax.psum_scatter(
            jnp.dot(hidden_act, full_down, preferred_element_type=jnp.float32).astype(jnp.bfloat16),
            "tensor",
            scatter_dimension=0,
            tiled=True,
        ).astype(jnp.float32)
        layer_rows.append(residual + feed_share + down_shift)
        grad_all = lax.all_gather(grad_rows, "tensor", axis=0, tiled=True)
        down_grad = jnp.dot(hidden_act.T, grad_all, preferred_element_type=jnp.float32)
        grad_act = jnp.dot(grad_all, full_down.T, preferred_element_type=jnp.float32)
        grad_pre = (grad_act * smooth_slope(hidden_pre)).astype(jnp.bfloat16)
        up_grad = jnp.dot(second_all.T, grad_pre, preferred_element_type=jnp.float32)
        up_part = jnp.sum(grad_pre.astype(jnp.float32), axis=0)
        up_bias_grad = up_bias_grad + lax.dynamic_update_slice(
            jnp.zeros_like(up_bias_grad), up_part, (offset_hidden,)
        )
        grad_second = lax.psum_scatter(
            jnp.dot(grad_pre, full_up.T, preferred_element_type=jnp.float32).astype(jnp.bfloat16),
            "tensor",
            scatter_dimension=0,
            tiled=True,
        ).astype(jnp.float32)
        gain_two_grad = gain_two_grad + jnp.sum(grad_second * scaled_two, axis=0)
        shift_two_grad = shift_two_grad + jnp.sum(grad_second, axis=0)
        grad_residual = grad_rows.astype(jnp.float32) + norm_backward(
            grad_second, scaled_two, inverse_two, gain_two
        )
        out_bias_grad = out_bias_grad + jnp.sum(grad_residual, axis=0)
        residual_all = lax.all_gather(
            grad_residual.astype(jnp.bfloat16), "tensor", axis=0, tiled=True
        )
        out_grad = jnp.dot(attended.T, residual_all, preferred_element_type=jnp.float32)
        grad_attended = jnp.dot(
            residual_all, full_out.T, preferred_element_type=jnp.float32
        ).astype(jnp.bfloat16)
        grad_queries, grad_keys, grad_values = attend_backward(
            queries_h, keys_h, values_h, grad_attended, log_totals, prefix_len
        )
        query_grad = jnp.dot(normed_all.T, grad_queries, preferred_element_type=jnp.float32)
        key_grad = jnp.dot(normed_all.T, grad_keys, preferred_element_type=jnp.float32)
        value_grad = jnp.dot(normed_all.T, grad_values, preferred_element_type=jnp.float32)
        query_part = jnp.sum(grad_queries.astype(jnp.float32), axis=0)
        value_part = jnp.sum(grad_values.astype(jnp.float32), axis=0)
        query_bias_grad = query_bias_grad + lax.dynamic_update_slice(
            zero_width, query_part, (offset_width,)
        )
        value_bias_grad = value_bias_grad + lax.dynamic_update_slice(
            zero_width, value_part, (offset_width,)
        )
        partial_sum = jnp.dot(grad_queries, full_query.T, preferred_element_type=jnp.float32)
        partial_sum = partial_sum + jnp.dot(
            grad_keys, full_key.T, preferred_element_type=jnp.float32
        )
        grad_normed = lax.psum_scatter(
            (
                partial_sum + jnp.dot(grad_values, full_value.T, preferred_element_type=jnp.float32)
            ).astype(jnp.bfloat16),
            "tensor",
            scatter_dimension=0,
            tiled=True,
        ).astype(jnp.float32)
        gain_one_grad = gain_one_grad + jnp.sum(grad_normed * scaled_one, axis=0)
        shift_one_grad = shift_one_grad + jnp.sum(grad_normed, axis=0)
        input_rows.append(
            grad_residual + norm_backward(grad_normed, scaled_one, inverse_one, gain_one)
        )
        reduced = (query_grad, key_grad, value_grad, out_grad, up_grad, down_grad)
        if weight_totals is None:
            weight_totals = reduced
        else:
            weight_totals = tuple((left + right for left, right in zip(weight_totals, reduced)))
    query_total, key_total, value_total, out_total, up_total, down_total = weight_totals
    query_total, key_total, value_total, out_total, up_total, down_total = (
        lax.psum_scatter(
            query_total.astype(jnp.bfloat16), "dp", scatter_dimension=0, tiled=True
        ).astype(jnp.float32),
        lax.psum_scatter(
            key_total.astype(jnp.bfloat16), "dp", scatter_dimension=0, tiled=True
        ).astype(jnp.float32),
        lax.psum_scatter(
            value_total.astype(jnp.bfloat16), "dp", scatter_dimension=0, tiled=True
        ).astype(jnp.float32),
        lax.psum_scatter(
            out_total.astype(jnp.bfloat16), "dp", scatter_dimension=1, tiled=True
        ).astype(jnp.float32),
        lax.psum_scatter(
            up_total.astype(jnp.bfloat16), "dp", scatter_dimension=0, tiled=True
        ).astype(jnp.float32),
        lax.psum_scatter(
            down_total.astype(jnp.bfloat16), "dp", scatter_dimension=1, tiled=True
        ).astype(jnp.float32),
    )
    vector_totals = (
        lax.psum_scatter(gain_one_grad, ("dp", "tensor"), scatter_dimension=0, tiled=True),
        lax.psum_scatter(shift_one_grad, ("dp", "tensor"), scatter_dimension=0, tiled=True),
        lax.psum_scatter(query_bias_grad, ("dp", "tensor"), scatter_dimension=0, tiled=True),
        lax.psum_scatter(value_bias_grad, ("dp", "tensor"), scatter_dimension=0, tiled=True),
        lax.psum_scatter(out_bias_grad, ("dp", "tensor"), scatter_dimension=0, tiled=True),
        lax.psum_scatter(gain_two_grad, ("dp", "tensor"), scatter_dimension=0, tiled=True),
        lax.psum_scatter(shift_two_grad, ("dp", "tensor"), scatter_dimension=0, tiled=True),
        lax.psum_scatter(up_bias_grad, ("dp", "tensor"), scatter_dimension=0, tiled=True),
        lax.psum_scatter(down_bias_grad, ("dp", "tensor"), scatter_dimension=0, tiled=True),
    )
    (
        gain_one_out,
        shift_one_out,
        query_bias_out,
        value_bias_out,
        out_bias_out,
        gain_two_out,
        shift_two_out,
        up_bias_out,
        down_bias_out,
    ) = vector_totals
    out_shape = (micro, 1, shard_rows, model_width)
    layer_out = jnp.stack(layer_rows).reshape(out_shape)
    input_grad = jnp.stack(input_rows).reshape(out_shape)
    return (
        layer_out,
        input_grad,
        gain_one_out,
        shift_one_out,
        query_total,
        query_bias_out,
        key_total,
        value_total,
        value_bias_out,
        out_total,
        out_bias_out,
        gain_two_out,
        shift_two_out,
        up_total,
        up_bias_out,
        down_total,
        down_bias_out,
    )


def _place(z, y, x):
    return z * 4 + y * 2 + x


def _coords():
    dp = lax.axis_index("dp")
    core = lax.axis_index("tensor")
    return dp // 4, (dp // 2) % 2, dp % 2, core


def _greet(peers):
    barrier = pltpu.get_barrier_semaphore()
    for peer in peers:
        pl.semaphore_signal(barrier, inc=1, device_id=peer, device_id_type=MESH)
    pl.semaphore_wait(barrier, len(peers))


def _peers():
    z, y, x, core = _coords()
    along = [(_place((z + j) % 4, y, x), core) for j in (1, 2, 3)]
    across = (_place(z, y, 1 - x), core)
    down = (_place(z, 1 - y, x), core)
    sibling = (_place(z, y, x), 1 - core)
    return along, across, down, sibling


def _send(src, dst, send_sem, recv_sem, peer):
    copy = pltpu.make_async_remote_copy(
        src_ref=src,
        dst_ref=dst,
        send_sem=send_sem,
        recv_sem=recv_sem,
        device_id=peer,
        device_id_type=MESH,
    )
    copy.start()
    return copy


def _local(src, dst, sem):
    copy = pltpu.make_async_copy(src, dst, sem)
    copy.start()
    return copy


def gather_kernel(win, vec, xin, gin, full, vfull, xfull, gfull, ssem, rsem, lsem, vs, vr, vl, ws, wr, wl):
    z, y, x, core = _coords()
    along, across, down, sibling = _peers()
    _greet(along + [across, down, sibling])
    chunks = win.shape[0]
    pending = []
    swaps = []
    for i, (part, whole) in enumerate(((xin, xfull), (gin, gfull))):
        swaps.append(_send(part.at[1 - core], whole.at[core], ws.at[i], wr.at[i], sibling))
        pending.append(_local(part.at[core], whole.at[core], wl.at[i]))
    lines = []
    for k in range(chunks):
        own = full.at[k, core, z, y, x]
        here = _local(win.at[k], own, lsem.at[k])
        lines.append(
            (here, [_send(win.at[k], own, ssem.at[k, j], rsem.at[k, j], along[j]) for j in range(3)])
        )
    vown = vfull.at[z, y, x, core]
    vline = (_local(vec, vown, vl.at[0]), [_send(vec, vown, vs.at[j], vr.at[j], along[j]) for j in range(3)])

    def stage_one(k):
        here, sends = lines[k]
        here.wait()
        for s in sends:
            s.wait()
        block = full.at[k, core, :, y, x]
        return [
            _send(block, block, ssem.at[k, 3], rsem.at[k, 3], across),
            _send(block, block, ssem.at[k, 4], rsem.at[k, 4], down),
        ]

    def stage_two(k, before):
        for s in before:
            s.wait()
        one = full.at[k, core, :, 1 - y, x, 0:32]
        two = full.at[k, core, :, y, 1 - x, 32:64]
        return [
            _send(one, one, ssem.at[k, 5], rsem.at[k, 5], across),
            _send(two, two, ssem.at[k, 6], rsem.at[k, 6], down),
        ]

    def stage_three(k, before):
        for s in before:
            s.wait()
        return _send(full.at[k, core], full.at[k, core], ssem.at[k, 7], rsem.at[k, 7], sibling)

    vline[0].wait()
    for s in vline[1]:
        s.wait()
    vblock = vfull.at[:, y, x, core]
    vone = [_send(vblock, vblock, vs.at[3], vr.at[3], across), _send(vblock, vblock, vs.at[4], vr.at[4], down)]
    first, second, third = {}, {}, {}
    lag = 2
    for t in range(chunks + 2 * lag):
        if t < chunks:
            first[t] = stage_one(t)
        if t == 0:
            for s in vone:
                s.wait()
            vblock = vfull.at[:, 1 - y, x, core]
            vtwo = _send(vblock, vblock, vs.at[5], vr.at[5], across)
        if t == 1:
            vtwo.wait()
            vblock = vfull.at[:, :, :, core]
            vthree = _send(vblock, vblock, vs.at[6], vr.at[6], sibling)
        if 0 <= t - lag < chunks:
            second[t - lag] = stage_two(t - lag, first[t - lag])
        if 0 <= t - 2 * lag < chunks:
            third[t - 2 * lag] = stage_three(t - 2 * lag, second[t - 2 * lag])
    for k in range(chunks):
        third[k].wait()
    vthree.wait()
    for s in swaps + pending:
        s.wait()


def gather(win, vec, xin, gin):
    chunks, rows, cols = win.shape
    hbm = pl.BlockSpec(memory_space=pltpu.HBM)
    dma = pltpu.SemaphoreType.DMA
    return pl.pallas_call(
        gather_kernel,
        out_shape=(
            jax.ShapeDtypeStruct((chunks, 2, 4, 2, 2, rows, cols), win.dtype),
            jax.ShapeDtypeStruct((4, 2, 2, 2) + vec.shape, vec.dtype),
            jax.ShapeDtypeStruct(xin.shape, xin.dtype),
            jax.ShapeDtypeStruct(gin.shape, gin.dtype),
        ),
        in_specs=[hbm] * 4,
        out_specs=(hbm,) * 4,
        scratch_shapes=[
            dma((chunks, 8)),
            dma((chunks, 8)),
            dma((chunks,)),
            dma((7,)),
            dma((7,)),
            dma((1,)),
            dma((2,)),
            dma((2,)),
            dma((2,)),
        ],
        compiler_params=pltpu.CompilerParams(collective_id=0, has_side_effects=True),
    )(win, vec, xin, gin)


def scatter_kernel(
    gq, gk, gv, go, gu, gd, vg, lo, ig,
    out, vout, lout, iout,
    acc, from_s, x_one, y_one, x_two, y_two, from_z,
    vacc, v_s, vx_one, vx_two, vy_two, v_z,
    ssem, rsem, lsem, vs, vr, vl, ws, wr, wl,
):
    z, y, x, core = _coords()
    along, across, down, sibling = _peers()
    _greet(along + [across, down, sibling])
    chunks = acc.shape[0]
    f32 = jnp.float32
    tail = []
    sources = [gq, gk, gv, go] + [gu.at[j] for j in range(4)] + [gd.at[j] for j in range(4)]
    order = list(range(chunks))
    begun = {}
    for k in order:
        begun[k] = (
            _local(sources[k].at[core], acc.at[k], lsem.at[k]),
            _send(sources[k].at[1 - core], from_s.at[k], ssem.at[k, 0], rsem.at[k, 0], sibling),
        )
        if k == 1:
            vbegun = (
                _local(vg.at[:, :, :, core], vacc, vl.at[0]),
                _send(vg.at[:, :, :, 1 - core], v_s, vs.at[0], vr.at[0], sibling),
            )
    for i, (rows, whole) in enumerate(((lo, lout), (ig, iout))):
        tail.append(_send(rows.at[1 - core], whole.at[core], ws.at[i], wr.at[i], sibling))
        tail.append(_local(rows.at[core], whole.at[core], wl.at[i]))

    def stage_one(k):
        for s in begun[k]:
            s.wait()

        @pl.loop(0, 4)
        def _(i):
            for j in range(2):
                for m in range(2):
                    acc[k, i, j, m] = (acc[k, i, j, m].astype(f32) + from_s[k, i, j, m].astype(f32)).astype(acc.dtype)

        return [
            _send(acc.at[k, :, 1 - y, 1 - x, 0:32], x_one.at[k], ssem.at[k, 1], rsem.at[k, 1], across),
            _send(acc.at[k, :, 1 - y, 1 - x, 32:64], y_one.at[k], ssem.at[k, 2], rsem.at[k, 2], down),
        ]

    def stage_two(k, before):
        for s in before:
            s.wait()
        acc[k, :, 1 - y, x, 0:32] = (acc[k, :, 1 - y, x, 0:32].astype(f32) + x_one[k].astype(f32)).astype(acc.dtype)
        acc[k, :, y, 1 - x, 32:64] = (acc[k, :, y, 1 - x, 32:64].astype(f32) + y_one[k].astype(f32)).astype(acc.dtype)
        return [
            _send(acc.at[k, :, y, 1 - x], x_two.at[k], ssem.at[k, 3], rsem.at[k, 3], across),
            _send(acc.at[k, :, 1 - y, x], y_two.at[k], ssem.at[k, 4], rsem.at[k, 4], down),
        ]

    def stage_three(k, before):
        for s in before:
            s.wait()
        acc[k, :, y, x] = (acc[k, :, y, x].astype(f32) + x_two[k].astype(f32) + y_two[k].astype(f32)).astype(acc.dtype)
        return [
            _send(acc.at[k, (z + j + 1) % 4, y, x], from_z.at[k, j], ssem.at[k, 5 + j], rsem.at[k, 5 + j], along[j])
            for j in range(3)
        ]

    def stage_four(k, before):
        for s in before:
            s.wait()
        total = acc[k, z, y, x].astype(f32)
        for j in range(3):
            total = total + from_z[k, j].astype(f32)
        out[k] = total

    lag = 1
    first, second, third = {}, {}, {}
    for t in range(chunks + 3 * lag):
        if t < chunks:
            first[t] = stage_one(order[t])
        if 0 <= t - lag < chunks:
            second[t - lag] = stage_two(order[t - lag], first[t - lag])
        if 0 <= t - 2 * lag < chunks:
            third[t - 2 * lag] = stage_three(order[t - 2 * lag], second[t - 2 * lag])
        if 0 <= t - 3 * lag < chunks:
            stage_four(order[t - 3 * lag], third[t - 3 * lag])
        if t == 0:
            for s in vbegun:
                s.wait()
            vacc[...] = vacc[...] + v_s[...]
            vone = _send(vacc.at[:, 1 - y, 1 - x], vx_one, vs.at[1], vr.at[1], across)
        if t == 2:
            vone.wait()
            vacc[:, 1 - y, x] = vacc[:, 1 - y, x] + vx_one[...]
            vtwo = [
                _send(vacc.at[:, y, 1 - x], vx_two, vs.at[2], vr.at[2], across),
                _send(vacc.at[:, 1 - y, x], vy_two, vs.at[3], vr.at[3], down),
            ]
        if t == 4:
            for s in vtwo:
                s.wait()
            vacc[:, y, x] = vacc[:, y, x] + vx_two[...] + vy_two[...]
            vthree = [
                _send(vacc.at[(z + j + 1) % 4, y, x], v_z.at[j], vs.at[4 + j], vr.at[4 + j], along[j])
                for j in range(3)
            ]
        if t == 6:
            for s in vthree:
                s.wait()
            vout[...] = vacc[z, y, x] + v_z[0] + v_z[1] + v_z[2]
    for s in tail:
        s.wait()


def scatter(gq, gk, gv, go, gu, gd, vg, lo, ig):
    chunks = 4 + gu.shape[0] + gd.shape[0]
    rows, cols = gq.shape[-2:]
    bf16, f32 = jnp.bfloat16, jnp.float32
    hbm = pl.BlockSpec(memory_space=pltpu.HBM)
    vmem = pl.BlockSpec(memory_space=pltpu.VMEM)
    dma = pltpu.SemaphoreType.DMA
    small = vg.shape[-2:]
    return pl.pallas_call(
        scatter_kernel,
        out_shape=(
            jax.ShapeDtypeStruct((chunks, rows, cols), f32),
            jax.ShapeDtypeStruct(small, f32),
            jax.ShapeDtypeStruct(lo.shape, lo.dtype),
            jax.ShapeDtypeStruct(ig.shape, ig.dtype),
        ),
        in_specs=[hbm] * 9,
        out_specs=(vmem, vmem, hbm, hbm),
        scratch_shapes=[
            pltpu.VMEM((chunks, 4, 2, 2, rows, cols), bf16),
            pltpu.VMEM((chunks, 4, 2, 2, rows, cols), bf16),
            pltpu.VMEM((chunks, 4, rows // 2, cols), bf16),
            pltpu.VMEM((chunks, 4, rows // 2, cols), bf16),
            pltpu.VMEM((chunks, 4, rows, cols), bf16),
            pltpu.VMEM((chunks, 4, rows, cols), bf16),
            pltpu.VMEM((chunks, 3, rows, cols), bf16),
            pltpu.VMEM((4, 2, 2) + small, f32),
            pltpu.VMEM((4, 2, 2) + small, f32),
            pltpu.VMEM((4,) + small, f32),
            pltpu.VMEM((4,) + small, f32),
            pltpu.VMEM((4,) + small, f32),
            pltpu.VMEM((3,) + small, f32),
            dma((chunks, 8)),
            dma((chunks, 8)),
            dma((chunks,)),
            dma((7,)),
            dma((7,)),
            dma((1,)),
            dma((2,)),
            dma((2,)),
            dma((2,)),
        ],
        compiler_params=pltpu.CompilerParams(
            collective_id=1, has_side_effects=True, vmem_limit_bytes=56 * 1024 * 1024
        ),
    )(gq, gk, gv, go, gu, gd, vg, lo, ig)


def _dot(left, right, contract):
    return lax.dot_general(left, right, (contract, ((), ())), preferred_element_type=jnp.float32)


NN = ((1,), (0,))
NT = ((1,), (1,))
TN = ((0,), (0,))
LOG2E = 1.4426950408889634


def _spans(seq_len, longest, step):
    spans = []
    for start in range(0, seq_len, step):
        spans.append((start, max(longest, start + step)))
    return spans


def attend_kernel(prefix, q, k, v, mixed, probs):
    seq_len = q.shape[1]
    step = 256
    factor = LOG2E / math.sqrt(HEAD_DIM)
    prefix_len = prefix[0]
    for start, stop in _spans(seq_len, LONGEST, step):
        query = q[0, start : start + step]
        scores = _dot(k[0, :stop], query, NT)
        rows = lax.broadcasted_iota(jnp.int32, scores.shape, 0)
        columns = lax.broadcasted_iota(jnp.int32, scores.shape, 1) + start
        scores = jnp.where((rows <= columns) | (rows < prefix_len), scores, -jnp.inf)
        peak = jnp.max(scores, axis=0, keepdims=True)
        weights = jnp.exp2((scores - peak) * factor)
        total = jnp.sum(weights, axis=0, keepdims=True)
        weights = (weights * (1.0 / total)).astype(jnp.bfloat16)
        probs[0, :stop, start : start + step] = weights
        mixed[0, start : start + step] = _dot(weights, v[0, :stop], TN).astype(jnp.bfloat16)


def attend(prefix_len, q, k, v):
    groups, seq_len, width = q.shape
    per = width // HEAD_DIM
    head = pl.BlockSpec((1, seq_len, HEAD_DIM), lambda h, p: (h // per, 0, h % per))
    heads = groups * per
    return pl.pallas_call(
        attend_kernel,
        grid_spec=pltpu.PrefetchScalarGridSpec(
            num_scalar_prefetch=1,
            grid=(heads,),
            in_specs=[head] * 3,
            out_specs=(head, pl.BlockSpec((1, seq_len, seq_len), lambda h, p: (h, 0, 0))),
        ),
        out_shape=(
            jax.ShapeDtypeStruct(q.shape, jnp.bfloat16),
            jax.ShapeDtypeStruct((heads, seq_len, seq_len), jnp.bfloat16),
        ),
        compiler_params=pltpu.CompilerParams(vmem_limit_bytes=40 * 1024 * 1024),
    )(prefix_len, q, k, v)


def attend_back_kernel(q, k, v, probs, dmix, dq, dk, dv, dk_acc, dv_acc):
    seq_len = q.shape[1]
    step = 256
    scale = 1.0 / math.sqrt(HEAD_DIM)
    dk_acc[...] = jnp.zeros_like(dk_acc)
    dv_acc[...] = jnp.zeros_like(dv_acc)
    for start, stop in _spans(seq_len, LONGEST, step):
        grad = dmix[0, start : start + step]
        weights_low = probs[0, :stop, start : start + step]
        weights = weights_low.astype(jnp.float32)
        dprobs = _dot(v[0, :stop], grad, NT)
        inner = jnp.sum(weights * dprobs, axis=0, keepdims=True)
        dscores = (weights * (dprobs - inner)).astype(jnp.bfloat16)
        dq[0, start : start + step] = (_dot(dscores, k[0, :stop], TN) * scale).astype(jnp.bfloat16)
        dk_acc[:stop] += _dot(dscores, q[0, start : start + step], NN)
        dv_acc[:stop] += _dot(weights_low, grad, NN)
    dk[0] = (dk_acc[...] * scale).astype(jnp.bfloat16)
    dv[0] = dv_acc[...].astype(jnp.bfloat16)


def attend_back(q, k, v, probs, dmix):
    groups, seq_len, width = q.shape
    per = width // HEAD_DIM
    head = pl.BlockSpec((1, seq_len, HEAD_DIM), lambda h: (h // per, 0, h % per))
    heads = groups * per
    return pl.pallas_call(
        attend_back_kernel,
        grid=(heads,),
        in_specs=[head] * 3 + [pl.BlockSpec((1, seq_len, seq_len), lambda h: (h, 0, 0)), head],
        out_specs=(head,) * 3,
        out_shape=(jax.ShapeDtypeStruct(q.shape, jnp.bfloat16),) * 3,
        scratch_shapes=[pltpu.VMEM((seq_len, HEAD_DIM), jnp.float32)] * 2,
        compiler_params=pltpu.CompilerParams(vmem_limit_bytes=40 * 1024 * 1024),
    )(q, k, v, probs, dmix)


def feed_kernel(second, second_t, grad, grad_t, up, down, bias, fed, gsec, gup, gdown, gbias, hid, gpre):
    step = 256
    first = pl.program_id(0) == 0

    @pl.loop(0, second.shape[0] // step)
    def _(i):
        rows = pl.ds(pl.multiple_of(i * step, step), step)
        pre = _dot(second[rows], up[0, 0], NN) + bias[0]
        phi = 0.5 * (1.0 + lax.erf(pre * (1.0 / math.sqrt(2.0))))
        density = jnp.exp2(pre * pre * (-0.5 * LOG2E)) * (1.0 / math.sqrt(2.0 * math.pi))
        act = (pre * phi).astype(jnp.bfloat16)
        slope = phi + pre * density
        back = (_dot(grad[rows], down[0, 0], NN) * slope).astype(jnp.bfloat16)
        hid[rows] = act
        gpre[rows] = back
        fed_part = _dot(act, down[0, 0], NT)
        gsec_part = _dot(back, up[0, 0], NT)
        fed[rows] = jnp.where(first, fed_part, fed[rows] + fed_part)
        gsec[rows] = jnp.where(first, gsec_part, gsec[rows] + gsec_part)
        part = jnp.sum(back.astype(jnp.float32), axis=0, keepdims=True)
        gbias[0] = jnp.where(i == 0, part, gbias[0] + part)

    gup[0, 0] = _dot(second_t[...], gpre[...], NN).astype(jnp.bfloat16)
    gdown[0, 0] = _dot(grad_t[...], hid[...], NN).astype(jnp.bfloat16)


def feed(second, second_t, grad, grad_t, weights, bias, up_at, down_at):
    seq_len, model = second.shape
    chunks, cols = bias.shape[0], bias.shape[2]
    whole = pl.BlockSpec((seq_len, model), lambda i: (0, 0))
    whole_t = pl.BlockSpec((model, seq_len), lambda i: (0, 0))
    bf16, f32 = jnp.bfloat16, jnp.float32
    grads = pl.BlockSpec((1, 1, model, cols), lambda i: (i // 2, i % 2, 0, 0))
    line = pl.BlockSpec((1, 1, cols), lambda i: (i, 0, 0))
    return pl.pallas_call(
        feed_kernel,
        grid=(chunks,),
        in_specs=[
            whole,
            whole_t,
            whole,
            whole_t,
            pl.BlockSpec((1, 1, model, cols), lambda i: (up_at + i // 2, i % 2, 0, 0)),
            pl.BlockSpec((1, 1, model, cols), lambda i: (down_at + i // 2, i % 2, 0, 0)),
            line,
        ],
        out_specs=(whole, whole, grads, grads, line),
        out_shape=(
            jax.ShapeDtypeStruct((seq_len, model), f32),
            jax.ShapeDtypeStruct((seq_len, model), f32),
            jax.ShapeDtypeStruct((chunks // 2, 2, model, cols), bf16),
            jax.ShapeDtypeStruct((chunks // 2, 2, model, cols), bf16),
            jax.ShapeDtypeStruct((chunks, 1, cols), f32),
        ),
        scratch_shapes=[pltpu.VMEM((seq_len, cols), bf16)] * 2,
        compiler_params=pltpu.CompilerParams(vmem_limit_bytes=56 * 1024 * 1024),
    )(second, second_t, grad, grad_t, weights, weights, bias)


def fast_body(
    inputs, prefix, ln1_gain, ln1_bias, query_weight, query_bias, key_weight, value_weight, value_bias,
    out_weight, out_bias, ln2_gain, ln2_bias, up_weight, up_bias, down_weight, down_bias, cotangent,
):
    bf16, f32 = jnp.bfloat16, jnp.float32
    core = lax.axis_index("tensor")
    half, model = inputs.shape[2], inputs.shape[3]
    rows, cols = query_weight.shape
    seq_len = 2 * half
    ff_chunks = up_weight.shape[1] // cols

    def split(matrix):
        return matrix.reshape(rows, ff_chunks, cols).transpose(1, 0, 2)

    win = jnp.concatenate(
        [jnp.stack([query_weight, key_weight, value_weight, out_weight.T]), split(up_weight), split(down_weight.T)]
    )
    names = (ln1_gain, ln1_bias, query_bias, value_bias, out_bias, ln2_gain, ln2_bias, down_bias)
    small = jnp.concatenate(names + (up_bias,)).reshape(3, 128)
    vec = jnp.pad(small, ((0, 5), (0, 0)))
    full, vfull, x_rows, grad_rows = gather(win, vec, inputs[:, 0], cotangent[:, 0])
    weights = full.reshape(full.shape[0], 2, model, cols)
    parts = vfull.reshape(32, 8 * 128)
    lines = parts[:, :256].reshape(32, 8, 32).transpose(1, 0, 2).reshape(8, model)
    gain_one, shift_one, query_shift, value_shift, out_shift, gain_two, shift_two, down_shift = (
        lines[i] for i in range(8)
    )
    up_shift = parts[:, 256:384].reshape(2, ff_chunks, 1, cols).transpose(1, 0, 2, 3).reshape(2 * ff_chunks, 1, cols)

    x = x_rows.reshape(seq_len, model).astype(f32)
    grad_low = grad_rows.reshape(seq_len, model)
    grad = grad_low.astype(f32)
    normed_f, scaled_one, inverse_one = norm_forward(x, gain_one, shift_one)
    normed = normed_f.astype(bf16)

    def project(k, shift):
        value = jnp.stack([jnp.dot(normed, weights[k, c], preferred_element_type=f32) for c in range(2)])
        if shift is not None:
            value = value + shift.reshape(2, 1, cols)
        return value.astype(bf16)

    queries, keys, values = project(0, query_shift), project(1, None), project(2, value_shift)
    prefix_len = lax.dynamic_slice_in_dim(prefix[:, 0], core, 1)
    mixed, probs = attend(prefix_len, queries, keys, values)

    def back(k, pieces):
        return sum(
            lax.dot_general(pieces[c], weights[k, c], (NT, ((), ())), preferred_element_type=f32) for c in range(2)
        )

    def weight_grad(left, pieces):
        return jnp.stack(
            [
                lax.dot_general(left, pieces[c], (TN, ((), ())), preferred_element_type=f32).astype(bf16)
                for c in range(2)
            ]
        ).reshape(2, 4, 2, 2, rows, cols)

    residual = x + back(3, mixed) + out_shift
    second_f, scaled_two, inverse_two = norm_forward(residual, gain_two, shift_two)
    second = second_f.astype(bf16)
    fed, grad_second, gup, gdown, gup_bias = feed(
        second, second.T, grad_low, grad_low.T, weights, up_shift, 4, 4 + ff_chunks
    )
    layer_rows = residual + fed + down_shift
    grad_residual = grad + norm_backward(grad_second, scaled_two, inverse_two, gain_two)
    grad_res_low = grad_residual.astype(bf16)
    grad_mixed = jnp.stack(
        [jnp.dot(grad_res_low, weights[3, c], preferred_element_type=f32).astype(bf16) for c in range(2)]
    )
    gout = weight_grad(grad_res_low, mixed)
    gqueries, gkeys, gvalues = attend_back(queries, keys, values, probs, grad_mixed)
    gq, gk, gv = (weight_grad(normed, g) for g in (gqueries, gkeys, gvalues))
    grad_normed = back(0, gqueries) + back(1, gkeys) + back(2, gvalues)
    input_rows = grad_residual + norm_backward(grad_normed, scaled_one, inverse_one, gain_one)

    def column_sum(pieces):
        return jnp.sum(pieces.astype(f32), axis=1).reshape(model)

    sums = (
        jnp.sum(grad_normed * scaled_one, axis=0),
        jnp.sum(grad_normed, axis=0),
        column_sum(gqueries),
        column_sum(gvalues),
        jnp.sum(grad_residual, axis=0),
        jnp.sum(grad_second * scaled_two, axis=0),
        jnp.sum(grad_second, axis=0),
        jnp.sum(grad, axis=0),
    )
    vector = jnp.stack(sums).reshape(8, 32, 32).transpose(1, 0, 2).reshape(32, 256)
    up_vector = gup_bias.reshape(ff_chunks, 2, cols).transpose(1, 0, 2).reshape(32, 128)
    vg = jnp.pad(jnp.concatenate([vector, up_vector], axis=1), ((0, 0), (0, 640)))
    vg = vg.reshape(4, 2, 2, 2, 8, 128)
    seven = (ff_chunks, 2, 4, 2, 2, rows, cols)
    out, vout, layer_out, input_grad = scatter(
        gq, gk, gv, gout, gup.reshape(seven), gdown.reshape(seven), vg,
        layer_rows.reshape(2, half, model), input_rows.reshape(2, half, model),
    )
    flat = vout.reshape(-1)
    vectors = [flat[32 * i : 32 * i + 32] for i in range(8)]

    def join(pieces):
        return pieces.transpose(1, 0, 2).reshape(rows, ff_chunks * cols)

    return (
        layer_out.reshape(2, 1, half, model),
        input_grad.reshape(2, 1, half, model),
        vectors[0],
        vectors[1],
        out[0],
        vectors[2],
        out[1],
        out[2],
        vectors[3],
        out[3].T,
        vectors[4],
        vectors[5],
        vectors[6],
        join(out[4 : 4 + ff_chunks]),
        flat[256:384],
        join(out[4 + ff_chunks :]).T,
        vectors[7],
    )


def solution(mesh):
    in_specs = (
        P(None, "dp", "tensor", None),
        P(None, "dp"),
        P(("dp", "tensor")),
        P(("dp", "tensor")),
        P("dp", "tensor"),
        P(("dp", "tensor")),
        P("dp", "tensor"),
        P("dp", "tensor"),
        P(("dp", "tensor")),
        P("tensor", "dp"),
        P(("dp", "tensor")),
        P(("dp", "tensor")),
        P(("dp", "tensor")),
        P("dp", "tensor"),
        P(("dp", "tensor")),
        P("tensor", "dp"),
        P(("dp", "tensor")),
        P(None, "dp", "tensor", None),
    )
    out_specs = (
        P(None, "dp", "tensor", None),
        P(None, "dp", "tensor", None),
        P(("dp", "tensor")),
        P(("dp", "tensor")),
        P("dp", "tensor"),
        P(("dp", "tensor")),
        P("dp", "tensor"),
        P("dp", "tensor"),
        P(("dp", "tensor")),
        P("tensor", "dp"),
        P(("dp", "tensor")),
        P(("dp", "tensor")),
        P(("dp", "tensor")),
        P("dp", "tensor"),
        P(("dp", "tensor")),
        P("tensor", "dp"),
        P(("dp", "tensor")),
    )
    sizes = (mesh.shape["dp"], mesh.shape["tensor"])
    chosen = fast_body if sizes == (16, 2) else body
    return jax.shard_map(chosen, mesh=mesh, in_specs=in_specs, out_specs=out_specs, check_vma=False)
```

```python
import math

import jax
import jax.numpy as jnp
from jax import lax
from jax.experimental import pallas as pl
from jax.experimental.pallas import tpu as pltpu
from jax.sharding import PartitionSpec as P

MESH = pl.DeviceIdType.MESH
LONGEST = 512
HELD = 3

HEAD_DIM = 128
BLOCK = 512


EPSILON = 1e-05


def norm_forward(values, gain, shift):
    center = values - jnp.mean(values, axis=-1, keepdims=True)
    inverse = lax.rsqrt(jnp.mean(center * center, axis=-1, keepdims=True) + EPSILON)
    scaled = center * inverse
    return (scaled * gain + shift, scaled, inverse)


def norm_backward(grad_out, scaled, inverse, gain):
    weighted = grad_out * gain
    mean_plain = jnp.mean(weighted, axis=-1, keepdims=True)
    mean_scaled = jnp.mean(weighted * scaled, axis=-1, keepdims=True)
    return inverse * (weighted - mean_plain - scaled * mean_scaled)


def smooth_gate(values):
    return jax.nn.gelu(values, approximate=False)


def smooth_slope(values):
    normal_cdf = 0.5 * (1.0 + jax.scipy.special.erf(values / math.sqrt(2.0)))
    density = jnp.exp(-0.5 * values * values) / math.sqrt(2.0 * math.pi)
    return normal_cdf + values * density


def masked_scores(query_block, key_rows, start, prefix_len):
    scale = 1.0 / math.sqrt(key_rows.shape[2])
    scores = (
        jnp.einsum("qhd,khd->hqk", query_block, key_rows, preferred_element_type=jnp.float32)
        * scale
    )
    places = start + jnp.arange(query_block.shape[0], dtype=jnp.int32)
    columns = jnp.arange(key_rows.shape[0], dtype=jnp.int32)
    allowed = (columns[None, :] <= places[:, None]) | (columns[None, :] < prefix_len)
    return jnp.where(allowed[None], scores, -jnp.inf)


def attend_forward(queries, key_rows, value_rows, prefix_len):
    seq_len, heads_local, head_size = queries.shape
    count = seq_len // BLOCK

    def one_block(items):
        query_block, start = items
        scores = masked_scores(query_block, key_rows, start, prefix_len)
        peak = jnp.max(scores, axis=-1, keepdims=True)
        raw_weights = jnp.exp(scores - peak)
        totals = jnp.sum(raw_weights, axis=-1, keepdims=True)
        probs = (raw_weights / totals).astype(jnp.bfloat16)
        mixed = jnp.einsum("hqk,khd->qhd", probs, value_rows, preferred_element_type=jnp.float32)
        return (mixed.astype(jnp.bfloat16), (peak + jnp.log(totals))[..., 0])

    starts = jnp.arange(count, dtype=jnp.int32) * BLOCK
    mixed, log_totals = lax.map(
        one_block, (queries.reshape(count, BLOCK, heads_local, head_size), starts)
    )
    return (mixed.reshape(seq_len, heads_local * head_size), log_totals)


def attend_backward(queries, key_rows, value_rows, grad_mixed, log_totals, prefix_len):
    seq_len, heads_local, head_size = queries.shape
    count = seq_len // BLOCK
    scale = 1.0 / math.sqrt(head_size)

    def one_block(carry, items):
        key_total, value_total = carry
        query_block, grad_block, log_block, start = items
        scores = masked_scores(query_block, key_rows, start, prefix_len)
        probs = jnp.exp(scores - log_block[..., None])
        grad_probs = jnp.einsum(
            "qhd,khd->hqk", grad_block, value_rows, preferred_element_type=jnp.float32
        )
        inner = jnp.sum(probs * grad_probs, axis=-1, keepdims=True)
        grad_scores = (probs * (grad_probs - inner)).astype(jnp.bfloat16)
        grad_query = (
            jnp.einsum("hqk,khd->qhd", grad_scores, key_rows, preferred_element_type=jnp.float32)
            * scale
        )
        key_total = (
            key_total
            + jnp.einsum(
                "hqk,qhd->khd", grad_scores, query_block, preferred_element_type=jnp.float32
            )
            * scale
        )
        value_total = value_total + jnp.einsum(
            "hqk,qhd->khd",
            probs.astype(jnp.bfloat16),
            grad_block,
            preferred_element_type=jnp.float32,
        )
        return ((key_total, value_total), grad_query.astype(jnp.bfloat16))

    empty_total = jnp.zeros(queries.shape, jnp.float32)
    starts = jnp.arange(count, dtype=jnp.int32) * BLOCK
    blocked = (count, BLOCK, heads_local, head_size)
    (key_total, value_total), grad_queries = lax.scan(
        one_block,
        (empty_total, empty_total),
        (queries.reshape(blocked), grad_mixed.reshape(blocked), log_totals, starts),
    )
    width = heads_local * head_size
    return (
        grad_queries.reshape(seq_len, width),
        key_total.astype(jnp.bfloat16).reshape(seq_len, width),
        value_total.astype(jnp.bfloat16).reshape(seq_len, width),
    )


def body(
    inputs,
    prefix,
    ln1_gain,
    ln1_bias,
    query_weight,
    query_bias,
    key_weight,
    value_weight,
    value_bias,
    out_weight,
    out_bias,
    ln2_gain,
    ln2_bias,
    up_weight,
    up_bias,
    down_weight,
    down_bias,
    cotangent,
):
    local_width = query_weight.shape[1]
    local_hidden = up_weight.shape[1]
    shard_rows = inputs.shape[2]
    micro = inputs.shape[0]
    model_width = inputs.shape[3]
    heads_local = local_width // HEAD_DIM
    offset_width = lax.axis_index("tensor") * local_width
    offset_hidden = lax.axis_index("tensor") * local_hidden
    vectors = (
        lax.all_gather(ln1_gain, ("dp", "tensor"), axis=0, tiled=True),
        lax.all_gather(ln1_bias, ("dp", "tensor"), axis=0, tiled=True),
        lax.all_gather(query_bias, ("dp", "tensor"), axis=0, tiled=True),
        lax.all_gather(value_bias, ("dp", "tensor"), axis=0, tiled=True),
        lax.all_gather(out_bias, ("dp", "tensor"), axis=0, tiled=True),
        lax.all_gather(ln2_gain, ("dp", "tensor"), axis=0, tiled=True),
        lax.all_gather(ln2_bias, ("dp", "tensor"), axis=0, tiled=True),
        lax.all_gather(up_bias, ("dp", "tensor"), axis=0, tiled=True),
        lax.all_gather(down_bias, ("dp", "tensor"), axis=0, tiled=True),
    )
    (
        gain_one,
        shift_one,
        query_full_bias,
        value_full_bias,
        out_shift,
        gain_two,
        shift_two,
        up_full_bias,
        down_shift,
    ) = vectors
    query_shift = lax.dynamic_slice_in_dim(query_full_bias, offset_width, local_width)
    value_shift = lax.dynamic_slice_in_dim(value_full_bias, offset_width, local_width)
    up_shift = lax.dynamic_slice_in_dim(up_full_bias, offset_hidden, local_hidden)
    zero_width = jnp.zeros((model_width,), jnp.float32)
    gain_one_grad = zero_width
    shift_one_grad = zero_width
    query_bias_grad = zero_width
    value_bias_grad = zero_width
    out_bias_grad = zero_width
    gain_two_grad = zero_width
    shift_two_grad = zero_width
    up_bias_grad = jnp.zeros((up_full_bias.shape[0],), jnp.float32)
    down_bias_grad = zero_width
    weight_totals = None
    layer_rows = []
    input_rows = []
    for index in range(micro):
        gathered = (
            lax.all_gather(query_weight, "dp", axis=0, tiled=True),
            lax.all_gather(key_weight, "dp", axis=0, tiled=True),
            lax.all_gather(value_weight, "dp", axis=0, tiled=True),
            lax.all_gather(out_weight, "dp", axis=1, tiled=True),
            lax.all_gather(up_weight, "dp", axis=0, tiled=True),
            lax.all_gather(down_weight, "dp", axis=1, tiled=True),
        )
        full_query, full_key, full_value, full_out, full_up, full_down = gathered
        rows_in = inputs[index, 0].astype(jnp.float32)
        prefix_len = prefix[index, 0]
        normed, scaled_one, inverse_one = norm_forward(rows_in, gain_one, shift_one)
        normed_all = lax.all_gather(normed.astype(jnp.bfloat16), "tensor", axis=0, tiled=True)
        seq_len = normed_all.shape[0]
        queries = (
            jnp.dot(normed_all, full_query, preferred_element_type=jnp.float32) + query_shift
        ).astype(jnp.bfloat16)
        key_rows = jnp.dot(normed_all, full_key, preferred_element_type=jnp.float32).astype(
            jnp.bfloat16
        )
        value_rows = (
            jnp.dot(normed_all, full_value, preferred_element_type=jnp.float32) + value_shift
        ).astype(jnp.bfloat16)
        head_shape = (seq_len, heads_local, HEAD_DIM)
        queries_h = queries.reshape(head_shape)
        keys_h = key_rows.reshape(head_shape)
        values_h = value_rows.reshape(head_shape)
        attended, log_totals = attend_forward(queries_h, keys_h, values_h, prefix_len)
        attention_share = lax.psum_scatter(
            jnp.dot(attended, full_out, preferred_element_type=jnp.float32).astype(jnp.bfloat16),
            "tensor",
            scatter_dimension=0,
            tiled=True,
        ).astype(jnp.float32)
        residual = rows_in + attention_share + out_shift
        second, scaled_two, inverse_two = norm_forward(residual, gain_two, shift_two)
        grad_rows = cotangent[index, 0]
        down_bias_grad = down_bias_grad + jnp.sum(grad_rows.astype(jnp.float32), axis=0)
        second_all = lax.all_gather(second.astype(jnp.bfloat16), "tensor", axis=0, tiled=True)
        hidden_pre = jnp.dot(second_all, full_up, preferred_element_type=jnp.float32) + up_shift
        hidden_act = smooth_gate(hidden_pre).astype(jnp.bfloat16)
        feed_share = lax.psum_scatter(
            jnp.dot(hidden_act, full_down, preferred_element_type=jnp.float32).astype(jnp.bfloat16),
            "tensor",
            scatter_dimension=0,
            tiled=True,
        ).astype(jnp.float32)
        layer_rows.append(residual + feed_share + down_shift)
        grad_all = lax.all_gather(grad_rows, "tensor", axis=0, tiled=True)
        down_grad = jnp.dot(hidden_act.T, grad_all, preferred_element_type=jnp.float32)
        grad_act = jnp.dot(grad_all, full_down.T, preferred_element_type=jnp.float32)
        grad_pre = (grad_act * smooth_slope(hidden_pre)).astype(jnp.bfloat16)
        up_grad = jnp.dot(second_all.T, grad_pre, preferred_element_type=jnp.float32)
        up_part = jnp.sum(grad_pre.astype(jnp.float32), axis=0)
        up_bias_grad = up_bias_grad + lax.dynamic_update_slice(
            jnp.zeros_like(up_bias_grad), up_part, (offset_hidden,)
        )
        grad_second = lax.psum_scatter(
            jnp.dot(grad_pre, full_up.T, preferred_element_type=jnp.float32).astype(jnp.bfloat16),
            "tensor",
            scatter_dimension=0,
            tiled=True,
        ).astype(jnp.float32)
        gain_two_grad = gain_two_grad + jnp.sum(grad_second * scaled_two, axis=0)
        shift_two_grad = shift_two_grad + jnp.sum(grad_second, axis=0)
        grad_residual = grad_rows.astype(jnp.float32) + norm_backward(
            grad_second, scaled_two, inverse_two, gain_two
        )
        out_bias_grad = out_bias_grad + jnp.sum(grad_residual, axis=0)
        residual_all = lax.all_gather(
            grad_residual.astype(jnp.bfloat16), "tensor", axis=0, tiled=True
        )
        out_grad = jnp.dot(attended.T, residual_all, preferred_element_type=jnp.float32)
        grad_attended = jnp.dot(
            residual_all, full_out.T, preferred_element_type=jnp.float32
        ).astype(jnp.bfloat16)
        grad_queries, grad_keys, grad_values = attend_backward(
            queries_h, keys_h, values_h, grad_attended, log_totals, prefix_len
        )
        query_grad = jnp.dot(normed_all.T, grad_queries, preferred_element_type=jnp.float32)
        key_grad = jnp.dot(normed_all.T, grad_keys, preferred_element_type=jnp.float32)
        value_grad = jnp.dot(normed_all.T, grad_values, preferred_element_type=jnp.float32)
        query_part = jnp.sum(grad_queries.astype(jnp.float32), axis=0)
        value_part = jnp.sum(grad_values.astype(jnp.float32), axis=0)
        query_bias_grad = query_bias_grad + lax.dynamic_update_slice(
            zero_width, query_part, (offset_width,)
        )
        value_bias_grad = value_bias_grad + lax.dynamic_update_slice(
            zero_width, value_part, (offset_width,)
        )
        partial_sum = jnp.dot(grad_queries, full_query.T, preferred_element_type=jnp.float32)
        partial_sum = partial_sum + jnp.dot(
            grad_keys, full_key.T, preferred_element_type=jnp.float32
        )
        grad_normed = lax.psum_scatter(
            (
                partial_sum + jnp.dot(grad_values, full_value.T, preferred_element_type=jnp.float32)
            ).astype(jnp.bfloat16),
            "tensor",
            scatter_dimension=0,
            tiled=True,
        ).astype(jnp.float32)
        gain_one_grad = gain_one_grad + jnp.sum(grad_normed * scaled_one, axis=0)
        shift_one_grad = shift_one_grad + jnp.sum(grad_normed, axis=0)
        input_rows.append(
            grad_residual + norm_backward(grad_normed, scaled_one, inverse_one, gain_one)
        )
        reduced = (query_grad, key_grad, value_grad, out_grad, up_grad, down_grad)
        if weight_totals is None:
            weight_totals = reduced
        else:
            weight_totals = tuple((left + right for left, right in zip(weight_totals, reduced)))
    query_total, key_total, value_total, out_total, up_total, down_total = weight_totals
    query_total, key_total, value_total, out_total, up_total, down_total = (
        lax.psum_scatter(
            query_total.astype(jnp.bfloat16), "dp", scatter_dimension=0, tiled=True
        ).astype(jnp.float32),
        lax.psum_scatter(
            key_total.astype(jnp.bfloat16), "dp", scatter_dimension=0, tiled=True
        ).astype(jnp.float32),
        lax.psum_scatter(
            value_total.astype(jnp.bfloat16), "dp", scatter_dimension=0, tiled=True
        ).astype(jnp.float32),
        lax.psum_scatter(
            out_total.astype(jnp.bfloat16), "dp", scatter_dimension=1, tiled=True
        ).astype(jnp.float32),
        lax.psum_scatter(
            up_total.astype(jnp.bfloat16), "dp", scatter_dimension=0, tiled=True
        ).astype(jnp.float32),
        lax.psum_scatter(
            down_total.astype(jnp.bfloat16), "dp", scatter_dimension=1, tiled=True
        ).astype(jnp.float32),
    )
    vector_totals = (
        lax.psum_scatter(gain_one_grad, ("dp", "tensor"), scatter_dimension=0, tiled=True),
        lax.psum_scatter(shift_one_grad, ("dp", "tensor"), scatter_dimension=0, tiled=True),
        lax.psum_scatter(query_bias_grad, ("dp", "tensor"), scatter_dimension=0, tiled=True),
        lax.psum_scatter(value_bias_grad, ("dp", "tensor"), scatter_dimension=0, tiled=True),
        lax.psum_scatter(out_bias_grad, ("dp", "tensor"), scatter_dimension=0, tiled=True),
        lax.psum_scatter(gain_two_grad, ("dp", "tensor"), scatter_dimension=0, tiled=True),
        lax.psum_scatter(shift_two_grad, ("dp", "tensor"), scatter_dimension=0, tiled=True),
        lax.psum_scatter(up_bias_grad, ("dp", "tensor"), scatter_dimension=0, tiled=True),
        lax.psum_scatter(down_bias_grad, ("dp", "tensor"), scatter_dimension=0, tiled=True),
    )
    (
        gain_one_out,
        shift_one_out,
        query_bias_out,
        value_bias_out,
        out_bias_out,
        gain_two_out,
        shift_two_out,
        up_bias_out,
        down_bias_out,
    ) = vector_totals
    out_shape = (micro, 1, shard_rows, model_width)
    layer_out = jnp.stack(layer_rows).reshape(out_shape)
    input_grad = jnp.stack(input_rows).reshape(out_shape)
    return (
        layer_out,
        input_grad,
        gain_one_out,
        shift_one_out,
        query_total,
        query_bias_out,
        key_total,
        value_total,
        value_bias_out,
        out_total,
        out_bias_out,
        gain_two_out,
        shift_two_out,
        up_total,
        up_bias_out,
        down_total,
        down_bias_out,
    )


def _place(z, y, x):
    return z * 4 + y * 2 + x


def _coords():
    dp = lax.axis_index("dp")
    core = lax.axis_index("tensor")
    return dp // 4, (dp // 2) % 2, dp % 2, core


def _greet(peers):
    barrier = pltpu.get_barrier_semaphore()
    for peer in peers:
        pl.semaphore_signal(barrier, inc=1, device_id=peer, device_id_type=MESH)
    pl.semaphore_wait(barrier, len(peers))


def _peers():
    z, y, x, core = _coords()
    along = [(_place((z + j) % 4, y, x), core) for j in (1, 2, 3)]
    across = (_place(z, y, 1 - x), core)
    down = (_place(z, 1 - y, x), core)
    sibling = (_place(z, y, x), 1 - core)
    return along, across, down, sibling


def _send(src, dst, send_sem, recv_sem, peer):
    copy = pltpu.make_async_remote_copy(
        src_ref=src,
        dst_ref=dst,
        send_sem=send_sem,
        recv_sem=recv_sem,
        device_id=peer,
        device_id_type=MESH,
    )
    copy.start()
    return copy


def _local(src, dst, sem):
    copy = pltpu.make_async_copy(src, dst, sem)
    copy.start()
    return copy


class Gather:
    def __init__(self, win, full, send_sem, recv_sem, local_sem, at=0):
        self.z, self.y, self.x, self.core = _coords()
        self.along, self.across, self.down, self.sibling = _peers()
        self.win, self.full, self.at = win, full, at
        self.send_sem, self.recv_sem, self.local_sem = send_sem, recv_sem, local_sem

    def _remote(self, k, slot, src, dst, peer):
        return pltpu.make_async_remote_copy(
            src_ref=src,
            dst_ref=dst,
            send_sem=self.send_sem.at[k, slot],
            recv_sem=self.recv_sem.at[k, slot],
            device_id=peer,
            device_id_type=MESH,
        )

    def line(self, k):
        own = self.full.at[self.at + k, self.core, self.z, self.y, self.x]
        here = pltpu.make_async_copy(self.win.at[k], own, self.local_sem.at[k])
        return [here] + [self._remote(k, j, self.win.at[k], own, self.along[j]) for j in range(3)]

    def plane(self, k):
        block = self.full.at[self.at + k, self.core, :, self.y, self.x]
        return [self._remote(k, 3, block, block, self.across), self._remote(k, 4, block, block, self.down)]

    def corner(self, k):
        part = self.win.shape[1] // 2
        one = self.full.at[self.at + k, self.core, :, 1 - self.y, self.x, 0:part]
        two = self.full.at[self.at + k, self.core, :, self.y, 1 - self.x, part : 2 * part]
        return [self._remote(k, 5, one, one, self.across), self._remote(k, 6, two, two, self.down)]

    def twin(self, k):
        block = self.full.at[self.at + k, self.core]
        return [self._remote(k, 7, block, block, self.sibling)]

    def step(self, stage, k):
        stages = (self.line, self.plane, self.corner, self.twin)
        if stage > 0:
            for copy in stages[stage - 1](k):
                copy.wait()
        if stage < 4:
            for copy in stages[stage](k):
                copy.start()


def _run(table, gather, slot, grid_index=None, per_step=1):
    for (stage, k), at in table:
        if grid_index is None:
            if at == slot:
                gather.step(stage, k)
        elif at % per_step == slot:

            @pl.when(grid_index == at // per_step)
            def _(stage=stage, k=k):
                gather.step(stage, k)


def scatter_kernel(
    gq, gk, gv, go, gu, gd, vg, lo, ig,
    out, vout, lout, iout,
    acc, from_s, x_one, y_one, x_two, y_two, from_z,
    vacc, v_s, vx_one, vx_two, vy_two, v_z,
    ssem, rsem, lsem, vs, vr, vl, ws, wr, wl,
):
    z, y, x, core = _coords()
    along, across, down, sibling = _peers()
    _greet(along + [across, down, sibling])
    chunks = acc.shape[0]
    f32 = jnp.float32
    tail = []
    sources = [gq, gk, gv, go] + [gu.at[j] for j in range(4)] + [gd.at[j] for j in range(4)]
    order = list(range(chunks))
    begun = {}
    for k in order:
        begun[k] = (
            _local(sources[k].at[core], acc.at[k], lsem.at[k]),
            _send(sources[k].at[1 - core], from_s.at[k], ssem.at[k, 0], rsem.at[k, 0], sibling),
        )
        if k == 1:
            vbegun = (
                _local(vg.at[:, :, :, core], vacc, vl.at[0]),
                _send(vg.at[:, :, :, 1 - core], v_s, vs.at[0], vr.at[0], sibling),
            )
    for i, (rows, whole) in enumerate(((lo, lout), (ig, iout))):
        tail.append(_send(rows.at[1 - core], whole.at[core], ws.at[i], wr.at[i], sibling))
        tail.append(_local(rows.at[core], whole.at[core], wl.at[i]))

    def stage_one(k):
        for s in begun[k]:
            s.wait()

        @pl.loop(0, 4)
        def _(i):
            for j in range(2):
                for m in range(2):
                    acc[k, i, j, m] = (acc[k, i, j, m].astype(f32) + from_s[k, i, j, m].astype(f32)).astype(acc.dtype)

        return [
            _send(acc.at[k, :, 1 - y, 1 - x, 0:32], x_one.at[k], ssem.at[k, 1], rsem.at[k, 1], across),
            _send(acc.at[k, :, 1 - y, 1 - x, 32:64], y_one.at[k], ssem.at[k, 2], rsem.at[k, 2], down),
        ]

    def stage_two(k, before):
        for s in before:
            s.wait()
        acc[k, :, 1 - y, x, 0:32] = (acc[k, :, 1 - y, x, 0:32].astype(f32) + x_one[k].astype(f32)).astype(acc.dtype)
        acc[k, :, y, 1 - x, 32:64] = (acc[k, :, y, 1 - x, 32:64].astype(f32) + y_one[k].astype(f32)).astype(acc.dtype)
        return [
            _send(acc.at[k, :, y, 1 - x], x_two.at[k], ssem.at[k, 3], rsem.at[k, 3], across),
            _send(acc.at[k, :, 1 - y, x], y_two.at[k], ssem.at[k, 4], rsem.at[k, 4], down),
        ]

    def stage_three(k, before):
        for s in before:
            s.wait()
        acc[k, :, y, x] = (acc[k, :, y, x].astype(f32) + x_two[k].astype(f32) + y_two[k].astype(f32)).astype(acc.dtype)
        return [
            _send(acc.at[k, (z + j + 1) % 4, y, x], from_z.at[k, j], ssem.at[k, 5 + j], rsem.at[k, 5 + j], along[j])
            for j in range(3)
        ]

    def stage_four(k, before):
        for s in before:
            s.wait()
        total = acc[k, z, y, x].astype(f32)
        for j in range(3):
            total = total + from_z[k, j].astype(f32)
        out[k] = total

    lag = 1
    first, second, third = {}, {}, {}
    for t in range(chunks + 3 * lag):
        if t < chunks:
            first[t] = stage_one(order[t])
        if 0 <= t - lag < chunks:
            second[t - lag] = stage_two(order[t - lag], first[t - lag])
        if 0 <= t - 2 * lag < chunks:
            third[t - 2 * lag] = stage_three(order[t - 2 * lag], second[t - 2 * lag])
        if 0 <= t - 3 * lag < chunks:
            stage_four(order[t - 3 * lag], third[t - 3 * lag])
        if t == 0:
            for s in vbegun:
                s.wait()
            vacc[...] = vacc[...] + v_s[...]
            vone = _send(vacc.at[:, 1 - y, 1 - x], vx_one, vs.at[1], vr.at[1], across)
        if t == 2:
            vone.wait()
            vacc[:, 1 - y, x] = vacc[:, 1 - y, x] + vx_one[...]
            vtwo = [
                _send(vacc.at[:, y, 1 - x], vx_two, vs.at[2], vr.at[2], across),
                _send(vacc.at[:, 1 - y, x], vy_two, vs.at[3], vr.at[3], down),
            ]
        if t == 4:
            for s in vtwo:
                s.wait()
            vacc[:, y, x] = vacc[:, y, x] + vx_two[...] + vy_two[...]
            vthree = [
                _send(vacc.at[(z + j + 1) % 4, y, x], v_z.at[j], vs.at[4 + j], vr.at[4 + j], along[j])
                for j in range(3)
            ]
        if t == 6:
            for s in vthree:
                s.wait()
            vout[...] = vacc[z, y, x] + v_z[0] + v_z[1] + v_z[2]
    for s in tail:
        s.wait()


def scatter(gq, gk, gv, go, gu, gd, vg, lo, ig):
    chunks = 4 + gu.shape[0] + gd.shape[0]
    rows, cols = gq.shape[-2:]
    bf16, f32 = jnp.bfloat16, jnp.float32
    hbm = pl.BlockSpec(memory_space=pltpu.HBM)
    vmem = pl.BlockSpec(memory_space=pltpu.VMEM)
    dma = pltpu.SemaphoreType.DMA
    small = vg.shape[-2:]
    return pl.pallas_call(
        scatter_kernel,
        out_shape=(
            jax.ShapeDtypeStruct((chunks, rows, cols), f32),
            jax.ShapeDtypeStruct(small, f32),
            jax.ShapeDtypeStruct(lo.shape, lo.dtype),
            jax.ShapeDtypeStruct(ig.shape, ig.dtype),
        ),
        in_specs=[hbm] * 9,
        out_specs=(vmem, vmem, hbm, hbm),
        scratch_shapes=[
            pltpu.VMEM((chunks, 4, 2, 2, rows, cols), bf16),
            pltpu.VMEM((chunks, 4, 2, 2, rows, cols), bf16),
            pltpu.VMEM((chunks, 4, rows // 2, cols), bf16),
            pltpu.VMEM((chunks, 4, rows // 2, cols), bf16),
            pltpu.VMEM((chunks, 4, rows, cols), bf16),
            pltpu.VMEM((chunks, 4, rows, cols), bf16),
            pltpu.VMEM((chunks, 3, rows, cols), bf16),
            pltpu.VMEM((4, 2, 2) + small, f32),
            pltpu.VMEM((4, 2, 2) + small, f32),
            pltpu.VMEM((4,) + small, f32),
            pltpu.VMEM((4,) + small, f32),
            pltpu.VMEM((4,) + small, f32),
            pltpu.VMEM((3,) + small, f32),
            dma((chunks, 8)),
            dma((chunks, 8)),
            dma((chunks,)),
            dma((7,)),
            dma((7,)),
            dma((1,)),
            dma((2,)),
            dma((2,)),
            dma((2,)),
        ],
        compiler_params=pltpu.CompilerParams(
            collective_id=1, has_side_effects=True, vmem_limit_bytes=56 * 1024 * 1024
        ),
    )(gq, gk, gv, go, gu, gd, vg, lo, ig)


def gather_kernel(win, vec, xin, gin, full, vfull, xfull, gfull, ssem, rsem, lsem, vs, vr, vl, ws, wr, wl):
    z, y, x, core = _coords()
    along, across, down, sibling = _peers()
    _greet(along + [across, down, sibling])
    chunks = win.shape[0]
    gather = Gather(win, full, ssem, rsem, lsem)
    vown = vfull.at[z, y, x, core]
    vline = [_local(vec, vown, vl.at[0])] + [_send(vec, vown, vs.at[j], vr.at[j], along[j]) for j in range(3)]
    for k in range(chunks):
        gather.step(0, k)
    swaps = []
    for i, (part, whole) in enumerate(((xin, xfull), (gin, gfull))):
        swaps.append(_send(part.at[1 - core], whole.at[core], ws.at[i], wr.at[i], sibling))
        swaps.append(_local(part.at[core], whole.at[core], wl.at[i]))
    for s in vline:
        s.wait()
    vblock = vfull.at[:, y, x, core]
    vone = [_send(vblock, vblock, vs.at[3], vr.at[3], across), _send(vblock, vblock, vs.at[4], vr.at[4], down)]
    for k in range(chunks):
        gather.step(1, k)
    for s in vone:
        s.wait()
    vblock = vfull.at[:, 1 - y, x, core]
    vtwo = _send(vblock, vblock, vs.at[5], vr.at[5], across)
    for k in range(chunks):
        gather.step(2, k)
        if k == 0:
            vtwo.wait()
            vblock = vfull.at[:, :, :, core]
            vthree = _send(vblock, vblock, vs.at[6], vr.at[6], sibling)
    for k in range(chunks):
        gather.step(3, k)
    for k in range(chunks):
        gather.step(4, k)
    vthree.wait()
    for s in swaps:
        s.wait()


def gather(win, vec, xin, gin):
    chunks, rows, cols = win.shape
    hbm = pl.BlockSpec(memory_space=pltpu.HBM)
    vmem = pl.BlockSpec(memory_space=pltpu.VMEM)
    dma = pltpu.SemaphoreType.DMA
    return pl.pallas_call(
        gather_kernel,
        out_shape=(
            jax.ShapeDtypeStruct((chunks, 2, 4, 2, 2, rows, cols), win.dtype),
            jax.ShapeDtypeStruct((4, 2, 2, 2) + vec.shape, vec.dtype),
            jax.ShapeDtypeStruct(xin.shape, xin.dtype),
            jax.ShapeDtypeStruct(gin.shape, gin.dtype),
        ),
        in_specs=[vmem] * 4,
        out_specs=(hbm,) * 4,
        scratch_shapes=[
            dma((chunks, 8)),
            dma((chunks, 8)),
            dma((chunks,)),
            dma((7,)),
            dma((7,)),
            dma((1,)),
            dma((2,)),
            dma((2,)),
            dma((2,)),
        ],
        compiler_params=pltpu.CompilerParams(collective_id=0, has_side_effects=True),
    )(win, vec, xin, gin)


def _dot(left, right, contract):
    return lax.dot_general(left, right, (contract, ((), ())), preferred_element_type=jnp.float32)


NN = ((1,), (0,))
NT = ((1,), (1,))
TN = ((0,), (0,))
LOG2E = 1.4426950408889634
MIB = 1024 * 1024


def _normal(values):
    center = values - jnp.mean(values, axis=-1, keepdims=True)
    inverse = lax.rsqrt(jnp.mean(center * center, axis=-1, keepdims=True) + EPSILON)
    return center * inverse, inverse


def _spans(seq_len, longest, step):
    return [(start, max(longest, start + step)) for start in range(0, seq_len, step)]


ATTEND_SITES = 9
ATTEND_TABLE = (
    ((0, 0), 0), ((0, 1), 1), ((1, 0), 5), ((0, 2), 6), ((2, 0), 12), ((1, 1), 13), ((0, 3), 14),
    ((3, 0), 18), ((2, 1), 20), ((1, 2), 21), ((4, 0), 23), ((3, 1), 24), ((2, 2), 27), ((1, 3), 28),
    ((4, 1), 32), ((3, 2), 33), ((2, 3), 34),
)
ATTEND_LAST = ((3, 3), (4, 2), (4, 3))


def attend_kernel(
    prefix, x, lines, wq, wk, wv, win,
    normed, q, k, v, mixed, probs, residual, second, full,
    wout, ssem, rsem, lsem, osem,
):
    pair = pl.program_id(0)
    seq_len, model = x.shape
    f32, bf16 = jnp.float32, jnp.bfloat16
    gather = Gather(win, full, ssem, rsem, lsem)
    block = 128

    @pl.when(pair == 0)
    def _():
        _greet(gather.along + [gather.across, gather.down, gather.sibling])

    _run(ATTEND_TABLE, gather, 0, pair, ATTEND_SITES)

    @pl.when(pair == 0)
    def _():
        @pl.loop(0, seq_len // block)
        def _(i):
            rows = pl.ds(pl.multiple_of(i * block, block), block)
            scaled, _ = _normal(x[rows].astype(f32))
            normed[rows] = (scaled * lines[0:1] + lines[1:2]).astype(bf16)

    wide = q.shape[2]
    lanes = pl.ds(pl.multiple_of(pair * wide, wide), wide)
    q[0] = (_dot(normed[...], wq[0, 0], NN) + lines[2:3, lanes]).astype(bf16)
    k[0] = _dot(normed[...], wk[0, 0], NN).astype(bf16)
    v[0] = (_dot(normed[...], wv[0, 0], NN) + lines[3:4, lanes]).astype(bf16)
    step = 256
    factor = LOG2E / math.sqrt(HEAD_DIM)
    prefix_len = prefix[0]
    site = 1
    for head in range(wide // HEAD_DIM):
        part = slice(head * HEAD_DIM, (head + 1) * HEAD_DIM)
        for start, stop in _spans(seq_len, LONGEST, step):
            scores = _dot(k[0, :stop, part], q[0, start : start + step, part], NT)
            keys = lax.broadcasted_iota(jnp.int32, scores.shape, 0)
            queries = lax.broadcasted_iota(jnp.int32, scores.shape, 1) + start
            scores = jnp.where((keys <= queries) | (keys < prefix_len), scores, -jnp.inf)
            peak = jnp.max(scores, axis=0, keepdims=True)
            weights = jnp.exp2((scores - peak) * factor)
            total = jnp.sum(weights, axis=0, keepdims=True)
            weights = (weights * (1.0 / total)).astype(bf16)
            probs[head, :stop, start : start + step] = weights
            to = pl.ds(pl.multiple_of((pair % 2) * wide + head * HEAD_DIM, HEAD_DIM), HEAD_DIM)
            mixed[pair // 2, start : start + step, to] = _dot(weights, v[0, :stop, part], TN).astype(bf16)
            if site < ATTEND_SITES:
                _run(ATTEND_TABLE, gather, site, pair, ATTEND_SITES)
            site += 1

    @pl.when(pair == pl.num_programs(0) - 1)
    def _():
        copy = pltpu.make_async_copy(full.at[0], wout, osem.at[0])
        copy.start()
        copy.wait()
        weight = [wout[c].reshape(model, -1) for c in range(2)]

        @pl.loop(0, seq_len // step)
        def _(i):
            rows = pl.ds(pl.multiple_of(i * step, step), step)
            branch = _dot(mixed[0, rows], weight[0], NT) + _dot(mixed[1, rows], weight[1], NT)
            total = x[rows].astype(f32) + branch + lines[4:5]
            residual[rows] = total
            scaled, _ = _normal(total)
            second[rows] = (scaled * lines[5:6] + lines[6:7]).astype(bf16)

        for stage, k_last in ATTEND_LAST:
            gather.step(stage, k_last)


def attend(prefix_len, x, lines, first, win):
    seq_len, model = x.shape
    cols = first.shape[-1]
    chunks, rows, _ = win.shape
    wide = 256
    per = cols // wide
    pairs = 2 * per
    bf16, f32 = jnp.bfloat16, jnp.float32
    whole = pl.BlockSpec(memory_space=pltpu.VMEM)

    def weight(i):
        return pl.BlockSpec((1, 1, model, wide), lambda p, s, i=i: (i, p // per, 0, p % per))

    heads = pl.BlockSpec((1, seq_len, wide), lambda p, s: (p // per, 0, p % per))
    dma = pltpu.SemaphoreType.DMA
    split = jax.ShapeDtypeStruct((2, seq_len, cols), bf16)
    return pl.pallas_call(
        attend_kernel,
        grid_spec=pltpu.PrefetchScalarGridSpec(
            num_scalar_prefetch=1,
            grid=(pairs,),
            in_specs=[whole, whole, weight(0), weight(1), weight(2), whole],
            out_specs=(
                whole, heads, heads, heads, whole,
                pl.BlockSpec((wide // HEAD_DIM, seq_len, seq_len), lambda p, s: (p, 0, 0)),
                whole, whole, pl.BlockSpec(memory_space=pltpu.HBM),
            ),
            scratch_shapes=[
                pltpu.VMEM((2, 4, 2, 2, rows, cols), bf16),
                dma((chunks, 8)),
                dma((chunks, 8)),
                dma((chunks,)),
                dma((1,)),
            ],
        ),
        out_shape=(
            jax.ShapeDtypeStruct((seq_len, model), bf16),
            split, split, split, split,
            jax.ShapeDtypeStruct((2 * cols // HEAD_DIM, seq_len, seq_len), bf16),
            jax.ShapeDtypeStruct((seq_len, model), f32),
            jax.ShapeDtypeStruct((seq_len, model), bf16),
            jax.ShapeDtypeStruct((chunks, 2, 4, 2, 2, rows, cols), bf16),
        ),
        compiler_params=pltpu.CompilerParams(
            collective_id=2, has_side_effects=True, vmem_limit_bytes=56 * MIB
        ),
    )(prefix_len, x, lines, first, first, first, win)


FEED_SITES = 6
FEED_TABLE = (
    ((0, 0), 0), ((0, 1), 0), ((1, 0), 4), ((0, 2), 6), ((2, 0), 8), ((1, 1), 10), ((3, 0), 11),
    ((0, 3), 12), ((4, 0), 12), ((2, 1), 13), ((1, 2), 15), ((3, 1), 17), ((2, 2), 18), ((0, 4), 20),
    ((1, 3), 21), ((3, 2), 23), ((4, 1), 24), ((4, 2), 24), ((2, 3), 25), ((1, 4), 26), ((3, 3), 30),
    ((2, 4), 31), ((3, 4), 35), ((4, 3), 36),
)


def feed_kernel(
    second, grad, residual, lines, bias, before, win,
    layer, gres, low, sums, gup, gdown, gbias,
    weights, hid, gpre, ssem, rsem, lsem, bsem,
):
    pid = pl.program_id(0)
    seq_len, model = second.shape
    chunks = win.shape[0]
    f32, bf16 = jnp.float32, jnp.bfloat16
    held = weights.shape[0] - chunks
    gather = Gather(win, weights, ssem, rsem, lsem, held)
    block = 128

    def fetch(k):
        return pltpu.make_async_copy(before.at[1 + k], weights.at[k], bsem.at[k])

    def site(i):
        _run(FEED_TABLE, gather, i, pid, FEED_SITES)

    @pl.when(pid == 0)
    def _():
        for k in range(held):
            fetch(k).start()
        _greet(gather.along + [gather.across, gather.down, gather.sibling])

    site(0)

    @pl.when(pid == 0)
    def _():
        gres[...] = jnp.zeros_like(gres)

        @pl.loop(0, seq_len // block)
        def _(i):
            rows = pl.ds(pl.multiple_of(i * block, block), block)
            layer[rows] = residual[rows] + lines[7:8]

        for k in range(held):
            fetch(k).wait()

    @pl.when(pid == 2 * ((chunks + held) // 2 - 1))
    def _():
        gather.step(4, chunks - 1)

    piece, half = pid // 2, pid % 2
    up = weights[2 * piece, half].reshape(model, -1)
    down = weights[2 * piece + 1, half].reshape(model, -1)
    pre = _dot(second[...], up, NN) + bias[0]
    site(1)
    phi = 0.5 * (1.0 + lax.erf(pre * (1.0 / math.sqrt(2.0))))
    density = jnp.exp2(pre * pre * (-0.5 * LOG2E)) * (1.0 / math.sqrt(2.0 * math.pi))
    hid[...] = (pre * phi).astype(bf16)
    slope = phi + pre * density
    back = (_dot(grad[...], down, NN) * slope).astype(bf16)
    gpre[...] = back
    gbias[0] = jnp.sum(back.astype(f32), axis=0, keepdims=True)
    site(2)
    layer[...] += _dot(hid[...], down, NT)
    site(3)
    gres[...] += _dot(gpre[...], up, NT)
    site(4)
    gup[0, 0] = _dot(second[...], gpre[...], TN).astype(bf16)
    site(5)
    gdown[0, 0] = _dot(grad[...], hid[...], TN).astype(bf16)

    @pl.when(pid == pl.num_programs(0) - 1)
    def _():
        sums[...] = jnp.zeros_like(sums)

        @pl.loop(0, seq_len // block)
        def _(i):
            rows = pl.ds(pl.multiple_of(i * block, block), block)
            scaled, inverse = _normal(residual[rows])
            grow = gres[rows]
            upstream = grad[rows].astype(f32)
            weighted = grow * lines[5:6]
            mean_plain = jnp.mean(weighted, axis=-1, keepdims=True)
            mean_scaled = jnp.mean(weighted * scaled, axis=-1, keepdims=True)
            total = upstream + inverse * (weighted - mean_plain - scaled * mean_scaled)
            gres[rows] = total
            low[rows] = total.astype(bf16)
            sums[0:1] += jnp.sum(grow * scaled, axis=0, keepdims=True)
            sums[1:2] += jnp.sum(grow, axis=0, keepdims=True)
            sums[2:3] += jnp.sum(total, axis=0, keepdims=True)
            sums[3:4] += jnp.sum(upstream, axis=0, keepdims=True)


def feed(second, grad, residual, lines, bias, before, win):
    seq_len, model = second.shape
    chunks, rows, cols = win.shape
    pieces = bias.shape[0]
    bf16, f32 = jnp.bfloat16, jnp.float32
    whole = pl.BlockSpec(memory_space=pltpu.VMEM)
    grads = pl.BlockSpec((1, 1, model, cols), lambda i: (i // 2, i % 2, 0, 0))
    line = pl.BlockSpec((1, 1, cols), lambda i: (i, 0, 0))
    dma = pltpu.SemaphoreType.DMA
    held = pieces - chunks
    return pl.pallas_call(
        feed_kernel,
        grid=(pieces,),
        in_specs=[whole, whole, whole, whole, line, pl.BlockSpec(memory_space=pltpu.HBM), whole],
        out_specs=(whole, whole, whole, whole, grads, grads, line),
        out_shape=(
            jax.ShapeDtypeStruct((seq_len, model), f32),
            jax.ShapeDtypeStruct((seq_len, model), f32),
            jax.ShapeDtypeStruct((seq_len, model), bf16),
            jax.ShapeDtypeStruct((8, model), f32),
            jax.ShapeDtypeStruct((pieces // 2, 2, model, cols), bf16),
            jax.ShapeDtypeStruct((pieces // 2, 2, model, cols), bf16),
            jax.ShapeDtypeStruct((pieces, 1, cols), f32),
        ),
        scratch_shapes=[
            pltpu.VMEM((pieces, 2, 4, 2, 2, rows, cols), bf16),
            pltpu.VMEM((seq_len, cols), bf16),
            pltpu.VMEM((seq_len, cols), bf16),
            dma((chunks, 8)),
            dma((chunks, 8)),
            dma((chunks,)),
            dma((held,)),
        ],
        compiler_params=pltpu.CompilerParams(
            collective_id=3, has_side_effects=True, vmem_limit_bytes=62 * MIB
        ),
    )(second, grad, residual, lines, bias, before, win)


def retreat_kernel(
    q, k, v, mixed, probs, low, normed, x, gres, lines, wq, wk, wv, wo,
    ingrad, gq, gk, gv, go, sums, bsums, dq, dk, dv, dmix, dk_acc, dv_acc,
):
    pair = pl.program_id(0)
    seq_len, model = x.shape
    f32, bf16 = jnp.float32, jnp.bfloat16
    step, block = 256, 128
    scale = 1.0 / math.sqrt(HEAD_DIM)

    @pl.when(pair == 0)
    def _():
        ingrad[...] = jnp.zeros_like(ingrad)

    dmix[...] = _dot(low[...], wo[0, 0], NN).astype(bf16)
    go[0] = _dot(low[...], mixed[0], TN).astype(bf16)
    for head in range(dq.shape[1] // HEAD_DIM):
        part = slice(head * HEAD_DIM, (head + 1) * HEAD_DIM)
        dk_acc[...] = jnp.zeros_like(dk_acc)
        dv_acc[...] = jnp.zeros_like(dv_acc)
        for start, stop in _spans(seq_len, LONGEST, step):
            grad = dmix[start : start + step, part]
            weights_low = probs[head, :stop, start : start + step]
            weights = weights_low.astype(f32)
            dprobs = _dot(v[0, :stop, part], grad, NT)
            inner = jnp.sum(weights * dprobs, axis=0, keepdims=True)
            dscores = (weights * (dprobs - inner)).astype(bf16)
            dq[start : start + step, part] = (_dot(dscores, k[0, :stop, part], TN) * scale).astype(bf16)
            dk_acc[:stop] += _dot(dscores, q[0, start : start + step, part], NN)
            dv_acc[:stop] += _dot(weights_low, grad, NN)
        dk[:, part] = (dk_acc[...] * scale).astype(bf16)
        dv[:, part] = dv_acc[...].astype(bf16)
    gq[0] = _dot(normed[...], dq[...], TN).astype(bf16)
    gk[0] = _dot(normed[...], dk[...], TN).astype(bf16)
    gv[0] = _dot(normed[...], dv[...], TN).astype(bf16)
    ingrad[...] += _dot(dq[...], wq[0, 0], NT) + _dot(dk[...], wk[0, 0], NT) + _dot(dv[...], wv[0, 0], NT)
    bsums[0, 0:1] = jnp.sum(dq[...].astype(f32), axis=0, keepdims=True)
    bsums[0, 1:2] = jnp.sum(dv[...].astype(f32), axis=0, keepdims=True)

    @pl.when(pair == pl.num_programs(0) - 1)
    def _():
        sums[...] = jnp.zeros_like(sums)

        @pl.loop(0, seq_len // block)
        def _(i):
            rows = pl.ds(pl.multiple_of(i * block, block), block)
            scaled, inverse = _normal(x[rows].astype(f32))
            grow = ingrad[rows]
            weighted = grow * lines[0:1]
            mean_plain = jnp.mean(weighted, axis=-1, keepdims=True)
            mean_scaled = jnp.mean(weighted * scaled, axis=-1, keepdims=True)
            ingrad[rows] = gres[rows] + inverse * (weighted - mean_plain - scaled * mean_scaled)
            sums[0:1] += jnp.sum(grow * scaled, axis=0, keepdims=True)
            sums[1:2] += jnp.sum(grow, axis=0, keepdims=True)


def retreat(q, k, v, mixed, probs, low, normed, x, gres, lines, first, wout):
    seq_len, model = x.shape
    cols = q.shape[2]
    wide = 256
    per = cols // wide
    bf16, f32 = jnp.bfloat16, jnp.float32
    whole = pl.BlockSpec(memory_space=pltpu.VMEM)

    def weight(i):
        return pl.BlockSpec((1, 1, model, wide), lambda p, i=i: (i, p // per, 0, p % per))

    heads = pl.BlockSpec((1, seq_len, wide), lambda p: (p // per, 0, p % per))
    grads = pl.BlockSpec((1, model, wide), lambda p: (p // per, 0, p % per))
    gshape = jax.ShapeDtypeStruct((2, model, cols), bf16)
    return pl.pallas_call(
        retreat_kernel,
        grid=(2 * per,),
        in_specs=[heads] * 4
        + [pl.BlockSpec((wide // HEAD_DIM, seq_len, seq_len), lambda p: (p, 0, 0))]
        + [whole] * 5
        + [weight(0), weight(1), weight(2), weight(0)],
        out_specs=(whole, grads, grads, grads, grads, whole, pl.BlockSpec((1, 8, wide), lambda p: (p, 0, 0))),
        out_shape=(
            jax.ShapeDtypeStruct((seq_len, model), f32),
            gshape, gshape, gshape, gshape,
            jax.ShapeDtypeStruct((8, model), f32),
            jax.ShapeDtypeStruct((2 * per, 8, wide), f32),
        ),
        scratch_shapes=[pltpu.VMEM((seq_len, wide), bf16)] * 4 + [pltpu.VMEM((seq_len, HEAD_DIM), f32)] * 2,
        compiler_params=pltpu.CompilerParams(vmem_limit_bytes=56 * MIB),
    )(q, k, v, mixed, probs, low, normed, x, gres, lines, first, first, first, wout)


def fast_body(
    inputs, prefix, ln1_gain, ln1_bias, query_weight, query_bias, key_weight, value_weight, value_bias,
    out_weight, out_bias, ln2_gain, ln2_bias, up_weight, up_bias, down_weight, down_bias, cotangent,
):
    f32 = jnp.float32
    core = lax.axis_index("tensor")
    half, model = inputs.shape[2], inputs.shape[3]
    rows, cols = query_weight.shape
    seq_len = 2 * half
    pieces = up_weight.shape[1] // cols

    def split(matrix):
        return [matrix[:, i * cols : (i + 1) * cols] for i in range(pieces)]

    ups, downs = split(up_weight), split(down_weight.T)
    feeds = [m for pair in zip(ups, downs) for m in pair]
    win_a = jnp.stack([query_weight, key_weight, value_weight])
    win_b = jnp.stack([out_weight.T] + feeds[:HELD])
    win_c = jnp.stack(feeds[HELD:])
    names = (ln1_gain, ln1_bias, query_bias, value_bias, out_bias, ln2_gain, ln2_bias, down_bias)
    small = jnp.concatenate(names + (up_bias,)).reshape(3, 128)
    vec = jnp.pad(small, ((0, 5), (0, 0)))
    full_a, vfull, x_rows, grad_rows = gather(win_a, vec, inputs[:, 0], cotangent[:, 0])
    first = full_a.reshape(3, 2, model, cols)
    parts = vfull.reshape(32, 8 * 128)
    lines = parts[:, :256].reshape(32, 8, 32).transpose(1, 0, 2).reshape(8, model)
    up_shift = parts[:, 256:384].reshape(2, pieces, 1, cols).transpose(1, 0, 2, 3).reshape(2 * pieces, 1, cols)
    x = x_rows.reshape(seq_len, model)
    grad = grad_rows.reshape(seq_len, model)
    prefix_len = lax.dynamic_slice_in_dim(prefix[:, 0], core, 1)
    normed, q, k, v, mixed, probs, residual, second, full_b = attend(prefix_len, x, lines, first, win_b)
    layer_rows, gres, low, sums_two, gup, gdown, gup_bias = feed(second, grad, residual, lines, up_shift, full_b, win_c)
    wout = full_b[:1].reshape(1, 2, model, cols)
    input_rows, gq, gk, gv, gout, sums_one, bsums = retreat(
        q, k, v, mixed, probs, low, normed, x, gres, lines, first, wout
    )
    sums = jnp.stack(
        [
            sums_one[0],
            sums_one[1],
            bsums[:, 0].reshape(model),
            bsums[:, 1].reshape(model),
            sums_two[2],
            sums_two[0],
            sums_two[1],
            sums_two[3],
        ]
    )
    vector = sums.reshape(8, 32, 32).transpose(1, 0, 2).reshape(32, 256)
    up_vector = gup_bias.reshape(pieces, 2, cols).transpose(1, 0, 2).reshape(32, 128)
    vg = jnp.pad(jnp.concatenate([vector, up_vector], axis=1), ((0, 0), (0, 640)))
    vg = vg.reshape(4, 2, 2, 2, 8, 128)
    six = (2, 4, 2, 2, rows, cols)
    out, vout, layer_out, input_grad = scatter(
        gq.reshape(six), gk.reshape(six), gv.reshape(six), gout.reshape(six),
        gup.reshape((pieces,) + six), gdown.reshape((pieces,) + six), vg,
        layer_rows.reshape(2, half, model), input_rows.reshape(2, half, model),
    )
    flat = vout.reshape(-1)
    vectors = [flat[32 * i : 32 * i + 32] for i in range(8)]

    def join(pieces_of):
        return pieces_of.transpose(1, 0, 2).reshape(rows, pieces * cols)

    return (
        layer_out.reshape(2, 1, half, model),
        input_grad.reshape(2, 1, half, model),
        vectors[0],
        vectors[1],
        out[0],
        vectors[2],
        out[1],
        out[2],
        vectors[3],
        out[3].T,
        vectors[4],
        vectors[5],
        vectors[6],
        join(out[4 : 4 + pieces]),
        flat[256:384],
        join(out[4 + pieces :]).T,
        vectors[7],
    )


def solution(mesh):
    in_specs = (
        P(None, "dp", "tensor", None),
        P(None, "dp"),
        P(("dp", "tensor")),
        P(("dp", "tensor")),
        P("dp", "tensor"),
        P(("dp", "tensor")),
        P("dp", "tensor"),
        P("dp", "tensor"),
        P(("dp", "tensor")),
        P("tensor", "dp"),
        P(("dp", "tensor")),
        P(("dp", "tensor")),
        P(("dp", "tensor")),
        P("dp", "tensor"),
        P(("dp", "tensor")),
        P("tensor", "dp"),
        P(("dp", "tensor")),
        P(None, "dp", "tensor", None),
    )
    out_specs = (
        P(None, "dp", "tensor", None),
        P(None, "dp", "tensor", None),
        P(("dp", "tensor")),
        P(("dp", "tensor")),
        P("dp", "tensor"),
        P(("dp", "tensor")),
        P("dp", "tensor"),
        P("dp", "tensor"),
        P(("dp", "tensor")),
        P("tensor", "dp"),
        P(("dp", "tensor")),
        P(("dp", "tensor")),
        P(("dp", "tensor")),
        P("dp", "tensor"),
        P(("dp", "tensor")),
        P("tensor", "dp"),
        P(("dp", "tensor")),
    )
    sizes = (mesh.shape["dp"], mesh.shape["tensor"])
    chosen = fast_body if sizes == (16, 2) else body
    return jax.shard_map(chosen, mesh=mesh, in_specs=in_specs, out_specs=out_specs, check_vma=False)
```

```python
import math

import jax
import jax.numpy as jnp
from jax import lax
from jax.experimental import pallas as pl
from jax.experimental.pallas import tpu as pltpu
from jax.sharding import PartitionSpec as P

MESH = pl.DeviceIdType.MESH
LONGEST = 512

HEAD_DIM = 128
BLOCK = 512


EPSILON = 1e-05


def norm_forward(values, gain, shift):
    center = values - jnp.mean(values, axis=-1, keepdims=True)
    inverse = lax.rsqrt(jnp.mean(center * center, axis=-1, keepdims=True) + EPSILON)
    scaled = center * inverse
    return (scaled * gain + shift, scaled, inverse)


def norm_backward(grad_out, scaled, inverse, gain):
    weighted = grad_out * gain
    mean_plain = jnp.mean(weighted, axis=-1, keepdims=True)
    mean_scaled = jnp.mean(weighted * scaled, axis=-1, keepdims=True)
    return inverse * (weighted - mean_plain - scaled * mean_scaled)


def smooth_gate(values):
    return jax.nn.gelu(values, approximate=False)


def smooth_slope(values):
    normal_cdf = 0.5 * (1.0 + jax.scipy.special.erf(values / math.sqrt(2.0)))
    density = jnp.exp(-0.5 * values * values) / math.sqrt(2.0 * math.pi)
    return normal_cdf + values * density


def masked_scores(query_block, key_rows, start, prefix_len):
    scale = 1.0 / math.sqrt(key_rows.shape[2])
    scores = (
        jnp.einsum("qhd,khd->hqk", query_block, key_rows, preferred_element_type=jnp.float32)
        * scale
    )
    places = start + jnp.arange(query_block.shape[0], dtype=jnp.int32)
    columns = jnp.arange(key_rows.shape[0], dtype=jnp.int32)
    allowed = (columns[None, :] <= places[:, None]) | (columns[None, :] < prefix_len)
    return jnp.where(allowed[None], scores, -jnp.inf)


def attend_forward(queries, key_rows, value_rows, prefix_len):
    seq_len, heads_local, head_size = queries.shape
    count = seq_len // BLOCK

    def one_block(items):
        query_block, start = items
        scores = masked_scores(query_block, key_rows, start, prefix_len)
        peak = jnp.max(scores, axis=-1, keepdims=True)
        raw_weights = jnp.exp(scores - peak)
        totals = jnp.sum(raw_weights, axis=-1, keepdims=True)
        probs = (raw_weights / totals).astype(jnp.bfloat16)
        mixed = jnp.einsum("hqk,khd->qhd", probs, value_rows, preferred_element_type=jnp.float32)
        return (mixed.astype(jnp.bfloat16), (peak + jnp.log(totals))[..., 0])

    starts = jnp.arange(count, dtype=jnp.int32) * BLOCK
    mixed, log_totals = lax.map(
        one_block, (queries.reshape(count, BLOCK, heads_local, head_size), starts)
    )
    return (mixed.reshape(seq_len, heads_local * head_size), log_totals)


def attend_backward(queries, key_rows, value_rows, grad_mixed, log_totals, prefix_len):
    seq_len, heads_local, head_size = queries.shape
    count = seq_len // BLOCK
    scale = 1.0 / math.sqrt(head_size)

    def one_block(carry, items):
        key_total, value_total = carry
        query_block, grad_block, log_block, start = items
        scores = masked_scores(query_block, key_rows, start, prefix_len)
        probs = jnp.exp(scores - log_block[..., None])
        grad_probs = jnp.einsum(
            "qhd,khd->hqk", grad_block, value_rows, preferred_element_type=jnp.float32
        )
        inner = jnp.sum(probs * grad_probs, axis=-1, keepdims=True)
        grad_scores = (probs * (grad_probs - inner)).astype(jnp.bfloat16)
        grad_query = (
            jnp.einsum("hqk,khd->qhd", grad_scores, key_rows, preferred_element_type=jnp.float32)
            * scale
        )
        key_total = (
            key_total
            + jnp.einsum(
                "hqk,qhd->khd", grad_scores, query_block, preferred_element_type=jnp.float32
            )
            * scale
        )
        value_total = value_total + jnp.einsum(
            "hqk,qhd->khd",
            probs.astype(jnp.bfloat16),
            grad_block,
            preferred_element_type=jnp.float32,
        )
        return ((key_total, value_total), grad_query.astype(jnp.bfloat16))

    empty_total = jnp.zeros(queries.shape, jnp.float32)
    starts = jnp.arange(count, dtype=jnp.int32) * BLOCK
    blocked = (count, BLOCK, heads_local, head_size)
    (key_total, value_total), grad_queries = lax.scan(
        one_block,
        (empty_total, empty_total),
        (queries.reshape(blocked), grad_mixed.reshape(blocked), log_totals, starts),
    )
    width = heads_local * head_size
    return (
        grad_queries.reshape(seq_len, width),
        key_total.astype(jnp.bfloat16).reshape(seq_len, width),
        value_total.astype(jnp.bfloat16).reshape(seq_len, width),
    )


def body(
    inputs,
    prefix,
    ln1_gain,
    ln1_bias,
    query_weight,
    query_bias,
    key_weight,
    value_weight,
    value_bias,
    out_weight,
    out_bias,
    ln2_gain,
    ln2_bias,
    up_weight,
    up_bias,
    down_weight,
    down_bias,
    cotangent,
):
    local_width = query_weight.shape[1]
    local_hidden = up_weight.shape[1]
    shard_rows = inputs.shape[2]
    micro = inputs.shape[0]
    model_width = inputs.shape[3]
    heads_local = local_width // HEAD_DIM
    offset_width = lax.axis_index("tensor") * local_width
    offset_hidden = lax.axis_index("tensor") * local_hidden
    vectors = (
        lax.all_gather(ln1_gain, ("dp", "tensor"), axis=0, tiled=True),
        lax.all_gather(ln1_bias, ("dp", "tensor"), axis=0, tiled=True),
        lax.all_gather(query_bias, ("dp", "tensor"), axis=0, tiled=True),
        lax.all_gather(value_bias, ("dp", "tensor"), axis=0, tiled=True),
        lax.all_gather(out_bias, ("dp", "tensor"), axis=0, tiled=True),
        lax.all_gather(ln2_gain, ("dp", "tensor"), axis=0, tiled=True),
        lax.all_gather(ln2_bias, ("dp", "tensor"), axis=0, tiled=True),
        lax.all_gather(up_bias, ("dp", "tensor"), axis=0, tiled=True),
        lax.all_gather(down_bias, ("dp", "tensor"), axis=0, tiled=True),
    )
    (
        gain_one,
        shift_one,
        query_full_bias,
        value_full_bias,
        out_shift,
        gain_two,
        shift_two,
        up_full_bias,
        down_shift,
    ) = vectors
    query_shift = lax.dynamic_slice_in_dim(query_full_bias, offset_width, local_width)
    value_shift = lax.dynamic_slice_in_dim(value_full_bias, offset_width, local_width)
    up_shift = lax.dynamic_slice_in_dim(up_full_bias, offset_hidden, local_hidden)
    zero_width = jnp.zeros((model_width,), jnp.float32)
    gain_one_grad = zero_width
    shift_one_grad = zero_width
    query_bias_grad = zero_width
    value_bias_grad = zero_width
    out_bias_grad = zero_width
    gain_two_grad = zero_width
    shift_two_grad = zero_width
    up_bias_grad = jnp.zeros((up_full_bias.shape[0],), jnp.float32)
    down_bias_grad = zero_width
    weight_totals = None
    layer_rows = []
    input_rows = []
    for index in range(micro):
        gathered = (
            lax.all_gather(query_weight, "dp", axis=0, tiled=True),
            lax.all_gather(key_weight, "dp", axis=0, tiled=True),
            lax.all_gather(value_weight, "dp", axis=0, tiled=True),
            lax.all_gather(out_weight, "dp", axis=1, tiled=True),
            lax.all_gather(up_weight, "dp", axis=0, tiled=True),
            lax.all_gather(down_weight, "dp", axis=1, tiled=True),
        )
        full_query, full_key, full_value, full_out, full_up, full_down = gathered
        rows_in = inputs[index, 0].astype(jnp.float32)
        prefix_len = prefix[index, 0]
        normed, scaled_one, inverse_one = norm_forward(rows_in, gain_one, shift_one)
        normed_all = lax.all_gather(normed.astype(jnp.bfloat16), "tensor", axis=0, tiled=True)
        seq_len = normed_all.shape[0]
        queries = (
            jnp.dot(normed_all, full_query, preferred_element_type=jnp.float32) + query_shift
        ).astype(jnp.bfloat16)
        key_rows = jnp.dot(normed_all, full_key, preferred_element_type=jnp.float32).astype(
            jnp.bfloat16
        )
        value_rows = (
            jnp.dot(normed_all, full_value, preferred_element_type=jnp.float32) + value_shift
        ).astype(jnp.bfloat16)
        head_shape = (seq_len, heads_local, HEAD_DIM)
        queries_h = queries.reshape(head_shape)
        keys_h = key_rows.reshape(head_shape)
        values_h = value_rows.reshape(head_shape)
        attended, log_totals = attend_forward(queries_h, keys_h, values_h, prefix_len)
        attention_share = lax.psum_scatter(
            jnp.dot(attended, full_out, preferred_element_type=jnp.float32).astype(jnp.bfloat16),
            "tensor",
            scatter_dimension=0,
            tiled=True,
        ).astype(jnp.float32)
        residual = rows_in + attention_share + out_shift
        second, scaled_two, inverse_two = norm_forward(residual, gain_two, shift_two)
        grad_rows = cotangent[index, 0]
        down_bias_grad = down_bias_grad + jnp.sum(grad_rows.astype(jnp.float32), axis=0)
        second_all = lax.all_gather(second.astype(jnp.bfloat16), "tensor", axis=0, tiled=True)
        hidden_pre = jnp.dot(second_all, full_up, preferred_element_type=jnp.float32) + up_shift
        hidden_act = smooth_gate(hidden_pre).astype(jnp.bfloat16)
        feed_share = lax.psum_scatter(
            jnp.dot(hidden_act, full_down, preferred_element_type=jnp.float32).astype(jnp.bfloat16),
            "tensor",
            scatter_dimension=0,
            tiled=True,
        ).astype(jnp.float32)
        layer_rows.append(residual + feed_share + down_shift)
        grad_all = lax.all_gather(grad_rows, "tensor", axis=0, tiled=True)
        down_grad = jnp.dot(hidden_act.T, grad_all, preferred_element_type=jnp.float32)
        grad_act = jnp.dot(grad_all, full_down.T, preferred_element_type=jnp.float32)
        grad_pre = (grad_act * smooth_slope(hidden_pre)).astype(jnp.bfloat16)
        up_grad = jnp.dot(second_all.T, grad_pre, preferred_element_type=jnp.float32)
        up_part = jnp.sum(grad_pre.astype(jnp.float32), axis=0)
        up_bias_grad = up_bias_grad + lax.dynamic_update_slice(
            jnp.zeros_like(up_bias_grad), up_part, (offset_hidden,)
        )
        grad_second = lax.psum_scatter(
            jnp.dot(grad_pre, full_up.T, preferred_element_type=jnp.float32).astype(jnp.bfloat16),
            "tensor",
            scatter_dimension=0,
            tiled=True,
        ).astype(jnp.float32)
        gain_two_grad = gain_two_grad + jnp.sum(grad_second * scaled_two, axis=0)
        shift_two_grad = shift_two_grad + jnp.sum(grad_second, axis=0)
        grad_residual = grad_rows.astype(jnp.float32) + norm_backward(
            grad_second, scaled_two, inverse_two, gain_two
        )
        out_bias_grad = out_bias_grad + jnp.sum(grad_residual, axis=0)
        residual_all = lax.all_gather(
            grad_residual.astype(jnp.bfloat16), "tensor", axis=0, tiled=True
        )
        out_grad = jnp.dot(attended.T, residual_all, preferred_element_type=jnp.float32)
        grad_attended = jnp.dot(
            residual_all, full_out.T, preferred_element_type=jnp.float32
        ).astype(jnp.bfloat16)
        grad_queries, grad_keys, grad_values = attend_backward(
            queries_h, keys_h, values_h, grad_attended, log_totals, prefix_len
        )
        query_grad = jnp.dot(normed_all.T, grad_queries, preferred_element_type=jnp.float32)
        key_grad = jnp.dot(normed_all.T, grad_keys, preferred_element_type=jnp.float32)
        value_grad = jnp.dot(normed_all.T, grad_values, preferred_element_type=jnp.float32)
        query_part = jnp.sum(grad_queries.astype(jnp.float32), axis=0)
        value_part = jnp.sum(grad_values.astype(jnp.float32), axis=0)
        query_bias_grad = query_bias_grad + lax.dynamic_update_slice(
            zero_width, query_part, (offset_width,)
        )
        value_bias_grad = value_bias_grad + lax.dynamic_update_slice(
            zero_width, value_part, (offset_width,)
        )
        partial_sum = jnp.dot(grad_queries, full_query.T, preferred_element_type=jnp.float32)
        partial_sum = partial_sum + jnp.dot(
            grad_keys, full_key.T, preferred_element_type=jnp.float32
        )
        grad_normed = lax.psum_scatter(
            (
                partial_sum + jnp.dot(grad_values, full_value.T, preferred_element_type=jnp.float32)
            ).astype(jnp.bfloat16),
            "tensor",
            scatter_dimension=0,
            tiled=True,
        ).astype(jnp.float32)
        gain_one_grad = gain_one_grad + jnp.sum(grad_normed * scaled_one, axis=0)
        shift_one_grad = shift_one_grad + jnp.sum(grad_normed, axis=0)
        input_rows.append(
            grad_residual + norm_backward(grad_normed, scaled_one, inverse_one, gain_one)
        )
        reduced = (query_grad, key_grad, value_grad, out_grad, up_grad, down_grad)
        if weight_totals is None:
            weight_totals = reduced
        else:
            weight_totals = tuple((left + right for left, right in zip(weight_totals, reduced)))
    query_total, key_total, value_total, out_total, up_total, down_total = weight_totals
    query_total, key_total, value_total, out_total, up_total, down_total = (
        lax.psum_scatter(
            query_total.astype(jnp.bfloat16), "dp", scatter_dimension=0, tiled=True
        ).astype(jnp.float32),
        lax.psum_scatter(
            key_total.astype(jnp.bfloat16), "dp", scatter_dimension=0, tiled=True
        ).astype(jnp.float32),
        lax.psum_scatter(
            value_total.astype(jnp.bfloat16), "dp", scatter_dimension=0, tiled=True
        ).astype(jnp.float32),
        lax.psum_scatter(
            out_total.astype(jnp.bfloat16), "dp", scatter_dimension=1, tiled=True
        ).astype(jnp.float32),
        lax.psum_scatter(
            up_total.astype(jnp.bfloat16), "dp", scatter_dimension=0, tiled=True
        ).astype(jnp.float32),
        lax.psum_scatter(
            down_total.astype(jnp.bfloat16), "dp", scatter_dimension=1, tiled=True
        ).astype(jnp.float32),
    )
    vector_totals = (
        lax.psum_scatter(gain_one_grad, ("dp", "tensor"), scatter_dimension=0, tiled=True),
        lax.psum_scatter(shift_one_grad, ("dp", "tensor"), scatter_dimension=0, tiled=True),
        lax.psum_scatter(query_bias_grad, ("dp", "tensor"), scatter_dimension=0, tiled=True),
        lax.psum_scatter(value_bias_grad, ("dp", "tensor"), scatter_dimension=0, tiled=True),
        lax.psum_scatter(out_bias_grad, ("dp", "tensor"), scatter_dimension=0, tiled=True),
        lax.psum_scatter(gain_two_grad, ("dp", "tensor"), scatter_dimension=0, tiled=True),
        lax.psum_scatter(shift_two_grad, ("dp", "tensor"), scatter_dimension=0, tiled=True),
        lax.psum_scatter(up_bias_grad, ("dp", "tensor"), scatter_dimension=0, tiled=True),
        lax.psum_scatter(down_bias_grad, ("dp", "tensor"), scatter_dimension=0, tiled=True),
    )
    (
        gain_one_out,
        shift_one_out,
        query_bias_out,
        value_bias_out,
        out_bias_out,
        gain_two_out,
        shift_two_out,
        up_bias_out,
        down_bias_out,
    ) = vector_totals
    out_shape = (micro, 1, shard_rows, model_width)
    layer_out = jnp.stack(layer_rows).reshape(out_shape)
    input_grad = jnp.stack(input_rows).reshape(out_shape)
    return (
        layer_out,
        input_grad,
        gain_one_out,
        shift_one_out,
        query_total,
        query_bias_out,
        key_total,
        value_total,
        value_bias_out,
        out_total,
        out_bias_out,
        gain_two_out,
        shift_two_out,
        up_total,
        up_bias_out,
        down_total,
        down_bias_out,
    )


def _place(z, y, x):
    return z * 4 + y * 2 + x


def _coords():
    dp = lax.axis_index("dp")
    core = lax.axis_index("tensor")
    return dp // 4, (dp // 2) % 2, dp % 2, core


def _greet(peers):
    barrier = pltpu.get_barrier_semaphore()
    for peer in peers:
        pl.semaphore_signal(barrier, inc=1, device_id=peer, device_id_type=MESH)
    pl.semaphore_wait(barrier, len(peers))


def _peers():
    z, y, x, core = _coords()
    along = [(_place((z + j) % 4, y, x), core) for j in (1, 2, 3)]
    across = (_place(z, y, 1 - x), core)
    down = (_place(z, 1 - y, x), core)
    sibling = (_place(z, y, x), 1 - core)
    return along, across, down, sibling


def _send(src, dst, send_sem, recv_sem, peer):
    copy = pltpu.make_async_remote_copy(
        src_ref=src,
        dst_ref=dst,
        send_sem=send_sem,
        recv_sem=recv_sem,
        device_id=peer,
        device_id_type=MESH,
    )
    copy.start()
    return copy


def _local(src, dst, sem):
    copy = pltpu.make_async_copy(src, dst, sem)
    copy.start()
    return copy


def _dot(left, right, contract):
    return lax.dot_general(left, right, (contract, ((), ())), preferred_element_type=jnp.float32)


NN = ((1,), (0,))
NT = ((1,), (1,))
TN = ((0,), (0,))
LOG2E = 1.4426950408889634
MIB = 1024 * 1024
WIDE = 256


def _normal(values):
    center = values - jnp.mean(values, axis=-1, keepdims=True)
    inverse = lax.rsqrt(jnp.mean(center * center, axis=-1, keepdims=True) + EPSILON)
    return center * inverse, inverse


def _spans(seq_len, longest, step):
    return [(start, max(longest, start + step)) for start in range(0, seq_len, step)]


class Gather:
    def __init__(self, win, place, send_sem, recv_sem, local_sem):
        self.z, self.y, self.x, self.core = _coords()
        self.along, self.across, self.down, self.sibling = _peers()
        self.win, self.place, self.count = win, place, win.shape[0]
        self.send_sem, self.recv_sem, self.local_sem = send_sem, recv_sem, local_sem

    def _remote(self, k, slot, src, dst, peer):
        return pltpu.make_async_remote_copy(
            src_ref=src,
            dst_ref=dst,
            send_sem=self.send_sem.at[k, slot],
            recv_sem=self.recv_sem.at[k, slot],
            device_id=peer,
            device_id_type=MESH,
        )

    def line(self, k):
        own = self.place(k).at[self.core, self.z, self.y, self.x]
        here = pltpu.make_async_copy(self.win.at[k], own, self.local_sem.at[k])
        return [here] + [self._remote(k, j, self.win.at[k], own, self.along[j]) for j in range(3)]

    def plane(self, k):
        block = self.place(k).at[self.core, :, self.y, self.x]
        return [self._remote(k, 3, block, block, self.across), self._remote(k, 4, block, block, self.down)]

    def corner(self, k):
        part = self.win.shape[1] // 2
        one = self.place(k).at[self.core, :, 1 - self.y, self.x, 0:part]
        two = self.place(k).at[self.core, :, self.y, 1 - self.x, part : 2 * part]
        return [self._remote(k, 5, one, one, self.across), self._remote(k, 6, two, two, self.down)]

    def twin(self, k):
        block = self.place(k).at[self.core]
        return [self._remote(k, 7, block, block, self.sibling)]

    def start(self, stage, k):
        if 0 <= k < self.count:
            for copy in stage(k):
                copy.start()

    def wait(self, stage, k):
        if 0 <= k < self.count:
            for copy in stage(k):
                copy.wait()

    def tick(self, k, twin=True):
        self.wait(self.plane, k)
        self.start(self.corner, k)
        self.wait(self.line, k + 2)
        self.start(self.plane, k + 2)
        self.start(self.line, k + 4)
        if twin:
            self.wait(self.corner, k - 1)
            self.start(self.twin, k - 1)


ATTEND_SITES = 9
ATTEND_TICKS = {3: 0, 4: 8, 5: 17, 6: 25, 7: 34}
FEED_SITES = 6
FEED_TICKS = {8: 4, 9: 10, 10: 17, 11: 23, 12: 30}


def front_kernel(
    prefix, win, vec, xin, gin,
    full, qkv, mixed_out, probs_out, normed_out, x_out, lines, layer_out, gres_out, low_out, sums, gown, grecv, gbias,
    vfull, x, grad, second, residual, weights, ubias,
    ssem, rsem, lsem, vs, vr, vl, ws, wr, wl, wsem, osem, fs, fr, fl, es, er, el,
):
    f32, bf16 = jnp.float32, jnp.bfloat16
    seq_len, model = x.shape
    half = seq_len // 2
    block = 128

    def place(k):
        return full.at[k] if k < 4 else weights.at[k - 4]

    gather = Gather(win, place, ssem, rsem, lsem)
    z, y, xx, core = gather.z, gather.y, gather.x, gather.core
    along, across, down, sibling = gather.along, gather.across, gather.down, gather.sibling
    _greet(along + [across, down, sibling])

    gather.start(gather.line, 0)
    vown = vfull.at[z, y, xx, core]
    vline = [_local(vec, vown, vl.at[0])] + [_send(vec, vown, vs.at[j], vr.at[j], along[j]) for j in range(3)]
    for k in (1, 2, 3):
        gather.start(gather.line, k)
    mine = pl.ds(pl.multiple_of(core * half, half), half)
    swaps = []
    for i, (part, whole) in enumerate(((xin, x), (gin, grad))):
        swaps.append(_local(part.at[core], whole.at[mine], wl.at[i]))
        swaps.append(_send(part.at[1 - core], whole.at[mine], ws.at[i], wr.at[i], sibling))
    gather.wait(gather.line, 0)
    gather.start(gather.plane, 0)
    for s in vline:
        s.wait()
    vblock = vfull.at[:, y, xx, core]
    vone = [_send(vblock, vblock, vs.at[3], vr.at[3], across), _send(vblock, vblock, vs.at[4], vr.at[4], down)]
    gather.wait(gather.line, 1)
    gather.start(gather.plane, 1)
    for s in swaps:
        s.wait()
    saved = [_local(x, x_out, osem.at[0])]
    for s in vone:
        s.wait()
    vblock = vfull.at[:, 1 - y, xx, core]
    vtwo = _send(vblock, vblock, vs.at[5], vr.at[5], across)
    gather.tick(0)
    vtwo.wait()
    vblock = vfull.at[:, :, :, core]
    vthree = _send(vblock, vblock, vs.at[6], vr.at[6], sibling)
    vthree.wait()
    for zi in range(4):
        for yi in range(2):
            at = (zi * 2 + yi) * 128
            group = vfull[zi, yi, 0, 0] + vfull[zi, yi, 0, 1] + vfull[zi, yi, 1, 0] + vfull[zi, yi, 1, 1]
            lines[:, at : at + 128] = group[0:8]
            for xi in range(2):
                for ci in range(2):
                    i = ((zi * 2 + yi) * 2 + xi) * 2 + ci
                    piece = 2 * ((i % 16) // 4) + i // 16
                    ubias[piece, 0:1, (i % 4) * 128 : (i % 4) * 128 + 128] = vfull[zi, yi, xi, ci, 8:9]

    def attention(normed, wblk, stage, mixed, wout, probs):
        @pl.loop(0, seq_len // block)
        def _(i):
            rows = pl.ds(pl.multiple_of(i * block, block), block)
            scaled, _ = _normal(x[rows].astype(f32))
            normed[rows] = (scaled * lines[0:1] + lines[1:2]).astype(bf16)

        gather.tick(1)
        gather.tick(2)
        gather.wait(gather.corner, 2)
        gather.start(gather.twin, 2)
        keep = _local(normed, normed_out, osem.at[1])
        for k in range(3):
            gather.wait(gather.twin, k)

        def columns(pair):
            return pl.ds(pl.multiple_of((pair % 2) * WIDE, WIDE), WIDE)

        def load(pair):
            return [
                pltpu.make_async_copy(
                    full.at[i, pair // 2, :, :, :, :, columns(pair)], wblk.at[pair % 2, i], wsem.at[pair % 2, i]
                )
                for i in range(3)
            ]

        def store(pair):
            slot = pair % 2
            copies = [
                pltpu.make_async_copy(
                    stage.at[slot, i], qkv.at[i, pair // 2, :, columns(pair)], wsem.at[slot, 3 + i]
                )
                for i in range(3)
            ]
            heads = pl.ds(pair * 2, 2)
            return copies + [pltpu.make_async_copy(probs.at[slot], probs_out.at[heads], wsem.at[slot, 6])]

        for c in load(0):
            c.start()

        def ticks(site, pair):
            for k, at in ATTEND_TICKS.items():
                if at % ATTEND_SITES == site:

                    @pl.when(pair == at // ATTEND_SITES)
                    def _(k=k):
                        gather.tick(k, twin=k != 3)

        @pl.loop(0, 4)
        def _(pair):
            slot = pair % 2
            for c in load(pair):
                c.wait()

            @pl.when(pair < 3)
            def _():
                for c in load(pair + 1):
                    c.start()

            @pl.when(pair >= 2)
            def _():
                for c in store(pair - 2):
                    c.wait()

            ticks(0, pair)
            lanes = pl.ds(pl.multiple_of(pair * WIDE, WIDE), WIDE)
            wq, wk, wv = (wblk[slot, i].reshape(model, WIDE) for i in range(3))
            stage[slot, 0] = (_dot(normed[...], wq, NN) + lines[2:3, lanes]).astype(bf16)
            stage[slot, 1] = _dot(normed[...], wk, NN).astype(bf16)
            stage[slot, 2] = (_dot(normed[...], wv, NN) + lines[3:4, lanes]).astype(bf16)
            step = 256
            factor = LOG2E / math.sqrt(HEAD_DIM)
            prefix_len = prefix[0]
            site = 1
            for head in range(WIDE // HEAD_DIM):
                part = slice(head * HEAD_DIM, (head + 1) * HEAD_DIM)
                for start, stop in _spans(seq_len, LONGEST, step):
                    scores = _dot(stage[slot, 1, :stop, part], stage[slot, 0, start : start + step, part], NT)
                    keys = lax.broadcasted_iota(jnp.int32, scores.shape, 0)
                    queries = lax.broadcasted_iota(jnp.int32, scores.shape, 1) + start
                    scores = jnp.where((keys <= queries) | (keys < prefix_len), scores, -jnp.inf)
                    peak = jnp.max(scores, axis=0, keepdims=True)
                    raw = jnp.exp2((scores - peak) * factor)
                    total = jnp.sum(raw, axis=0, keepdims=True)
                    share = (raw * (1.0 / total)).astype(bf16)
                    probs[slot, head, :stop, start : start + step] = share
                    to = pl.ds(pl.multiple_of((pair % 2) * WIDE + head * HEAD_DIM, HEAD_DIM), HEAD_DIM)
                    mixed[pair // 2, start : start + step, to] = _dot(
                        share, stage[slot, 2, :stop, part], TN
                    ).astype(bf16)
                    if site < ATTEND_SITES:
                        ticks(site, pair)
                    site += 1
            for c in store(pair):
                c.start()

        gather.wait(gather.twin, 3)
        fetch = _local(full.at[3], wout, osem.at[3])
        done = _local(mixed, mixed_out, osem.at[2])
        fetch.wait()
        weight = [wout[c].reshape(model, seq_len // 2) for c in range(2)]
        step = 256

        @pl.loop(0, seq_len // step)
        def _(i):
            rows = pl.ds(pl.multiple_of(i * step, step), step)
            branch = _dot(mixed[0, rows], weight[0], NT) + _dot(mixed[1, rows], weight[1], NT)
            total = x[rows].astype(f32) + branch + lines[4:5]
            residual[rows] = total
            scaled, _ = _normal(total)
            second[rows] = (scaled * lines[5:6] + lines[6:7]).astype(bf16)

        for pair in (2, 3):
            for c in store(pair):
                c.wait()
        done.wait()
        keep.wait()

    pl.run_scoped(
        attention,
        pltpu.VMEM((seq_len, model), bf16),
        pltpu.VMEM((2, 3, 4, 2, 2, 64, WIDE), bf16),
        pltpu.VMEM((2, 3, seq_len, WIDE), bf16),
        pltpu.VMEM((2, seq_len, model // 2), bf16),
        pltpu.VMEM((2, 4, 2, 2, 64, model // 2), bf16),
        pltpu.VMEM((2, 2, seq_len, seq_len), bf16),
    )

    def feed(layer, gres, stage, hid, gpre):
        pieces = weights.shape[0]

        def ticks(site, t):
            for k, at in FEED_TICKS.items():
                if at % FEED_SITES == site:

                    @pl.when(t == at // FEED_SITES)
                    def _(k=k):
                        gather.tick(k)

        @pl.loop(0, seq_len // block)
        def _(i):
            rows = pl.ds(pl.multiple_of(i * block, block), block)
            layer[rows] = residual[rows] + lines[7:8]
            gres[rows] = jnp.zeros((block, model), f32)

        def away(piece):
            return [
                pltpu.make_async_remote_copy(
                    src_ref=stage.at[0, i],
                    dst_ref=grecv.at[2 * piece + i],
                    send_sem=fs.at[piece, i],
                    recv_sem=fr.at[piece, i],
                    device_id=sibling,
                    device_id_type=MESH,
                )
                for i in range(2)
            ]

        def stay(piece):
            return [pltpu.make_async_copy(stage.at[1, i], gown.at[2 * piece + i], fl.at[i]) for i in range(2)]

        @pl.loop(0, pieces)
        def _(t):
            piece, turn = t // 2, t % 2
            side = (t + 1 + core) % 2
            for p in range(pieces // 2):

                @pl.when(t == 2 * p)
                def _(p=p):
                    gather.wait(gather.twin, 4 + 2 * p)
                    gather.wait(gather.twin, 5 + 2 * p)

            ticks(0, t)
            up = weights[2 * piece, side].reshape(model, model // 2)
            lower = weights[2 * piece + 1, side].reshape(model, model // 2)
            line = 2 * piece + side
            pre = _dot(second[...], up, NN) + ubias[line]
            ticks(1, t)
            phi = 0.5 * (1.0 + lax.erf(pre * (1.0 / math.sqrt(2.0))))
            density = jnp.exp2(pre * pre * (-0.5 * LOG2E)) * (1.0 / math.sqrt(2.0 * math.pi))
            hid[...] = (pre * phi).astype(bf16)
            slope = phi + pre * density
            back = (_dot(grad[...], lower, NN) * slope).astype(bf16)
            gpre[...] = back
            gbias[line] = jnp.sum(back.astype(f32), axis=0, keepdims=True)
            ticks(2, t)
            layer[...] += _dot(hid[...], lower, NT)
            ticks(3, t)
            gres[...] += _dot(gpre[...], up, NT)
            ticks(4, t)

            @pl.when((t >= 2) & (turn == 0))
            def _():
                for c in away(piece - 1):
                    c.wait_send()

            @pl.when((t >= 2) & (turn == 1))
            def _():
                for c in stay(piece - 1):
                    c.wait()

            stage[turn, 0] = _dot(second[...], gpre[...], TN).astype(bf16)
            ticks(5, t)
            stage[turn, 1] = _dot(grad[...], hid[...], TN).astype(bf16)

            @pl.when(turn == 0)
            def _():
                for c in away(piece):
                    c.start()

            @pl.when(turn == 1)
            def _():
                for c in stay(piece):
                    c.start()

        theirs = pl.ds(pl.multiple_of((1 - core) * half, half), half)
        final = [
            _local(layer.at[mine], layer_out.at[core], el.at[0]),
            _send(layer.at[theirs], layer_out.at[core], es.at[0], er.at[0], sibling),
        ]
        sums[...] = jnp.zeros_like(sums)

        @pl.loop(0, seq_len // block)
        def _(i):
            rows = pl.ds(pl.multiple_of(i * block, block), block)
            scaled, inverse = _normal(residual[rows])
            grow = gres[rows]
            upstream = grad[rows].astype(f32)
            weighted = grow * lines[5:6]
            mean_plain = jnp.mean(weighted, axis=-1, keepdims=True)
            mean_scaled = jnp.mean(weighted * scaled, axis=-1, keepdims=True)
            total = upstream + inverse * (weighted - mean_plain - scaled * mean_scaled)
            gres[rows] = total
            second[rows] = total.astype(bf16)
            sums[0:1] += jnp.sum(grow * scaled, axis=0, keepdims=True)
            sums[1:2] += jnp.sum(grow, axis=0, keepdims=True)
            sums[2:3] += jnp.sum(total, axis=0, keepdims=True)
            sums[3:4] += jnp.sum(upstream, axis=0, keepdims=True)

        final.append(_local(gres, gres_out, el.at[1]))
        final.append(_local(second, low_out, el.at[2]))
        last = pieces // 2 - 1
        for c in away(last):
            c.wait_send()
        for c in stay(last):
            c.wait()
        for p in range(pieces // 2):
            for c in away(p):
                c.wait_recv()
        for c in final:
            c.wait()

    pl.run_scoped(
        feed,
        pltpu.VMEM((seq_len, model), f32),
        pltpu.VMEM((seq_len, model), f32),
        pltpu.VMEM((2, 2, model, model // 2), bf16),
        pltpu.VMEM((seq_len, model // 2), bf16),
        pltpu.VMEM((seq_len, model // 2), bf16),
    )
    for s in saved:
        s.wait()


def front(prefix_len, win, vec, xin, gin):
    chunks, rows, cols = win.shape
    half, model = xin.shape[1:]
    seq_len = 2 * half
    pieces = chunks - 4
    bf16, f32 = jnp.bfloat16, jnp.float32
    hbm = pl.BlockSpec(memory_space=pltpu.HBM)
    vmem = pl.BlockSpec(memory_space=pltpu.VMEM)
    dma = pltpu.SemaphoreType.DMA

    def shape(dims, dtype):
        return jax.ShapeDtypeStruct(dims, dtype)

    heads = model // HEAD_DIM
    return pl.pallas_call(
        front_kernel,
        out_shape=(
            shape((4, 2, 4, 2, 2, rows, cols), bf16),
            shape((3, 2, seq_len, cols), bf16),
            shape((2, seq_len, cols), bf16),
            shape((heads, seq_len, seq_len), bf16),
            shape((seq_len, model), bf16),
            shape((seq_len, model), bf16),
            shape((8, model), f32),
            shape((2, half, model), f32),
            shape((seq_len, model), f32),
            shape((seq_len, model), bf16),
            shape((8, model), f32),
            shape((pieces, model, cols), bf16),
            shape((pieces, model, cols), bf16),
            shape((pieces, 1, cols), f32),
        ),
        in_specs=[pl.BlockSpec(memory_space=pltpu.SMEM), vmem, vmem, hbm, hbm],
        out_specs=(hbm, hbm, hbm, hbm, hbm, hbm, vmem, hbm, hbm, hbm, vmem, hbm, hbm, vmem),
        scratch_shapes=[
            pltpu.VMEM((4, 2, 2, 2) + vec.shape, f32),
            pltpu.VMEM((seq_len, model), bf16),
            pltpu.VMEM((seq_len, model), bf16),
            pltpu.VMEM((seq_len, model), bf16),
            pltpu.VMEM((seq_len, model), f32),
            pltpu.VMEM((pieces, 2, 4, 2, 2, rows, cols), bf16),
            pltpu.VMEM((pieces, 1, cols), f32),
            dma((chunks, 8)),
            dma((chunks, 8)),
            dma((chunks,)),
            dma((7,)),
            dma((7,)),
            dma((1,)),
            dma((2,)),
            dma((2,)),
            dma((2,)),
            dma((2, 7)),
            dma((4,)),
            dma((pieces // 2, 2)),
            dma((pieces // 2, 2)),
            dma((2,)),
            dma((1,)),
            dma((1,)),
            dma((3,)),
        ],
        compiler_params=pltpu.CompilerParams(
            collective_id=0, has_side_effects=True, vmem_limit_bytes=63 * MIB
        ),
    )(prefix_len, win, vec, xin, gin)


def scatter_kernel(
    gq, gk, gv, go, gown, grecv, vg, ig,
    out, vout, iout,
    acc, from_s, x_one, y_one, x_two, y_two, from_z,
    vacc, v_s, vx_one, vx_two, vy_two, v_z,
    ssem, rsem, lsem, vs, vr, vl, ws, wr, wl,
):
    z, y, x, core = _coords()
    along, across, down, sibling = _peers()
    _greet(along + [across, down, sibling])
    chunks = acc.shape[0]
    f32 = jnp.float32
    tail = []
    sources = [gq, gk, gv, go]
    order = list(range(4, chunks)) + [3, 0, 1, 2]
    begun = {}
    for k in order:
        if k < 4:
            begun[k] = (
                _local(sources[k].at[core], acc.at[k], lsem.at[k, 0]),
                _send(sources[k].at[1 - core], from_s.at[k], ssem.at[k, 0], rsem.at[k, 0], sibling),
            )
        else:
            begun[k] = (
                _local(gown.at[k - 4], acc.at[k], lsem.at[k, 0]),
                _local(grecv.at[k - 4], from_s.at[k], lsem.at[k, 1]),
            )
        if k == 6:
            vbegun = (
                _local(vg.at[:, :, :, core], vacc, vl.at[0]),
                _send(vg.at[:, :, :, 1 - core], v_s, vs.at[0], vr.at[0], sibling),
            )
    for i, (rows, whole) in enumerate(((ig, iout),)):
        tail.append(_send(rows.at[1 - core], whole.at[core], ws.at[i], wr.at[i], sibling))
        tail.append(_local(rows.at[core], whole.at[core], wl.at[i]))

    def stage_one(k):
        for s in begun[k]:
            s.wait()

        @pl.loop(0, 4)
        def _(i):
            for j in range(2):
                for m in range(2):
                    acc[k, i, j, m] = (acc[k, i, j, m].astype(f32) + from_s[k, i, j, m].astype(f32)).astype(acc.dtype)

        return [
            _send(acc.at[k, :, 1 - y, 1 - x, 0:32], x_one.at[k], ssem.at[k, 1], rsem.at[k, 1], across),
            _send(acc.at[k, :, 1 - y, 1 - x, 32:64], y_one.at[k], ssem.at[k, 2], rsem.at[k, 2], down),
        ]

    def stage_two(k, before):
        for s in before:
            s.wait()
        acc[k, :, 1 - y, x, 0:32] = (acc[k, :, 1 - y, x, 0:32].astype(f32) + x_one[k].astype(f32)).astype(acc.dtype)
        acc[k, :, y, 1 - x, 32:64] = (acc[k, :, y, 1 - x, 32:64].astype(f32) + y_one[k].astype(f32)).astype(acc.dtype)
        return [
            _send(acc.at[k, :, y, 1 - x], x_two.at[k], ssem.at[k, 3], rsem.at[k, 3], across),
            _send(acc.at[k, :, 1 - y, x], y_two.at[k], ssem.at[k, 4], rsem.at[k, 4], down),
        ]

    def stage_three(k, before):
        for s in before:
            s.wait()
        acc[k, :, y, x] = (acc[k, :, y, x].astype(f32) + x_two[k].astype(f32) + y_two[k].astype(f32)).astype(acc.dtype)
        return [
            _send(acc.at[k, (z + j + 1) % 4, y, x], from_z.at[k, j], ssem.at[k, 5 + j], rsem.at[k, 5 + j], along[j])
            for j in range(3)
        ]

    def stage_four(k, before):
        for s in before:
            s.wait()
        total = acc[k, z, y, x].astype(f32)
        for j in range(3):
            total = total + from_z[k, j].astype(f32)
        out[k] = total

    lag = 1
    first, second, third = {}, {}, {}
    for t in range(chunks + 3 * lag):
        if t < chunks:
            first[t] = stage_one(order[t])
        if 0 <= t - lag < chunks:
            second[t - lag] = stage_two(order[t - lag], first[t - lag])
        if 0 <= t - 2 * lag < chunks:
            third[t - 2 * lag] = stage_three(order[t - 2 * lag], second[t - 2 * lag])
        if 0 <= t - 3 * lag < chunks:
            stage_four(order[t - 3 * lag], third[t - 3 * lag])
        if t == 0:
            for s in vbegun:
                s.wait()
            vacc[...] = vacc[...] + v_s[...]
            vone = _send(vacc.at[:, 1 - y, 1 - x], vx_one, vs.at[1], vr.at[1], across)
        if t == 2:
            vone.wait()
            vacc[:, 1 - y, x] = vacc[:, 1 - y, x] + vx_one[...]
            vtwo = [
                _send(vacc.at[:, y, 1 - x], vx_two, vs.at[2], vr.at[2], across),
                _send(vacc.at[:, 1 - y, x], vy_two, vs.at[3], vr.at[3], down),
            ]
        if t == 4:
            for s in vtwo:
                s.wait()
            vacc[:, y, x] = vacc[:, y, x] + vx_two[...] + vy_two[...]
            vthree = [
                _send(vacc.at[(z + j + 1) % 4, y, x], v_z.at[j], vs.at[4 + j], vr.at[4 + j], along[j])
                for j in range(3)
            ]
        if t == 6:
            for s in vthree:
                s.wait()
            vout[...] = vacc[z, y, x] + v_z[0] + v_z[1] + v_z[2]
    for s in tail:
        s.wait()


def scatter(gq, gk, gv, go, gown, grecv, vg, ig):
    chunks = 4 + gown.shape[0]
    rows, cols = gq.shape[-2:]
    bf16, f32 = jnp.bfloat16, jnp.float32
    hbm = pl.BlockSpec(memory_space=pltpu.HBM)
    vmem = pl.BlockSpec(memory_space=pltpu.VMEM)
    dma = pltpu.SemaphoreType.DMA
    small = vg.shape[-2:]
    return pl.pallas_call(
        scatter_kernel,
        out_shape=(
            jax.ShapeDtypeStruct((chunks, rows, cols), f32),
            jax.ShapeDtypeStruct(small, f32),
            jax.ShapeDtypeStruct(ig.shape, ig.dtype),
        ),
        in_specs=[hbm] * 8,
        out_specs=(vmem, vmem, hbm),
        scratch_shapes=[
            pltpu.VMEM((chunks, 4, 2, 2, rows, cols), bf16),
            pltpu.VMEM((chunks, 4, 2, 2, rows, cols), bf16),
            pltpu.VMEM((chunks, 4, rows // 2, cols), bf16),
            pltpu.VMEM((chunks, 4, rows // 2, cols), bf16),
            pltpu.VMEM((chunks, 4, rows, cols), bf16),
            pltpu.VMEM((chunks, 4, rows, cols), bf16),
            pltpu.VMEM((chunks, 3, rows, cols), bf16),
            pltpu.VMEM((4, 2, 2) + small, f32),
            pltpu.VMEM((4, 2, 2) + small, f32),
            pltpu.VMEM((4,) + small, f32),
            pltpu.VMEM((4,) + small, f32),
            pltpu.VMEM((4,) + small, f32),
            pltpu.VMEM((3,) + small, f32),
            dma((chunks, 8)),
            dma((chunks, 8)),
            dma((chunks, 2)),
            dma((7,)),
            dma((7,)),
            dma((1,)),
            dma((2,)),
            dma((2,)),
            dma((2,)),
        ],
        compiler_params=pltpu.CompilerParams(
            collective_id=1, has_side_effects=True, vmem_limit_bytes=56 * 1024 * 1024
        ),
    )(gq, gk, gv, go, gown, grecv, vg, ig)


def retreat_kernel(
    q, k, v, mixed, probs, low, normed, x, gres, lines, wq, wk, wv, wo,
    ingrad, gq, gk, gv, go, sums, bsums, dq, dk, dv, dmix, dk_acc, dv_acc,
):
    pair = pl.program_id(0)
    seq_len, model = x.shape
    f32, bf16 = jnp.float32, jnp.bfloat16
    step, block = 256, 128
    scale = 1.0 / math.sqrt(HEAD_DIM)

    @pl.when(pair == 0)
    def _():
        ingrad[...] = jnp.zeros_like(ingrad)

    dmix[...] = _dot(low[...], wo[0, 0], NN).astype(bf16)
    go[0] = _dot(low[...], mixed[0], TN).astype(bf16)
    for head in range(dq.shape[1] // HEAD_DIM):
        part = slice(head * HEAD_DIM, (head + 1) * HEAD_DIM)
        dk_acc[...] = jnp.zeros_like(dk_acc)
        dv_acc[...] = jnp.zeros_like(dv_acc)
        for start, stop in _spans(seq_len, LONGEST, step):
            grad = dmix[start : start + step, part]
            weights_low = probs[head, :stop, start : start + step]
            weights = weights_low.astype(f32)
            dprobs = _dot(v[0, 0, :stop, part], grad, NT)
            inner = jnp.sum(weights * dprobs, axis=0, keepdims=True)
            dscores = (weights * (dprobs - inner)).astype(bf16)
            dq[start : start + step, part] = (_dot(dscores, k[0, 0, :stop, part], TN) * scale).astype(bf16)
            dk_acc[:stop] += _dot(dscores, q[0, 0, start : start + step, part], NN)
            dv_acc[:stop] += _dot(weights_low, grad, NN)
        dk[:, part] = (dk_acc[...] * scale).astype(bf16)
        dv[:, part] = dv_acc[...].astype(bf16)
    gq[0] = _dot(normed[...], dq[...], TN).astype(bf16)
    gk[0] = _dot(normed[...], dk[...], TN).astype(bf16)
    gv[0] = _dot(normed[...], dv[...], TN).astype(bf16)
    ingrad[...] += _dot(dq[...], wq[0, 0], NT) + _dot(dk[...], wk[0, 0], NT) + _dot(dv[...], wv[0, 0], NT)
    bsums[0, 0:1] = jnp.sum(dq[...].astype(f32), axis=0, keepdims=True)
    bsums[0, 1:2] = jnp.sum(dv[...].astype(f32), axis=0, keepdims=True)

    @pl.when(pair == pl.num_programs(0) - 1)
    def _():
        sums[...] = jnp.zeros_like(sums)

        @pl.loop(0, seq_len // block)
        def _(i):
            rows = pl.ds(pl.multiple_of(i * block, block), block)
            scaled, inverse = _normal(x[rows].astype(f32))
            grow = ingrad[rows]
            weighted = grow * lines[0:1]
            mean_plain = jnp.mean(weighted, axis=-1, keepdims=True)
            mean_scaled = jnp.mean(weighted * scaled, axis=-1, keepdims=True)
            ingrad[rows] = gres[rows] + inverse * (weighted - mean_plain - scaled * mean_scaled)
            sums[0:1] += jnp.sum(grow * scaled, axis=0, keepdims=True)
            sums[1:2] += jnp.sum(grow, axis=0, keepdims=True)


def retreat(qkv, mixed, probs, low, normed, x, gres, lines, first):
    seq_len, model = x.shape
    cols = mixed.shape[2]
    wide = 256
    per = cols // wide
    bf16, f32 = jnp.bfloat16, jnp.float32
    whole = pl.BlockSpec(memory_space=pltpu.VMEM)

    def weight(i):
        return pl.BlockSpec((1, 1, model, wide), lambda p, i=i: (i, p // per, 0, p % per))

    heads = pl.BlockSpec((1, seq_len, wide), lambda p: (p // per, 0, p % per))

    def part(i):
        return pl.BlockSpec((1, 1, seq_len, wide), lambda p, i=i: (i, p // per, 0, p % per))

    grads = pl.BlockSpec((1, model, wide), lambda p: (p // per, 0, p % per))
    gshape = jax.ShapeDtypeStruct((2, model, cols), bf16)
    return pl.pallas_call(
        retreat_kernel,
        grid=(2 * per,),
        in_specs=[part(0), part(1), part(2), heads]
        + [pl.BlockSpec((wide // HEAD_DIM, seq_len, seq_len), lambda p: (p, 0, 0))]
        + [whole] * 5
        + [weight(0), weight(1), weight(2), weight(3)],
        out_specs=(whole, grads, grads, grads, grads, whole, pl.BlockSpec((1, 8, wide), lambda p: (p, 0, 0))),
        out_shape=(
            jax.ShapeDtypeStruct((seq_len, model), f32),
            gshape, gshape, gshape, gshape,
            jax.ShapeDtypeStruct((8, model), f32),
            jax.ShapeDtypeStruct((2 * per, 8, wide), f32),
        ),
        scratch_shapes=[pltpu.VMEM((seq_len, wide), bf16)] * 4 + [pltpu.VMEM((seq_len, HEAD_DIM), f32)] * 2,
        compiler_params=pltpu.CompilerParams(vmem_limit_bytes=56 * MIB),
    )(qkv, qkv, qkv, mixed, probs, low, normed, x, gres, lines, first, first, first, first)


def fast_body(
    inputs, prefix, ln1_gain, ln1_bias, query_weight, query_bias, key_weight, value_weight, value_bias,
    out_weight, out_bias, ln2_gain, ln2_bias, up_weight, up_bias, down_weight, down_bias, cotangent,
):
    f32 = jnp.float32
    core = lax.axis_index("tensor")
    half, model = inputs.shape[2], inputs.shape[3]
    rows, cols = query_weight.shape
    pieces = up_weight.shape[1] // cols

    def split(matrix):
        return [matrix[:, i * cols : (i + 1) * cols] for i in range(pieces)]

    ups, downs = split(up_weight), split(down_weight.T)
    feeds = [m for pair in zip(ups, downs) for m in pair]
    win = jnp.stack([query_weight, key_weight, value_weight, out_weight.T] + feeds)
    small = jnp.stack([ln1_gain, ln1_bias, query_bias, value_bias, out_bias, ln2_gain, ln2_bias, down_bias])
    place = (lax.axis_index("dp") * 2 + core) % 4
    vec = jnp.pad(up_bias.reshape(1, 128), ((8, 7), (0, 0)))
    vec = lax.dynamic_update_slice(vec, small, (0, place * 32))
    prefix_len = lax.dynamic_slice_in_dim(prefix[:, 0], core, 1)
    (
        full, qkv, mixed, probs, normed, x, lines, layer_out, gres, low, sums_two, gown, grecv, gup_bias,
    ) = front(prefix_len, win, vec, inputs[:, 0], cotangent[:, 0])
    first = full.reshape(4, 2, model, cols)
    input_rows, gq, gk, gv, gout, sums_one, bsums = retreat(qkv, mixed, probs, low, normed, x, gres, lines, first)
    sums = jnp.stack(
        [
            sums_one[0],
            sums_one[1],
            bsums[:, 0].reshape(model),
            bsums[:, 1].reshape(model),
            sums_two[2],
            sums_two[0],
            sums_two[1],
            sums_two[3],
        ]
    )
    vector = sums.reshape(8, 32, 32).transpose(1, 0, 2).reshape(32, 256)
    up_vector = gup_bias.reshape(pieces, 2, cols).transpose(1, 0, 2).reshape(32, 128)
    vg = jnp.pad(jnp.concatenate([vector, up_vector], axis=1), ((0, 0), (0, 640)))
    vg = vg.reshape(4, 2, 2, 2, 8, 128)
    six = (2, 4, 2, 2, rows, cols)
    summed = (2 * pieces, 4, 2, 2, rows, cols)
    out, vout, input_grad = scatter(
        gq.reshape(six), gk.reshape(six), gv.reshape(six), gout.reshape(six),
        gown.reshape(summed), grecv.reshape(summed), vg, input_rows.reshape(2, half, model),
    )
    flat = vout.reshape(-1)
    vectors = [flat[32 * i : 32 * i + 32] for i in range(8)]

    def join(pieces_of):
        return pieces_of.transpose(1, 0, 2).reshape(rows, pieces * cols)

    return (
        layer_out.reshape(2, 1, half, model),
        input_grad.reshape(2, 1, half, model),
        vectors[0],
        vectors[1],
        out[0],
        vectors[2],
        out[1],
        out[2],
        vectors[3],
        out[3].T,
        vectors[4],
        vectors[5],
        vectors[6],
        join(out[4::2]),
        flat[256:384],
        join(out[5::2]).T,
        vectors[7],
    )


def solution(mesh):
    in_specs = (
        P(None, "dp", "tensor", None),
        P(None, "dp"),
        P(("dp", "tensor")),
        P(("dp", "tensor")),
        P("dp", "tensor"),
        P(("dp", "tensor")),
        P("dp", "tensor"),
        P("dp", "tensor"),
        P(("dp", "tensor")),
        P("tensor", "dp"),
        P(("dp", "tensor")),
        P(("dp", "tensor")),
        P(("dp", "tensor")),
        P("dp", "tensor"),
        P(("dp", "tensor")),
        P("tensor", "dp"),
        P(("dp", "tensor")),
        P(None, "dp", "tensor", None),
    )
    out_specs = (
        P(None, "dp", "tensor", None),
        P(None, "dp", "tensor", None),
        P(("dp", "tensor")),
        P(("dp", "tensor")),
        P("dp", "tensor"),
        P(("dp", "tensor")),
        P("dp", "tensor"),
        P("dp", "tensor"),
        P(("dp", "tensor")),
        P("tensor", "dp"),
        P(("dp", "tensor")),
        P(("dp", "tensor")),
        P(("dp", "tensor")),
        P("dp", "tensor"),
        P(("dp", "tensor")),
        P("tensor", "dp"),
        P(("dp", "tensor")),
    )
    sizes = (mesh.shape["dp"], mesh.shape["tensor"])
    chosen = fast_body if sizes == (16, 2) else body
    return jax.shard_map(chosen, mesh=mesh, in_specs=in_specs, out_specs=out_specs, check_vma=False)
```

```python
import math

import jax
import jax.numpy as jnp
from jax import lax
from jax.experimental import pallas as pl
from jax.experimental.pallas import tpu as pltpu
from jax.sharding import PartitionSpec as P

MESH = pl.DeviceIdType.MESH
LONGEST = 512

HEAD_DIM = 128
BLOCK = 512


EPSILON = 1e-05


def norm_forward(values, gain, shift):
    center = values - jnp.mean(values, axis=-1, keepdims=True)
    inverse = lax.rsqrt(jnp.mean(center * center, axis=-1, keepdims=True) + EPSILON)
    scaled = center * inverse
    return (scaled * gain + shift, scaled, inverse)


def norm_backward(grad_out, scaled, inverse, gain):
    weighted = grad_out * gain
    mean_plain = jnp.mean(weighted, axis=-1, keepdims=True)
    mean_scaled = jnp.mean(weighted * scaled, axis=-1, keepdims=True)
    return inverse * (weighted - mean_plain - scaled * mean_scaled)


def smooth_gate(values):
    return jax.nn.gelu(values, approximate=False)


def smooth_slope(values):
    normal_cdf = 0.5 * (1.0 + jax.scipy.special.erf(values / math.sqrt(2.0)))
    density = jnp.exp(-0.5 * values * values) / math.sqrt(2.0 * math.pi)
    return normal_cdf + values * density


def masked_scores(query_block, key_rows, start, prefix_len):
    scale = 1.0 / math.sqrt(key_rows.shape[2])
    scores = (
        jnp.einsum("qhd,khd->hqk", query_block, key_rows, preferred_element_type=jnp.float32)
        * scale
    )
    places = start + jnp.arange(query_block.shape[0], dtype=jnp.int32)
    columns = jnp.arange(key_rows.shape[0], dtype=jnp.int32)
    allowed = (columns[None, :] <= places[:, None]) | (columns[None, :] < prefix_len)
    return jnp.where(allowed[None], scores, -jnp.inf)


def attend_forward(queries, key_rows, value_rows, prefix_len):
    seq_len, heads_local, head_size = queries.shape
    count = seq_len // BLOCK

    def one_block(items):
        query_block, start = items
        scores = masked_scores(query_block, key_rows, start, prefix_len)
        peak = jnp.max(scores, axis=-1, keepdims=True)
        raw_weights = jnp.exp(scores - peak)
        totals = jnp.sum(raw_weights, axis=-1, keepdims=True)
        probs = (raw_weights / totals).astype(jnp.bfloat16)
        mixed = jnp.einsum("hqk,khd->qhd", probs, value_rows, preferred_element_type=jnp.float32)
        return (mixed.astype(jnp.bfloat16), (peak + jnp.log(totals))[..., 0])

    starts = jnp.arange(count, dtype=jnp.int32) * BLOCK
    mixed, log_totals = lax.map(
        one_block, (queries.reshape(count, BLOCK, heads_local, head_size), starts)
    )
    return (mixed.reshape(seq_len, heads_local * head_size), log_totals)


def attend_backward(queries, key_rows, value_rows, grad_mixed, log_totals, prefix_len):
    seq_len, heads_local, head_size = queries.shape
    count = seq_len // BLOCK
    scale = 1.0 / math.sqrt(head_size)

    def one_block(carry, items):
        key_total, value_total = carry
        query_block, grad_block, log_block, start = items
        scores = masked_scores(query_block, key_rows, start, prefix_len)
        probs = jnp.exp(scores - log_block[..., None])
        grad_probs = jnp.einsum(
            "qhd,khd->hqk", grad_block, value_rows, preferred_element_type=jnp.float32
        )
        inner = jnp.sum(probs * grad_probs, axis=-1, keepdims=True)
        grad_scores = (probs * (grad_probs - inner)).astype(jnp.bfloat16)
        grad_query = (
            jnp.einsum("hqk,khd->qhd", grad_scores, key_rows, preferred_element_type=jnp.float32)
            * scale
        )
        key_total = (
            key_total
            + jnp.einsum(
                "hqk,qhd->khd", grad_scores, query_block, preferred_element_type=jnp.float32
            )
            * scale
        )
        value_total = value_total + jnp.einsum(
            "hqk,qhd->khd",
            probs.astype(jnp.bfloat16),
            grad_block,
            preferred_element_type=jnp.float32,
        )
        return ((key_total, value_total), grad_query.astype(jnp.bfloat16))

    empty_total = jnp.zeros(queries.shape, jnp.float32)
    starts = jnp.arange(count, dtype=jnp.int32) * BLOCK
    blocked = (count, BLOCK, heads_local, head_size)
    (key_total, value_total), grad_queries = lax.scan(
        one_block,
        (empty_total, empty_total),
        (queries.reshape(blocked), grad_mixed.reshape(blocked), log_totals, starts),
    )
    width = heads_local * head_size
    return (
        grad_queries.reshape(seq_len, width),
        key_total.astype(jnp.bfloat16).reshape(seq_len, width),
        value_total.astype(jnp.bfloat16).reshape(seq_len, width),
    )


def body(
    inputs,
    prefix,
    ln1_gain,
    ln1_bias,
    query_weight,
    query_bias,
    key_weight,
    value_weight,
    value_bias,
    out_weight,
    out_bias,
    ln2_gain,
    ln2_bias,
    up_weight,
    up_bias,
    down_weight,
    down_bias,
    cotangent,
):
    local_width = query_weight.shape[1]
    local_hidden = up_weight.shape[1]
    shard_rows = inputs.shape[2]
    micro = inputs.shape[0]
    model_width = inputs.shape[3]
    heads_local = local_width // HEAD_DIM
    offset_width = lax.axis_index("tensor") * local_width
    offset_hidden = lax.axis_index("tensor") * local_hidden
    vectors = (
        lax.all_gather(ln1_gain, ("dp", "tensor"), axis=0, tiled=True),
        lax.all_gather(ln1_bias, ("dp", "tensor"), axis=0, tiled=True),
        lax.all_gather(query_bias, ("dp", "tensor"), axis=0, tiled=True),
        lax.all_gather(value_bias, ("dp", "tensor"), axis=0, tiled=True),
        lax.all_gather(out_bias, ("dp", "tensor"), axis=0, tiled=True),
        lax.all_gather(ln2_gain, ("dp", "tensor"), axis=0, tiled=True),
        lax.all_gather(ln2_bias, ("dp", "tensor"), axis=0, tiled=True),
        lax.all_gather(up_bias, ("dp", "tensor"), axis=0, tiled=True),
        lax.all_gather(down_bias, ("dp", "tensor"), axis=0, tiled=True),
    )
    (
        gain_one,
        shift_one,
        query_full_bias,
        value_full_bias,
        out_shift,
        gain_two,
        shift_two,
        up_full_bias,
        down_shift,
    ) = vectors
    query_shift = lax.dynamic_slice_in_dim(query_full_bias, offset_width, local_width)
    value_shift = lax.dynamic_slice_in_dim(value_full_bias, offset_width, local_width)
    up_shift = lax.dynamic_slice_in_dim(up_full_bias, offset_hidden, local_hidden)
    zero_width = jnp.zeros((model_width,), jnp.float32)
    gain_one_grad = zero_width
    shift_one_grad = zero_width
    query_bias_grad = zero_width
    value_bias_grad = zero_width
    out_bias_grad = zero_width
    gain_two_grad = zero_width
    shift_two_grad = zero_width
    up_bias_grad = jnp.zeros((up_full_bias.shape[0],), jnp.float32)
    down_bias_grad = zero_width
    weight_totals = None
    layer_rows = []
    input_rows = []
    for index in range(micro):
        gathered = (
            lax.all_gather(query_weight, "dp", axis=0, tiled=True),
            lax.all_gather(key_weight, "dp", axis=0, tiled=True),
            lax.all_gather(value_weight, "dp", axis=0, tiled=True),
            lax.all_gather(out_weight, "dp", axis=1, tiled=True),
            lax.all_gather(up_weight, "dp", axis=0, tiled=True),
            lax.all_gather(down_weight, "dp", axis=1, tiled=True),
        )
        full_query, full_key, full_value, full_out, full_up, full_down = gathered
        rows_in = inputs[index, 0].astype(jnp.float32)
        prefix_len = prefix[index, 0]
        normed, scaled_one, inverse_one = norm_forward(rows_in, gain_one, shift_one)
        normed_all = lax.all_gather(normed.astype(jnp.bfloat16), "tensor", axis=0, tiled=True)
        seq_len = normed_all.shape[0]
        queries = (
            jnp.dot(normed_all, full_query, preferred_element_type=jnp.float32) + query_shift
        ).astype(jnp.bfloat16)
        key_rows = jnp.dot(normed_all, full_key, preferred_element_type=jnp.float32).astype(
            jnp.bfloat16
        )
        value_rows = (
            jnp.dot(normed_all, full_value, preferred_element_type=jnp.float32) + value_shift
        ).astype(jnp.bfloat16)
        head_shape = (seq_len, heads_local, HEAD_DIM)
        queries_h = queries.reshape(head_shape)
        keys_h = key_rows.reshape(head_shape)
        values_h = value_rows.reshape(head_shape)
        attended, log_totals = attend_forward(queries_h, keys_h, values_h, prefix_len)
        attention_share = lax.psum_scatter(
            jnp.dot(attended, full_out, preferred_element_type=jnp.float32).astype(jnp.bfloat16),
            "tensor",
            scatter_dimension=0,
            tiled=True,
        ).astype(jnp.float32)
        residual = rows_in + attention_share + out_shift
        second, scaled_two, inverse_two = norm_forward(residual, gain_two, shift_two)
        grad_rows = cotangent[index, 0]
        down_bias_grad = down_bias_grad + jnp.sum(grad_rows.astype(jnp.float32), axis=0)
        second_all = lax.all_gather(second.astype(jnp.bfloat16), "tensor", axis=0, tiled=True)
        hidden_pre = jnp.dot(second_all, full_up, preferred_element_type=jnp.float32) + up_shift
        hidden_act = smooth_gate(hidden_pre).astype(jnp.bfloat16)
        feed_share = lax.psum_scatter(
            jnp.dot(hidden_act, full_down, preferred_element_type=jnp.float32).astype(jnp.bfloat16),
            "tensor",
            scatter_dimension=0,
            tiled=True,
        ).astype(jnp.float32)
        layer_rows.append(residual + feed_share + down_shift)
        grad_all = lax.all_gather(grad_rows, "tensor", axis=0, tiled=True)
        down_grad = jnp.dot(hidden_act.T, grad_all, preferred_element_type=jnp.float32)
        grad_act = jnp.dot(grad_all, full_down.T, preferred_element_type=jnp.float32)
        grad_pre = (grad_act * smooth_slope(hidden_pre)).astype(jnp.bfloat16)
        up_grad = jnp.dot(second_all.T, grad_pre, preferred_element_type=jnp.float32)
        up_part = jnp.sum(grad_pre.astype(jnp.float32), axis=0)
        up_bias_grad = up_bias_grad + lax.dynamic_update_slice(
            jnp.zeros_like(up_bias_grad), up_part, (offset_hidden,)
        )
        grad_second = lax.psum_scatter(
            jnp.dot(grad_pre, full_up.T, preferred_element_type=jnp.float32).astype(jnp.bfloat16),
            "tensor",
            scatter_dimension=0,
            tiled=True,
        ).astype(jnp.float32)
        gain_two_grad = gain_two_grad + jnp.sum(grad_second * scaled_two, axis=0)
        shift_two_grad = shift_two_grad + jnp.sum(grad_second, axis=0)
        grad_residual = grad_rows.astype(jnp.float32) + norm_backward(
            grad_second, scaled_two, inverse_two, gain_two
        )
        out_bias_grad = out_bias_grad + jnp.sum(grad_residual, axis=0)
        residual_all = lax.all_gather(
            grad_residual.astype(jnp.bfloat16), "tensor", axis=0, tiled=True
        )
        out_grad = jnp.dot(attended.T, residual_all, preferred_element_type=jnp.float32)
        grad_attended = jnp.dot(
            residual_all, full_out.T, preferred_element_type=jnp.float32
        ).astype(jnp.bfloat16)
        grad_queries, grad_keys, grad_values = attend_backward(
            queries_h, keys_h, values_h, grad_attended, log_totals, prefix_len
        )
        query_grad = jnp.dot(normed_all.T, grad_queries, preferred_element_type=jnp.float32)
        key_grad = jnp.dot(normed_all.T, grad_keys, preferred_element_type=jnp.float32)
        value_grad = jnp.dot(normed_all.T, grad_values, preferred_element_type=jnp.float32)
        query_part = jnp.sum(grad_queries.astype(jnp.float32), axis=0)
        value_part = jnp.sum(grad_values.astype(jnp.float32), axis=0)
        query_bias_grad = query_bias_grad + lax.dynamic_update_slice(
            zero_width, query_part, (offset_width,)
        )
        value_bias_grad = value_bias_grad + lax.dynamic_update_slice(
            zero_width, value_part, (offset_width,)
        )
        partial_sum = jnp.dot(grad_queries, full_query.T, preferred_element_type=jnp.float32)
        partial_sum = partial_sum + jnp.dot(
            grad_keys, full_key.T, preferred_element_type=jnp.float32
        )
        grad_normed = lax.psum_scatter(
            (
                partial_sum + jnp.dot(grad_values, full_value.T, preferred_element_type=jnp.float32)
            ).astype(jnp.bfloat16),
            "tensor",
            scatter_dimension=0,
            tiled=True,
        ).astype(jnp.float32)
        gain_one_grad = gain_one_grad + jnp.sum(grad_normed * scaled_one, axis=0)
        shift_one_grad = shift_one_grad + jnp.sum(grad_normed, axis=0)
        input_rows.append(
            grad_residual + norm_backward(grad_normed, scaled_one, inverse_one, gain_one)
        )
        reduced = (query_grad, key_grad, value_grad, out_grad, up_grad, down_grad)
        if weight_totals is None:
            weight_totals = reduced
        else:
            weight_totals = tuple((left + right for left, right in zip(weight_totals, reduced)))
    query_total, key_total, value_total, out_total, up_total, down_total = weight_totals
    query_total, key_total, value_total, out_total, up_total, down_total = (
        lax.psum_scatter(
            query_total.astype(jnp.bfloat16), "dp", scatter_dimension=0, tiled=True
        ).astype(jnp.float32),
        lax.psum_scatter(
            key_total.astype(jnp.bfloat16), "dp", scatter_dimension=0, tiled=True
        ).astype(jnp.float32),
        lax.psum_scatter(
            value_total.astype(jnp.bfloat16), "dp", scatter_dimension=0, tiled=True
        ).astype(jnp.float32),
        lax.psum_scatter(
            out_total.astype(jnp.bfloat16), "dp", scatter_dimension=1, tiled=True
        ).astype(jnp.float32),
        lax.psum_scatter(
            up_total.astype(jnp.bfloat16), "dp", scatter_dimension=0, tiled=True
        ).astype(jnp.float32),
        lax.psum_scatter(
            down_total.astype(jnp.bfloat16), "dp", scatter_dimension=1, tiled=True
        ).astype(jnp.float32),
    )
    vector_totals = (
        lax.psum_scatter(gain_one_grad, ("dp", "tensor"), scatter_dimension=0, tiled=True),
        lax.psum_scatter(shift_one_grad, ("dp", "tensor"), scatter_dimension=0, tiled=True),
        lax.psum_scatter(query_bias_grad, ("dp", "tensor"), scatter_dimension=0, tiled=True),
        lax.psum_scatter(value_bias_grad, ("dp", "tensor"), scatter_dimension=0, tiled=True),
        lax.psum_scatter(out_bias_grad, ("dp", "tensor"), scatter_dimension=0, tiled=True),
        lax.psum_scatter(gain_two_grad, ("dp", "tensor"), scatter_dimension=0, tiled=True),
        lax.psum_scatter(shift_two_grad, ("dp", "tensor"), scatter_dimension=0, tiled=True),
        lax.psum_scatter(up_bias_grad, ("dp", "tensor"), scatter_dimension=0, tiled=True),
        lax.psum_scatter(down_bias_grad, ("dp", "tensor"), scatter_dimension=0, tiled=True),
    )
    (
        gain_one_out,
        shift_one_out,
        query_bias_out,
        value_bias_out,
        out_bias_out,
        gain_two_out,
        shift_two_out,
        up_bias_out,
        down_bias_out,
    ) = vector_totals
    out_shape = (micro, 1, shard_rows, model_width)
    layer_out = jnp.stack(layer_rows).reshape(out_shape)
    input_grad = jnp.stack(input_rows).reshape(out_shape)
    return (
        layer_out,
        input_grad,
        gain_one_out,
        shift_one_out,
        query_total,
        query_bias_out,
        key_total,
        value_total,
        value_bias_out,
        out_total,
        out_bias_out,
        gain_two_out,
        shift_two_out,
        up_total,
        up_bias_out,
        down_total,
        down_bias_out,
    )


def _place(z, y, x):
    return z * 4 + y * 2 + x


def _coords():
    dp = lax.axis_index("dp")
    core = lax.axis_index("tensor")
    return dp // 4, (dp // 2) % 2, dp % 2, core


def _greet(peers):
    barrier = pltpu.get_barrier_semaphore()
    for peer in peers:
        pl.semaphore_signal(barrier, inc=1, device_id=peer, device_id_type=MESH)
    pl.semaphore_wait(barrier, len(peers))


def _peers():
    z, y, x, core = _coords()
    along = [(_place((z + j) % 4, y, x), core) for j in (1, 2, 3)]
    across = (_place(z, y, 1 - x), core)
    down = (_place(z, 1 - y, x), core)
    sibling = (_place(z, y, x), 1 - core)
    return along, across, down, sibling


def _send(src, dst, send_sem, recv_sem, peer):
    copy = pltpu.make_async_remote_copy(
        src_ref=src,
        dst_ref=dst,
        send_sem=send_sem,
        recv_sem=recv_sem,
        device_id=peer,
        device_id_type=MESH,
    )
    copy.start()
    return copy


def _local(src, dst, sem):
    copy = pltpu.make_async_copy(src, dst, sem)
    copy.start()
    return copy


def _dot(left, right, contract):
    return lax.dot_general(left, right, (contract, ((), ())), preferred_element_type=jnp.float32)


NN = ((1,), (0,))
NT = ((1,), (1,))
TN = ((0,), (0,))
LOG2E = 1.4426950408889634
MIB = 1024 * 1024
WIDE = 256


def _normal(values):
    center = values - jnp.mean(values, axis=-1, keepdims=True)
    inverse = lax.rsqrt(jnp.mean(center * center, axis=-1, keepdims=True) + EPSILON)
    return center * inverse, inverse


def _spans(seq_len, longest, step):
    return [(start, max(longest, start + step)) for start in range(0, seq_len, step)]


class Gather:
    def __init__(self, win, place, send_sem, recv_sem, local_sem):
        self.z, self.y, self.x, self.core = _coords()
        self.along, self.across, self.down, self.sibling = _peers()
        self.win, self.place, self.count = win, place, win.shape[0]
        self.send_sem, self.recv_sem, self.local_sem = send_sem, recv_sem, local_sem

    def _remote(self, k, slot, src, dst, peer):
        return pltpu.make_async_remote_copy(
            src_ref=src,
            dst_ref=dst,
            send_sem=self.send_sem.at[k, slot],
            recv_sem=self.recv_sem.at[k, slot],
            device_id=peer,
            device_id_type=MESH,
        )

    def line(self, k):
        own = self.place(k).at[self.core, self.z, self.y, self.x]
        here = pltpu.make_async_copy(self.win.at[k], own, self.local_sem.at[k])
        return [here] + [self._remote(k, j, self.win.at[k], own, self.along[j]) for j in range(3)]

    def plane(self, k):
        block = self.place(k).at[self.core, :, self.y, self.x]
        return [self._remote(k, 3, block, block, self.across), self._remote(k, 4, block, block, self.down)]

    def corner(self, k):
        part = self.win.shape[1] // 2
        one = self.place(k).at[self.core, :, 1 - self.y, self.x, 0:part]
        two = self.place(k).at[self.core, :, self.y, 1 - self.x, part : 2 * part]
        return [self._remote(k, 5, one, one, self.across), self._remote(k, 6, two, two, self.down)]

    def twin(self, k):
        block = self.place(k).at[self.core]
        return [self._remote(k, 7, block, block, self.sibling)]

    def start(self, stage, k):
        if 0 <= k < self.count:
            for copy in stage(k):
                copy.start()

    def wait(self, stage, k):
        if 0 <= k < self.count:
            for copy in stage(k):
                copy.wait()

    def tick(self, k, twin=True):
        self.wait(self.plane, k)
        self.start(self.corner, k)
        self.wait(self.line, k + 2)
        self.start(self.plane, k + 2)
        self.start(self.line, k + 4)
        if twin:
            self.wait(self.corner, k - 1)
            self.start(self.twin, k - 1)


ATTEND_SITES = 9
ATTEND_TICKS = {3: 0, 4: 8, 5: 17, 6: 25, 7: 34}
FEED_SITES = 6
FEED_TICKS = {8: 4, 9: 10, 10: 17, 11: 23, 12: 30}


def front_kernel(
    prefix, win, vec, xin, gin,
    full, qkv, mixed_out, probs_out, normed_out, x_out, lines, layer_out, gres_out, low_out, sums, gown, grecv, gbias,
    vfull, x, grad, second, residual, weights, ubias,
    ssem, rsem, lsem, vs, vr, vl, ws, wr, wl, wsem, osem, fs, fr, fl, es, er, el,
):
    f32, bf16 = jnp.float32, jnp.bfloat16
    seq_len, model = x.shape
    half = seq_len // 2
    block = 128

    def place(k):
        return full.at[k] if k < 4 else weights.at[k - 4]

    gather = Gather(win, place, ssem, rsem, lsem)
    z, y, xx, core = gather.z, gather.y, gather.x, gather.core
    along, across, down, sibling = gather.along, gather.across, gather.down, gather.sibling
    _greet(along + [across, down, sibling])

    gather.start(gather.line, 0)
    vown = vfull.at[z, y, xx, core]
    vline = [_local(vec, vown, vl.at[0])] + [_send(vec, vown, vs.at[j], vr.at[j], along[j]) for j in range(3)]
    for k in (1, 2, 3):
        gather.start(gather.line, k)
    mine = pl.ds(pl.multiple_of(core * half, half), half)
    swaps = []
    for i, (part, whole) in enumerate(((xin, x), (gin, grad))):
        swaps.append(_local(part.at[core], whole.at[mine], wl.at[i]))
        swaps.append(_send(part.at[1 - core], whole.at[mine], ws.at[i], wr.at[i], sibling))
    gather.wait(gather.line, 0)
    gather.start(gather.plane, 0)
    for s in vline:
        s.wait()
    vblock = vfull.at[:, y, xx, core]
    vone = [_send(vblock, vblock, vs.at[3], vr.at[3], across), _send(vblock, vblock, vs.at[4], vr.at[4], down)]
    gather.wait(gather.line, 1)
    gather.start(gather.plane, 1)
    for s in swaps:
        s.wait()
    saved = [_local(x, x_out, osem.at[0])]
    for s in vone:
        s.wait()
    vblock = vfull.at[:, 1 - y, xx, core]
    vtwo = _send(vblock, vblock, vs.at[5], vr.at[5], across)
    gather.tick(0)
    vtwo.wait()
    vblock = vfull.at[:, :, :, core]
    vthree = _send(vblock, vblock, vs.at[6], vr.at[6], sibling)
    vthree.wait()
    for zi in range(4):
        for yi in range(2):
            at = (zi * 2 + yi) * 128
            group = vfull[zi, yi, 0, 0] + vfull[zi, yi, 0, 1] + vfull[zi, yi, 1, 0] + vfull[zi, yi, 1, 1]
            lines[:, at : at + 128] = group[0:8]
            for xi in range(2):
                for ci in range(2):
                    i = ((zi * 2 + yi) * 2 + xi) * 2 + ci
                    piece = 2 * ((i % 16) // 4) + i // 16
                    ubias[piece, 0:1, (i % 4) * 128 : (i % 4) * 128 + 128] = vfull[zi, yi, xi, ci, 8:9]

    def attention(normed, wblk, stage, mixed, wout, probs):
        @pl.loop(0, seq_len // block)
        def _(i):
            rows = pl.ds(pl.multiple_of(i * block, block), block)
            scaled, _ = _normal(x[rows].astype(f32))
            normed[rows] = (scaled * lines[0:1] + lines[1:2]).astype(bf16)

        gather.tick(1)
        gather.tick(2)
        gather.wait(gather.corner, 2)
        gather.start(gather.twin, 2)
        keep = _local(normed, normed_out, osem.at[1])
        for k in range(3):
            gather.wait(gather.twin, k)

        def columns(pair):
            return pl.ds(pl.multiple_of((pair % 2) * WIDE, WIDE), WIDE)

        def load(pair):
            return [
                pltpu.make_async_copy(
                    full.at[i, pair // 2, :, :, :, :, columns(pair)], wblk.at[pair % 2, i], wsem.at[pair % 2, i]
                )
                for i in range(3)
            ]

        def store(pair):
            slot = pair % 2
            copies = [
                pltpu.make_async_copy(
                    stage.at[slot, i], qkv.at[i, pair // 2, :, columns(pair)], wsem.at[slot, 3 + i]
                )
                for i in range(3)
            ]
            heads = pl.ds(pair * 2, 2)
            return copies + [pltpu.make_async_copy(probs.at[slot], probs_out.at[heads], wsem.at[slot, 6])]

        for c in load(0):
            c.start()

        def ticks(site, pair):
            for k, at in ATTEND_TICKS.items():
                if at % ATTEND_SITES == site:

                    @pl.when(pair == at // ATTEND_SITES)
                    def _(k=k):
                        gather.tick(k, twin=k != 3)

        @pl.loop(0, 4)
        def _(pair):
            slot = pair % 2
            for c in load(pair):
                c.wait()

            @pl.when(pair < 3)
            def _():
                for c in load(pair + 1):
                    c.start()

            @pl.when(pair >= 2)
            def _():
                for c in store(pair - 2):
                    c.wait()

            ticks(0, pair)
            lanes = pl.ds(pl.multiple_of(pair * WIDE, WIDE), WIDE)
            wq, wk, wv = (wblk[slot, i].reshape(model, WIDE) for i in range(3))
            stage[slot, 0] = (_dot(normed[...], wq, NN) + lines[2:3, lanes]).astype(bf16)
            stage[slot, 1] = _dot(normed[...], wk, NN).astype(bf16)
            stage[slot, 2] = (_dot(normed[...], wv, NN) + lines[3:4, lanes]).astype(bf16)
            step = 256
            factor = LOG2E / math.sqrt(HEAD_DIM)
            prefix_len = prefix[0]
            site = 1
            for head in range(WIDE // HEAD_DIM):
                part = slice(head * HEAD_DIM, (head + 1) * HEAD_DIM)
                for start, stop in _spans(seq_len, LONGEST, step):
                    scores = _dot(stage[slot, 1, :stop, part], stage[slot, 0, start : start + step, part], NT)
                    keys = lax.broadcasted_iota(jnp.int32, scores.shape, 0)
                    queries = lax.broadcasted_iota(jnp.int32, scores.shape, 1) + start
                    scores = jnp.where((keys <= queries) | (keys < prefix_len), scores, -jnp.inf)
                    peak = jnp.max(scores, axis=0, keepdims=True)
                    raw = jnp.exp2((scores - peak) * factor)
                    total = jnp.sum(raw, axis=0, keepdims=True)
                    share = (raw * (1.0 / total)).astype(bf16)
                    probs[slot, head, :stop, start : start + step] = share
                    to = pl.ds(pl.multiple_of((pair % 2) * WIDE + head * HEAD_DIM, HEAD_DIM), HEAD_DIM)
                    mixed[pair // 2, start : start + step, to] = _dot(
                        share, stage[slot, 2, :stop, part], TN
                    ).astype(bf16)
                    if site < ATTEND_SITES:
                        ticks(site, pair)
                    site += 1
            for c in store(pair):
                c.start()

        gather.wait(gather.twin, 3)
        fetch = _local(full.at[3], wout, osem.at[3])
        done = _local(mixed, mixed_out, osem.at[2])
        fetch.wait()
        weight = [wout[c].reshape(model, seq_len // 2) for c in range(2)]
        step = 256

        @pl.loop(0, seq_len // step)
        def _(i):
            rows = pl.ds(pl.multiple_of(i * step, step), step)
            branch = _dot(mixed[0, rows], weight[0], NT) + _dot(mixed[1, rows], weight[1], NT)
            total = x[rows].astype(f32) + branch + lines[4:5]
            residual[rows] = total
            scaled, _ = _normal(total)
            second[rows] = (scaled * lines[5:6] + lines[6:7]).astype(bf16)

        for pair in (2, 3):
            for c in store(pair):
                c.wait()
        done.wait()
        keep.wait()

    pl.run_scoped(
        attention,
        pltpu.VMEM((seq_len, model), bf16),
        pltpu.VMEM((2, 3, 4, 2, 2, 64, WIDE), bf16),
        pltpu.VMEM((2, 3, seq_len, WIDE), bf16),
        pltpu.VMEM((2, seq_len, model // 2), bf16),
        pltpu.VMEM((2, 4, 2, 2, 64, model // 2), bf16),
        pltpu.VMEM((2, 2, seq_len, seq_len), bf16),
    )

    def feed(layer, gres, stage, hid, gpre):
        pieces = weights.shape[0]

        def ticks(site, t):
            for k, at in FEED_TICKS.items():
                if at % FEED_SITES == site:

                    @pl.when(t == at // FEED_SITES)
                    def _(k=k):
                        gather.tick(k)

        @pl.loop(0, seq_len // block)
        def _(i):
            rows = pl.ds(pl.multiple_of(i * block, block), block)
            layer[rows] = residual[rows] + lines[7:8]
            gres[rows] = jnp.zeros((block, model), f32)

        def away(piece):
            return [
                pltpu.make_async_remote_copy(
                    src_ref=stage.at[0, i],
                    dst_ref=grecv.at[2 * piece + i],
                    send_sem=fs.at[piece, i],
                    recv_sem=fr.at[piece, i],
                    device_id=sibling,
                    device_id_type=MESH,
                )
                for i in range(2)
            ]

        def stay(piece):
            return [pltpu.make_async_copy(stage.at[1, i], gown.at[2 * piece + i], fl.at[i]) for i in range(2)]

        @pl.loop(0, pieces)
        def _(t):
            piece, turn = t // 2, t % 2
            side = (t + 1 + core) % 2
            for p in range(pieces // 2):

                @pl.when(t == 2 * p)
                def _(p=p):
                    gather.wait(gather.twin, 4 + 2 * p)
                    gather.wait(gather.twin, 5 + 2 * p)

            ticks(0, t)
            up = weights[2 * piece, side].reshape(model, model // 2)
            lower = weights[2 * piece + 1, side].reshape(model, model // 2)
            line = 2 * piece + side
            pre = _dot(second[...], up, NN) + ubias[line]
            ticks(1, t)
            phi = 0.5 * (1.0 + lax.erf(pre * (1.0 / math.sqrt(2.0))))
            density = jnp.exp2(pre * pre * (-0.5 * LOG2E)) * (1.0 / math.sqrt(2.0 * math.pi))
            hid[...] = (pre * phi).astype(bf16)
            slope = phi + pre * density
            back = (_dot(grad[...], lower, NN) * slope).astype(bf16)
            gpre[...] = back
            gbias[line] = jnp.sum(back.astype(f32), axis=0, keepdims=True)
            ticks(2, t)
            layer[...] += _dot(hid[...], lower, NT)
            ticks(3, t)
            gres[...] += _dot(gpre[...], up, NT)
            ticks(4, t)

            @pl.when((t >= 2) & (turn == 0))
            def _():
                for c in away(piece - 1):
                    c.wait_send()

            @pl.when((t >= 2) & (turn == 1))
            def _():
                for c in stay(piece - 1):
                    c.wait()

            stage[turn, 0] = _dot(second[...], gpre[...], TN).astype(bf16)
            ticks(5, t)
            stage[turn, 1] = _dot(grad[...], hid[...], TN).astype(bf16)

            @pl.when(turn == 0)
            def _():
                for c in away(piece):
                    c.start()

            @pl.when(turn == 1)
            def _():
                for c in stay(piece):
                    c.start()

        theirs = pl.ds(pl.multiple_of((1 - core) * half, half), half)
        final = [
            _local(layer.at[mine], layer_out.at[core], el.at[0]),
            _send(layer.at[theirs], layer_out.at[core], es.at[0], er.at[0], sibling),
        ]
        sums[...] = jnp.zeros_like(sums)

        @pl.loop(0, seq_len // block)
        def _(i):
            rows = pl.ds(pl.multiple_of(i * block, block), block)
            scaled, inverse = _normal(residual[rows])
            grow = gres[rows]
            upstream = grad[rows].astype(f32)
            weighted = grow * lines[5:6]
            mean_plain = jnp.mean(weighted, axis=-1, keepdims=True)
            mean_scaled = jnp.mean(weighted * scaled, axis=-1, keepdims=True)
            total = upstream + inverse * (weighted - mean_plain - scaled * mean_scaled)
            gres[rows] = total
            second[rows] = total.astype(bf16)
            sums[0:1] += jnp.sum(grow * scaled, axis=0, keepdims=True)
            sums[1:2] += jnp.sum(grow, axis=0, keepdims=True)
            sums[2:3] += jnp.sum(total, axis=0, keepdims=True)
            sums[3:4] += jnp.sum(upstream, axis=0, keepdims=True)

        final.append(_local(gres, gres_out, el.at[1]))
        final.append(_local(second, low_out, el.at[2]))
        last = pieces // 2 - 1
        for c in away(last):
            c.wait_send()
        for c in stay(last):
            c.wait()
        for p in range(pieces // 2):
            for c in away(p):
                c.wait_recv()
        for c in final:
            c.wait()

    pl.run_scoped(
        feed,
        pltpu.VMEM((seq_len, model), f32),
        pltpu.VMEM((seq_len, model), f32),
        pltpu.VMEM((2, 2, model, model // 2), bf16),
        pltpu.VMEM((seq_len, model // 2), bf16),
        pltpu.VMEM((seq_len, model // 2), bf16),
    )
    for s in saved:
        s.wait()


def front(prefix_len, win, vec, xin, gin):
    chunks, rows, cols = win.shape
    half, model = xin.shape[1:]
    seq_len = 2 * half
    pieces = chunks - 4
    bf16, f32 = jnp.bfloat16, jnp.float32
    hbm = pl.BlockSpec(memory_space=pltpu.HBM)
    vmem = pl.BlockSpec(memory_space=pltpu.VMEM)
    dma = pltpu.SemaphoreType.DMA

    def shape(dims, dtype):
        return jax.ShapeDtypeStruct(dims, dtype)

    heads = model // HEAD_DIM
    return pl.pallas_call(
        front_kernel,
        out_shape=(
            shape((4, 2, 4, 2, 2, rows, cols), bf16),
            shape((3, 2, seq_len, cols), bf16),
            shape((2, seq_len, cols), bf16),
            shape((heads, seq_len, seq_len), bf16),
            shape((seq_len, model), bf16),
            shape((seq_len, model), bf16),
            shape((8, model), f32),
            shape((2, half, model), f32),
            shape((seq_len, model), f32),
            shape((seq_len, model), bf16),
            shape((8, model), f32),
            shape((pieces, model, cols), bf16),
            shape((pieces, model, cols), bf16),
            shape((pieces, 1, cols), f32),
        ),
        in_specs=[pl.BlockSpec(memory_space=pltpu.SMEM), vmem, vmem, hbm, hbm],
        out_specs=(hbm, hbm, hbm, hbm, hbm, hbm, vmem, hbm, hbm, hbm, vmem, hbm, hbm, vmem),
        scratch_shapes=[
            pltpu.VMEM((4, 2, 2, 2) + vec.shape, f32),
            pltpu.VMEM((seq_len, model), bf16),
            pltpu.VMEM((seq_len, model), bf16),
            pltpu.VMEM((seq_len, model), bf16),
            pltpu.VMEM((seq_len, model), f32),
            pltpu.VMEM((pieces, 2, 4, 2, 2, rows, cols), bf16),
            pltpu.VMEM((pieces, 1, cols), f32),
            dma((chunks, 8)),
            dma((chunks, 8)),
            dma((chunks,)),
            dma((7,)),
            dma((7,)),
            dma((1,)),
            dma((2,)),
            dma((2,)),
            dma((2,)),
            dma((2, 7)),
            dma((4,)),
            dma((pieces // 2, 2)),
            dma((pieces // 2, 2)),
            dma((2,)),
            dma((1,)),
            dma((1,)),
            dma((3,)),
        ],
        compiler_params=pltpu.CompilerParams(
            collective_id=0, has_side_effects=True, vmem_limit_bytes=63 * MIB
        ),
    )(prefix_len, win, vec, xin, gin)


def _if(condition, action):
    if isinstance(condition, bool):
        if condition:
            action()
    else:
        pl.when(condition)(action)


class Reduce:
    def __init__(self, acc, out, x_one, y_one, x_two, y_two, from_z, send_sem, recv_sem):
        self.z, self.y, self.x, self.core = _coords()
        self.along, self.across, self.down, self.sibling = _peers()
        self.acc, self.out = acc, out
        self.x_one, self.y_one, self.x_two, self.y_two, self.from_z = x_one, y_one, x_two, y_two, from_z
        self.send_sem, self.recv_sem = send_sem, recv_sem

    def _remote(self, k, slot, src, dst, peer):
        return pltpu.make_async_remote_copy(
            src_ref=src,
            dst_ref=dst,
            send_sem=self.send_sem.at[k, slot],
            recv_sem=self.recv_sem.at[k, slot],
            device_id=peer,
            device_id_type=MESH,
        )

    def corner(self, k):
        block = self.acc(k).at[:, 1 - self.y, 1 - self.x]
        part = block.shape[1] // 2
        return [
            self._remote(k, 0, block.at[:, 0:part], self.x_one.at[k], self.across),
            self._remote(k, 1, block.at[:, part : 2 * part], self.y_one.at[k], self.down),
        ]

    def plane(self, k):
        acc = self.acc(k)
        return [
            self._remote(k, 2, acc.at[:, self.y, 1 - self.x], self.x_two.at[k], self.across),
            self._remote(k, 3, acc.at[:, 1 - self.y, self.x], self.y_two.at[k], self.down),
        ]

    def line(self, k):
        acc = self.acc(k)
        return [
            self._remote(k, 4 + j, acc.at[(self.z + j + 1) % 4, self.y, self.x], self.from_z.at[k, j], self.along[j])
            for j in range(3)
        ]

    @staticmethod
    def start(copies):
        for copy in copies:
            copy.start()

    @staticmethod
    def wait(copies):
        for copy in copies:
            copy.wait()

    def after_corner(self, k):
        acc, y, x = self.acc(k), self.y, self.x
        part = acc.shape[3] // 2
        self.wait(self.corner(k))
        one = acc.at[:, 1 - y, x, 0:part]
        two = acc.at[:, y, 1 - x, part : 2 * part]
        one[...] = _add(one[...], self.x_one[k])
        two[...] = _add(two[...], self.y_one[k])
        self.start(self.plane(k))

    def after_plane(self, k):
        acc = self.acc(k)
        self.wait(self.plane(k))
        here = acc.at[:, self.y, self.x]
        here[...] = _add(here[...], self.x_two[k], self.y_two[k])
        self.start(self.line(k))

    def after_line(self, k):
        self.wait(self.line(k))
        total = self.acc(k)[self.z, self.y, self.x].astype(self.out.dtype)
        for j in range(3):
            total = total + self.from_z[k, j].astype(self.out.dtype)
        self.out[k] = total


def _add(first, *others):
    total = first.astype(jnp.float32)
    for other in others:
        total = total + other.astype(jnp.float32)
    return total.astype(first.dtype)


RING = 4


def back_kernel(
    lines, sums_two, gbias, qkv, mixed_in, probs_in, full, low_in, normed_in, x_in, gres_in, gown, grecv,
    out, vout, iout, qrecv,
    ring, theirs_in, own, x_one, y_one, x_two, y_two, from_z,
    vacc, v_s, vx_one, vx_two, vy_two, v_z,
    low, normed, ingrad, sums, bsums,
    ssem, rsem, lsem, qs, qr, vs, vr, bsem, msem, es, er,
):
    f32, bf16 = jnp.float32, jnp.bfloat16
    seq_len, model = low.shape
    half, block, step = seq_len // 2, 128, 256
    feeds = gown.shape[0]
    count = out.shape[0]
    scale = 1.0 / math.sqrt(HEAD_DIM)

    def acc(k):
        return own.at[k - feeds] if isinstance(k, int) and k >= feeds else ring.at[k % RING]

    reduce = Reduce(acc, out, x_one, y_one, x_two, y_two, from_z, ssem, rsem)
    z, y, x, core = reduce.z, reduce.y, reduce.x, reduce.core
    along, across, down, sibling = reduce.along, reduce.across, reduce.down, reduce.sibling

    def load(k):
        if isinstance(k, int) and k >= feeds:
            return [pltpu.make_async_copy(qrecv.at[k - feeds], theirs_in.at[k % 2], lsem.at[k % 2, 1])]
        return [
            pltpu.make_async_copy(gown.at[k], ring.at[k % RING], lsem.at[k % 2, 0]),
            pltpu.make_async_copy(grecv.at[k], theirs_in.at[k % 2], lsem.at[k % 2, 1]),
        ]

    def begin(k):
        reduce.wait(load(k))
        mine, other = acc(k), theirs_in.at[k % 2]

        @pl.loop(0, 4)
        def _(i):
            for j in range(2):
                mine[i, j] = _add(mine[i, j], other[i, j])

        reduce.start(reduce.corner(k))

    def tick(k):
        if not isinstance(k, int) or k < count:
            begin(k)
        _if((k >= 1) & (k - 1 < count), lambda: reduce.after_corner(k - 1))
        _if((k >= 2) & (k - 2 < count), lambda: reduce.after_plane(k - 2))
        _if((k >= 3) & (k - 3 < count), lambda: reduce.after_line(k - 3))

    reduce.start(load(0))
    start = [_local(low_in, low, msem.at[0]), _local(normed_in, normed, msem.at[1])]
    _greet(along + [across, down, sibling])

    def away(turn_pair, stage, i):
        side, sub = 1 - core, turn_pair
        columns = pl.ds(pl.multiple_of(sub * WIDE, WIDE), WIDE)
        return pltpu.make_async_remote_copy(
            src_ref=stage.at[sub, i],
            dst_ref=qrecv.at[i, :, :, :, :, columns],
            send_sem=qs.at[i, sub],
            recv_sem=qr.at[i, sub],
            device_id=sibling,
            device_id_type=MESH,
        )

    def retreat(heads_in, probs, wblk, stage, dq, dk, dv, dmix, dk_acc, dv_acc):
        def fetch(i):
            turn, sub = i // 2, i % 2
            side = (turn + 1 + core) % 2
            columns = pl.ds(pl.multiple_of(sub * WIDE, WIDE), WIDE)
            slot = i % 2
            copies = [
                pltpu.make_async_copy(qkv.at[n, side, :, columns], heads_in.at[slot, n], bsem.at[slot, n])
                for n in range(3)
            ]
            copies.append(pltpu.make_async_copy(mixed_in.at[side, :, columns], heads_in.at[slot, 3], bsem.at[slot, 3]))
            copies += [
                pltpu.make_async_copy(full.at[n, side, :, :, :, :, columns], wblk.at[slot, n], bsem.at[slot, 4 + n])
                for n in range(4)
            ]
            heads = pl.ds((side * 2 + sub) * 2, 2)
            copies.append(pltpu.make_async_copy(probs_in.at[heads], probs.at[slot], bsem.at[slot, 8]))
            return copies

        reduce.start(fetch(0))

        @pl.loop(0, seq_len // block)
        def _(i):
            ingrad[pl.ds(pl.multiple_of(i * block, block), block)] = jnp.zeros((block, model), f32)

        reduce.wait(start)

        @pl.loop(0, 4)
        def _(i):
            turn, sub, slot = i // 2, i % 2, i % 2
            side = (turn + 1 + core) % 2
            reduce.wait(fetch(i))

            @pl.when(i < 3)
            def _():
                reduce.start(fetch(i + 1))

            columns = pl.ds(pl.multiple_of(sub * WIDE, WIDE), WIDE)

            def put(n, value):
                pieces = value.astype(bf16).reshape(4, 2, 2, model // 16, WIDE)

                @pl.when(turn == 0)
                def _():
                    stage[sub, n] = pieces
                    away(sub, stage, n).start()

                @pl.when(turn == 1)
                def _():
                    own[n, :, :, :, :, columns] = pieces

            def tick_and_load(k):
                tick(k)

                @pl.when(k + 1 < feeds)
                def _():
                    reduce.start(load(k + 1))

            tick_and_load(2 * i)
            wq, wk, wv, wo = (wblk[slot, n].reshape(model, WIDE) for n in range(4))
            dmix[...] = _dot(low[...], wo, NN).astype(bf16)
            put(0, _dot(low[...], heads_in[slot, 3], TN))
            for head in range(WIDE // HEAD_DIM):
                part = slice(head * HEAD_DIM, (head + 1) * HEAD_DIM)
                dk_acc[...] = jnp.zeros_like(dk_acc)
                dv_acc[...] = jnp.zeros_like(dv_acc)
                for first, stop in _spans(seq_len, LONGEST, step):
                    grad = dmix[first : first + step, part]
                    weights_low = probs[slot, head, :stop, first : first + step]
                    weights = weights_low.astype(f32)
                    dprobs = _dot(heads_in[slot, 2, :stop, part], grad, NT)
                    inner = jnp.sum(weights * dprobs, axis=0, keepdims=True)
                    dscores = (weights * (dprobs - inner)).astype(bf16)
                    dq[first : first + step, part] = (
                        _dot(dscores, heads_in[slot, 1, :stop, part], TN) * scale
                    ).astype(bf16)
                    dk_acc[:stop] += _dot(dscores, heads_in[slot, 0, first : first + step, part], NN)
                    dv_acc[:stop] += _dot(weights_low, grad, NN)
                dk[:, part] = (dk_acc[...] * scale).astype(bf16)
                dv[:, part] = dv_acc[...].astype(bf16)
                if head == 0:
                    tick_and_load(2 * i + 1)
            put(1, _dot(normed[...], dq[...], TN))
            put(2, _dot(normed[...], dk[...], TN))
            put(3, _dot(normed[...], dv[...], TN))
            ingrad[...] += _dot(dq[...], wq, NT) + _dot(dk[...], wk, NT) + _dot(dv[...], wv, NT)
            at = side * 2 + sub
            bsums[at, 0:1] = jnp.sum(dq[...].astype(f32), axis=0, keepdims=True)
            bsums[at, 1:2] = jnp.sum(dv[...].astype(f32), axis=0, keepdims=True)

        for sub in range(2):
            for n in range(4):
                away(sub, stage, n).wait_send()

    pl.run_scoped(
        retreat,
        pltpu.VMEM((2, 4, seq_len, WIDE), bf16),
        pltpu.VMEM((2, 2, seq_len, seq_len), bf16),
        pltpu.VMEM((2, 4, 4, 2, 2, model // 16, WIDE), bf16),
        pltpu.VMEM((2, 4, 4, 2, 2, model // 16, WIDE), bf16),
        pltpu.VMEM((seq_len, WIDE), bf16),
        pltpu.VMEM((seq_len, WIDE), bf16),
        pltpu.VMEM((seq_len, WIDE), bf16),
        pltpu.VMEM((seq_len, WIDE), bf16),
        pltpu.VMEM((seq_len, HEAD_DIM), f32),
        pltpu.VMEM((seq_len, HEAD_DIM), f32),
    )

    def landed(n):
        for sub in range(2):
            pltpu.make_async_remote_copy(
                src_ref=qrecv.at[n, :, :, :, :, sub * WIDE : (sub + 1) * WIDE],
                dst_ref=qrecv.at[n, :, :, :, :, sub * WIDE : (sub + 1) * WIDE],
                send_sem=qs.at[n, sub],
                recv_sem=qr.at[n, sub],
                device_id=sibling,
                device_id_type=MESH,
            ).wait_recv()

    def finish(gres, xs):
        bring = [_local(gres_in, gres, msem.at[0]), _local(x_in, xs, msem.at[1])]
        landed(0)
        landed(1)
        reduce.start(load(feeds))
        reduce.start(load(feeds + 1))
        tick(feeds)
        reduce.wait(bring)
        sums[...] = jnp.zeros_like(sums)

        @pl.loop(0, seq_len // block)
        def _(i):
            rows = pl.ds(pl.multiple_of(i * block, block), block)
            scaled, inverse = _normal(xs[rows].astype(f32))
            grow = ingrad[rows]
            weighted = grow * lines[0:1]
            mean_plain = jnp.mean(weighted, axis=-1, keepdims=True)
            mean_scaled = jnp.mean(weighted * scaled, axis=-1, keepdims=True)
            ingrad[rows] = gres[rows] + inverse * (weighted - mean_plain - scaled * mean_scaled)
            sums[0:1] += jnp.sum(grow * scaled, axis=0, keepdims=True)
            sums[1:2] += jnp.sum(grow, axis=0, keepdims=True)

    pl.run_scoped(finish, pltpu.VMEM((seq_len, model), f32), pltpu.VMEM((seq_len, model), bf16))
    mine = pl.ds(pl.multiple_of(core * half, half), half)
    theirs = pl.ds(pl.multiple_of((1 - core) * half, half), half)
    final = [
        _local(ingrad.at[mine], iout.at[core], msem.at[0]),
        _send(ingrad.at[theirs], iout.at[core], es.at[0], er.at[0], sibling),
    ]
    for pair in range(4):
        at = slice(pair * WIDE, (pair + 1) * WIDE)
        sums[2:4, at] = bsums[pair, 0:2]
    sums[4:5] = sums_two[2:3]
    sums[5:7] = sums_two[0:2]
    sums[7:8] = sums_two[3:4]
    vacc[...] = jnp.zeros_like(vacc)
    for zi in range(4):
        for yi in range(2):
            at = (zi * 2 + yi) * 128
            for xi in range(2):
                for ci in range(2):
                    i = ((zi * 2 + yi) * 2 + xi) * 2 + ci
                    piece = 2 * ((i % 16) // 4) + i // 16
                    vacc[ci, zi, yi, xi, 0:8] = sums[:, at : at + 128]
                    vacc[ci, zi, yi, xi, 8:9] = gbias[piece, 0:1, (i % 4) * 128 : (i % 4) * 128 + 128]
    vzero = _send(vacc.at[1 - core], v_s, vs.at[0], vr.at[0], sibling)
    landed(2)
    landed(3)
    tick(feeds + 1)
    reduce.start(load(feeds + 2))
    vzero.wait()
    vmine = vacc.at[core]
    vmine[...] = vmine[...] + v_s[...]
    vone = _send(vmine.at[:, 1 - y, 1 - x], vx_one, vs.at[1], vr.at[1], across)
    tick(feeds + 2)
    reduce.start(load(feeds + 3))
    vone.wait()
    vmine[:, 1 - y, x] = vmine[:, 1 - y, x] + vx_one[...]
    vtwo = [
        _send(vmine.at[:, y, 1 - x], vx_two, vs.at[2], vr.at[2], across),
        _send(vmine.at[:, 1 - y, x], vy_two, vs.at[3], vr.at[3], down),
    ]
    tick(feeds + 3)
    reduce.wait(vtwo)
    vmine[:, y, x] = vmine[:, y, x] + vx_two[...] + vy_two[...]
    vthree = [
        _send(vmine.at[(z + j + 1) % 4, y, x], v_z.at[j], vs.at[4 + j], vr.at[4 + j], along[j]) for j in range(3)
    ]
    tick(feeds + 4)
    reduce.wait(vthree)
    vout[...] = vmine[z, y, x] + v_z[0] + v_z[1] + v_z[2]
    tick(feeds + 5)
    tick(feeds + 6)
    reduce.wait(final)


def back(lines, sums_two, gbias, qkv, mixed, probs, full, low, normed, x, gres, gown, grecv):
    feeds = gown.shape[0]
    count = feeds + 4
    seq_len, model = x.shape
    rows, cols = gown.shape[-2:]
    half = seq_len // 2
    bf16, f32 = jnp.bfloat16, jnp.float32
    hbm = pl.BlockSpec(memory_space=pltpu.HBM)
    vmem = pl.BlockSpec(memory_space=pltpu.VMEM)
    dma = pltpu.SemaphoreType.DMA
    small = (16, 128)
    return pl.pallas_call(
        back_kernel,
        out_shape=(
            jax.ShapeDtypeStruct((count, rows, cols), f32),
            jax.ShapeDtypeStruct(small, f32),
            jax.ShapeDtypeStruct((2, half, model), f32),
            jax.ShapeDtypeStruct((4, 4, 2, 2, rows, cols), bf16),
        ),
        in_specs=[vmem] * 3 + [hbm] * 10,
        out_specs=(vmem, vmem, hbm, hbm),
        scratch_shapes=[
            pltpu.VMEM((RING, 4, 2, 2, rows, cols), bf16),
            pltpu.VMEM((2, 4, 2, 2, rows, cols), bf16),
            pltpu.VMEM((4, 4, 2, 2, rows, cols), bf16),
            pltpu.VMEM((count, 4, rows // 2, cols), bf16),
            pltpu.VMEM((count, 4, rows // 2, cols), bf16),
            pltpu.VMEM((count, 4, rows, cols), bf16),
            pltpu.VMEM((count, 4, rows, cols), bf16),
            pltpu.VMEM((count, 3, rows, cols), bf16),
            pltpu.VMEM((2, 4, 2, 2) + small, f32),
            pltpu.VMEM((4, 2, 2) + small, f32),
            pltpu.VMEM((4,) + small, f32),
            pltpu.VMEM((4,) + small, f32),
            pltpu.VMEM((4,) + small, f32),
            pltpu.VMEM((3,) + small, f32),
            pltpu.VMEM((seq_len, model), bf16),
            pltpu.VMEM((seq_len, model), bf16),
            pltpu.VMEM((seq_len, model), f32),
            pltpu.VMEM((8, model), f32),
            pltpu.VMEM((4, 8, WIDE), f32),
            dma((count, 7)),
            dma((count, 7)),
            dma((2, 2)),
            dma((4, 2)),
            dma((4, 2)),
            dma((7,)),
            dma((7,)),
            dma((2, 9)),
            dma((2,)),
            dma((1,)),
            dma((1,)),
        ],
        compiler_params=pltpu.CompilerParams(
            collective_id=1, has_side_effects=True, vmem_limit_bytes=63 * MIB
        ),
    )(lines, sums_two, gbias, qkv, mixed, probs, full, low, normed, x, gres, gown, grecv)


def fast_body(
    inputs, prefix, ln1_gain, ln1_bias, query_weight, query_bias, key_weight, value_weight, value_bias,
    out_weight, out_bias, ln2_gain, ln2_bias, up_weight, up_bias, down_weight, down_bias, cotangent,
):
    core = lax.axis_index("tensor")
    half, model = inputs.shape[2], inputs.shape[3]
    rows, cols = query_weight.shape
    pieces = up_weight.shape[1] // cols

    def split(matrix):
        return [matrix[:, i * cols : (i + 1) * cols] for i in range(pieces)]

    ups, downs = split(up_weight), split(down_weight.T)
    feeds = [m for pair in zip(ups, downs) for m in pair]
    win = jnp.stack([query_weight, key_weight, value_weight, out_weight.T] + feeds)
    small = jnp.stack([ln1_gain, ln1_bias, query_bias, value_bias, out_bias, ln2_gain, ln2_bias, down_bias])
    place = (lax.axis_index("dp") * 2 + core) % 4
    vec = jnp.pad(up_bias.reshape(1, 128), ((8, 7), (0, 0)))
    vec = lax.dynamic_update_slice(vec, small, (0, place * 32))
    prefix_len = lax.dynamic_slice_in_dim(prefix[:, 0], core, 1)
    (
        full, qkv, mixed, probs, normed, x, lines, layer_out, gres, low, sums_two, gown, grecv, gup_bias,
    ) = front(prefix_len, win, vec, inputs[:, 0], cotangent[:, 0])
    summed = (2 * pieces, 4, 2, 2, rows, cols)
    out, vout, input_grad, _ = back(
        lines, sums_two, gup_bias, qkv, mixed, probs, full, low, normed, x, gres,
        gown.reshape(summed), grecv.reshape(summed),
    )
    vectors = lax.dynamic_slice(vout, (0, place * 32), (8, 32))

    def join(pieces_of):
        return pieces_of.transpose(1, 0, 2).reshape(rows, pieces * cols)

    ffn, (gout, gq, gk, gv) = out[: 2 * pieces], out[2 * pieces :]
    return (
        layer_out.reshape(2, 1, half, model),
        input_grad.reshape(2, 1, half, model),
        vectors[0],
        vectors[1],
        gq,
        vectors[2],
        gk,
        gv,
        vectors[3],
        gout.T,
        vectors[4],
        vectors[5],
        vectors[6],
        join(ffn[0::2]),
        vout[8],
        join(ffn[1::2]).T,
        vectors[7],
    )


def solution(mesh):
    in_specs = (
        P(None, "dp", "tensor", None),
        P(None, "dp"),
        P(("dp", "tensor")),
        P(("dp", "tensor")),
        P("dp", "tensor"),
        P(("dp", "tensor")),
        P("dp", "tensor"),
        P("dp", "tensor"),
        P(("dp", "tensor")),
        P("tensor", "dp"),
        P(("dp", "tensor")),
        P(("dp", "tensor")),
        P(("dp", "tensor")),
        P("dp", "tensor"),
        P(("dp", "tensor")),
        P("tensor", "dp"),
        P(("dp", "tensor")),
        P(None, "dp", "tensor", None),
    )
    out_specs = (
        P(None, "dp", "tensor", None),
        P(None, "dp", "tensor", None),
        P(("dp", "tensor")),
        P(("dp", "tensor")),
        P("dp", "tensor"),
        P(("dp", "tensor")),
        P("dp", "tensor"),
        P("dp", "tensor"),
        P(("dp", "tensor")),
        P("tensor", "dp"),
        P(("dp", "tensor")),
        P(("dp", "tensor")),
        P(("dp", "tensor")),
        P("dp", "tensor"),
        P(("dp", "tensor")),
        P("tensor", "dp"),
        P(("dp", "tensor")),
    )
    sizes = (mesh.shape["dp"], mesh.shape["tensor"])
    chosen = fast_body if sizes == (16, 2) else body
    return jax.shard_map(chosen, mesh=mesh, in_specs=in_specs, out_specs=out_specs, check_vma=False)
```

```python
import math

import jax
import jax.numpy as jnp
from jax import lax
from jax.experimental import pallas as pl
from jax.experimental.pallas import tpu as pltpu
from jax.sharding import PartitionSpec as P

MESH = pl.DeviceIdType.MESH
LONGEST = 512

HEAD_DIM = 128
BLOCK = 512


EPSILON = 1e-05


def norm_forward(values, gain, shift):
    center = values - jnp.mean(values, axis=-1, keepdims=True)
    inverse = lax.rsqrt(jnp.mean(center * center, axis=-1, keepdims=True) + EPSILON)
    scaled = center * inverse
    return (scaled * gain + shift, scaled, inverse)


def norm_backward(grad_out, scaled, inverse, gain):
    weighted = grad_out * gain
    mean_plain = jnp.mean(weighted, axis=-1, keepdims=True)
    mean_scaled = jnp.mean(weighted * scaled, axis=-1, keepdims=True)
    return inverse * (weighted - mean_plain - scaled * mean_scaled)


def smooth_gate(values):
    return jax.nn.gelu(values, approximate=False)


def smooth_slope(values):
    normal_cdf = 0.5 * (1.0 + jax.scipy.special.erf(values / math.sqrt(2.0)))
    density = jnp.exp(-0.5 * values * values) / math.sqrt(2.0 * math.pi)
    return normal_cdf + values * density


def masked_scores(query_block, key_rows, start, prefix_len):
    scale = 1.0 / math.sqrt(key_rows.shape[2])
    scores = (
        jnp.einsum("qhd,khd->hqk", query_block, key_rows, preferred_element_type=jnp.float32)
        * scale
    )
    places = start + jnp.arange(query_block.shape[0], dtype=jnp.int32)
    columns = jnp.arange(key_rows.shape[0], dtype=jnp.int32)
    allowed = (columns[None, :] <= places[:, None]) | (columns[None, :] < prefix_len)
    return jnp.where(allowed[None], scores, -jnp.inf)


def attend_forward(queries, key_rows, value_rows, prefix_len):
    seq_len, heads_local, head_size = queries.shape
    count = seq_len // BLOCK

    def one_block(items):
        query_block, start = items
        scores = masked_scores(query_block, key_rows, start, prefix_len)
        peak = jnp.max(scores, axis=-1, keepdims=True)
        raw_weights = jnp.exp(scores - peak)
        totals = jnp.sum(raw_weights, axis=-1, keepdims=True)
        probs = (raw_weights / totals).astype(jnp.bfloat16)
        mixed = jnp.einsum("hqk,khd->qhd", probs, value_rows, preferred_element_type=jnp.float32)
        return (mixed.astype(jnp.bfloat16), (peak + jnp.log(totals))[..., 0])

    starts = jnp.arange(count, dtype=jnp.int32) * BLOCK
    mixed, log_totals = lax.map(
        one_block, (queries.reshape(count, BLOCK, heads_local, head_size), starts)
    )
    return (mixed.reshape(seq_len, heads_local * head_size), log_totals)


def attend_backward(queries, key_rows, value_rows, grad_mixed, log_totals, prefix_len):
    seq_len, heads_local, head_size = queries.shape
    count = seq_len // BLOCK
    scale = 1.0 / math.sqrt(head_size)

    def one_block(carry, items):
        key_total, value_total = carry
        query_block, grad_block, log_block, start = items
        scores = masked_scores(query_block, key_rows, start, prefix_len)
        probs = jnp.exp(scores - log_block[..., None])
        grad_probs = jnp.einsum(
            "qhd,khd->hqk", grad_block, value_rows, preferred_element_type=jnp.float32
        )
        inner = jnp.sum(probs * grad_probs, axis=-1, keepdims=True)
        grad_scores = (probs * (grad_probs - inner)).astype(jnp.bfloat16)
        grad_query = (
            jnp.einsum("hqk,khd->qhd", grad_scores, key_rows, preferred_element_type=jnp.float32)
            * scale
        )
        key_total = (
            key_total
            + jnp.einsum(
                "hqk,qhd->khd", grad_scores, query_block, preferred_element_type=jnp.float32
            )
            * scale
        )
        value_total = value_total + jnp.einsum(
            "hqk,qhd->khd",
            probs.astype(jnp.bfloat16),
            grad_block,
            preferred_element_type=jnp.float32,
        )
        return ((key_total, value_total), grad_query.astype(jnp.bfloat16))

    empty_total = jnp.zeros(queries.shape, jnp.float32)
    starts = jnp.arange(count, dtype=jnp.int32) * BLOCK
    blocked = (count, BLOCK, heads_local, head_size)
    (key_total, value_total), grad_queries = lax.scan(
        one_block,
        (empty_total, empty_total),
        (queries.reshape(blocked), grad_mixed.reshape(blocked), log_totals, starts),
    )
    width = heads_local * head_size
    return (
        grad_queries.reshape(seq_len, width),
        key_total.astype(jnp.bfloat16).reshape(seq_len, width),
        value_total.astype(jnp.bfloat16).reshape(seq_len, width),
    )


def body(
    inputs,
    prefix,
    ln1_gain,
    ln1_bias,
    query_weight,
    query_bias,
    key_weight,
    value_weight,
    value_bias,
    out_weight,
    out_bias,
    ln2_gain,
    ln2_bias,
    up_weight,
    up_bias,
    down_weight,
    down_bias,
    cotangent,
):
    local_width = query_weight.shape[1]
    local_hidden = up_weight.shape[1]
    shard_rows = inputs.shape[2]
    micro = inputs.shape[0]
    model_width = inputs.shape[3]
    heads_local = local_width // HEAD_DIM
    offset_width = lax.axis_index("tensor") * local_width
    offset_hidden = lax.axis_index("tensor") * local_hidden
    vectors = (
        lax.all_gather(ln1_gain, ("dp", "tensor"), axis=0, tiled=True),
        lax.all_gather(ln1_bias, ("dp", "tensor"), axis=0, tiled=True),
        lax.all_gather(query_bias, ("dp", "tensor"), axis=0, tiled=True),
        lax.all_gather(value_bias, ("dp", "tensor"), axis=0, tiled=True),
        lax.all_gather(out_bias, ("dp", "tensor"), axis=0, tiled=True),
        lax.all_gather(ln2_gain, ("dp", "tensor"), axis=0, tiled=True),
        lax.all_gather(ln2_bias, ("dp", "tensor"), axis=0, tiled=True),
        lax.all_gather(up_bias, ("dp", "tensor"), axis=0, tiled=True),
        lax.all_gather(down_bias, ("dp", "tensor"), axis=0, tiled=True),
    )
    (
        gain_one,
        shift_one,
        query_full_bias,
        value_full_bias,
        out_shift,
        gain_two,
        shift_two,
        up_full_bias,
        down_shift,
    ) = vectors
    query_shift = lax.dynamic_slice_in_dim(query_full_bias, offset_width, local_width)
    value_shift = lax.dynamic_slice_in_dim(value_full_bias, offset_width, local_width)
    up_shift = lax.dynamic_slice_in_dim(up_full_bias, offset_hidden, local_hidden)
    zero_width = jnp.zeros((model_width,), jnp.float32)
    gain_one_grad = zero_width
    shift_one_grad = zero_width
    query_bias_grad = zero_width
    value_bias_grad = zero_width
    out_bias_grad = zero_width
    gain_two_grad = zero_width
    shift_two_grad = zero_width
    up_bias_grad = jnp.zeros((up_full_bias.shape[0],), jnp.float32)
    down_bias_grad = zero_width
    weight_totals = None
    layer_rows = []
    input_rows = []
    for index in range(micro):
        gathered = (
            lax.all_gather(query_weight, "dp", axis=0, tiled=True),
            lax.all_gather(key_weight, "dp", axis=0, tiled=True),
            lax.all_gather(value_weight, "dp", axis=0, tiled=True),
            lax.all_gather(out_weight, "dp", axis=1, tiled=True),
            lax.all_gather(up_weight, "dp", axis=0, tiled=True),
            lax.all_gather(down_weight, "dp", axis=1, tiled=True),
        )
        full_query, full_key, full_value, full_out, full_up, full_down = gathered
        rows_in = inputs[index, 0].astype(jnp.float32)
        prefix_len = prefix[index, 0]
        normed, scaled_one, inverse_one = norm_forward(rows_in, gain_one, shift_one)
        normed_all = lax.all_gather(normed.astype(jnp.bfloat16), "tensor", axis=0, tiled=True)
        seq_len = normed_all.shape[0]
        queries = (
            jnp.dot(normed_all, full_query, preferred_element_type=jnp.float32) + query_shift
        ).astype(jnp.bfloat16)
        key_rows = jnp.dot(normed_all, full_key, preferred_element_type=jnp.float32).astype(
            jnp.bfloat16
        )
        value_rows = (
            jnp.dot(normed_all, full_value, preferred_element_type=jnp.float32) + value_shift
        ).astype(jnp.bfloat16)
        head_shape = (seq_len, heads_local, HEAD_DIM)
        queries_h = queries.reshape(head_shape)
        keys_h = key_rows.reshape(head_shape)
        values_h = value_rows.reshape(head_shape)
        attended, log_totals = attend_forward(queries_h, keys_h, values_h, prefix_len)
        attention_share = lax.psum_scatter(
            jnp.dot(attended, full_out, preferred_element_type=jnp.float32).astype(jnp.bfloat16),
            "tensor",
            scatter_dimension=0,
            tiled=True,
        ).astype(jnp.float32)
        residual = rows_in + attention_share + out_shift
        second, scaled_two, inverse_two = norm_forward(residual, gain_two, shift_two)
        grad_rows = cotangent[index, 0]
        down_bias_grad = down_bias_grad + jnp.sum(grad_rows.astype(jnp.float32), axis=0)
        second_all = lax.all_gather(second.astype(jnp.bfloat16), "tensor", axis=0, tiled=True)
        hidden_pre = jnp.dot(second_all, full_up, preferred_element_type=jnp.float32) + up_shift
        hidden_act = smooth_gate(hidden_pre).astype(jnp.bfloat16)
        feed_share = lax.psum_scatter(
            jnp.dot(hidden_act, full_down, preferred_element_type=jnp.float32).astype(jnp.bfloat16),
            "tensor",
            scatter_dimension=0,
            tiled=True,
        ).astype(jnp.float32)
        layer_rows.append(residual + feed_share + down_shift)
        grad_all = lax.all_gather(grad_rows, "tensor", axis=0, tiled=True)
        down_grad = jnp.dot(hidden_act.T, grad_all, preferred_element_type=jnp.float32)
        grad_act = jnp.dot(grad_all, full_down.T, preferred_element_type=jnp.float32)
        grad_pre = (grad_act * smooth_slope(hidden_pre)).astype(jnp.bfloat16)
        up_grad = jnp.dot(second_all.T, grad_pre, preferred_element_type=jnp.float32)
        up_part = jnp.sum(grad_pre.astype(jnp.float32), axis=0)
        up_bias_grad = up_bias_grad + lax.dynamic_update_slice(
            jnp.zeros_like(up_bias_grad), up_part, (offset_hidden,)
        )
        grad_second = lax.psum_scatter(
            jnp.dot(grad_pre, full_up.T, preferred_element_type=jnp.float32).astype(jnp.bfloat16),
            "tensor",
            scatter_dimension=0,
            tiled=True,
        ).astype(jnp.float32)
        gain_two_grad = gain_two_grad + jnp.sum(grad_second * scaled_two, axis=0)
        shift_two_grad = shift_two_grad + jnp.sum(grad_second, axis=0)
        grad_residual = grad_rows.astype(jnp.float32) + norm_backward(
            grad_second, scaled_two, inverse_two, gain_two
        )
        out_bias_grad = out_bias_grad + jnp.sum(grad_residual, axis=0)
        residual_all = lax.all_gather(
            grad_residual.astype(jnp.bfloat16), "tensor", axis=0, tiled=True
        )
        out_grad = jnp.dot(attended.T, residual_all, preferred_element_type=jnp.float32)
        grad_attended = jnp.dot(
            residual_all, full_out.T, preferred_element_type=jnp.float32
        ).astype(jnp.bfloat16)
        grad_queries, grad_keys, grad_values = attend_backward(
            queries_h, keys_h, values_h, grad_attended, log_totals, prefix_len
        )
        query_grad = jnp.dot(normed_all.T, grad_queries, preferred_element_type=jnp.float32)
        key_grad = jnp.dot(normed_all.T, grad_keys, preferred_element_type=jnp.float32)
        value_grad = jnp.dot(normed_all.T, grad_values, preferred_element_type=jnp.float32)
        query_part = jnp.sum(grad_queries.astype(jnp.float32), axis=0)
        value_part = jnp.sum(grad_values.astype(jnp.float32), axis=0)
        query_bias_grad = query_bias_grad + lax.dynamic_update_slice(
            zero_width, query_part, (offset_width,)
        )
        value_bias_grad = value_bias_grad + lax.dynamic_update_slice(
            zero_width, value_part, (offset_width,)
        )
        partial_sum = jnp.dot(grad_queries, full_query.T, preferred_element_type=jnp.float32)
        partial_sum = partial_sum + jnp.dot(
            grad_keys, full_key.T, preferred_element_type=jnp.float32
        )
        grad_normed = lax.psum_scatter(
            (
                partial_sum + jnp.dot(grad_values, full_value.T, preferred_element_type=jnp.float32)
            ).astype(jnp.bfloat16),
            "tensor",
            scatter_dimension=0,
            tiled=True,
        ).astype(jnp.float32)
        gain_one_grad = gain_one_grad + jnp.sum(grad_normed * scaled_one, axis=0)
        shift_one_grad = shift_one_grad + jnp.sum(grad_normed, axis=0)
        input_rows.append(
            grad_residual + norm_backward(grad_normed, scaled_one, inverse_one, gain_one)
        )
        reduced = (query_grad, key_grad, value_grad, out_grad, up_grad, down_grad)
        if weight_totals is None:
            weight_totals = reduced
        else:
            weight_totals = tuple((left + right for left, right in zip(weight_totals, reduced)))
    query_total, key_total, value_total, out_total, up_total, down_total = weight_totals
    query_total, key_total, value_total, out_total, up_total, down_total = (
        lax.psum_scatter(
            query_total.astype(jnp.bfloat16), "dp", scatter_dimension=0, tiled=True
        ).astype(jnp.float32),
        lax.psum_scatter(
            key_total.astype(jnp.bfloat16), "dp", scatter_dimension=0, tiled=True
        ).astype(jnp.float32),
        lax.psum_scatter(
            value_total.astype(jnp.bfloat16), "dp", scatter_dimension=0, tiled=True
        ).astype(jnp.float32),
        lax.psum_scatter(
            out_total.astype(jnp.bfloat16), "dp", scatter_dimension=1, tiled=True
        ).astype(jnp.float32),
        lax.psum_scatter(
            up_total.astype(jnp.bfloat16), "dp", scatter_dimension=0, tiled=True
        ).astype(jnp.float32),
        lax.psum_scatter(
            down_total.astype(jnp.bfloat16), "dp", scatter_dimension=1, tiled=True
        ).astype(jnp.float32),
    )
    vector_totals = (
        lax.psum_scatter(gain_one_grad, ("dp", "tensor"), scatter_dimension=0, tiled=True),
        lax.psum_scatter(shift_one_grad, ("dp", "tensor"), scatter_dimension=0, tiled=True),
        lax.psum_scatter(query_bias_grad, ("dp", "tensor"), scatter_dimension=0, tiled=True),
        lax.psum_scatter(value_bias_grad, ("dp", "tensor"), scatter_dimension=0, tiled=True),
        lax.psum_scatter(out_bias_grad, ("dp", "tensor"), scatter_dimension=0, tiled=True),
        lax.psum_scatter(gain_two_grad, ("dp", "tensor"), scatter_dimension=0, tiled=True),
        lax.psum_scatter(shift_two_grad, ("dp", "tensor"), scatter_dimension=0, tiled=True),
        lax.psum_scatter(up_bias_grad, ("dp", "tensor"), scatter_dimension=0, tiled=True),
        lax.psum_scatter(down_bias_grad, ("dp", "tensor"), scatter_dimension=0, tiled=True),
    )
    (
        gain_one_out,
        shift_one_out,
        query_bias_out,
        value_bias_out,
        out_bias_out,
        gain_two_out,
        shift_two_out,
        up_bias_out,
        down_bias_out,
    ) = vector_totals
    out_shape = (micro, 1, shard_rows, model_width)
    layer_out = jnp.stack(layer_rows).reshape(out_shape)
    input_grad = jnp.stack(input_rows).reshape(out_shape)
    return (
        layer_out,
        input_grad,
        gain_one_out,
        shift_one_out,
        query_total,
        query_bias_out,
        key_total,
        value_total,
        value_bias_out,
        out_total,
        out_bias_out,
        gain_two_out,
        shift_two_out,
        up_total,
        up_bias_out,
        down_total,
        down_bias_out,
    )


def _place(z, y, x):
    return z * 4 + y * 2 + x


def _coords():
    dp = lax.axis_index("dp")
    core = lax.axis_index("tensor")
    return dp // 4, (dp // 2) % 2, dp % 2, core


def _greet(peers):
    barrier = pltpu.get_barrier_semaphore()
    for peer in peers:
        pl.semaphore_signal(barrier, inc=1, device_id=peer, device_id_type=MESH)
    pl.semaphore_wait(barrier, len(peers))


def _peers():
    z, y, x, core = _coords()
    along = [(_place((z + j) % 4, y, x), core) for j in (1, 2, 3)]
    across = (_place(z, y, 1 - x), core)
    down = (_place(z, 1 - y, x), core)
    sibling = (_place(z, y, x), 1 - core)
    return along, across, down, sibling


def _send(src, dst, send_sem, recv_sem, peer):
    copy = pltpu.make_async_remote_copy(
        src_ref=src,
        dst_ref=dst,
        send_sem=send_sem,
        recv_sem=recv_sem,
        device_id=peer,
        device_id_type=MESH,
    )
    copy.start()
    return copy


def _local(src, dst, sem):
    copy = pltpu.make_async_copy(src, dst, sem)
    copy.start()
    return copy


def _dot(left, right, contract):
    return lax.dot_general(left, right, (contract, ((), ())), preferred_element_type=jnp.float32)


NN = ((1,), (0,))
NT = ((1,), (1,))
TN = ((0,), (0,))
LOG2E = 1.4426950408889634
MIB = 1024 * 1024
WIDE = 256


def _normal(values):
    center = values - jnp.mean(values, axis=-1, keepdims=True)
    inverse = lax.rsqrt(jnp.mean(center * center, axis=-1, keepdims=True) + EPSILON)
    return center * inverse, inverse


def _spans(seq_len, longest, step):
    return [(start, max(longest, start + step)) for start in range(0, seq_len, step)]


class Gather:
    def __init__(self, shards, places, send_sem, recv_sem, local_sem):
        self.z, self.y, self.x, self.core = _coords()
        self.along, self.across, self.down, self.sibling = _peers()
        self.shards, self.places, self.count = shards, places, len(shards)
        self.send_sem, self.recv_sem, self.local_sem = send_sem, recv_sem, local_sem

    def _remote(self, k, slot, src, dst, peer):
        return pltpu.make_async_remote_copy(
            src_ref=src,
            dst_ref=dst,
            send_sem=self.send_sem.at[k, slot],
            recv_sem=self.recv_sem.at[k, slot],
            device_id=peer,
            device_id_type=MESH,
        )

    def line(self, k):
        own = self.places[k].at[self.core, self.z, self.y, self.x]
        here = pltpu.make_async_copy(self.shards[k], own, self.local_sem.at[k])
        return [here] + [self._remote(k, j, self.shards[k], own, self.along[j]) for j in range(3)]

    def plane(self, k):
        block = self.places[k].at[self.core, :, self.y, self.x]
        return [self._remote(k, 3, block, block, self.across), self._remote(k, 4, block, block, self.down)]

    def corner(self, k):
        part = self.shards[k].shape[0] // 2
        one = self.places[k].at[self.core, :, 1 - self.y, self.x, 0:part]
        two = self.places[k].at[self.core, :, self.y, 1 - self.x, part : 2 * part]
        return [self._remote(k, 5, one, one, self.across), self._remote(k, 6, two, two, self.down)]

    def twin(self, k):
        block = self.places[k].at[self.core]
        return [self._remote(k, 7, block, block, self.sibling)]

    def near(self, k):
        own = self.places[k].at[self.core, self.z, self.y, self.x]
        here = pltpu.make_async_copy(self.shards[k], own, self.local_sem.at[k])
        src = self.shards[k]
        return [here, self._remote(k, 3, src, own, self.across), self._remote(k, 4, src, own, self.down)]

    def near_corner(self, k):
        part = self.shards[k].shape[0] // 2
        one = self.places[k].at[self.core, self.z, 1 - self.y, self.x, 0:part]
        two = self.places[k].at[self.core, self.z, self.y, 1 - self.x, part : 2 * part]
        return [self._remote(k, 5, one, one, self.across), self._remote(k, 6, two, two, self.down)]

    def far(self, k, i):
        block = self.places[k].at[self.core, self.z, i // 3]
        return [self._remote(k + i // 3, i % 3, block, block, self.along[i % 3])]

    def start(self, stage, k, *more):
        if 0 <= k < self.count and (more or k != self.count - 1 or stage in self.odd):
            for copy in stage(k, *more):
                copy.start()

    def wait(self, stage, k, *more):
        if 0 <= k < self.count and (more or k != self.count - 1 or stage in self.odd):
            for copy in stage(k, *more):
                copy.wait()

    @property
    def odd(self):
        return (self.near, self.near_corner)

    def last(self, step):
        k = self.count - 1
        if step == 0:
            self.start(self.near, k)
        if step == 1:
            self.wait(self.near, k)
            self.start(self.near_corner, k)
        if step == 2:
            self.wait(self.near_corner, k)
        if 2 <= step < 8:
            self.start(self.far, k, step - 2)
        if step == 9:
            for i in range(6):
                self.wait(self.far, k, i)
            self.twin(k)[0].start()
        if step == 20:
            self.twin(k)[0].wait()

    def tick(self, k, twin=True):
        self.last(k - 3)
        self.wait(self.plane, k)
        self.start(self.corner, k)
        self.wait(self.line, k + 2)
        self.start(self.plane, k + 2)
        self.start(self.line, k + 4)
        if twin:
            self.wait(self.corner, k - 1)
            self.start(self.twin, k - 1)


def _if(condition, action):
    if isinstance(condition, bool):
        if condition:
            action()
    else:
        pl.when(condition)(action)


class Reduce:
    def __init__(self, acc, out, x_one, y_one, x_two, y_two, from_z, send_sem, recv_sem):
        self.z, self.y, self.x, self.core = _coords()
        self.along, self.across, self.down, self.sibling = _peers()
        self.acc, self.out = acc, out
        self.x_one, self.y_one, self.x_two, self.y_two, self.from_z = x_one, y_one, x_two, y_two, from_z
        self.send_sem, self.recv_sem = send_sem, recv_sem

    def _remote(self, k, slot, src, dst, peer):
        return pltpu.make_async_remote_copy(
            src_ref=src,
            dst_ref=dst,
            send_sem=self.send_sem.at[k, slot],
            recv_sem=self.recv_sem.at[k, slot],
            device_id=peer,
            device_id_type=MESH,
        )

    def corner(self, k):
        block = self.acc(k).at[:, 1 - self.y, 1 - self.x]
        part = block.shape[1] // 2
        return [
            self._remote(k, 0, block.at[:, 0:part], self.x_one.at[k], self.across),
            self._remote(k, 1, block.at[:, part : 2 * part], self.y_one.at[k], self.down),
        ]

    def plane(self, k):
        acc = self.acc(k)
        return [
            self._remote(k, 2, acc.at[:, self.y, 1 - self.x], self.x_two.at[k], self.across),
            self._remote(k, 3, acc.at[:, 1 - self.y, self.x], self.y_two.at[k], self.down),
        ]

    def line(self, k):
        acc = self.acc(k)
        return [
            self._remote(k, 4 + j, acc.at[(self.z + j + 1) % 4, self.y, self.x], self.from_z.at[k, j], self.along[j])
            for j in range(3)
        ]

    @staticmethod
    def start(copies):
        for copy in copies:
            copy.start()

    @staticmethod
    def wait(copies):
        for copy in copies:
            copy.wait()

    def after_corner(self, k):
        acc, y, x = self.acc(k), self.y, self.x
        part = acc.shape[3] // 2
        self.wait(self.corner(k))
        one = acc.at[:, 1 - y, x, 0:part]
        two = acc.at[:, y, 1 - x, part : 2 * part]
        one[...] = _add(one[...], self.x_one[k])
        two[...] = _add(two[...], self.y_one[k])
        self.start(self.plane(k))

    def after_plane(self, k):
        acc = self.acc(k)
        self.wait(self.plane(k))
        here = acc.at[:, self.y, self.x]
        here[...] = _add(here[...], self.x_two[k], self.y_two[k])
        self.start(self.line(k))

    def after_line(self, k):
        self.wait(self.line(k))
        total = self.acc(k)[self.z, self.y, self.x].astype(self.out.dtype)
        for j in range(3):
            total = total + self.from_z[k, j].astype(self.out.dtype)
        self.out[k] = total


def _add(first, *others):
    total = first.astype(jnp.float32)
    for other in others:
        total = total + other.astype(jnp.float32)
    return total.astype(first.dtype)


def _combine(mine, other):
    @pl.loop(0, mine.shape[0])
    def _(i):
        for j in range(2):
            mine[i, j] = _add(mine[i, j], other[i, j])


EARLY = 2
ATTEND_SITES = 3
ATTEND_TICKS = {4: 1, 5: 3, 7: 9}
FEED_TICKS = {9: 0, 10: 1, 11: 2, 12: 3, 13: 4, 14: 6}


def front_kernel(
    prefix, wq_in, wk_in, wv_in, wo_in, up_in, down_in, vec, xin, gin,
    full, fullo, qkv, mixed_out, probs_out, normed_out, x_out, lines, layer_out, gres_out, low_out, sums, gown, grecv, gbias, early_out,
    vfull, x, grad, second, residual, weights, ubias,
    ssem, rsem, lsem, vs, vr, vl, ws, wr, wl, wsem, osem, fs, fr, fl, es, er, el,
    racc, rtheirs, x_one, y_one, x_two, y_two, from_z, rs, rr, rl,
):
    f32, bf16 = jnp.float32, jnp.bfloat16
    seq_len, model = x.shape
    half = seq_len // 2
    block = 128

    cols = wq_in.shape[1]
    shards = [w.at[:, sub * WIDE : (sub + 1) * WIDE] for sub in range(2) for w in (wq_in, wk_in, wv_in)] + [wo_in]
    places = [full.at[k] for k in range(6)] + [fullo]
    for piece in range(weights.shape[0] // 2):
        shards += [w.at[:, piece * cols : (piece + 1) * cols] for w in (up_in, down_in)]
        places += [weights.at[2 * piece], weights.at[2 * piece + 1]]
    early = len(shards) - weights.shape[0]
    gather = Gather(shards, places, ssem, rsem, lsem)
    reduce = Reduce(lambda k: racc.at[k], early_out, x_one, y_one, x_two, y_two, from_z, rs, rr)
    z, y, xx, core = gather.z, gather.y, gather.x, gather.core
    along, across, down, sibling = gather.along, gather.across, gather.down, gather.sibling
    _greet(along + [across, down, sibling])

    gather.start(gather.line, 0)
    vown = vfull.at[z, y, xx, core]
    vline = [_local(vec, vown, vl.at[0])] + [_send(vec, vown, vs.at[j], vr.at[j], along[j]) for j in range(3)]
    for k in (1, 2, 3):
        gather.start(gather.line, k)
    mine = pl.ds(pl.multiple_of(core * half, half), half)
    swaps = []
    for i, (part, whole) in enumerate(((xin, x), (gin, grad))):
        swaps.append(_local(part.at[core], whole.at[mine], wl.at[i]))
        swaps.append(_send(part.at[1 - core], whole.at[mine], ws.at[i], wr.at[i], sibling))
    gather.wait(gather.line, 0)
    gather.start(gather.plane, 0)
    for s in vline:
        s.wait()
    vblock = vfull.at[:, y, xx, core]
    vone = [_send(vblock, vblock, vs.at[3], vr.at[3], across), _send(vblock, vblock, vs.at[4], vr.at[4], down)]
    gather.wait(gather.line, 1)
    gather.start(gather.plane, 1)
    gather.tick(0)
    for s in vone:
        s.wait()
    vblock = vfull.at[:, 1 - y, xx, core]
    vtwo = _send(vblock, vblock, vs.at[5], vr.at[5], across)
    gather.tick(1)
    vtwo.wait()
    vblock = vfull.at[:, :, :, core]
    vthree = _send(vblock, vblock, vs.at[6], vr.at[6], sibling)
    for s in swaps:
        s.wait()
    saved = [_local(x, x_out, osem.at[0])]
    gather.tick(2)
    vthree.wait()
    for zi in range(4):
        for yi in range(2):
            at = (zi * 2 + yi) * 128
            group = vfull[zi, yi, 0, 0] + vfull[zi, yi, 0, 1] + vfull[zi, yi, 1, 0] + vfull[zi, yi, 1, 1]
            lines[:, at : at + 128] = group[0:8]
            for xi in range(2):
                for ci in range(2):
                    i = ((zi * 2 + yi) * 2 + xi) * 2 + ci
                    piece = 2 * ((i % 16) // 4) + i // 16
                    ubias[piece, 0:1, (i % 4) * 128 : (i % 4) * 128 + 128] = vfull[zi, yi, xi, ci, 8:9]

    def attention(normed, wblk, stage, mixed, wout, probs):
        @pl.loop(0, seq_len // block)
        def _(i):
            rows = pl.ds(pl.multiple_of(i * block, block), block)
            scaled, _ = _normal(x[rows].astype(f32))
            normed[rows] = (scaled * lines[0:1] + lines[1:2]).astype(bf16)

        gather.wait(gather.corner, 2)
        gather.start(gather.twin, 2)
        gather.tick(3, twin=False)
        keep = _local(normed, normed_out, osem.at[1])

        def side_of(pair):
            return (pair + core) % 2

        def load(pair):
            return [
                pltpu.make_async_copy(full.at[3 * (pair // 2) + i, side_of(pair)], wblk.at[pair % 2, i], wsem.at[pair % 2, i])
                for i in range(3)
            ]

        def store(pair):
            slot = pair % 2
            columns = pl.ds(pl.multiple_of((pair // 2) * WIDE, WIDE), WIDE)
            copies = [
                pltpu.make_async_copy(stage.at[slot, i], qkv.at[i, side_of(pair), :, columns], wsem.at[slot, 3 + i])
                for i in range(3)
            ]
            heads = pl.ds((side_of(pair) * 2 + pair // 2) * 2, 2)
            return copies + [pltpu.make_async_copy(probs.at[slot], probs_out.at[heads], wsem.at[slot, 6])]

        for c in load(0):
            c.start()

        def ticks(site, pair):
            for k, at in ATTEND_TICKS.items():
                if at % ATTEND_SITES == site:

                    @pl.when(pair == at // ATTEND_SITES)
                    def _(k=k):
                        gather.tick(k)

        @pl.loop(0, 4)
        def _(pair):
            slot = pair % 2
            for c in load(pair):
                c.wait()

            @pl.when(pair >= 2)
            def _():
                for c in store(pair - 2):
                    c.wait()

            ticks(0, pair)
            lanes = pl.ds(pl.multiple_of((side_of(pair) * 2 + pair // 2) * WIDE, WIDE), WIDE)
            wq, wk, wv = (wblk[slot, i].reshape(model, WIDE) for i in range(3))
            stage[slot, 0] = (_dot(normed[...], wq, NN) + lines[2:3, lanes]).astype(bf16)
            stage[slot, 1] = _dot(normed[...], wk, NN).astype(bf16)
            stage[slot, 2] = (_dot(normed[...], wv, NN) + lines[3:4, lanes]).astype(bf16)
            ticks(1, pair)
            for sub in range(2):

                @pl.when(pair == 2 * sub)
                def _(sub=sub):
                    for k in range(3 * sub, 3 * sub + 3):
                        gather.wait(gather.twin, k)
                    for c in load(2 * sub + 1):
                        c.start()

            step = 256
            factor = LOG2E / math.sqrt(HEAD_DIM)
            prefix_len = prefix[0]
            for head in range(WIDE // HEAD_DIM):
                part = slice(head * HEAD_DIM, (head + 1) * HEAD_DIM)
                for start, stop in _spans(seq_len, LONGEST, step):
                    scores = _dot(stage[slot, 1, :stop, part], stage[slot, 0, start : start + step, part], NT)
                    keys = lax.broadcasted_iota(jnp.int32, scores.shape, 0)
                    queries = lax.broadcasted_iota(jnp.int32, scores.shape, 1) + start
                    scores = jnp.where((keys <= queries) | (keys < prefix_len), scores, -jnp.inf)
                    peak = jnp.max(scores, axis=0, keepdims=True)
                    raw = jnp.exp2((scores - peak) * factor)
                    total = jnp.sum(raw, axis=0, keepdims=True)
                    share = (raw * (1.0 / total)).astype(bf16)
                    probs[slot, head, :stop, start : start + step] = share
                    to = pl.ds(pl.multiple_of((pair // 2) * WIDE + head * HEAD_DIM, HEAD_DIM), HEAD_DIM)
                    mixed[side_of(pair), start : start + step, to] = _dot(
                        share, stage[slot, 2, :stop, part], TN
                    ).astype(bf16)
                if head == 0:
                    ticks(2, pair)
            for c in store(pair):
                c.start()

            @pl.when(pair == 1)
            def _():
                gather.tick(6)
                for c in load(2):
                    c.start()

        gather.wait(gather.twin, 6)
        fetch = _local(fullo, wout, osem.at[3])
        done = _local(mixed, mixed_out, osem.at[2])
        fetch.wait()
        weight = [wout[c].reshape(model, seq_len // 2) for c in range(2)]
        step = 256

        @pl.loop(0, seq_len // step)
        def _(i):
            rows = pl.ds(pl.multiple_of(i * step, step), step)
            branch = _dot(mixed[0, rows], weight[0], NT) + _dot(mixed[1, rows], weight[1], NT)
            total = x[rows].astype(f32) + branch + lines[4:5]
            residual[rows] = total
            scaled, _ = _normal(total)
            second[rows] = (scaled * lines[5:6] + lines[6:7]).astype(bf16)

        gather.tick(8)
        for pair in (2, 3):
            for c in store(pair):
                c.wait()
        done.wait()
        keep.wait()

    pl.run_scoped(
        attention,
        pltpu.VMEM((seq_len, model), bf16),
        pltpu.VMEM((2, 3, 4, 2, 2, 64, WIDE), bf16),
        pltpu.VMEM((2, 3, seq_len, WIDE), bf16),
        pltpu.VMEM((2, seq_len, model // 2), bf16),
        pltpu.VMEM((2, 4, 2, 2, 64, model // 2), bf16),
        pltpu.VMEM((2, 2, seq_len, seq_len), bf16),
    )

    def feed(layer, gres, stage, hid, gpre):
        pieces = weights.shape[0]

        @pl.loop(0, seq_len // block)
        def _(i):
            rows = pl.ds(pl.multiple_of(i * block, block), block)
            layer[rows] = residual[rows] + lines[7:8]
            gres[rows] = jnp.zeros((block, model), f32)

        def away(piece):
            return [
                pltpu.make_async_remote_copy(
                    src_ref=stage.at[1, i],
                    dst_ref=grecv.at[2 * piece + i],
                    send_sem=fs.at[piece, i],
                    recv_sem=fr.at[piece, i],
                    device_id=sibling,
                    device_id_type=MESH,
                )
                for i in range(2)
            ]

        def stay(piece):
            return [pltpu.make_async_copy(stage.at[0, i], gown.at[2 * piece + i], fl.at[i]) for i in range(2)]

        def bring(k):
            return [
                pltpu.make_async_copy(gown.at[k], racc.at[k], rl.at[k, 0]),
                pltpu.make_async_copy(grecv.at[k], rtheirs.at[k], rl.at[k, 1]),
            ]

        @pl.loop(0, pieces)
        def _(t):
            piece, turn = t // 2, t % 2
            side = (t + core) % 2
            for k, at in FEED_TICKS.items():

                @pl.when(t == at)
                def _(k=k):
                    gather.tick(k)

            for p in range(pieces // 2):

                @pl.when(t == 2 * p + 1)
                def _(p=p):
                    gather.wait(gather.twin, early + 2 * p)
                    if p < pieces // 2 - 1:
                        gather.wait(gather.twin, early + 2 * p + 1)
                    else:
                        gather.last(20)

            @pl.when(t == pieces - 3)
            def _():
                for c in away(0):
                    c.wait_recv()
                reduce.start(bring(0) + bring(1))

            @pl.when(t == pieces - 2)
            def _():
                for k in range(EARLY):
                    reduce.wait(bring(k))
                    _combine(racc.at[k], rtheirs.at[k])
                    reduce.start(reduce.corner(k))

            @pl.when(t == pieces - 1)
            def _():
                for k in range(EARLY):
                    reduce.after_corner(k)

            @pl.when((t >= 2) & (turn == 1))
            def _():
                for c in away(piece - 1):
                    c.wait_send()

            @pl.when((t >= 2) & (turn == 0))
            def _():
                for c in stay(piece - 1):
                    c.wait()

            up = weights[2 * piece, side].reshape(model, model // 2)
            lower = weights[2 * piece + 1, side].reshape(model, model // 2)
            line = 2 * piece + side
            pre = _dot(second[...], up, NN) + ubias[line]
            phi = 0.5 * (1.0 + lax.erf(pre * (1.0 / math.sqrt(2.0))))
            density = jnp.exp2(pre * pre * (-0.5 * LOG2E)) * (1.0 / math.sqrt(2.0 * math.pi))
            hid[...] = (pre * phi).astype(bf16)
            slope = phi + pre * density
            back = (_dot(grad[...], lower, NN) * slope).astype(bf16)
            gpre[...] = back
            gbias[line] = jnp.sum(back.astype(f32), axis=0, keepdims=True)
            layer[...] += _dot(hid[...], lower, NT)
            gres[...] += _dot(gpre[...], up, NT)
            blocks = stage.shape[2:]
            stage[turn, 0] = _dot(second[...], gpre[...], TN).astype(bf16).reshape(blocks)
            stage[turn, 1] = _dot(grad[...], hid[...], TN).astype(bf16).reshape(blocks)

            @pl.when(turn == 1)
            def _():
                for c in away(piece):
                    c.start()

            @pl.when(turn == 0)
            def _():
                for c in stay(piece):
                    c.start()

        theirs = pl.ds(pl.multiple_of((1 - core) * half, half), half)
        final = [
            _local(layer.at[mine], layer_out.at[core], el.at[0]),
            _send(layer.at[theirs], layer_out.at[core], es.at[0], er.at[0], sibling),
        ]
        for k in range(EARLY):
            reduce.after_plane(k)
        sums[...] = jnp.zeros_like(sums)

        @pl.loop(0, seq_len // block)
        def _(i):
            rows = pl.ds(pl.multiple_of(i * block, block), block)
            scaled, inverse = _normal(residual[rows])
            grow = gres[rows]
            upstream = grad[rows].astype(f32)
            weighted = grow * lines[5:6]
            mean_plain = jnp.mean(weighted, axis=-1, keepdims=True)
            mean_scaled = jnp.mean(weighted * scaled, axis=-1, keepdims=True)
            total = upstream + inverse * (weighted - mean_plain - scaled * mean_scaled)
            gres[rows] = total
            second[rows] = total.astype(bf16)
            sums[0:1] += jnp.sum(grow * scaled, axis=0, keepdims=True)
            sums[1:2] += jnp.sum(grow, axis=0, keepdims=True)
            sums[2:3] += jnp.sum(total, axis=0, keepdims=True)
            sums[3:4] += jnp.sum(upstream, axis=0, keepdims=True)

        final.append(_local(gres, gres_out, el.at[1]))
        final.append(_local(second, low_out, el.at[2]))
        last = pieces // 2 - 1
        for c in away(last):
            c.wait_send()
        for c in stay(last):
            c.wait()
        for p in range(1, pieces // 2):
            for c in away(p):
                c.wait_recv()
        for k in range(EARLY):
            reduce.after_line(k)
        for c in final:
            c.wait()

    pl.run_scoped(
        feed,
        pltpu.VMEM((seq_len, model), f32),
        pltpu.VMEM((seq_len, model), f32),
        pltpu.VMEM((2, 2, 4, 2, 2, model // 16, model // 2), bf16),
        pltpu.VMEM((seq_len, model // 2), bf16),
        pltpu.VMEM((seq_len, model // 2), bf16),
    )
    for s in saved:
        s.wait()


def front(prefix_len, wq, wk, wv, wo, up, down, vec, xin, gin):
    rows, cols = wq.shape
    half, model = xin.shape[1:]
    seq_len = 2 * half
    pieces = 2 * (up.shape[1] // cols)
    chunks = 7 + pieces
    bf16, f32 = jnp.bfloat16, jnp.float32
    hbm = pl.BlockSpec(memory_space=pltpu.HBM)
    vmem = pl.BlockSpec(memory_space=pltpu.VMEM)
    dma = pltpu.SemaphoreType.DMA

    def shape(dims, dtype):
        return jax.ShapeDtypeStruct(dims, dtype)

    heads = model // HEAD_DIM
    return pl.pallas_call(
        front_kernel,
        out_shape=(
            shape((6, 2, 4, 2, 2, rows, WIDE), bf16),
            shape((2, 4, 2, 2, rows, cols), bf16),
            shape((3, 2, seq_len, cols), bf16),
            shape((2, seq_len, cols), bf16),
            shape((heads, seq_len, seq_len), bf16),
            shape((seq_len, model), bf16),
            shape((seq_len, model), bf16),
            shape((8, model), f32),
            shape((2, half, model), f32),
            shape((seq_len, model), f32),
            shape((seq_len, model), bf16),
            shape((8, model), f32),
            shape((pieces, 4, 2, 2, rows, cols), bf16),
            shape((pieces, 4, 2, 2, rows, cols), bf16),
            shape((pieces, 1, cols), f32),
            shape((EARLY, rows, cols), f32),
        ),
        in_specs=[pl.BlockSpec(memory_space=pltpu.SMEM)] + [vmem] * 7 + [hbm, hbm],
        out_specs=(hbm, hbm, hbm, hbm, hbm, hbm, hbm, vmem, hbm, hbm, hbm, vmem, hbm, hbm, vmem, vmem),
        scratch_shapes=[
            pltpu.VMEM((4, 2, 2, 2) + vec.shape, f32),
            pltpu.VMEM((seq_len, model), bf16),
            pltpu.VMEM((seq_len, model), bf16),
            pltpu.VMEM((seq_len, model), bf16),
            pltpu.VMEM((seq_len, model), f32),
            pltpu.VMEM((pieces, 2, 4, 2, 2, rows, cols), bf16),
            pltpu.VMEM((pieces, 1, cols), f32),
            dma((chunks + 1, 8)),
            dma((chunks + 1, 8)),
            dma((chunks,)),
            dma((7,)),
            dma((7,)),
            dma((1,)),
            dma((2,)),
            dma((2,)),
            dma((2,)),
            dma((2, 7)),
            dma((4,)),
            dma((pieces // 2, 2)),
            dma((pieces // 2, 2)),
            dma((2,)),
            dma((1,)),
            dma((1,)),
            dma((3,)),
            pltpu.VMEM((EARLY, 4, 2, 2, rows, cols), bf16),
            pltpu.VMEM((EARLY, 4, 2, 2, rows, cols), bf16),
            pltpu.VMEM((EARLY, 4, rows // 2, cols), bf16),
            pltpu.VMEM((EARLY, 4, rows // 2, cols), bf16),
            pltpu.VMEM((EARLY, 4, rows, cols), bf16),
            pltpu.VMEM((EARLY, 4, rows, cols), bf16),
            pltpu.VMEM((EARLY, 3, rows, cols), bf16),
            dma((EARLY, 7)),
            dma((EARLY, 7)),
            dma((EARLY, 2)),
        ],
        compiler_params=pltpu.CompilerParams(
            collective_id=0, has_side_effects=True, vmem_limit_bytes=63 * MIB
        ),
    )(prefix_len, wq, wk, wv, wo, up, down, vec, xin, gin)


RING = 4


def back_kernel(
    lines, sums_two, gbias, qkv, mixed_in, probs_in, full, fullo, low_in, normed_in, x_in, gres_in, gown, grecv,
    out, vout, iout, qrecv,
    ring, theirs_in, gbuf, x_one, y_one, x_two, y_two, from_z,
    vacc, v_s, vx_one, vx_two, vy_two, v_z,
    low, normed, ingrad, sums, bsums,
    ssem, rsem, lsem, qs, qr, vs, vr, bsem, msem, es, er,
):
    f32, bf16 = jnp.float32, jnp.bfloat16
    seq_len, model = low.shape
    half, block, step = seq_len // 2, 128, 256
    feeds = gown.shape[0] - EARLY
    count = out.shape[0]
    scale = 1.0 / math.sqrt(HEAD_DIM)

    own = gbuf.at[1]

    def acc(k):
        return own.at[k - feeds] if isinstance(k, int) and k >= feeds else ring.at[k % RING]

    reduce = Reduce(acc, out, x_one, y_one, x_two, y_two, from_z, ssem, rsem)
    z, y, x, core = reduce.z, reduce.y, reduce.x, reduce.core
    along, across, down, sibling = reduce.along, reduce.across, reduce.down, reduce.sibling

    def load(k):
        if isinstance(k, int) and k >= feeds:
            return [pltpu.make_async_copy(qrecv.at[k - feeds], theirs_in.at[k % 2], lsem.at[k % 2, 1])]
        return [
            pltpu.make_async_copy(gown.at[EARLY + k], ring.at[k % RING], lsem.at[k % 2, 0]),
            pltpu.make_async_copy(grecv.at[EARLY + k], theirs_in.at[k % 2], lsem.at[k % 2, 1]),
        ]

    def begin(k):
        reduce.wait(load(k))
        _combine(acc(k), theirs_in.at[k % 2])
        reduce.start(reduce.corner(k))

    def tick(k):
        if not isinstance(k, int) or k < count:
            begin(k)
        _if((k >= 1) & (k - 1 < count), lambda: reduce.after_corner(k - 1))
        _if((k >= 2) & (k - 2 < count), lambda: reduce.after_plane(k - 2))
        _if((k >= 3) & (k - 3 < count), lambda: reduce.after_line(k - 3))

    reduce.start(load(0))
    start = [_local(low_in, low, msem.at[0]), _local(normed_in, normed, msem.at[1])]
    _greet(along + [across, down, sibling])

    def away(sub, i):
        unit = sub * 2 + i
        return pltpu.make_async_remote_copy(
            src_ref=gbuf.at[0, unit],
            dst_ref=qrecv.at[unit],
            send_sem=qs.at[unit],
            recv_sem=qr.at[unit],
            device_id=sibling,
            device_id_type=MESH,
        )

    def landed(unit):
        away(unit // 2, unit % 2).wait_recv()

    def retreat(heads_in, probs, wblk, dq, dk, dv, dmix, dk_acc, dv_acc):
        def fetch(i):
            turn, sub = i // 2, i % 2
            side = (turn + 1 + core) % 2
            columns = pl.ds(pl.multiple_of(sub * WIDE, WIDE), WIDE)
            slot = i % 2
            copies = [
                pltpu.make_async_copy(qkv.at[n, side, :, columns], heads_in.at[slot, n], bsem.at[slot, n])
                for n in range(3)
            ]
            copies.append(pltpu.make_async_copy(mixed_in.at[side, :, columns], heads_in.at[slot, 3], bsem.at[slot, 3]))
            copies += [
                pltpu.make_async_copy(full.at[3 * sub + n, side], wblk.at[slot, n], bsem.at[slot, 4 + n])
                for n in range(3)
            ]
            copies.append(
                pltpu.make_async_copy(fullo.at[side, :, :, :, :, columns], wblk.at[slot, 3], bsem.at[slot, 7])
            )
            heads = pl.ds((side * 2 + sub) * 2, 2)
            copies.append(pltpu.make_async_copy(probs_in.at[heads], probs.at[slot], bsem.at[slot, 8]))
            return copies

        reduce.start(fetch(0))

        @pl.loop(0, seq_len // block)
        def _(i):
            ingrad[pl.ds(pl.multiple_of(i * block, block), block)] = jnp.zeros((block, model), f32)

        reduce.wait(start)

        @pl.loop(0, 4)
        def _(i):
            turn, sub, slot = i // 2, i % 2, i % 2
            side = (turn + 1 + core) % 2
            reduce.wait(fetch(i))

            @pl.when(i < 3)
            def _():
                reduce.start(fetch(i + 1))

            columns = pl.ds(pl.multiple_of(sub * WIDE, WIDE), WIDE)

            def put(n, value):
                at = slice((n % 2) * WIDE, (n % 2 + 1) * WIDE)
                gbuf[turn, sub * 2 + n // 2, :, :, :, :, at] = value.astype(bf16).reshape(4, 2, 2, model // 16, WIDE)

            def tick_and_load(n):
                k = 2 * i + n

                @pl.when(k < feeds)
                def _():
                    tick(k)

                @pl.when(k + 1 < feeds)
                def _():
                    reduce.start(load(k + 1))

                @pl.when(k == feeds + n)
                def _():
                    if n == 0:
                        for u in range(2):
                            landed(u)
                            reduce.start(load(feeds + u))
                    tick(feeds + n)

            tick_and_load(0)
            wq, wk, wv, wo = (wblk[slot, n].reshape(model, WIDE) for n in range(4))
            dmix[...] = _dot(low[...], wo, NN).astype(bf16)
            put(0, _dot(low[...], heads_in[slot, 3], TN))
            for head in range(WIDE // HEAD_DIM):
                part = slice(head * HEAD_DIM, (head + 1) * HEAD_DIM)
                dk_acc[...] = jnp.zeros_like(dk_acc)
                dv_acc[...] = jnp.zeros_like(dv_acc)
                for first, stop in _spans(seq_len, LONGEST, step):
                    grad = dmix[first : first + step, part]
                    weights_low = probs[slot, head, :stop, first : first + step]
                    weights = weights_low.astype(f32)
                    dprobs = _dot(heads_in[slot, 2, :stop, part], grad, NT)
                    inner = jnp.sum(weights * dprobs, axis=0, keepdims=True)
                    dscores = (weights * (dprobs - inner)).astype(bf16)
                    dq[first : first + step, part] = (
                        _dot(dscores, heads_in[slot, 1, :stop, part], TN) * scale
                    ).astype(bf16)
                    dk_acc[:stop] += _dot(dscores, heads_in[slot, 0, first : first + step, part], NN)
                    dv_acc[:stop] += _dot(weights_low, grad, NN)
                dk[:, part] = (dk_acc[...] * scale).astype(bf16)
                dv[:, part] = dv_acc[...].astype(bf16)
                if head == 0:
                    tick_and_load(1)
            put(1, _dot(normed[...], dq[...], TN))
            put(2, _dot(normed[...], dk[...], TN))
            put(3, _dot(normed[...], dv[...], TN))
            ingrad[...] += _dot(dq[...], wq, NT) + _dot(dk[...], wk, NT) + _dot(dv[...], wv, NT)

            @pl.when(turn == 0)
            def _():
                for n in range(2):
                    away(sub, n).start()

            at = side * 2 + sub
            bsums[at, 0:1] = jnp.sum(dq[...].astype(f32), axis=0, keepdims=True)
            bsums[at, 1:2] = jnp.sum(dv[...].astype(f32), axis=0, keepdims=True)

        for sub in range(2):
            for n in range(2):
                away(sub, n).wait_send()

    pl.run_scoped(
        retreat,
        pltpu.VMEM((2, 4, seq_len, WIDE), bf16),
        pltpu.VMEM((2, 2, seq_len, seq_len), bf16),
        pltpu.VMEM((2, 4, 4, 2, 2, model // 16, WIDE), bf16),
        pltpu.VMEM((seq_len, WIDE), bf16),
        pltpu.VMEM((seq_len, WIDE), bf16),
        pltpu.VMEM((seq_len, WIDE), bf16),
        pltpu.VMEM((seq_len, WIDE), bf16),
        pltpu.VMEM((seq_len, HEAD_DIM), f32),
        pltpu.VMEM((seq_len, HEAD_DIM), f32),
    )

    def finish(gres, xs):
        bring = [_local(gres_in, gres, msem.at[0]), _local(x_in, xs, msem.at[1])]
        for unit in (2, 3):
            landed(unit)
            reduce.start(load(feeds + unit))
        tick(feeds + 2)
        reduce.wait(bring)
        sums[...] = jnp.zeros_like(sums)

        @pl.loop(0, seq_len // block)
        def _(i):
            rows = pl.ds(pl.multiple_of(i * block, block), block)
            scaled, inverse = _normal(xs[rows].astype(f32))
            grow = ingrad[rows]
            weighted = grow * lines[0:1]
            mean_plain = jnp.mean(weighted, axis=-1, keepdims=True)
            mean_scaled = jnp.mean(weighted * scaled, axis=-1, keepdims=True)
            ingrad[rows] = gres[rows] + inverse * (weighted - mean_plain - scaled * mean_scaled)
            sums[0:1] += jnp.sum(grow * scaled, axis=0, keepdims=True)
            sums[1:2] += jnp.sum(grow, axis=0, keepdims=True)

    pl.run_scoped(finish, pltpu.VMEM((seq_len, model), f32), pltpu.VMEM((seq_len, model), bf16))
    mine = pl.ds(pl.multiple_of(core * half, half), half)
    theirs = pl.ds(pl.multiple_of((1 - core) * half, half), half)
    final = [
        _local(ingrad.at[mine], iout.at[core], msem.at[0]),
        _send(ingrad.at[theirs], iout.at[core], es.at[0], er.at[0], sibling),
    ]
    for pair in range(4):
        at = slice(pair * WIDE, (pair + 1) * WIDE)
        sums[2:4, at] = bsums[pair, 0:2]
    sums[4:5] = sums_two[2:3]
    sums[5:7] = sums_two[0:2]
    sums[7:8] = sums_two[3:4]
    vacc[...] = jnp.zeros_like(vacc)
    for zi in range(4):
        for yi in range(2):
            at = (zi * 2 + yi) * 128
            for xi in range(2):
                for ci in range(2):
                    i = ((zi * 2 + yi) * 2 + xi) * 2 + ci
                    piece = 2 * ((i % 16) // 4) + i // 16
                    vacc[ci, zi, yi, xi, 0:8] = sums[:, at : at + 128]
                    vacc[ci, zi, yi, xi, 8:9] = gbias[piece, 0:1, (i % 4) * 128 : (i % 4) * 128 + 128]
    vzero = _send(vacc.at[1 - core], v_s, vs.at[0], vr.at[0], sibling)
    tick(feeds + 3)
    vzero.wait()
    vmine = vacc.at[core]
    vmine[...] = vmine[...] + v_s[...]
    vone = _send(vmine.at[:, 1 - y, 1 - x], vx_one, vs.at[1], vr.at[1], across)
    tick(feeds + 4)
    vone.wait()
    vmine[:, 1 - y, x] = vmine[:, 1 - y, x] + vx_one[...]
    vtwo = [
        _send(vmine.at[:, y, 1 - x], vx_two, vs.at[2], vr.at[2], across),
        _send(vmine.at[:, 1 - y, x], vy_two, vs.at[3], vr.at[3], down),
    ]
    tick(feeds + 5)
    reduce.wait(vtwo)
    vmine[:, y, x] = vmine[:, y, x] + vx_two[...] + vy_two[...]
    vthree = [
        _send(vmine.at[(z + j + 1) % 4, y, x], v_z.at[j], vs.at[4 + j], vr.at[4 + j], along[j]) for j in range(3)
    ]
    tick(feeds + 6)
    reduce.wait(vthree)
    vout[...] = vmine[z, y, x] + v_z[0] + v_z[1] + v_z[2]
    reduce.wait(final)


def back(lines, sums_two, gbias, qkv, mixed, probs, full, fullo, low, normed, x, gres, gown, grecv):
    count = gown.shape[0] - EARLY + 4
    seq_len, model = x.shape
    rows, cols = gown.shape[-2:]
    half = seq_len // 2
    bf16, f32 = jnp.bfloat16, jnp.float32
    hbm = pl.BlockSpec(memory_space=pltpu.HBM)
    vmem = pl.BlockSpec(memory_space=pltpu.VMEM)
    dma = pltpu.SemaphoreType.DMA
    small = (16, 128)
    return pl.pallas_call(
        back_kernel,
        out_shape=(
            jax.ShapeDtypeStruct((count, rows, cols), f32),
            jax.ShapeDtypeStruct(small, f32),
            jax.ShapeDtypeStruct((2, half, model), f32),
            jax.ShapeDtypeStruct((4, 4, 2, 2, rows, cols), bf16),
        ),
        in_specs=[vmem] * 3 + [hbm] * 11,
        out_specs=(vmem, vmem, hbm, hbm),
        scratch_shapes=[
            pltpu.VMEM((RING, 4, 2, 2, rows, cols), bf16),
            pltpu.VMEM((2, 4, 2, 2, rows, cols), bf16),
            pltpu.VMEM((2, 4, 4, 2, 2, rows, cols), bf16),
            pltpu.VMEM((count, 4, rows // 2, cols), bf16),
            pltpu.VMEM((count, 4, rows // 2, cols), bf16),
            pltpu.VMEM((count, 4, rows, cols), bf16),
            pltpu.VMEM((count, 4, rows, cols), bf16),
            pltpu.VMEM((count, 3, rows, cols), bf16),
            pltpu.VMEM((2, 4, 2, 2) + small, f32),
            pltpu.VMEM((4, 2, 2) + small, f32),
            pltpu.VMEM((4,) + small, f32),
            pltpu.VMEM((4,) + small, f32),
            pltpu.VMEM((4,) + small, f32),
            pltpu.VMEM((3,) + small, f32),
            pltpu.VMEM((seq_len, model), bf16),
            pltpu.VMEM((seq_len, model), bf16),
            pltpu.VMEM((seq_len, model), f32),
            pltpu.VMEM((8, model), f32),
            pltpu.VMEM((4, 8, WIDE), f32),
            dma((count, 7)),
            dma((count, 7)),
            dma((2, 2)),
            dma((4,)),
            dma((4,)),
            dma((7,)),
            dma((7,)),
            dma((2, 9)),
            dma((2,)),
            dma((1,)),
            dma((1,)),
        ],
        compiler_params=pltpu.CompilerParams(
            collective_id=1, has_side_effects=True, vmem_limit_bytes=63 * MIB
        ),
    )(lines, sums_two, gbias, qkv, mixed, probs, full, fullo, low, normed, x, gres, gown, grecv)


def fast_body(
    inputs, prefix, ln1_gain, ln1_bias, query_weight, query_bias, key_weight, value_weight, value_bias,
    out_weight, out_bias, ln2_gain, ln2_bias, up_weight, up_bias, down_weight, down_bias, cotangent,
):
    core = lax.axis_index("tensor")
    half, model = inputs.shape[2], inputs.shape[3]
    rows, cols = query_weight.shape
    pieces = up_weight.shape[1] // cols

    small = jnp.stack([ln1_gain, ln1_bias, query_bias, value_bias, out_bias, ln2_gain, ln2_bias, down_bias])
    place = (lax.axis_index("dp") * 2 + core) % 4
    vec = jnp.pad(up_bias.reshape(1, 128), ((8, 7), (0, 0)))
    vec = lax.dynamic_update_slice(vec, small, (0, place * 32))
    prefix_len = lax.dynamic_slice_in_dim(prefix[:, 0], core, 1)
    (
        full, fullo, qkv, mixed, probs, normed, x, lines, layer_out, gres, low, sums_two, gown, grecv, gup_bias,
        early,
    ) = front(
        prefix_len, query_weight, key_weight, value_weight, out_weight.T, up_weight, down_weight.T, vec,
        inputs[:, 0], cotangent[:, 0],
    )
    out, vout, input_grad, _ = back(
        lines, sums_two, gup_bias, qkv, mixed, probs, full, fullo, low, normed, x, gres,
        gown, grecv,
    )
    vectors = lax.dynamic_slice(vout, (0, place * 32), (8, 32))

    def join(pieces_of):
        return pieces_of.transpose(1, 0, 2).reshape(rows, pieces * cols)

    ffn = jnp.concatenate([early, out[:-4]])
    units = out[-4:].reshape(2, 2, rows, 2, WIDE).transpose(1, 3, 2, 0, 4).reshape(4, rows, cols)
    gout, gq, gk, gv = units[0], units[1], units[2], units[3]
    return (
        layer_out.reshape(2, 1, half, model),
        input_grad.reshape(2, 1, half, model),
        vectors[0],
        vectors[1],
        gq,
        vectors[2],
        gk,
        gv,
        vectors[3],
        gout.T,
        vectors[4],
        vectors[5],
        vectors[6],
        join(ffn[0::2]),
        vout[8],
        join(ffn[1::2]).T,
        vectors[7],
    )


def solution(mesh):
    in_specs = (
        P(None, "dp", "tensor", None),
        P(None, "dp"),
        P(("dp", "tensor")),
        P(("dp", "tensor")),
        P("dp", "tensor"),
        P(("dp", "tensor")),
        P("dp", "tensor"),
        P("dp", "tensor"),
        P(("dp", "tensor")),
        P("tensor", "dp"),
        P(("dp", "tensor")),
        P(("dp", "tensor")),
        P(("dp", "tensor")),
        P("dp", "tensor"),
        P(("dp", "tensor")),
        P("tensor", "dp"),
        P(("dp", "tensor")),
        P(None, "dp", "tensor", None),
    )
    out_specs = (
        P(None, "dp", "tensor", None),
        P(None, "dp", "tensor", None),
        P(("dp", "tensor")),
        P(("dp", "tensor")),
        P("dp", "tensor"),
        P(("dp", "tensor")),
        P("dp", "tensor"),
        P("dp", "tensor"),
        P(("dp", "tensor")),
        P("tensor", "dp"),
        P(("dp", "tensor")),
        P(("dp", "tensor")),
        P(("dp", "tensor")),
        P("dp", "tensor"),
        P(("dp", "tensor")),
        P("tensor", "dp"),
        P(("dp", "tensor")),
    )
    sizes = (mesh.shape["dp"], mesh.shape["tensor"])
    chosen = fast_body if sizes == (16, 2) else body
    return jax.shard_map(chosen, mesh=mesh, in_specs=in_specs, out_specs=out_specs, check_vma=False)
```

```python
import math

import jax
import jax.numpy as jnp
from jax import lax
from jax.experimental import pallas as pl
from jax.experimental.pallas import tpu as pltpu
from jax.sharding import PartitionSpec as P

MESH = pl.DeviceIdType.MESH
LONGEST = 512

HEAD_DIM = 128
BLOCK = 512


EPSILON = 1e-05


def norm_forward(values, gain, shift):
    center = values - jnp.mean(values, axis=-1, keepdims=True)
    inverse = lax.rsqrt(jnp.mean(center * center, axis=-1, keepdims=True) + EPSILON)
    scaled = center * inverse
    return (scaled * gain + shift, scaled, inverse)


def norm_backward(grad_out, scaled, inverse, gain):
    weighted = grad_out * gain
    mean_plain = jnp.mean(weighted, axis=-1, keepdims=True)
    mean_scaled = jnp.mean(weighted * scaled, axis=-1, keepdims=True)
    return inverse * (weighted - mean_plain - scaled * mean_scaled)


def smooth_gate(values):
    return jax.nn.gelu(values, approximate=False)


def smooth_slope(values):
    normal_cdf = 0.5 * (1.0 + jax.scipy.special.erf(values / math.sqrt(2.0)))
    density = jnp.exp(-0.5 * values * values) / math.sqrt(2.0 * math.pi)
    return normal_cdf + values * density


def masked_scores(query_block, key_rows, start, prefix_len):
    scale = 1.0 / math.sqrt(key_rows.shape[2])
    scores = (
        jnp.einsum("qhd,khd->hqk", query_block, key_rows, preferred_element_type=jnp.float32)
        * scale
    )
    places = start + jnp.arange(query_block.shape[0], dtype=jnp.int32)
    columns = jnp.arange(key_rows.shape[0], dtype=jnp.int32)
    allowed = (columns[None, :] <= places[:, None]) | (columns[None, :] < prefix_len)
    return jnp.where(allowed[None], scores, -jnp.inf)


def attend_forward(queries, key_rows, value_rows, prefix_len):
    seq_len, heads_local, head_size = queries.shape
    count = seq_len // BLOCK

    def one_block(items):
        query_block, start = items
        scores = masked_scores(query_block, key_rows, start, prefix_len)
        peak = jnp.max(scores, axis=-1, keepdims=True)
        raw_weights = jnp.exp(scores - peak)
        totals = jnp.sum(raw_weights, axis=-1, keepdims=True)
        probs = (raw_weights / totals).astype(jnp.bfloat16)
        mixed = jnp.einsum("hqk,khd->qhd", probs, value_rows, preferred_element_type=jnp.float32)
        return (mixed.astype(jnp.bfloat16), (peak + jnp.log(totals))[..., 0])

    starts = jnp.arange(count, dtype=jnp.int32) * BLOCK
    mixed, log_totals = lax.map(
        one_block, (queries.reshape(count, BLOCK, heads_local, head_size), starts)
    )
    return (mixed.reshape(seq_len, heads_local * head_size), log_totals)


def attend_backward(queries, key_rows, value_rows, grad_mixed, log_totals, prefix_len):
    seq_len, heads_local, head_size = queries.shape
    count = seq_len // BLOCK
    scale = 1.0 / math.sqrt(head_size)

    def one_block(carry, items):
        key_total, value_total = carry
        query_block, grad_block, log_block, start = items
        scores = masked_scores(query_block, key_rows, start, prefix_len)
        probs = jnp.exp(scores - log_block[..., None])
        grad_probs = jnp.einsum(
            "qhd,khd->hqk", grad_block, value_rows, preferred_element_type=jnp.float32
        )
        inner = jnp.sum(probs * grad_probs, axis=-1, keepdims=True)
        grad_scores = (probs * (grad_probs - inner)).astype(jnp.bfloat16)
        grad_query = (
            jnp.einsum("hqk,khd->qhd", grad_scores, key_rows, preferred_element_type=jnp.float32)
            * scale
        )
        key_total = (
            key_total
            + jnp.einsum(
                "hqk,qhd->khd", grad_scores, query_block, preferred_element_type=jnp.float32
            )
            * scale
        )
        value_total = value_total + jnp.einsum(
            "hqk,qhd->khd",
            probs.astype(jnp.bfloat16),
            grad_block,
            preferred_element_type=jnp.float32,
        )
        return ((key_total, value_total), grad_query.astype(jnp.bfloat16))

    empty_total = jnp.zeros(queries.shape, jnp.float32)
    starts = jnp.arange(count, dtype=jnp.int32) * BLOCK
    blocked = (count, BLOCK, heads_local, head_size)
    (key_total, value_total), grad_queries = lax.scan(
        one_block,
        (empty_total, empty_total),
        (queries.reshape(blocked), grad_mixed.reshape(blocked), log_totals, starts),
    )
    width = heads_local * head_size
    return (
        grad_queries.reshape(seq_len, width),
        key_total.astype(jnp.bfloat16).reshape(seq_len, width),
        value_total.astype(jnp.bfloat16).reshape(seq_len, width),
    )


def body(
    inputs,
    prefix,
    ln1_gain,
    ln1_bias,
    query_weight,
    query_bias,
    key_weight,
    value_weight,
    value_bias,
    out_weight,
    out_bias,
    ln2_gain,
    ln2_bias,
    up_weight,
    up_bias,
    down_weight,
    down_bias,
    cotangent,
):
    local_width = query_weight.shape[1]
    local_hidden = up_weight.shape[1]
    shard_rows = inputs.shape[2]
    micro = inputs.shape[0]
    model_width = inputs.shape[3]
    heads_local = local_width // HEAD_DIM
    offset_width = lax.axis_index("tensor") * local_width
    offset_hidden = lax.axis_index("tensor") * local_hidden
    vectors = (
        lax.all_gather(ln1_gain, ("dp", "tensor"), axis=0, tiled=True),
        lax.all_gather(ln1_bias, ("dp", "tensor"), axis=0, tiled=True),
        lax.all_gather(query_bias, ("dp", "tensor"), axis=0, tiled=True),
        lax.all_gather(value_bias, ("dp", "tensor"), axis=0, tiled=True),
        lax.all_gather(out_bias, ("dp", "tensor"), axis=0, tiled=True),
        lax.all_gather(ln2_gain, ("dp", "tensor"), axis=0, tiled=True),
        lax.all_gather(ln2_bias, ("dp", "tensor"), axis=0, tiled=True),
        lax.all_gather(up_bias, ("dp", "tensor"), axis=0, tiled=True),
        lax.all_gather(down_bias, ("dp", "tensor"), axis=0, tiled=True),
    )
    (
        gain_one,
        shift_one,
        query_full_bias,
        value_full_bias,
        out_shift,
        gain_two,
        shift_two,
        up_full_bias,
        down_shift,
    ) = vectors
    query_shift = lax.dynamic_slice_in_dim(query_full_bias, offset_width, local_width)
    value_shift = lax.dynamic_slice_in_dim(value_full_bias, offset_width, local_width)
    up_shift = lax.dynamic_slice_in_dim(up_full_bias, offset_hidden, local_hidden)
    zero_width = jnp.zeros((model_width,), jnp.float32)
    gain_one_grad = zero_width
    shift_one_grad = zero_width
    query_bias_grad = zero_width
    value_bias_grad = zero_width
    out_bias_grad = zero_width
    gain_two_grad = zero_width
    shift_two_grad = zero_width
    up_bias_grad = jnp.zeros((up_full_bias.shape[0],), jnp.float32)
    down_bias_grad = zero_width
    weight_totals = None
    layer_rows = []
    input_rows = []
    for index in range(micro):
        gathered = (
            lax.all_gather(query_weight, "dp", axis=0, tiled=True),
            lax.all_gather(key_weight, "dp", axis=0, tiled=True),
            lax.all_gather(value_weight, "dp", axis=0, tiled=True),
            lax.all_gather(out_weight, "dp", axis=1, tiled=True),
            lax.all_gather(up_weight, "dp", axis=0, tiled=True),
            lax.all_gather(down_weight, "dp", axis=1, tiled=True),
        )
        full_query, full_key, full_value, full_out, full_up, full_down = gathered
        rows_in = inputs[index, 0].astype(jnp.float32)
        prefix_len = prefix[index, 0]
        normed, scaled_one, inverse_one = norm_forward(rows_in, gain_one, shift_one)
        normed_all = lax.all_gather(normed.astype(jnp.bfloat16), "tensor", axis=0, tiled=True)
        seq_len = normed_all.shape[0]
        queries = (
            jnp.dot(normed_all, full_query, preferred_element_type=jnp.float32) + query_shift
        ).astype(jnp.bfloat16)
        key_rows = jnp.dot(normed_all, full_key, preferred_element_type=jnp.float32).astype(
            jnp.bfloat16
        )
        value_rows = (
            jnp.dot(normed_all, full_value, preferred_element_type=jnp.float32) + value_shift
        ).astype(jnp.bfloat16)
        head_shape = (seq_len, heads_local, HEAD_DIM)
        queries_h = queries.reshape(head_shape)
        keys_h = key_rows.reshape(head_shape)
        values_h = value_rows.reshape(head_shape)
        attended, log_totals = attend_forward(queries_h, keys_h, values_h, prefix_len)
        attention_share = lax.psum_scatter(
            jnp.dot(attended, full_out, preferred_element_type=jnp.float32).astype(jnp.bfloat16),
            "tensor",
            scatter_dimension=0,
            tiled=True,
        ).astype(jnp.float32)
        residual = rows_in + attention_share + out_shift
        second, scaled_two, inverse_two = norm_forward(residual, gain_two, shift_two)
        grad_rows = cotangent[index, 0]
        down_bias_grad = down_bias_grad + jnp.sum(grad_rows.astype(jnp.float32), axis=0)
        second_all = lax.all_gather(second.astype(jnp.bfloat16), "tensor", axis=0, tiled=True)
        hidden_pre = jnp.dot(second_all, full_up, preferred_element_type=jnp.float32) + up_shift
        hidden_act = smooth_gate(hidden_pre).astype(jnp.bfloat16)
        feed_share = lax.psum_scatter(
            jnp.dot(hidden_act, full_down, preferred_element_type=jnp.float32).astype(jnp.bfloat16),
            "tensor",
            scatter_dimension=0,
            tiled=True,
        ).astype(jnp.float32)
        layer_rows.append(residual + feed_share + down_shift)
        grad_all = lax.all_gather(grad_rows, "tensor", axis=0, tiled=True)
        down_grad = jnp.dot(hidden_act.T, grad_all, preferred_element_type=jnp.float32)
        grad_act = jnp.dot(grad_all, full_down.T, preferred_element_type=jnp.float32)
        grad_pre = (grad_act * smooth_slope(hidden_pre)).astype(jnp.bfloat16)
        up_grad = jnp.dot(second_all.T, grad_pre, preferred_element_type=jnp.float32)
        up_part = jnp.sum(grad_pre.astype(jnp.float32), axis=0)
        up_bias_grad = up_bias_grad + lax.dynamic_update_slice(
            jnp.zeros_like(up_bias_grad), up_part, (offset_hidden,)
        )
        grad_second = lax.psum_scatter(
            jnp.dot(grad_pre, full_up.T, preferred_element_type=jnp.float32).astype(jnp.bfloat16),
            "tensor",
            scatter_dimension=0,
            tiled=True,
        ).astype(jnp.float32)
        gain_two_grad = gain_two_grad + jnp.sum(grad_second * scaled_two, axis=0)
        shift_two_grad = shift_two_grad + jnp.sum(grad_second, axis=0)
        grad_residual = grad_rows.astype(jnp.float32) + norm_backward(
            grad_second, scaled_two, inverse_two, gain_two
        )
        out_bias_grad = out_bias_grad + jnp.sum(grad_residual, axis=0)
        residual_all = lax.all_gather(
            grad_residual.astype(jnp.bfloat16), "tensor", axis=0, tiled=True
        )
        out_grad = jnp.dot(attended.T, residual_all, preferred_element_type=jnp.float32)
        grad_attended = jnp.dot(
            residual_all, full_out.T, preferred_element_type=jnp.float32
        ).astype(jnp.bfloat16)
        grad_queries, grad_keys, grad_values = attend_backward(
            queries_h, keys_h, values_h, grad_attended, log_totals, prefix_len
        )
        query_grad = jnp.dot(normed_all.T, grad_queries, preferred_element_type=jnp.float32)
        key_grad = jnp.dot(normed_all.T, grad_keys, preferred_element_type=jnp.float32)
        value_grad = jnp.dot(normed_all.T, grad_values, preferred_element_type=jnp.float32)
        query_part = jnp.sum(grad_queries.astype(jnp.float32), axis=0)
        value_part = jnp.sum(grad_values.astype(jnp.float32), axis=0)
        query_bias_grad = query_bias_grad + lax.dynamic_update_slice(
            zero_width, query_part, (offset_width,)
        )
        value_bias_grad = value_bias_grad + lax.dynamic_update_slice(
            zero_width, value_part, (offset_width,)
        )
        partial_sum = jnp.dot(grad_queries, full_query.T, preferred_element_type=jnp.float32)
        partial_sum = partial_sum + jnp.dot(
            grad_keys, full_key.T, preferred_element_type=jnp.float32
        )
        grad_normed = lax.psum_scatter(
            (
                partial_sum + jnp.dot(grad_values, full_value.T, preferred_element_type=jnp.float32)
            ).astype(jnp.bfloat16),
            "tensor",
            scatter_dimension=0,
            tiled=True,
        ).astype(jnp.float32)
        gain_one_grad = gain_one_grad + jnp.sum(grad_normed * scaled_one, axis=0)
        shift_one_grad = shift_one_grad + jnp.sum(grad_normed, axis=0)
        input_rows.append(
            grad_residual + norm_backward(grad_normed, scaled_one, inverse_one, gain_one)
        )
        reduced = (query_grad, key_grad, value_grad, out_grad, up_grad, down_grad)
        if weight_totals is None:
            weight_totals = reduced
        else:
            weight_totals = tuple((left + right for left, right in zip(weight_totals, reduced)))
    query_total, key_total, value_total, out_total, up_total, down_total = weight_totals
    query_total, key_total, value_total, out_total, up_total, down_total = (
        lax.psum_scatter(
            query_total.astype(jnp.bfloat16), "dp", scatter_dimension=0, tiled=True
        ).astype(jnp.float32),
        lax.psum_scatter(
            key_total.astype(jnp.bfloat16), "dp", scatter_dimension=0, tiled=True
        ).astype(jnp.float32),
        lax.psum_scatter(
            value_total.astype(jnp.bfloat16), "dp", scatter_dimension=0, tiled=True
        ).astype(jnp.float32),
        lax.psum_scatter(
            out_total.astype(jnp.bfloat16), "dp", scatter_dimension=1, tiled=True
        ).astype(jnp.float32),
        lax.psum_scatter(
            up_total.astype(jnp.bfloat16), "dp", scatter_dimension=0, tiled=True
        ).astype(jnp.float32),
        lax.psum_scatter(
            down_total.astype(jnp.bfloat16), "dp", scatter_dimension=1, tiled=True
        ).astype(jnp.float32),
    )
    vector_totals = (
        lax.psum_scatter(gain_one_grad, ("dp", "tensor"), scatter_dimension=0, tiled=True),
        lax.psum_scatter(shift_one_grad, ("dp", "tensor"), scatter_dimension=0, tiled=True),
        lax.psum_scatter(query_bias_grad, ("dp", "tensor"), scatter_dimension=0, tiled=True),
        lax.psum_scatter(value_bias_grad, ("dp", "tensor"), scatter_dimension=0, tiled=True),
        lax.psum_scatter(out_bias_grad, ("dp", "tensor"), scatter_dimension=0, tiled=True),
        lax.psum_scatter(gain_two_grad, ("dp", "tensor"), scatter_dimension=0, tiled=True),
        lax.psum_scatter(shift_two_grad, ("dp", "tensor"), scatter_dimension=0, tiled=True),
        lax.psum_scatter(up_bias_grad, ("dp", "tensor"), scatter_dimension=0, tiled=True),
        lax.psum_scatter(down_bias_grad, ("dp", "tensor"), scatter_dimension=0, tiled=True),
    )
    (
        gain_one_out,
        shift_one_out,
        query_bias_out,
        value_bias_out,
        out_bias_out,
        gain_two_out,
        shift_two_out,
        up_bias_out,
        down_bias_out,
    ) = vector_totals
    out_shape = (micro, 1, shard_rows, model_width)
    layer_out = jnp.stack(layer_rows).reshape(out_shape)
    input_grad = jnp.stack(input_rows).reshape(out_shape)
    return (
        layer_out,
        input_grad,
        gain_one_out,
        shift_one_out,
        query_total,
        query_bias_out,
        key_total,
        value_total,
        value_bias_out,
        out_total,
        out_bias_out,
        gain_two_out,
        shift_two_out,
        up_total,
        up_bias_out,
        down_total,
        down_bias_out,
    )


def _place(z, y, x):
    return z * 4 + y * 2 + x


def _coords():
    dp = lax.axis_index("dp")
    core = lax.axis_index("tensor")
    return dp // 4, (dp // 2) % 2, dp % 2, core


def _greet(peers):
    barrier = pltpu.get_barrier_semaphore()
    for peer in peers:
        pl.semaphore_signal(barrier, inc=1, device_id=peer, device_id_type=MESH)
    pl.semaphore_wait(barrier, len(peers))


def _peers():
    z, y, x, core = _coords()
    along = [(_place((z + j) % 4, y, x), core) for j in (1, 2, 3)]
    across = (_place(z, y, 1 - x), core)
    down = (_place(z, 1 - y, x), core)
    sibling = (_place(z, y, x), 1 - core)
    return along, across, down, sibling


def _send(src, dst, send_sem, recv_sem, peer):
    copy = pltpu.make_async_remote_copy(
        src_ref=src,
        dst_ref=dst,
        send_sem=send_sem,
        recv_sem=recv_sem,
        device_id=peer,
        device_id_type=MESH,
    )
    copy.start()
    return copy


def _local(src, dst, sem):
    copy = pltpu.make_async_copy(src, dst, sem)
    copy.start()
    return copy


def _dot(left, right, contract):
    return lax.dot_general(left, right, (contract, ((), ())), preferred_element_type=jnp.float32)


NN = ((1,), (0,))
NT = ((1,), (1,))
TN = ((0,), (0,))
LOG2E = 1.4426950408889634
MIB = 1024 * 1024
WIDE = 256


def _normal(values):
    center = values - jnp.mean(values, axis=-1, keepdims=True)
    inverse = lax.rsqrt(jnp.mean(center * center, axis=-1, keepdims=True) + EPSILON)
    return center * inverse, inverse


def _spans(seq_len, longest, step):
    return [(start, max(longest, start + step)) for start in range(0, seq_len, step)]


class Gather:
    def __init__(self, shards, places, send_sem, recv_sem, local_sem):
        self.z, self.y, self.x, self.core = _coords()
        self.along, self.across, self.down, self.sibling = _peers()
        self.shards, self.places, self.count = shards, places, len(shards)
        self.send_sem, self.recv_sem, self.local_sem = send_sem, recv_sem, local_sem

    def _remote(self, k, slot, src, dst, peer):
        return pltpu.make_async_remote_copy(
            src_ref=src,
            dst_ref=dst,
            send_sem=self.send_sem.at[k, slot],
            recv_sem=self.recv_sem.at[k, slot],
            device_id=peer,
            device_id_type=MESH,
        )

    def line(self, k):
        own = self.places[k].at[self.core, self.z, self.y, self.x]
        here = pltpu.make_async_copy(self.shards[k], own, self.local_sem.at[k])
        return [here] + [self._remote(k, j, self.shards[k], own, self.along[j]) for j in range(3)]

    def plane(self, k):
        block = self.places[k].at[self.core, :, self.y, self.x]
        return [self._remote(k, 3, block, block, self.across), self._remote(k, 4, block, block, self.down)]

    def corner(self, k):
        part = self.shards[k].shape[0] // 2
        one = self.places[k].at[self.core, :, 1 - self.y, self.x, 0:part]
        two = self.places[k].at[self.core, :, self.y, 1 - self.x, part : 2 * part]
        return [self._remote(k, 5, one, one, self.across), self._remote(k, 6, two, two, self.down)]

    def twin(self, k):
        block = self.places[k].at[self.core]
        return [self._remote(k, 7, block, block, self.sibling)]

    def near(self, k):
        own = self.places[k].at[self.core, self.z, self.y, self.x]
        here = pltpu.make_async_copy(self.shards[k], own, self.local_sem.at[k])
        src = self.shards[k]
        return [here, self._remote(k, 3, src, own, self.across), self._remote(k, 4, src, own, self.down)]

    def near_corner(self, k):
        part = self.shards[k].shape[0] // 2
        one = self.places[k].at[self.core, self.z, 1 - self.y, self.x, 0:part]
        two = self.places[k].at[self.core, self.z, self.y, 1 - self.x, part : 2 * part]
        return [self._remote(k, 5, one, one, self.across), self._remote(k, 6, two, two, self.down)]

    def far(self, k, i):
        block = self.places[k].at[self.core, self.z, i // 3]
        return [self._remote(k + i // 3, i % 3, block, block, self.along[i % 3])]

    def start(self, stage, k, *more):
        if 0 <= k < self.count and (more or k != self.count - 1 or stage in self.odd):
            for copy in stage(k, *more):
                copy.start()

    def wait(self, stage, k, *more):
        if 0 <= k < self.count and (more or k != self.count - 1 or stage in self.odd):
            for copy in stage(k, *more):
                copy.wait()

    @property
    def odd(self):
        return (self.near, self.near_corner)

    def last(self, step):
        k = self.count - 1
        if step == 0:
            self.start(self.near, k)
        if step == 1:
            self.wait(self.near, k)
            self.start(self.near_corner, k)
        if step == 2:
            self.wait(self.near_corner, k)
        if 2 <= step < 8:
            self.start(self.far, k, step - 2)
        if step == 9:
            for i in range(6):
                self.wait(self.far, k, i)
            self.twin(k)[0].start()
        if step == 20:
            self.twin(k)[0].wait()

    def tick(self, k, twin=True):
        self.last(k - 3)
        self.wait(self.plane, k)
        self.start(self.corner, k)
        self.wait(self.line, k + 2)
        self.start(self.plane, k + 2)
        self.start(self.line, k + 4)
        if twin:
            self.wait(self.corner, k - 1)
            self.start(self.twin, k - 1)


def _if(condition, action):
    if isinstance(condition, bool):
        if condition:
            action()
    else:
        pl.when(condition)(action)


class Reduce:
    def __init__(self, acc, out, x_one, y_one, x_two, y_two, from_z, send_sem, recv_sem):
        self.z, self.y, self.x, self.core = _coords()
        self.along, self.across, self.down, self.sibling = _peers()
        self.acc, self.out = acc, out
        self.x_one, self.y_one, self.x_two, self.y_two, self.from_z = x_one, y_one, x_two, y_two, from_z
        self.send_sem, self.recv_sem = send_sem, recv_sem

    def _remote(self, k, slot, src, dst, peer):
        return pltpu.make_async_remote_copy(
            src_ref=src,
            dst_ref=dst,
            send_sem=self.send_sem.at[k, slot],
            recv_sem=self.recv_sem.at[k, slot],
            device_id=peer,
            device_id_type=MESH,
        )

    def corner(self, k):
        block = self.acc(k).at[:, 1 - self.y, 1 - self.x]
        part = block.shape[1] // 2
        return [
            self._remote(k, 0, block.at[:, 0:part], self.x_one.at[k], self.across),
            self._remote(k, 1, block.at[:, part : 2 * part], self.y_one.at[k], self.down),
        ]

    def plane(self, k):
        acc = self.acc(k)
        return [
            self._remote(k, 2, acc.at[:, self.y, 1 - self.x], self.x_two.at[k], self.across),
            self._remote(k, 3, acc.at[:, 1 - self.y, self.x], self.y_two.at[k], self.down),
        ]

    def line(self, k):
        acc = self.acc(k)
        return [
            self._remote(k, 4 + j, acc.at[(self.z + j + 1) % 4, self.y, self.x], self.from_z.at[k, j], self.along[j])
            for j in range(3)
        ]

    @staticmethod
    def start(copies):
        for copy in copies:
            copy.start()

    @staticmethod
    def wait(copies):
        for copy in copies:
            copy.wait()

    def after_corner(self, k):
        acc, y, x = self.acc(k), self.y, self.x
        part = acc.shape[3] // 2
        self.wait(self.corner(k))
        one = acc.at[:, 1 - y, x, 0:part]
        two = acc.at[:, y, 1 - x, part : 2 * part]
        one[...] = _add(one[...], self.x_one[k])
        two[...] = _add(two[...], self.y_one[k])
        self.start(self.plane(k))

    def after_plane(self, k):
        acc = self.acc(k)
        self.wait(self.plane(k))
        here = acc.at[:, self.y, self.x]
        here[...] = _add(here[...], self.x_two[k], self.y_two[k])
        self.start(self.line(k))

    def after_line(self, k):
        self.wait(self.line(k))
        total = self.acc(k)[self.z, self.y, self.x].astype(self.out.dtype)
        for j in range(3):
            total = total + self.from_z[k, j].astype(self.out.dtype)
        self.out[k] = total


def _add(first, *others):
    if len(others) == 1:
        return first + others[0]
    total = first.astype(jnp.float32)
    for other in others:
        total = total + other.astype(jnp.float32)
    return total.astype(first.dtype)


def _combine(mine, other):
    @pl.loop(0, mine.shape[0])
    def _(i):
        for j in range(2):
            mine[i, j] = _add(mine[i, j], other[i, j])


EARLY = 2
ATTEND_SITES = 3
ATTEND_TICKS = {4: 1, 5: 3, 7: 9}
FEED_TICKS = {9: 0, 10: 1, 11: 2, 12: 3, 13: 4, 14: 6}


def front_kernel(
    prefix, wq_in, wk_in, wv_in, wo_in, up_in, down_in, vec, xin, gin,
    full, fullo, qkv, mixed_out, probs_out, normed_out, x_out, lines, layer_out, gres_out, low_out, sums, gown, grecv, gbias, early_out,
    vfull, x, grad, second, residual, weights, ubias,
    ssem, rsem, lsem, vs, vr, vl, ws, wr, wl, wsem, osem, fs, fr, fl, es, er, el,
    racc, rtheirs, x_one, y_one, x_two, y_two, from_z, rs, rr, rl,
):
    f32, bf16 = jnp.float32, jnp.bfloat16
    seq_len, model = x.shape
    half = seq_len // 2
    block = 128

    cols = wq_in.shape[1]
    shards = [w.at[:, sub * WIDE : (sub + 1) * WIDE] for sub in range(2) for w in (wq_in, wk_in, wv_in)] + [wo_in]
    places = [full.at[k] for k in range(6)] + [fullo]
    for piece in range(weights.shape[0] // 2):
        shards += [w.at[:, piece * cols : (piece + 1) * cols] for w in (up_in, down_in)]
        places += [weights.at[2 * piece], weights.at[2 * piece + 1]]
    early = len(shards) - weights.shape[0]
    gather = Gather(shards, places, ssem, rsem, lsem)
    reduce = Reduce(lambda k: racc.at[k], early_out, x_one, y_one, x_two, y_two, from_z, rs, rr)
    z, y, xx, core = gather.z, gather.y, gather.x, gather.core
    along, across, down, sibling = gather.along, gather.across, gather.down, gather.sibling
    _greet(along + [across, down, sibling])

    gather.start(gather.line, 0)
    vown = vfull.at[z, y, xx, core]
    vline = [_local(vec, vown, vl.at[0])] + [_send(vec, vown, vs.at[j], vr.at[j], along[j]) for j in range(3)]
    for k in (1, 2, 3):
        gather.start(gather.line, k)
    mine = pl.ds(pl.multiple_of(core * half, half), half)
    swaps = []
    for i, (part, whole) in enumerate(((xin, x), (gin, grad))):
        swaps.append(_local(part.at[core], whole.at[mine], wl.at[i]))
        swaps.append(_send(part.at[1 - core], whole.at[mine], ws.at[i], wr.at[i], sibling))
    gather.wait(gather.line, 0)
    gather.start(gather.plane, 0)
    for s in vline:
        s.wait()
    vblock = vfull.at[:, y, xx, core]
    vone = [_send(vblock, vblock, vs.at[3], vr.at[3], across), _send(vblock, vblock, vs.at[4], vr.at[4], down)]
    gather.wait(gather.line, 1)
    gather.start(gather.plane, 1)
    gather.tick(0)
    for s in vone:
        s.wait()
    vblock = vfull.at[:, 1 - y, xx, core]
    vtwo = _send(vblock, vblock, vs.at[5], vr.at[5], across)
    gather.tick(1)
    vtwo.wait()
    vblock = vfull.at[:, :, :, core]
    vthree = _send(vblock, vblock, vs.at[6], vr.at[6], sibling)
    for s in swaps:
        s.wait()
    saved = [_local(x, x_out, osem.at[0])]
    gather.tick(2)
    vthree.wait()
    for zi in range(4):
        for yi in range(2):
            at = (zi * 2 + yi) * 128
            group = vfull[zi, yi, 0, 0] + vfull[zi, yi, 0, 1] + vfull[zi, yi, 1, 0] + vfull[zi, yi, 1, 1]
            lines[:, at : at + 128] = group[0:8]
            for xi in range(2):
                for ci in range(2):
                    i = ((zi * 2 + yi) * 2 + xi) * 2 + ci
                    piece = 2 * ((i % 16) // 4) + i // 16
                    ubias[piece, 0:1, (i % 4) * 128 : (i % 4) * 128 + 128] = vfull[zi, yi, xi, ci, 8:9]

    def attention(normed, wblk, stage, mixed, wout, probs):
        @pl.loop(0, seq_len // block)
        def _(i):
            rows = pl.ds(pl.multiple_of(i * block, block), block)
            scaled, _ = _normal(x[rows].astype(f32))
            normed[rows] = (scaled * lines[0:1] + lines[1:2]).astype(bf16)

        gather.wait(gather.corner, 2)
        gather.start(gather.twin, 2)
        gather.tick(3, twin=False)
        keep = _local(normed, normed_out, osem.at[1])

        def side_of(pair):
            return (pair + core) % 2

        def load(pair):
            return [
                pltpu.make_async_copy(full.at[3 * (pair // 2) + i, side_of(pair)], wblk.at[pair % 2, i], wsem.at[pair % 2, i])
                for i in range(3)
            ]

        def store(pair):
            slot = pair % 2
            columns = pl.ds(pl.multiple_of((pair // 2) * WIDE, WIDE), WIDE)
            copies = [
                pltpu.make_async_copy(stage.at[slot, i], qkv.at[i, side_of(pair), :, columns], wsem.at[slot, 3 + i])
                for i in range(3)
            ]
            heads = pl.ds((side_of(pair) * 2 + pair // 2) * 2, 2)
            return copies + [pltpu.make_async_copy(probs.at[slot], probs_out.at[heads], wsem.at[slot, 6])]

        for c in load(0):
            c.start()

        def ticks(site, pair):
            for k, at in ATTEND_TICKS.items():
                if at % ATTEND_SITES == site:

                    @pl.when(pair == at // ATTEND_SITES)
                    def _(k=k):
                        gather.tick(k)

        @pl.loop(0, 4)
        def _(pair):
            slot = pair % 2
            for c in load(pair):
                c.wait()

            @pl.when(pair >= 2)
            def _():
                for c in store(pair - 2):
                    c.wait()

            ticks(0, pair)
            lanes = pl.ds(pl.multiple_of((side_of(pair) * 2 + pair // 2) * WIDE, WIDE), WIDE)
            wq, wk, wv = (wblk[slot, i].reshape(model, WIDE) for i in range(3))
            stage[slot, 0] = (_dot(normed[...], wq, NN) + lines[2:3, lanes]).astype(bf16)
            stage[slot, 1] = _dot(normed[...], wk, NN).astype(bf16)
            stage[slot, 2] = (_dot(normed[...], wv, NN) + lines[3:4, lanes]).astype(bf16)
            ticks(1, pair)
            for sub in range(2):

                @pl.when(pair == 2 * sub)
                def _(sub=sub):
                    for k in range(3 * sub, 3 * sub + 3):
                        gather.wait(gather.twin, k)
                    for c in load(2 * sub + 1):
                        c.start()

            step = 256
            factor = LOG2E / math.sqrt(HEAD_DIM)
            prefix_len = prefix[core]
            for head in range(WIDE // HEAD_DIM):
                part = slice(head * HEAD_DIM, (head + 1) * HEAD_DIM)
                for start, stop in _spans(seq_len, LONGEST, step):
                    scores = _dot(stage[slot, 1, :stop, part], stage[slot, 0, start : start + step, part], NT)
                    keys = lax.broadcasted_iota(jnp.int32, scores.shape, 0)
                    queries = lax.broadcasted_iota(jnp.int32, scores.shape, 1) + start
                    scores = jnp.where((keys <= queries) | (keys < prefix_len), scores, -jnp.inf)
                    peak = jnp.max(scores, axis=0, keepdims=True)
                    raw = jnp.exp2((scores - peak) * factor)
                    total = jnp.sum(raw, axis=0, keepdims=True)
                    share = (raw * (1.0 / total)).astype(bf16)
                    probs[slot, head, :stop, start : start + step] = share
                    to = pl.ds(pl.multiple_of((pair // 2) * WIDE + head * HEAD_DIM, HEAD_DIM), HEAD_DIM)
                    mixed[side_of(pair), start : start + step, to] = _dot(
                        share, stage[slot, 2, :stop, part], TN
                    ).astype(bf16)
                if head == 0:
                    ticks(2, pair)
            for c in store(pair):
                c.start()

            @pl.when(pair == 1)
            def _():
                gather.tick(6)
                for c in load(2):
                    c.start()

        gather.wait(gather.twin, 6)
        fetch = _local(fullo, wout, osem.at[3])
        done = _local(mixed, mixed_out, osem.at[2])
        fetch.wait()
        weight = [wout[c].reshape(model, seq_len // 2) for c in range(2)]
        step = 256

        @pl.loop(0, seq_len // step)
        def _(i):
            rows = pl.ds(pl.multiple_of(i * step, step), step)
            branch = _dot(mixed[0, rows], weight[0], NT) + _dot(mixed[1, rows], weight[1], NT)
            total = x[rows].astype(f32) + branch + lines[4:5]
            residual[rows] = total
            scaled, _ = _normal(total)
            second[rows] = (scaled * lines[5:6] + lines[6:7]).astype(bf16)

        gather.tick(8)
        for pair in (2, 3):
            for c in store(pair):
                c.wait()
        done.wait()
        keep.wait()

    pl.run_scoped(
        attention,
        pltpu.VMEM((seq_len, model), bf16),
        pltpu.VMEM((2, 3, 4, 2, 2, 64, WIDE), bf16),
        pltpu.VMEM((2, 3, seq_len, WIDE), bf16),
        pltpu.VMEM((2, seq_len, model // 2), bf16),
        pltpu.VMEM((2, 4, 2, 2, 64, model // 2), bf16),
        pltpu.VMEM((2, 2, seq_len, seq_len), bf16),
    )

    def feed(layer, gres, stage, hid, gpre):
        pieces = weights.shape[0]

        @pl.loop(0, seq_len // block)
        def _(i):
            rows = pl.ds(pl.multiple_of(i * block, block), block)
            layer[rows] = residual[rows] + lines[7:8]
            gres[rows] = jnp.zeros((block, model), f32)

        def away(piece):
            return [
                pltpu.make_async_remote_copy(
                    src_ref=stage.at[1, i],
                    dst_ref=grecv.at[2 * piece + i],
                    send_sem=fs.at[piece, i],
                    recv_sem=fr.at[piece, i],
                    device_id=sibling,
                    device_id_type=MESH,
                )
                for i in range(2)
            ]

        def stay(piece):
            return [pltpu.make_async_copy(stage.at[0, i], gown.at[2 * piece + i], fl.at[i]) for i in range(2)]

        def bring(k):
            return [
                pltpu.make_async_copy(gown.at[k], racc.at[k], rl.at[k, 0]),
                pltpu.make_async_copy(grecv.at[k], rtheirs.at[k], rl.at[k, 1]),
            ]

        @pl.loop(0, pieces)
        def _(t):
            piece, turn = t // 2, t % 2
            side = (t + core) % 2
            for k, at in FEED_TICKS.items():

                @pl.when(t == at)
                def _(k=k):
                    gather.tick(k)

            for p in range(pieces // 2):

                @pl.when(t == 2 * p + 1)
                def _(p=p):
                    gather.wait(gather.twin, early + 2 * p)
                    if p < pieces // 2 - 1:
                        gather.wait(gather.twin, early + 2 * p + 1)
                    else:
                        gather.last(20)

            @pl.when(t == pieces - 3)
            def _():
                for c in away(0):
                    c.wait_recv()
                reduce.start(bring(0) + bring(1))

            @pl.when(t == pieces - 2)
            def _():
                for k in range(EARLY):
                    reduce.wait(bring(k))
                    _combine(racc.at[k], rtheirs.at[k])
                    reduce.start(reduce.corner(k))

            @pl.when(t == pieces - 1)
            def _():
                for k in range(EARLY):
                    reduce.after_corner(k)

            @pl.when((t >= 2) & (turn == 1))
            def _():
                for c in away(piece - 1):
                    c.wait_send()

            @pl.when((t >= 2) & (turn == 0))
            def _():
                for c in stay(piece - 1):
                    c.wait()

            up = weights[2 * piece, side].reshape(model, model // 2)
            lower = weights[2 * piece + 1, side].reshape(model, model // 2)
            line = 2 * piece + side
            pre = _dot(second[...], up, NN) + ubias[line]
            phi = 0.5 * (1.0 + lax.erf(pre * (1.0 / math.sqrt(2.0))))
            density = jnp.exp2(pre * pre * (-0.5 * LOG2E)) * (1.0 / math.sqrt(2.0 * math.pi))
            hid[...] = (pre * phi).astype(bf16)
            slope = phi + pre * density
            back = (_dot(grad[...], lower, NN) * slope).astype(bf16)
            gpre[...] = back
            gbias[line] = jnp.sum(back.astype(f32), axis=0, keepdims=True)
            layer[...] += _dot(hid[...], lower, NT)
            gres[...] += _dot(gpre[...], up, NT)
            blocks = stage.shape[2:]
            stage[turn, 0] = _dot(second[...], gpre[...], TN).astype(bf16).reshape(blocks)
            stage[turn, 1] = _dot(grad[...], hid[...], TN).astype(bf16).reshape(blocks)

            @pl.when(turn == 1)
            def _():
                for c in away(piece):
                    c.start()

            @pl.when(turn == 0)
            def _():
                for c in stay(piece):
                    c.start()

        theirs = pl.ds(pl.multiple_of((1 - core) * half, half), half)
        final = [
            _local(layer.at[mine], layer_out.at[core], el.at[0]),
            _send(layer.at[theirs], layer_out.at[core], es.at[0], er.at[0], sibling),
        ]
        for k in range(EARLY):
            reduce.after_plane(k)
        sums[...] = jnp.zeros_like(sums)

        @pl.loop(0, seq_len // block)
        def _(i):
            rows = pl.ds(pl.multiple_of(i * block, block), block)
            scaled, inverse = _normal(residual[rows])
            grow = gres[rows]
            upstream = grad[rows].astype(f32)
            weighted = grow * lines[5:6]
            mean_plain = jnp.mean(weighted, axis=-1, keepdims=True)
            mean_scaled = jnp.mean(weighted * scaled, axis=-1, keepdims=True)
            total = upstream + inverse * (weighted - mean_plain - scaled * mean_scaled)
            gres[rows] = total
            second[rows] = total.astype(bf16)
            sums[0:1] += jnp.sum(grow * scaled, axis=0, keepdims=True)
            sums[1:2] += jnp.sum(grow, axis=0, keepdims=True)
            sums[2:3] += jnp.sum(total, axis=0, keepdims=True)
            sums[3:4] += jnp.sum(upstream, axis=0, keepdims=True)

        final.append(_local(gres, gres_out, el.at[1]))
        final.append(_local(second, low_out, el.at[2]))
        last = pieces // 2 - 1
        for c in away(last):
            c.wait_send()
        for c in stay(last):
            c.wait()
        for p in range(1, pieces // 2):
            for c in away(p):
                c.wait_recv()
        for k in range(EARLY):
            reduce.after_line(k)
        for c in final:
            c.wait()

    pl.run_scoped(
        feed,
        pltpu.VMEM((seq_len, model), f32),
        pltpu.VMEM((seq_len, model), f32),
        pltpu.VMEM((2, 2, 4, 2, 2, model // 16, model // 2), bf16),
        pltpu.VMEM((seq_len, model // 2), bf16),
        pltpu.VMEM((seq_len, model // 2), bf16),
    )
    for s in saved:
        s.wait()


def front(prefix_len, wq, wk, wv, wo, up, down, vec, xin, gin):
    rows, cols = wq.shape
    half, model = xin.shape[1:]
    seq_len = 2 * half
    pieces = 2 * (up.shape[1] // cols)
    chunks = 7 + pieces
    bf16, f32 = jnp.bfloat16, jnp.float32
    hbm = pl.BlockSpec(memory_space=pltpu.HBM)
    vmem = pl.BlockSpec(memory_space=pltpu.VMEM)
    dma = pltpu.SemaphoreType.DMA

    def shape(dims, dtype):
        return jax.ShapeDtypeStruct(dims, dtype)

    heads = model // HEAD_DIM
    return pl.pallas_call(
        front_kernel,
        out_shape=(
            shape((6, 2, 4, 2, 2, rows, WIDE), bf16),
            shape((2, 4, 2, 2, rows, cols), bf16),
            shape((3, 2, seq_len, cols), bf16),
            shape((2, seq_len, cols), bf16),
            shape((heads, seq_len, seq_len), bf16),
            shape((seq_len, model), bf16),
            shape((seq_len, model), bf16),
            shape((8, model), f32),
            shape((2, half, model), f32),
            shape((seq_len, model), f32),
            shape((seq_len, model), bf16),
            shape((8, model), f32),
            shape((pieces, 4, 2, 2, rows, cols), bf16),
            shape((pieces, 4, 2, 2, rows, cols), bf16),
            shape((pieces, 1, cols), f32),
            shape((EARLY, rows, cols), f32),
        ),
        in_specs=[pl.BlockSpec(memory_space=pltpu.SMEM)] + [vmem] * 7 + [hbm, hbm],
        out_specs=(hbm, hbm, hbm, hbm, hbm, hbm, hbm, vmem, hbm, hbm, hbm, vmem, hbm, hbm, vmem, vmem),
        scratch_shapes=[
            pltpu.VMEM((4, 2, 2, 2) + vec.shape, f32),
            pltpu.VMEM((seq_len, model), bf16),
            pltpu.VMEM((seq_len, model), bf16),
            pltpu.VMEM((seq_len, model), bf16),
            pltpu.VMEM((seq_len, model), f32),
            pltpu.VMEM((pieces, 2, 4, 2, 2, rows, cols), bf16),
            pltpu.VMEM((pieces, 1, cols), f32),
            dma((chunks + 1, 8)),
            dma((chunks + 1, 8)),
            dma((chunks,)),
            dma((7,)),
            dma((7,)),
            dma((1,)),
            dma((2,)),
            dma((2,)),
            dma((2,)),
            dma((2, 7)),
            dma((4,)),
            dma((pieces // 2, 2)),
            dma((pieces // 2, 2)),
            dma((2,)),
            dma((1,)),
            dma((1,)),
            dma((3,)),
            pltpu.VMEM((EARLY, 4, 2, 2, rows, cols), bf16),
            pltpu.VMEM((EARLY, 4, 2, 2, rows, cols), bf16),
            pltpu.VMEM((EARLY, 4, rows // 2, cols), bf16),
            pltpu.VMEM((EARLY, 4, rows // 2, cols), bf16),
            pltpu.VMEM((EARLY, 4, rows, cols), bf16),
            pltpu.VMEM((EARLY, 4, rows, cols), bf16),
            pltpu.VMEM((EARLY, 3, rows, cols), bf16),
            dma((EARLY, 7)),
            dma((EARLY, 7)),
            dma((EARLY, 2)),
        ],
        compiler_params=pltpu.CompilerParams(
            collective_id=0, has_side_effects=True, vmem_limit_bytes=63 * MIB
        ),
    )(prefix_len, wq, wk, wv, wo, up, down, vec, xin, gin)


RING = 4


def back_kernel(
    lines, sums_two, gbias, qkv, mixed_in, probs_in, full, fullo, low_in, normed_in, x_in, gres_in, gown, grecv,
    out, vout, iout, qrecv,
    ring, theirs_in, gbuf, x_one, y_one, x_two, y_two, from_z,
    vacc, v_s, vx_one, vx_two, vy_two, v_z,
    low, normed, ingrad, sums, bsums,
    ssem, rsem, lsem, qs, qr, vs, vr, bsem, msem, es, er,
):
    f32, bf16 = jnp.float32, jnp.bfloat16
    seq_len, model = low.shape
    half, block, step = seq_len // 2, 128, 256
    feeds = gown.shape[0] - EARLY
    count = out.shape[0]
    scale = 1.0 / math.sqrt(HEAD_DIM)

    own = gbuf.at[1]

    def acc(k):
        return own.at[k - feeds] if isinstance(k, int) and k >= feeds else ring.at[k % RING]

    reduce = Reduce(acc, out, x_one, y_one, x_two, y_two, from_z, ssem, rsem)
    z, y, x, core = reduce.z, reduce.y, reduce.x, reduce.core
    along, across, down, sibling = reduce.along, reduce.across, reduce.down, reduce.sibling

    def load(k):
        if isinstance(k, int) and k >= feeds:
            return [pltpu.make_async_copy(qrecv.at[k - feeds], theirs_in.at[k % 2], lsem.at[k % 2, 1])]
        return [
            pltpu.make_async_copy(gown.at[EARLY + k], ring.at[k % RING], lsem.at[k % 2, 0]),
            pltpu.make_async_copy(grecv.at[EARLY + k], theirs_in.at[k % 2], lsem.at[k % 2, 1]),
        ]

    def begin(k):
        reduce.wait(load(k))
        _combine(acc(k), theirs_in.at[k % 2])
        reduce.start(reduce.corner(k))

    def tick(k):
        if not isinstance(k, int) or k < count:
            begin(k)
        _if((k >= 1) & (k - 1 < count), lambda: reduce.after_corner(k - 1))
        _if((k >= 2) & (k - 2 < count), lambda: reduce.after_plane(k - 2))
        _if((k >= 3) & (k - 3 < count), lambda: reduce.after_line(k - 3))

    reduce.start(load(0))
    start = [_local(low_in, low, msem.at[0]), _local(normed_in, normed, msem.at[1])]
    _greet(along + [across, down, sibling])

    def away(sub, i):
        unit = sub * 2 + i
        return pltpu.make_async_remote_copy(
            src_ref=gbuf.at[0, unit],
            dst_ref=qrecv.at[unit],
            send_sem=qs.at[unit],
            recv_sem=qr.at[unit],
            device_id=sibling,
            device_id_type=MESH,
        )

    def landed(unit):
        away(unit // 2, unit % 2).wait_recv()

    def retreat(heads_in, probs, wblk, dq, dk, dv, dmix):
        def fetch(i):
            turn, sub = i // 2, i % 2
            side = (turn + 1 + core) % 2
            columns = pl.ds(pl.multiple_of(sub * WIDE, WIDE), WIDE)
            slot = i % 2
            copies = [
                pltpu.make_async_copy(qkv.at[n, side, :, columns], heads_in.at[slot, n], bsem.at[slot, n])
                for n in range(3)
            ]
            copies.append(pltpu.make_async_copy(mixed_in.at[side, :, columns], heads_in.at[slot, 3], bsem.at[slot, 3]))
            copies += [
                pltpu.make_async_copy(full.at[3 * sub + n, side], wblk.at[slot, n], bsem.at[slot, 4 + n])
                for n in range(3)
            ]
            copies.append(
                pltpu.make_async_copy(fullo.at[side, :, :, :, :, columns], wblk.at[slot, 3], bsem.at[slot, 7])
            )
            heads = pl.ds((side * 2 + sub) * 2, 2)
            copies.append(pltpu.make_async_copy(probs_in.at[heads], probs.at[slot], bsem.at[slot, 8]))
            return copies

        reduce.start(fetch(0))

        @pl.loop(0, seq_len // block)
        def _(i):
            ingrad[pl.ds(pl.multiple_of(i * block, block), block)] = jnp.zeros((block, model), f32)

        reduce.wait(start)

        @pl.loop(0, 4)
        def _(i):
            turn, sub, slot = i // 2, i % 2, i % 2
            side = (turn + 1 + core) % 2
            reduce.wait(fetch(i))

            @pl.when(i < 3)
            def _():
                reduce.start(fetch(i + 1))

            columns = pl.ds(pl.multiple_of(sub * WIDE, WIDE), WIDE)

            def put(n, value):
                at = slice((n % 2) * WIDE, (n % 2 + 1) * WIDE)
                gbuf[turn, sub * 2 + n // 2, :, :, :, :, at] = value.astype(bf16).reshape(4, 2, 2, model // 16, WIDE)

            def tick_and_load(n):
                k = 2 * i + n

                @pl.when(k < feeds)
                def _():
                    tick(k)

                @pl.when(k + 1 < feeds)
                def _():
                    reduce.start(load(k + 1))

                @pl.when(k == feeds + n)
                def _():
                    if n == 0:
                        for u in range(2):
                            landed(u)
                            reduce.start(load(feeds + u))
                    tick(feeds + n)

            tick_and_load(0)
            wq, wk, wv, wo = (wblk[slot, n].reshape(model, WIDE) for n in range(4))
            dmix[...] = _dot(low[...], wo, NN).astype(bf16)
            put(0, _dot(low[...], heads_in[slot, 3], TN))
            parts = [slice(h * HEAD_DIM, (h + 1) * HEAD_DIM) for h in range(WIDE // HEAD_DIM)]
            spans = _spans(seq_len, LONGEST, step)
            bands = [(0, LONGEST)] + [(first, first + step) for first in range(LONGEST, seq_len, step)]
            for head, part in enumerate(parts):
                for low_key, high_key in bands:
                    dv[low_key:high_key, part] = _dot(
                        probs[slot, head, low_key:high_key, low_key:], dmix[low_key:, part], NN
                    ).astype(bf16)
            for head, part in enumerate(parts):
                for first, stop in spans:
                    block_at = (slot, head, slice(0, stop), slice(first, first + step))
                    weights = probs[block_at].astype(f32)
                    dprobs = _dot(heads_in[slot, 2, :stop, part], dmix[first : first + step, part], NT)
                    inner = jnp.sum(weights * dprobs, axis=0, keepdims=True)
                    probs[block_at] = (weights * (dprobs - inner)).astype(bf16)
            tick_and_load(1)
            for head, part in enumerate(parts):
                for low_key, high_key in bands:
                    dk[low_key:high_key, part] = (
                        _dot(probs[slot, head, low_key:high_key, low_key:], heads_in[slot, 0, low_key:, part], NN)
                        * scale
                    ).astype(bf16)
                for first, last in bands:
                    dq[first:last, part] = (
                        _dot(probs[slot, head, :last, first:last], heads_in[slot, 1, :last, part], TN) * scale
                    ).astype(bf16)
            put(1, _dot(normed[...], dq[...], TN))
            put(2, _dot(normed[...], dk[...], TN))
            put(3, _dot(normed[...], dv[...], TN))
            ingrad[...] += _dot(dq[...], wq, NT) + _dot(dk[...], wk, NT) + _dot(dv[...], wv, NT)

            @pl.when(turn == 0)
            def _():
                for n in range(2):
                    away(sub, n).start()

            at = side * 2 + sub
            bsums[at, 0:1] = jnp.sum(dq[...].astype(f32), axis=0, keepdims=True)
            bsums[at, 1:2] = jnp.sum(dv[...].astype(f32), axis=0, keepdims=True)

        for sub in range(2):
            for n in range(2):
                away(sub, n).wait_send()

    pl.run_scoped(
        retreat,
        pltpu.VMEM((2, 4, seq_len, WIDE), bf16),
        pltpu.VMEM((2, 2, seq_len, seq_len), bf16),
        pltpu.VMEM((2, 4, 4, 2, 2, model // 16, WIDE), bf16),
        pltpu.VMEM((seq_len, WIDE), bf16),
        pltpu.VMEM((seq_len, WIDE), bf16),
        pltpu.VMEM((seq_len, WIDE), bf16),
        pltpu.VMEM((seq_len, WIDE), bf16),
    )

    def finish(gres, xs):
        bring = [_local(gres_in, gres, msem.at[0]), _local(x_in, xs, msem.at[1])]
        for unit in (2, 3):
            landed(unit)
            reduce.start(load(feeds + unit))
        begin(feeds + 2)
        begin(feeds + 3)
        reduce.after_corner(feeds + 1)
        reduce.after_plane(feeds)
        reduce.after_line(feeds - 1)
        reduce.after_corner(feeds + 2)
        reduce.after_corner(feeds + 3)
        reduce.wait(bring)
        sums[...] = jnp.zeros_like(sums)

        @pl.loop(0, seq_len // block)
        def _(i):
            rows = pl.ds(pl.multiple_of(i * block, block), block)
            scaled, inverse = _normal(xs[rows].astype(f32))
            grow = ingrad[rows]
            weighted = grow * lines[0:1]
            mean_plain = jnp.mean(weighted, axis=-1, keepdims=True)
            mean_scaled = jnp.mean(weighted * scaled, axis=-1, keepdims=True)
            ingrad[rows] = gres[rows] + inverse * (weighted - mean_plain - scaled * mean_scaled)
            sums[0:1] += jnp.sum(grow * scaled, axis=0, keepdims=True)
            sums[1:2] += jnp.sum(grow, axis=0, keepdims=True)

    pl.run_scoped(finish, pltpu.VMEM((seq_len, model), f32), pltpu.VMEM((seq_len, model), bf16))
    mine = pl.ds(pl.multiple_of(core * half, half), half)
    theirs = pl.ds(pl.multiple_of((1 - core) * half, half), half)
    final = [
        _local(ingrad.at[mine], iout.at[core], msem.at[0]),
        _send(ingrad.at[theirs], iout.at[core], es.at[0], er.at[0], sibling),
    ]
    for pair in range(4):
        at = slice(pair * WIDE, (pair + 1) * WIDE)
        sums[2:4, at] = bsums[pair, 0:2]
    sums[4:5] = sums_two[2:3]
    sums[5:7] = sums_two[0:2]
    sums[7:8] = sums_two[3:4]
    vacc[...] = jnp.zeros_like(vacc)
    for zi in range(4):
        for yi in range(2):
            at = (zi * 2 + yi) * 128
            for xi in range(2):
                for ci in range(2):
                    i = ((zi * 2 + yi) * 2 + xi) * 2 + ci
                    piece = 2 * ((i % 16) // 4) + i // 16
                    vacc[ci, zi, yi, xi, 0:8] = sums[:, at : at + 128]
                    vacc[ci, zi, yi, xi, 8:9] = gbias[piece, 0:1, (i % 4) * 128 : (i % 4) * 128 + 128]
    vzero = _send(vacc.at[1 - core], v_s, vs.at[0], vr.at[0], sibling)
    reduce.after_plane(feeds + 1)
    reduce.after_line(feeds)
    vzero.wait()
    vmine = vacc.at[core]
    vmine[...] = vmine[...] + v_s[...]
    vone = _send(vmine.at[:, 1 - y, 1 - x], vx_one, vs.at[1], vr.at[1], across)
    reduce.after_plane(feeds + 2)
    vone.wait()
    vmine[:, 1 - y, x] = vmine[:, 1 - y, x] + vx_one[...]
    vtwo = [
        _send(vmine.at[:, y, 1 - x], vx_two, vs.at[2], vr.at[2], across),
        _send(vmine.at[:, 1 - y, x], vy_two, vs.at[3], vr.at[3], down),
    ]
    reduce.after_plane(feeds + 3)
    reduce.after_line(feeds + 1)
    reduce.wait(vtwo)
    vmine[:, y, x] = vmine[:, y, x] + vx_two[...] + vy_two[...]
    vthree = [
        _send(vmine.at[(z + j + 1) % 4, y, x], v_z.at[j], vs.at[4 + j], vr.at[4 + j], along[j]) for j in range(3)
    ]
    reduce.after_line(feeds + 2)
    reduce.after_line(feeds + 3)
    reduce.wait(vthree)
    vout[...] = vmine[z, y, x] + v_z[0] + v_z[1] + v_z[2]
    reduce.wait(final)


def back(lines, sums_two, gbias, qkv, mixed, probs, full, fullo, low, normed, x, gres, gown, grecv):
    count = gown.shape[0] - EARLY + 4
    seq_len, model = x.shape
    rows, cols = gown.shape[-2:]
    half = seq_len // 2
    bf16, f32 = jnp.bfloat16, jnp.float32
    hbm = pl.BlockSpec(memory_space=pltpu.HBM)
    vmem = pl.BlockSpec(memory_space=pltpu.VMEM)
    dma = pltpu.SemaphoreType.DMA
    small = (16, 128)
    return pl.pallas_call(
        back_kernel,
        out_shape=(
            jax.ShapeDtypeStruct((count, rows, cols), f32),
            jax.ShapeDtypeStruct(small, f32),
            jax.ShapeDtypeStruct((2, half, model), f32),
            jax.ShapeDtypeStruct((4, 4, 2, 2, rows, cols), bf16),
        ),
        in_specs=[vmem] * 3 + [hbm] * 11,
        out_specs=(vmem, vmem, hbm, hbm),
        scratch_shapes=[
            pltpu.VMEM((RING, 4, 2, 2, rows, cols), bf16),
            pltpu.VMEM((2, 4, 2, 2, rows, cols), bf16),
            pltpu.VMEM((2, 4, 4, 2, 2, rows, cols), bf16),
            pltpu.VMEM((count, 4, rows // 2, cols), bf16),
            pltpu.VMEM((count, 4, rows // 2, cols), bf16),
            pltpu.VMEM((count, 4, rows, cols), bf16),
            pltpu.VMEM((count, 4, rows, cols), bf16),
            pltpu.VMEM((count, 3, rows, cols), bf16),
            pltpu.VMEM((2, 4, 2, 2) + small, f32),
            pltpu.VMEM((4, 2, 2) + small, f32),
            pltpu.VMEM((4,) + small, f32),
            pltpu.VMEM((4,) + small, f32),
            pltpu.VMEM((4,) + small, f32),
            pltpu.VMEM((3,) + small, f32),
            pltpu.VMEM((seq_len, model), bf16),
            pltpu.VMEM((seq_len, model), bf16),
            pltpu.VMEM((seq_len, model), f32),
            pltpu.VMEM((8, model), f32),
            pltpu.VMEM((4, 8, WIDE), f32),
            dma((count, 7)),
            dma((count, 7)),
            dma((2, 2)),
            dma((4,)),
            dma((4,)),
            dma((7,)),
            dma((7,)),
            dma((2, 9)),
            dma((2,)),
            dma((1,)),
            dma((1,)),
        ],
        compiler_params=pltpu.CompilerParams(
            collective_id=1, has_side_effects=True, vmem_limit_bytes=63 * MIB
        ),
    )(lines, sums_two, gbias, qkv, mixed, probs, full, fullo, low, normed, x, gres, gown, grecv)


def finish_kernel(early, late, layer, ingrad, gq, gk, gv, go, up, down, layer_out, ingrad_out, held, sem):
    moves = []
    parts = held.shape[1]
    for n, (source, target) in enumerate(((layer, layer_out), (ingrad, ingrad_out))):
        for i in range(parts):
            moves.append((_local(source.at[i], held.at[n, i], sem.at[0, n, i]), held.at[n, i], target.at[i], (n, i)))
    stores = []
    for fetch, here, target, (n, i) in moves:
        fetch.wait()
        stores.append(_local(here, target, sem.at[1, n, i]))
    pieces = (early.shape[0] + late.shape[0] - 4) // 2
    cols = late.shape[2]
    units = [early.at[i] for i in range(early.shape[0])] + [late.at[i] for i in range(late.shape[0])]
    for piece in range(pieces):
        at = slice(piece * cols, (piece + 1) * cols)
        up[:, at] = units[2 * piece][...]
        down[:, at] = units[2 * piece + 1][...]
    for sub in range(2):
        at = slice(sub * WIDE, (sub + 1) * WIDE)
        first, second = units[2 * pieces + 2 * sub], units[2 * pieces + 2 * sub + 1]
        go[:, at] = first[:, 0:WIDE]
        gq[:, at] = first[:, WIDE : 2 * WIDE]
        gk[:, at] = second[:, 0:WIDE]
        gv[:, at] = second[:, WIDE : 2 * WIDE]
    for store in stores:
        store.wait()


def finish(early, late, layer, ingrad):
    rows, cols = late.shape[1:]
    wide = (early.shape[0] + late.shape[0] - 4) // 2 * cols
    vmem = pl.BlockSpec(memory_space=pltpu.VMEM)
    hbm = pl.BlockSpec(memory_space=pltpu.HBM)
    parts = (8, layer.shape[0] * layer.shape[1] // 8, layer.shape[2])
    whole = jax.ShapeDtypeStruct(parts, layer.dtype)
    shapes = ((rows, cols),) * 4 + ((rows, wide),) * 2
    return pl.pallas_call(
        finish_kernel,
        out_shape=tuple(jax.ShapeDtypeStruct(s, late.dtype) for s in shapes) + (whole, whole),
        in_specs=[vmem] * 2 + [hbm] * 2,
        out_specs=(vmem,) * 6 + (hbm,) * 2,
        scratch_shapes=[pltpu.VMEM((2,) + parts, layer.dtype), pltpu.SemaphoreType.DMA((2, 2, 8))],
        compiler_params=pltpu.CompilerParams(vmem_limit_bytes=63 * MIB),
    )(early, late, layer.reshape(parts), ingrad.reshape(parts))


def fast_body(
    inputs, prefix, ln1_gain, ln1_bias, query_weight, query_bias, key_weight, value_weight, value_bias,
    out_weight, out_bias, ln2_gain, ln2_bias, up_weight, up_bias, down_weight, down_bias, cotangent,
):
    core = lax.axis_index("tensor")
    half, model = inputs.shape[2], inputs.shape[3]
    rows, cols = query_weight.shape
    pieces = up_weight.shape[1] // cols

    small = jnp.stack([ln1_gain, ln1_bias, query_bias, value_bias, out_bias, ln2_gain, ln2_bias, down_bias])
    place = (lax.axis_index("dp") * 2 + core) % 4
    vec = jnp.pad(up_bias.reshape(1, 128), ((8, 7), (0, 0)))
    vec = lax.dynamic_update_slice(vec, small, (0, place * 32))
    (
        full, fullo, qkv, mixed, probs, normed, x, lines, layer_out, gres, low, sums_two, gown, grecv, gup_bias,
        early,
    ) = front(
        prefix.reshape(-1), query_weight, key_weight, value_weight, out_weight.T, up_weight, down_weight.T, vec,
        inputs[:, 0], cotangent[:, 0],
    )
    out, vout, input_grad, _ = back(
        lines, sums_two, gup_bias, qkv, mixed, probs, full, fullo, low, normed, x, gres,
        gown, grecv,
    )
    vectors = lax.dynamic_slice(vout, (0, place * 32), (8, 32))

    gq, gk, gv, gout, gup, gdown, layer_out, input_grad = finish(early, out, layer_out, input_grad)
    return (
        layer_out.reshape(2, 1, half, model),
        input_grad.reshape(2, 1, half, model),
        vectors[0],
        vectors[1],
        gq,
        vectors[2],
        gk,
        gv,
        vectors[3],
        gout.T,
        vectors[4],
        vectors[5],
        vectors[6],
        gup,
        vout[8],
        gdown.T,
        vectors[7],
    )


def solution(mesh):
    in_specs = (
        P(None, "dp", "tensor", None),
        P(None, "dp"),
        P(("dp", "tensor")),
        P(("dp", "tensor")),
        P("dp", "tensor"),
        P(("dp", "tensor")),
        P("dp", "tensor"),
        P("dp", "tensor"),
        P(("dp", "tensor")),
        P("tensor", "dp"),
        P(("dp", "tensor")),
        P(("dp", "tensor")),
        P(("dp", "tensor")),
        P("dp", "tensor"),
        P(("dp", "tensor")),
        P("tensor", "dp"),
        P(("dp", "tensor")),
        P(None, "dp", "tensor", None),
    )
    out_specs = (
        P(None, "dp", "tensor", None),
        P(None, "dp", "tensor", None),
        P(("dp", "tensor")),
        P(("dp", "tensor")),
        P("dp", "tensor"),
        P(("dp", "tensor")),
        P("dp", "tensor"),
        P("dp", "tensor"),
        P(("dp", "tensor")),
        P("tensor", "dp"),
        P(("dp", "tensor")),
        P(("dp", "tensor")),
        P(("dp", "tensor")),
        P("dp", "tensor"),
        P(("dp", "tensor")),
        P("tensor", "dp"),
        P(("dp", "tensor")),
    )
    sizes = (mesh.shape["dp"], mesh.shape["tensor"])
    chosen = fast_body if sizes == (16, 2) else body
    return jax.shard_map(chosen, mesh=mesh, in_specs=in_specs, out_specs=out_specs, check_vma=False)
```

```python
import math

import jax
import jax.numpy as jnp
from jax import lax
from jax.experimental import pallas as pl
from jax.experimental.pallas import tpu as pltpu
from jax.sharding import PartitionSpec as P

MESH = pl.DeviceIdType.MESH
LONGEST = 512

HEAD_DIM = 128
BLOCK = 512


EPSILON = 1e-05


def norm_forward(values, gain, shift):
    center = values - jnp.mean(values, axis=-1, keepdims=True)
    inverse = lax.rsqrt(jnp.mean(center * center, axis=-1, keepdims=True) + EPSILON)
    scaled = center * inverse
    return (scaled * gain + shift, scaled, inverse)


def norm_backward(grad_out, scaled, inverse, gain):
    weighted = grad_out * gain
    mean_plain = jnp.mean(weighted, axis=-1, keepdims=True)
    mean_scaled = jnp.mean(weighted * scaled, axis=-1, keepdims=True)
    return inverse * (weighted - mean_plain - scaled * mean_scaled)


def smooth_gate(values):
    return jax.nn.gelu(values, approximate=False)


def smooth_slope(values):
    normal_cdf = 0.5 * (1.0 + jax.scipy.special.erf(values / math.sqrt(2.0)))
    density = jnp.exp(-0.5 * values * values) / math.sqrt(2.0 * math.pi)
    return normal_cdf + values * density


def masked_scores(query_block, key_rows, start, prefix_len):
    scale = 1.0 / math.sqrt(key_rows.shape[2])
    scores = (
        jnp.einsum("qhd,khd->hqk", query_block, key_rows, preferred_element_type=jnp.float32)
        * scale
    )
    places = start + jnp.arange(query_block.shape[0], dtype=jnp.int32)
    columns = jnp.arange(key_rows.shape[0], dtype=jnp.int32)
    allowed = (columns[None, :] <= places[:, None]) | (columns[None, :] < prefix_len)
    return jnp.where(allowed[None], scores, -jnp.inf)


def attend_forward(queries, key_rows, value_rows, prefix_len):
    seq_len, heads_local, head_size = queries.shape
    count = seq_len // BLOCK

    def one_block(items):
        query_block, start = items
        scores = masked_scores(query_block, key_rows, start, prefix_len)
        peak = jnp.max(scores, axis=-1, keepdims=True)
        raw_weights = jnp.exp(scores - peak)
        totals = jnp.sum(raw_weights, axis=-1, keepdims=True)
        probs = (raw_weights / totals).astype(jnp.bfloat16)
        mixed = jnp.einsum("hqk,khd->qhd", probs, value_rows, preferred_element_type=jnp.float32)
        return (mixed.astype(jnp.bfloat16), (peak + jnp.log(totals))[..., 0])

    starts = jnp.arange(count, dtype=jnp.int32) * BLOCK
    mixed, log_totals = lax.map(
        one_block, (queries.reshape(count, BLOCK, heads_local, head_size), starts)
    )
    return (mixed.reshape(seq_len, heads_local * head_size), log_totals)


def attend_backward(queries, key_rows, value_rows, grad_mixed, log_totals, prefix_len):
    seq_len, heads_local, head_size = queries.shape
    count = seq_len // BLOCK
    scale = 1.0 / math.sqrt(head_size)

    def one_block(carry, items):
        key_total, value_total = carry
        query_block, grad_block, log_block, start = items
        scores = masked_scores(query_block, key_rows, start, prefix_len)
        probs = jnp.exp(scores - log_block[..., None])
        grad_probs = jnp.einsum(
            "qhd,khd->hqk", grad_block, value_rows, preferred_element_type=jnp.float32
        )
        inner = jnp.sum(probs * grad_probs, axis=-1, keepdims=True)
        grad_scores = (probs * (grad_probs - inner)).astype(jnp.bfloat16)
        grad_query = (
            jnp.einsum("hqk,khd->qhd", grad_scores, key_rows, preferred_element_type=jnp.float32)
            * scale
        )
        key_total = (
            key_total
            + jnp.einsum(
                "hqk,qhd->khd", grad_scores, query_block, preferred_element_type=jnp.float32
            )
            * scale
        )
        value_total = value_total + jnp.einsum(
            "hqk,qhd->khd",
            probs.astype(jnp.bfloat16),
            grad_block,
            preferred_element_type=jnp.float32,
        )
        return ((key_total, value_total), grad_query.astype(jnp.bfloat16))

    empty_total = jnp.zeros(queries.shape, jnp.float32)
    starts = jnp.arange(count, dtype=jnp.int32) * BLOCK
    blocked = (count, BLOCK, heads_local, head_size)
    (key_total, value_total), grad_queries = lax.scan(
        one_block,
        (empty_total, empty_total),
        (queries.reshape(blocked), grad_mixed.reshape(blocked), log_totals, starts),
    )
    width = heads_local * head_size
    return (
        grad_queries.reshape(seq_len, width),
        key_total.astype(jnp.bfloat16).reshape(seq_len, width),
        value_total.astype(jnp.bfloat16).reshape(seq_len, width),
    )


def body(
    inputs,
    prefix,
    ln1_gain,
    ln1_bias,
    query_weight,
    query_bias,
    key_weight,
    value_weight,
    value_bias,
    out_weight,
    out_bias,
    ln2_gain,
    ln2_bias,
    up_weight,
    up_bias,
    down_weight,
    down_bias,
    cotangent,
):
    local_width = query_weight.shape[1]
    local_hidden = up_weight.shape[1]
    shard_rows = inputs.shape[2]
    micro = inputs.shape[0]
    model_width = inputs.shape[3]
    heads_local = local_width // HEAD_DIM
    offset_width = lax.axis_index("tensor") * local_width
    offset_hidden = lax.axis_index("tensor") * local_hidden
    vectors = (
        lax.all_gather(ln1_gain, ("dp", "tensor"), axis=0, tiled=True),
        lax.all_gather(ln1_bias, ("dp", "tensor"), axis=0, tiled=True),
        lax.all_gather(query_bias, ("dp", "tensor"), axis=0, tiled=True),
        lax.all_gather(value_bias, ("dp", "tensor"), axis=0, tiled=True),
        lax.all_gather(out_bias, ("dp", "tensor"), axis=0, tiled=True),
        lax.all_gather(ln2_gain, ("dp", "tensor"), axis=0, tiled=True),
        lax.all_gather(ln2_bias, ("dp", "tensor"), axis=0, tiled=True),
        lax.all_gather(up_bias, ("dp", "tensor"), axis=0, tiled=True),
        lax.all_gather(down_bias, ("dp", "tensor"), axis=0, tiled=True),
    )
    (
        gain_one,
        shift_one,
        query_full_bias,
        value_full_bias,
        out_shift,
        gain_two,
        shift_two,
        up_full_bias,
        down_shift,
    ) = vectors
    query_shift = lax.dynamic_slice_in_dim(query_full_bias, offset_width, local_width)
    value_shift = lax.dynamic_slice_in_dim(value_full_bias, offset_width, local_width)
    up_shift = lax.dynamic_slice_in_dim(up_full_bias, offset_hidden, local_hidden)
    zero_width = jnp.zeros((model_width,), jnp.float32)
    gain_one_grad = zero_width
    shift_one_grad = zero_width
    query_bias_grad = zero_width
    value_bias_grad = zero_width
    out_bias_grad = zero_width
    gain_two_grad = zero_width
    shift_two_grad = zero_width
    up_bias_grad = jnp.zeros((up_full_bias.shape[0],), jnp.float32)
    down_bias_grad = zero_width
    weight_totals = None
    layer_rows = []
    input_rows = []
    for index in range(micro):
        gathered = (
            lax.all_gather(query_weight, "dp", axis=0, tiled=True),
            lax.all_gather(key_weight, "dp", axis=0, tiled=True),
            lax.all_gather(value_weight, "dp", axis=0, tiled=True),
            lax.all_gather(out_weight, "dp", axis=1, tiled=True),
            lax.all_gather(up_weight, "dp", axis=0, tiled=True),
            lax.all_gather(down_weight, "dp", axis=1, tiled=True),
        )
        full_query, full_key, full_value, full_out, full_up, full_down = gathered
        rows_in = inputs[index, 0].astype(jnp.float32)
        prefix_len = prefix[index, 0]
        normed, scaled_one, inverse_one = norm_forward(rows_in, gain_one, shift_one)
        normed_all = lax.all_gather(normed.astype(jnp.bfloat16), "tensor", axis=0, tiled=True)
        seq_len = normed_all.shape[0]
        queries = (
            jnp.dot(normed_all, full_query, preferred_element_type=jnp.float32) + query_shift
        ).astype(jnp.bfloat16)
        key_rows = jnp.dot(normed_all, full_key, preferred_element_type=jnp.float32).astype(
            jnp.bfloat16
        )
        value_rows = (
            jnp.dot(normed_all, full_value, preferred_element_type=jnp.float32) + value_shift
        ).astype(jnp.bfloat16)
        head_shape = (seq_len, heads_local, HEAD_DIM)
        queries_h = queries.reshape(head_shape)
        keys_h = key_rows.reshape(head_shape)
        values_h = value_rows.reshape(head_shape)
        attended, log_totals = attend_forward(queries_h, keys_h, values_h, prefix_len)
        attention_share = lax.psum_scatter(
            jnp.dot(attended, full_out, preferred_element_type=jnp.float32).astype(jnp.bfloat16),
            "tensor",
            scatter_dimension=0,
            tiled=True,
        ).astype(jnp.float32)
        residual = rows_in + attention_share + out_shift
        second, scaled_two, inverse_two = norm_forward(residual, gain_two, shift_two)
        grad_rows = cotangent[index, 0]
        down_bias_grad = down_bias_grad + jnp.sum(grad_rows.astype(jnp.float32), axis=0)
        second_all = lax.all_gather(second.astype(jnp.bfloat16), "tensor", axis=0, tiled=True)
        hidden_pre = jnp.dot(second_all, full_up, preferred_element_type=jnp.float32) + up_shift
        hidden_act = smooth_gate(hidden_pre).astype(jnp.bfloat16)
        feed_share = lax.psum_scatter(
            jnp.dot(hidden_act, full_down, preferred_element_type=jnp.float32).astype(jnp.bfloat16),
            "tensor",
            scatter_dimension=0,
            tiled=True,
        ).astype(jnp.float32)
        layer_rows.append(residual + feed_share + down_shift)
        grad_all = lax.all_gather(grad_rows, "tensor", axis=0, tiled=True)
        down_grad = jnp.dot(hidden_act.T, grad_all, preferred_element_type=jnp.float32)
        grad_act = jnp.dot(grad_all, full_down.T, preferred_element_type=jnp.float32)
        grad_pre = (grad_act * smooth_slope(hidden_pre)).astype(jnp.bfloat16)
        up_grad = jnp.dot(second_all.T, grad_pre, preferred_element_type=jnp.float32)
        up_part = jnp.sum(grad_pre.astype(jnp.float32), axis=0)
        up_bias_grad = up_bias_grad + lax.dynamic_update_slice(
            jnp.zeros_like(up_bias_grad), up_part, (offset_hidden,)
        )
        grad_second = lax.psum_scatter(
            jnp.dot(grad_pre, full_up.T, preferred_element_type=jnp.float32).astype(jnp.bfloat16),
            "tensor",
            scatter_dimension=0,
            tiled=True,
        ).astype(jnp.float32)
        gain_two_grad = gain_two_grad + jnp.sum(grad_second * scaled_two, axis=0)
        shift_two_grad = shift_two_grad + jnp.sum(grad_second, axis=0)
        grad_residual = grad_rows.astype(jnp.float32) + norm_backward(
            grad_second, scaled_two, inverse_two, gain_two
        )
        out_bias_grad = out_bias_grad + jnp.sum(grad_residual, axis=0)
        residual_all = lax.all_gather(
            grad_residual.astype(jnp.bfloat16), "tensor", axis=0, tiled=True
        )
        out_grad = jnp.dot(attended.T, residual_all, preferred_element_type=jnp.float32)
        grad_attended = jnp.dot(
            residual_all, full_out.T, preferred_element_type=jnp.float32
        ).astype(jnp.bfloat16)
        grad_queries, grad_keys, grad_values = attend_backward(
            queries_h, keys_h, values_h, grad_attended, log_totals, prefix_len
        )
        query_grad = jnp.dot(normed_all.T, grad_queries, preferred_element_type=jnp.float32)
        key_grad = jnp.dot(normed_all.T, grad_keys, preferred_element_type=jnp.float32)
        value_grad = jnp.dot(normed_all.T, grad_values, preferred_element_type=jnp.float32)
        query_part = jnp.sum(grad_queries.astype(jnp.float32), axis=0)
        value_part = jnp.sum(grad_values.astype(jnp.float32), axis=0)
        query_bias_grad = query_bias_grad + lax.dynamic_update_slice(
            zero_width, query_part, (offset_width,)
        )
        value_bias_grad = value_bias_grad + lax.dynamic_update_slice(
            zero_width, value_part, (offset_width,)
        )
        partial_sum = jnp.dot(grad_queries, full_query.T, preferred_element_type=jnp.float32)
        partial_sum = partial_sum + jnp.dot(
            grad_keys, full_key.T, preferred_element_type=jnp.float32
        )
        grad_normed = lax.psum_scatter(
            (
                partial_sum + jnp.dot(grad_values, full_value.T, preferred_element_type=jnp.float32)
            ).astype(jnp.bfloat16),
            "tensor",
            scatter_dimension=0,
            tiled=True,
        ).astype(jnp.float32)
        gain_one_grad = gain_one_grad + jnp.sum(grad_normed * scaled_one, axis=0)
        shift_one_grad = shift_one_grad + jnp.sum(grad_normed, axis=0)
        input_rows.append(
            grad_residual + norm_backward(grad_normed, scaled_one, inverse_one, gain_one)
        )
        reduced = (query_grad, key_grad, value_grad, out_grad, up_grad, down_grad)
        if weight_totals is None:
            weight_totals = reduced
        else:
            weight_totals = tuple((left + right for left, right in zip(weight_totals, reduced)))
    query_total, key_total, value_total, out_total, up_total, down_total = weight_totals
    query_total, key_total, value_total, out_total, up_total, down_total = (
        lax.psum_scatter(
            query_total.astype(jnp.bfloat16), "dp", scatter_dimension=0, tiled=True
        ).astype(jnp.float32),
        lax.psum_scatter(
            key_total.astype(jnp.bfloat16), "dp", scatter_dimension=0, tiled=True
        ).astype(jnp.float32),
        lax.psum_scatter(
            value_total.astype(jnp.bfloat16), "dp", scatter_dimension=0, tiled=True
        ).astype(jnp.float32),
        lax.psum_scatter(
            out_total.astype(jnp.bfloat16), "dp", scatter_dimension=1, tiled=True
        ).astype(jnp.float32),
        lax.psum_scatter(
            up_total.astype(jnp.bfloat16), "dp", scatter_dimension=0, tiled=True
        ).astype(jnp.float32),
        lax.psum_scatter(
            down_total.astype(jnp.bfloat16), "dp", scatter_dimension=1, tiled=True
        ).astype(jnp.float32),
    )
    vector_totals = (
        lax.psum_scatter(gain_one_grad, ("dp", "tensor"), scatter_dimension=0, tiled=True),
        lax.psum_scatter(shift_one_grad, ("dp", "tensor"), scatter_dimension=0, tiled=True),
        lax.psum_scatter(query_bias_grad, ("dp", "tensor"), scatter_dimension=0, tiled=True),
        lax.psum_scatter(value_bias_grad, ("dp", "tensor"), scatter_dimension=0, tiled=True),
        lax.psum_scatter(out_bias_grad, ("dp", "tensor"), scatter_dimension=0, tiled=True),
        lax.psum_scatter(gain_two_grad, ("dp", "tensor"), scatter_dimension=0, tiled=True),
        lax.psum_scatter(shift_two_grad, ("dp", "tensor"), scatter_dimension=0, tiled=True),
        lax.psum_scatter(up_bias_grad, ("dp", "tensor"), scatter_dimension=0, tiled=True),
        lax.psum_scatter(down_bias_grad, ("dp", "tensor"), scatter_dimension=0, tiled=True),
    )
    (
        gain_one_out,
        shift_one_out,
        query_bias_out,
        value_bias_out,
        out_bias_out,
        gain_two_out,
        shift_two_out,
        up_bias_out,
        down_bias_out,
    ) = vector_totals
    out_shape = (micro, 1, shard_rows, model_width)
    layer_out = jnp.stack(layer_rows).reshape(out_shape)
    input_grad = jnp.stack(input_rows).reshape(out_shape)
    return (
        layer_out,
        input_grad,
        gain_one_out,
        shift_one_out,
        query_total,
        query_bias_out,
        key_total,
        value_total,
        value_bias_out,
        out_total,
        out_bias_out,
        gain_two_out,
        shift_two_out,
        up_total,
        up_bias_out,
        down_total,
        down_bias_out,
    )


def _place(z, y, x):
    return z * 4 + y * 2 + x


def _coords():
    dp = lax.axis_index("dp")
    core = lax.axis_index("tensor")
    return dp // 4, (dp // 2) % 2, dp % 2, core


def _greet(peers):
    barrier = pltpu.get_barrier_semaphore()
    for peer in peers:
        pl.semaphore_signal(barrier, inc=1, device_id=peer, device_id_type=MESH)
    pl.semaphore_wait(barrier, len(peers))


def _peers():
    z, y, x, core = _coords()
    along = [(_place((z + j) % 4, y, x), core) for j in (1, 2, 3)]
    across = (_place(z, y, 1 - x), core)
    down = (_place(z, 1 - y, x), core)
    sibling = (_place(z, y, x), 1 - core)
    return along, across, down, sibling


def _send(src, dst, send_sem, recv_sem, peer):
    copy = pltpu.make_async_remote_copy(
        src_ref=src,
        dst_ref=dst,
        send_sem=send_sem,
        recv_sem=recv_sem,
        device_id=peer,
        device_id_type=MESH,
    )
    copy.start()
    return copy


def _local(src, dst, sem):
    copy = pltpu.make_async_copy(src, dst, sem)
    copy.start()
    return copy


def _dot(left, right, contract):
    return lax.dot_general(left, right, (contract, ((), ())), preferred_element_type=jnp.float32)


NN = ((1,), (0,))
NT = ((1,), (1,))
TN = ((0,), (0,))
LOG2E = 1.4426950408889634
MIB = 1024 * 1024
WIDE = 256


def _normal(values):
    center = values - jnp.mean(values, axis=-1, keepdims=True)
    inverse = lax.rsqrt(jnp.mean(center * center, axis=-1, keepdims=True) + EPSILON)
    return center * inverse, inverse


def _spans(seq_len, longest, step):
    return [(start, max(longest, start + step)) for start in range(0, seq_len, step)]


class Gather:
    def __init__(self, shards, places, send_sem, recv_sem, local_sem):
        self.z, self.y, self.x, self.core = _coords()
        self.along, self.across, self.down, self.sibling = _peers()
        self.shards, self.places, self.count = shards, places, len(shards)
        self.send_sem, self.recv_sem, self.local_sem = send_sem, recv_sem, local_sem

    def _remote(self, k, slot, src, dst, peer):
        return pltpu.make_async_remote_copy(
            src_ref=src,
            dst_ref=dst,
            send_sem=self.send_sem.at[k, slot],
            recv_sem=self.recv_sem.at[k, slot],
            device_id=peer,
            device_id_type=MESH,
        )

    def line(self, k):
        own = self.places[k].at[self.core, self.z, self.y, self.x]
        here = pltpu.make_async_copy(self.shards[k], own, self.local_sem.at[k])
        return [here] + [self._remote(k, j, self.shards[k], own, self.along[j]) for j in range(3)]

    def plane(self, k):
        block = self.places[k].at[self.core, :, self.y, self.x]
        return [self._remote(k, 3, block, block, self.across), self._remote(k, 4, block, block, self.down)]

    def corner(self, k):
        part = self.shards[k].shape[0] // 2
        one = self.places[k].at[self.core, :, 1 - self.y, self.x, 0:part]
        two = self.places[k].at[self.core, :, self.y, 1 - self.x, part : 2 * part]
        return [self._remote(k, 5, one, one, self.across), self._remote(k, 6, two, two, self.down)]

    def twin(self, k):
        block = self.places[k].at[self.core]
        return [self._remote(k, 7, block, block, self.sibling)]

    def near(self, k):
        own = self.places[k].at[self.core, self.z, self.y, self.x]
        here = pltpu.make_async_copy(self.shards[k], own, self.local_sem.at[k])
        src = self.shards[k]
        return [here, self._remote(k, 3, src, own, self.across), self._remote(k, 4, src, own, self.down)]

    def near_corner(self, k):
        part = self.shards[k].shape[0] // 2
        one = self.places[k].at[self.core, self.z, 1 - self.y, self.x, 0:part]
        two = self.places[k].at[self.core, self.z, self.y, 1 - self.x, part : 2 * part]
        return [self._remote(k, 5, one, one, self.across), self._remote(k, 6, two, two, self.down)]

    def far(self, k, i):
        block = self.places[k].at[self.core, self.z, i // 3]
        return [self._remote(k + i // 3, i % 3, block, block, self.along[i % 3])]

    def start(self, stage, k, *more):
        if 0 <= k < self.count and (more or k != self.count - 1 or stage in self.odd):
            for copy in stage(k, *more):
                copy.start()

    def wait(self, stage, k, *more):
        if 0 <= k < self.count and (more or k != self.count - 1 or stage in self.odd):
            for copy in stage(k, *more):
                copy.wait()

    @property
    def odd(self):
        return (self.near, self.near_corner)

    def last(self, step):
        k = self.count - 1
        if step == 0:
            self.start(self.near, k)
        if step == 1:
            self.wait(self.near, k)
            self.start(self.near_corner, k)
        if step == 2:
            self.wait(self.near_corner, k)
        if 2 <= step < 8:
            self.start(self.far, k, step - 2)
        if step == 9:
            for i in range(6):
                self.wait(self.far, k, i)
            self.twin(k)[0].start()
        if step == 20:
            self.twin(k)[0].wait()

    def tick(self, k, twin=True):
        self.last(k - 3)
        self.wait(self.plane, k)
        self.start(self.corner, k)
        self.wait(self.line, k + 2)
        self.start(self.plane, k + 2)
        self.start(self.line, k + 4)
        if twin:
            self.wait(self.corner, k - 1)
            self.start(self.twin, k - 1)


def _if(condition, action):
    if isinstance(condition, bool):
        if condition:
            action()
    else:
        pl.when(condition)(action)


class Reduce:
    def __init__(self, acc, out, x_one, y_one, x_two, y_two, from_z, send_sem, recv_sem):
        self.z, self.y, self.x, self.core = _coords()
        self.along, self.across, self.down, self.sibling = _peers()
        self.acc, self.out = acc, out
        self.x_one, self.y_one, self.x_two, self.y_two, self.from_z = x_one, y_one, x_two, y_two, from_z
        self.send_sem, self.recv_sem = send_sem, recv_sem

    def _remote(self, k, slot, src, dst, peer):
        return pltpu.make_async_remote_copy(
            src_ref=src,
            dst_ref=dst,
            send_sem=self.send_sem.at[k, slot],
            recv_sem=self.recv_sem.at[k, slot],
            device_id=peer,
            device_id_type=MESH,
        )

    def corner(self, k):
        block = self.acc(k).at[:, 1 - self.y, 1 - self.x]
        part = block.shape[1] // 2
        return [
            self._remote(k, 0, block.at[:, 0:part], self.x_one.at[k], self.across),
            self._remote(k, 1, block.at[:, part : 2 * part], self.y_one.at[k], self.down),
        ]

    def plane(self, k):
        acc = self.acc(k)
        return [
            self._remote(k, 2, acc.at[:, self.y, 1 - self.x], self.x_two.at[k], self.across),
            self._remote(k, 3, acc.at[:, 1 - self.y, self.x], self.y_two.at[k], self.down),
        ]

    def line(self, k):
        acc = self.acc(k)
        return [
            self._remote(k, 4 + j, acc.at[(self.z + j + 1) % 4, self.y, self.x], self.from_z.at[k, j], self.along[j])
            for j in range(3)
        ]

    @staticmethod
    def start(copies):
        for copy in copies:
            copy.start()

    @staticmethod
    def wait(copies):
        for copy in copies:
            copy.wait()

    def after_corner(self, k):
        acc, y, x = self.acc(k), self.y, self.x
        part = acc.shape[3] // 2
        self.wait(self.corner(k))
        one = acc.at[:, 1 - y, x, 0:part]
        two = acc.at[:, y, 1 - x, part : 2 * part]
        one[...] = _add(one[...], self.x_one[k])
        two[...] = _add(two[...], self.y_one[k])
        self.start(self.plane(k))

    def after_plane(self, k):
        acc = self.acc(k)
        self.wait(self.plane(k))
        here = acc.at[:, self.y, self.x]
        here[...] = _add(here[...], self.x_two[k], self.y_two[k])
        self.start(self.line(k))

    def finish_plane(self, k, target):
        self.wait(self.plane(k))
        target[k] = _add(self.acc(k)[:, self.y, self.x], self.x_two[k], self.y_two[k])

    def after_line(self, k):
        self.wait(self.line(k))
        total = self.acc(k)[self.z, self.y, self.x].astype(self.out.dtype)
        for j in range(3):
            total = total + self.from_z[k, j].astype(self.out.dtype)
        self.out[k] = total


def _add(first, *others):
    if len(others) == 1:
        return first + others[0]
    total = first.astype(jnp.float32)
    for other in others:
        total = total + other.astype(jnp.float32)
    return total.astype(first.dtype)


def _combine(mine, other):
    @pl.loop(0, mine.shape[0])
    def _(i):
        for j in range(2):
            mine[i, j] = _add(mine[i, j], other[i, j])


EARLY = 2
ATTEND_SITES = 3
ATTEND_TICKS = {4: 1, 5: 3, 7: 9}
FEED_TICKS = {9: 0, 10: 1, 11: 2, 12: 3, 13: 4, 14: 6}


def front_kernel(
    prefix, wq_in, wk_in, wv_in, wo_in, up_in, down_in, vec, xin, gin,
    full, fullo, qkv, mixed_out, probs_out, normed_out, x_out, lines, layer_out, low_out, sums, gown, grecv, gbias, early_out,
    vfull, x, grad, second, residual, weights, ubias,
    ssem, rsem, lsem, vs, vr, vl, ws, wr, wl, wsem, osem, fs, fr, fl, es, er, el,
    racc, rtheirs, x_one, y_one, x_two, y_two, rs, rr, rl,
):
    f32, bf16 = jnp.float32, jnp.bfloat16
    seq_len, model = x.shape
    half = seq_len // 2
    block = 128

    cols = wq_in.shape[1]
    shards = [w.at[:, sub * WIDE : (sub + 1) * WIDE] for sub in range(2) for w in (wq_in, wk_in, wv_in)] + [wo_in]
    places = [full.at[k] for k in range(6)] + [fullo]
    for piece in range(weights.shape[0] // 2):
        shards += [w.at[:, piece * cols : (piece + 1) * cols] for w in (up_in, down_in)]
        places += [weights.at[2 * piece], weights.at[2 * piece + 1]]
    early = len(shards) - weights.shape[0]
    gather = Gather(shards, places, ssem, rsem, lsem)
    reduce = Reduce(lambda k: racc.at[k], None, x_one, y_one, x_two, y_two, None, rs, rr)
    z, y, xx, core = gather.z, gather.y, gather.x, gather.core
    along, across, down, sibling = gather.along, gather.across, gather.down, gather.sibling
    _greet(along + [across, down, sibling])

    gather.start(gather.line, 0)
    vown = vfull.at[z, y, xx, core]
    vline = [_local(vec, vown, vl.at[0])] + [_send(vec, vown, vs.at[j], vr.at[j], along[j]) for j in range(3)]
    for k in (1, 2, 3):
        gather.start(gather.line, k)
    mine = pl.ds(pl.multiple_of(core * half, half), half)
    swaps = []
    for i, (part, whole) in enumerate(((xin, x), (gin, grad))):
        swaps.append(_local(part.at[core], whole.at[mine], wl.at[i]))
        swaps.append(_send(part.at[1 - core], whole.at[mine], ws.at[i], wr.at[i], sibling))
    gather.wait(gather.line, 0)
    gather.start(gather.plane, 0)
    for s in vline:
        s.wait()
    vblock = vfull.at[:, y, xx, core]
    vone = [_send(vblock, vblock, vs.at[3], vr.at[3], across), _send(vblock, vblock, vs.at[4], vr.at[4], down)]
    gather.wait(gather.line, 1)
    gather.start(gather.plane, 1)
    gather.tick(0)
    for s in vone:
        s.wait()
    vblock = vfull.at[:, 1 - y, xx, core]
    vtwo = _send(vblock, vblock, vs.at[5], vr.at[5], across)
    gather.tick(1)
    vtwo.wait()
    vblock = vfull.at[:, :, :, core]
    vthree = _send(vblock, vblock, vs.at[6], vr.at[6], sibling)
    for s in swaps:
        s.wait()
    saved = [_local(x, x_out, osem.at[0])]
    gather.tick(2)
    vthree.wait()
    for zi in range(4):
        for yi in range(2):
            at = (zi * 2 + yi) * 128
            group = vfull[zi, yi, 0, 0] + vfull[zi, yi, 0, 1] + vfull[zi, yi, 1, 0] + vfull[zi, yi, 1, 1]
            lines[:, at : at + 128] = group[0:8]
            for xi in range(2):
                for ci in range(2):
                    i = ((zi * 2 + yi) * 2 + xi) * 2 + ci
                    piece = 2 * ((i % 16) // 4) + i // 16
                    ubias[piece, 0:1, (i % 4) * 128 : (i % 4) * 128 + 128] = vfull[zi, yi, xi, ci, 8:9]

    def attention(normed, wblk, stage, mixed, wout, probs):
        @pl.loop(0, seq_len // block)
        def _(i):
            rows = pl.ds(pl.multiple_of(i * block, block), block)
            scaled, _ = _normal(x[rows].astype(f32))
            normed[rows] = (scaled * lines[0:1] + lines[1:2]).astype(bf16)

        gather.wait(gather.corner, 2)
        gather.start(gather.twin, 2)
        gather.tick(3, twin=False)
        keep = _local(normed, normed_out, osem.at[1])

        def side_of(pair):
            return (pair + core) % 2

        def load(pair):
            return [
                pltpu.make_async_copy(full.at[3 * (pair // 2) + i, side_of(pair)], wblk.at[pair % 2, i], wsem.at[pair % 2, i])
                for i in range(3)
            ]

        def store(pair):
            slot = pair % 2
            columns = pl.ds(pl.multiple_of((pair // 2) * WIDE, WIDE), WIDE)
            copies = [
                pltpu.make_async_copy(stage.at[slot, i], qkv.at[i, side_of(pair), :, columns], wsem.at[slot, 3 + i])
                for i in range(3)
            ]
            heads = pl.ds((side_of(pair) * 2 + pair // 2) * 2, 2)
            return copies + [pltpu.make_async_copy(probs.at[slot], probs_out.at[heads], wsem.at[slot, 6])]

        for c in load(0):
            c.start()

        def ticks(site, pair):
            for k, at in ATTEND_TICKS.items():
                if at % ATTEND_SITES == site:

                    @pl.when(pair == at // ATTEND_SITES)
                    def _(k=k):
                        gather.tick(k)

        @pl.loop(0, 4)
        def _(pair):
            slot = pair % 2
            for c in load(pair):
                c.wait()

            @pl.when(pair >= 2)
            def _():
                for c in store(pair - 2):
                    c.wait()

            ticks(0, pair)
            lanes = pl.ds(pl.multiple_of((side_of(pair) * 2 + pair // 2) * WIDE, WIDE), WIDE)
            wq, wk, wv = (wblk[slot, i].reshape(model, WIDE) for i in range(3))
            stage[slot, 0] = (_dot(normed[...], wq, NN) + lines[2:3, lanes]).astype(bf16)
            stage[slot, 1] = _dot(normed[...], wk, NN).astype(bf16)
            stage[slot, 2] = (_dot(normed[...], wv, NN) + lines[3:4, lanes]).astype(bf16)
            ticks(1, pair)
            for sub in range(2):

                @pl.when(pair == 2 * sub)
                def _(sub=sub):
                    for k in range(3 * sub, 3 * sub + 3):
                        gather.wait(gather.twin, k)
                    for c in load(2 * sub + 1):
                        c.start()

            step = 256
            factor = LOG2E / math.sqrt(HEAD_DIM)
            prefix_len = prefix[core]
            for head in range(WIDE // HEAD_DIM):
                part = slice(head * HEAD_DIM, (head + 1) * HEAD_DIM)
                for start, stop in _spans(seq_len, LONGEST, step):
                    scores = _dot(stage[slot, 1, :stop, part], stage[slot, 0, start : start + step, part], NT)
                    keys = lax.broadcasted_iota(jnp.int32, scores.shape, 0)
                    queries = lax.broadcasted_iota(jnp.int32, scores.shape, 1) + start
                    scores = jnp.where((keys <= queries) | (keys < prefix_len), scores, -jnp.inf)
                    peak = jnp.max(scores, axis=0, keepdims=True)
                    raw = jnp.exp2((scores - peak) * factor)
                    total = jnp.sum(raw, axis=0, keepdims=True)
                    share = (raw * (1.0 / total)).astype(bf16)
                    probs[slot, head, :stop, start : start + step] = share
                    to = pl.ds(pl.multiple_of((pair // 2) * WIDE + head * HEAD_DIM, HEAD_DIM), HEAD_DIM)
                    mixed[side_of(pair), start : start + step, to] = _dot(
                        share, stage[slot, 2, :stop, part], TN
                    ).astype(bf16)
                if head == 0:
                    ticks(2, pair)
            for c in store(pair):
                c.start()

            @pl.when(pair == 1)
            def _():
                gather.tick(6)
                for c in load(2):
                    c.start()

        gather.wait(gather.twin, 6)
        fetch = _local(fullo, wout, osem.at[3])
        done = _local(mixed, mixed_out, osem.at[2])
        fetch.wait()
        weight = [wout[c].reshape(model, seq_len // 2) for c in range(2)]
        step = 256

        @pl.loop(0, seq_len // step)
        def _(i):
            rows = pl.ds(pl.multiple_of(i * step, step), step)
            branch = _dot(mixed[0, rows], weight[0], NT) + _dot(mixed[1, rows], weight[1], NT)
            total = x[rows].astype(f32) + branch + lines[4:5]
            residual[rows] = total
            scaled, _ = _normal(total)
            second[rows] = (scaled * lines[5:6] + lines[6:7]).astype(bf16)

        gather.tick(8)
        for pair in (2, 3):
            for c in store(pair):
                c.wait()
        done.wait()
        keep.wait()

    pl.run_scoped(
        attention,
        pltpu.VMEM((seq_len, model), bf16),
        pltpu.VMEM((2, 3, 4, 2, 2, 64, WIDE), bf16),
        pltpu.VMEM((2, 3, seq_len, WIDE), bf16),
        pltpu.VMEM((2, seq_len, model // 2), bf16),
        pltpu.VMEM((2, 4, 2, 2, 64, model // 2), bf16),
        pltpu.VMEM((2, 2, seq_len, seq_len), bf16),
    )

    def feed(layer, gres, stage, hid, gpre):
        pieces = weights.shape[0]

        @pl.loop(0, seq_len // block)
        def _(i):
            rows = pl.ds(pl.multiple_of(i * block, block), block)
            layer[rows] = residual[rows] + lines[7:8]
            gres[rows] = jnp.zeros((block, model), f32)

        def away(piece):
            return [
                pltpu.make_async_remote_copy(
                    src_ref=stage.at[1, i],
                    dst_ref=grecv.at[2 * piece + i],
                    send_sem=fs.at[piece, i],
                    recv_sem=fr.at[piece, i],
                    device_id=sibling,
                    device_id_type=MESH,
                )
                for i in range(2)
            ]

        def stay(piece):
            return [pltpu.make_async_copy(stage.at[0, i], gown.at[2 * piece + i], fl.at[i]) for i in range(2)]

        def bring(k):
            return [
                pltpu.make_async_copy(gown.at[k], racc.at[k], rl.at[k, 0]),
                pltpu.make_async_copy(grecv.at[k], rtheirs.at[k], rl.at[k, 1]),
            ]

        @pl.loop(0, pieces)
        def _(t):
            piece, turn = t // 2, t % 2
            side = (t + core) % 2
            for k, at in FEED_TICKS.items():

                @pl.when(t == at)
                def _(k=k):
                    gather.tick(k)

            for p in range(pieces // 2):

                @pl.when(t == 2 * p + 1)
                def _(p=p):
                    gather.wait(gather.twin, early + 2 * p)
                    if p < pieces // 2 - 1:
                        gather.wait(gather.twin, early + 2 * p + 1)
                    else:
                        gather.last(20)

            @pl.when(t == pieces - 3)
            def _():
                for c in away(0):
                    c.wait_recv()
                reduce.start(bring(0) + bring(1))

            @pl.when(t == pieces - 2)
            def _():
                for k in range(EARLY):
                    reduce.wait(bring(k))
                    _combine(racc.at[k], rtheirs.at[k])
                    reduce.start(reduce.corner(k))

            @pl.when(t == pieces - 1)
            def _():
                for k in range(EARLY):
                    reduce.after_corner(k)

            @pl.when((t >= 2) & (turn == 1))
            def _():
                for c in away(piece - 1):
                    c.wait_send()

            @pl.when((t >= 2) & (turn == 0))
            def _():
                for c in stay(piece - 1):
                    c.wait()

            up = weights[2 * piece, side].reshape(model, model // 2)
            lower = weights[2 * piece + 1, side].reshape(model, model // 2)
            line = 2 * piece + side
            pre = _dot(second[...], up, NN) + ubias[line]
            phi = 0.5 * (1.0 + lax.erf(pre * (1.0 / math.sqrt(2.0))))
            density = jnp.exp2(pre * pre * (-0.5 * LOG2E)) * (1.0 / math.sqrt(2.0 * math.pi))
            hid[...] = (pre * phi).astype(bf16)
            slope = phi + pre * density
            back = (_dot(grad[...], lower, NN) * slope).astype(bf16)
            gpre[...] = back
            gbias[line] = jnp.sum(back.astype(f32), axis=0, keepdims=True)
            layer[...] += _dot(hid[...], lower, NT)
            gres[...] += _dot(gpre[...], up, NT)
            blocks = stage.shape[2:]
            stage[turn, 0] = _dot(second[...], gpre[...], TN).astype(bf16).reshape(blocks)
            stage[turn, 1] = _dot(grad[...], hid[...], TN).astype(bf16).reshape(blocks)

            @pl.when(turn == 1)
            def _():
                for c in away(piece):
                    c.start()

            @pl.when(turn == 0)
            def _():
                for c in stay(piece):
                    c.start()

        for s in saved:
            s.wait()

        @pl.loop(0, seq_len // block)
        def _(i):
            rows = pl.ds(pl.multiple_of(i * block, block), block)
            x[rows] = layer[rows].astype(bf16)

        theirs = pl.ds(pl.multiple_of((1 - core) * half, half), half)
        final = [
            _local(x.at[mine], layer_out.at[core], el.at[0]),
            _send(x.at[theirs], layer_out.at[core], es.at[0], er.at[0], sibling),
        ]
        sums[...] = jnp.zeros_like(sums)

        @pl.loop(0, seq_len // block)
        def _(i):
            rows = pl.ds(pl.multiple_of(i * block, block), block)
            scaled, inverse = _normal(residual[rows])
            grow = gres[rows]
            upstream = grad[rows].astype(f32)
            weighted = grow * lines[5:6]
            mean_plain = jnp.mean(weighted, axis=-1, keepdims=True)
            mean_scaled = jnp.mean(weighted * scaled, axis=-1, keepdims=True)
            total = upstream + inverse * (weighted - mean_plain - scaled * mean_scaled)
            second[rows] = total.astype(bf16)
            sums[0:1] += jnp.sum(grow * scaled, axis=0, keepdims=True)
            sums[1:2] += jnp.sum(grow, axis=0, keepdims=True)
            sums[2:3] += jnp.sum(total, axis=0, keepdims=True)
            sums[3:4] += jnp.sum(upstream, axis=0, keepdims=True)

        final.append(_local(second, low_out, el.at[2]))
        for k in range(EARLY):
            reduce.finish_plane(k, early_out)
        last = pieces // 2 - 1
        for c in away(last):
            c.wait_send()
        for c in stay(last):
            c.wait()
        for p in range(1, pieces // 2):
            for c in away(p):
                c.wait_recv()
        for c in final:
            c.wait()

    pl.run_scoped(
        feed,
        pltpu.VMEM((seq_len, model), f32),
        pltpu.VMEM((seq_len, model), f32),
        pltpu.VMEM((2, 2, 4, 2, 2, model // 16, model // 2), bf16),
        pltpu.VMEM((seq_len, model // 2), bf16),
        pltpu.VMEM((seq_len, model // 2), bf16),
    )


def front(prefix_len, wq, wk, wv, wo, up, down, vec, xin, gin):
    rows, cols = wq.shape
    half, model = xin.shape[1:]
    seq_len = 2 * half
    pieces = 2 * (up.shape[1] // cols)
    chunks = 7 + pieces
    bf16, f32 = jnp.bfloat16, jnp.float32
    hbm = pl.BlockSpec(memory_space=pltpu.HBM)
    vmem = pl.BlockSpec(memory_space=pltpu.VMEM)
    dma = pltpu.SemaphoreType.DMA

    def shape(dims, dtype):
        return jax.ShapeDtypeStruct(dims, dtype)

    heads = model // HEAD_DIM
    return pl.pallas_call(
        front_kernel,
        out_shape=(
            shape((6, 2, 4, 2, 2, rows, WIDE), bf16),
            shape((2, 4, 2, 2, rows, cols), bf16),
            shape((3, 2, seq_len, cols), bf16),
            shape((2, seq_len, cols), bf16),
            shape((heads, seq_len, seq_len), bf16),
            shape((seq_len, model), bf16),
            shape((seq_len, model), bf16),
            shape((8, model), f32),
            shape((2, half, model), bf16),
            shape((seq_len, model), bf16),
            shape((8, model), f32),
            shape((pieces, 4, 2, 2, rows, cols), bf16),
            shape((pieces, 4, 2, 2, rows, cols), bf16),
            shape((pieces, 1, cols), f32),
            shape((EARLY, 4, rows, cols), bf16),
        ),
        in_specs=[pl.BlockSpec(memory_space=pltpu.SMEM)] + [vmem] * 7 + [hbm, hbm],
        out_specs=(hbm, hbm, hbm, hbm, hbm, hbm, hbm, vmem, hbm, hbm, vmem, hbm, hbm, vmem, vmem),
        scratch_shapes=[
            pltpu.VMEM((4, 2, 2, 2) + vec.shape, f32),
            pltpu.VMEM((seq_len, model), bf16),
            pltpu.VMEM((seq_len, model), bf16),
            pltpu.VMEM((seq_len, model), bf16),
            pltpu.VMEM((seq_len, model), f32),
            pltpu.VMEM((pieces, 2, 4, 2, 2, rows, cols), bf16),
            pltpu.VMEM((pieces, 1, cols), f32),
            dma((chunks + 1, 8)),
            dma((chunks + 1, 8)),
            dma((chunks,)),
            dma((7,)),
            dma((7,)),
            dma((1,)),
            dma((2,)),
            dma((2,)),
            dma((2,)),
            dma((2, 7)),
            dma((4,)),
            dma((pieces // 2, 2)),
            dma((pieces // 2, 2)),
            dma((2,)),
            dma((1,)),
            dma((1,)),
            dma((3,)),
            pltpu.VMEM((EARLY, 4, 2, 2, rows, cols), bf16),
            pltpu.VMEM((EARLY, 4, 2, 2, rows, cols), bf16),
            pltpu.VMEM((EARLY, 4, rows // 2, cols), bf16),
            pltpu.VMEM((EARLY, 4, rows // 2, cols), bf16),
            pltpu.VMEM((EARLY, 4, rows, cols), bf16),
            pltpu.VMEM((EARLY, 4, rows, cols), bf16),
            dma((EARLY, 7)),
            dma((EARLY, 7)),
            dma((EARLY, 2)),
        ],
        compiler_params=pltpu.CompilerParams(
            collective_id=0, has_side_effects=True, vmem_limit_bytes=63 * MIB
        ),
    )(prefix_len, wq, wk, wv, wo, up, down, vec, xin, gin)


RING = 4


def back_kernel(
    lines, sums_two, gbias, early, qkv, mixed_in, probs_in, full, fullo, low_in, normed_in, x_in, gown, grecv,
    out, vout, iout, qrecv,
    ring, theirs_in, gbuf, x_one, y_one, x_two, y_two, from_z,
    vacc, v_s, vx_one, vx_two, vy_two, v_z,
    low, normed, ingrad, sums, bsums,
    from_e, esend, erecv, ssem, rsem, lsem, qs, qr, vs, vr, bsem, msem, es, er,
):
    f32, bf16 = jnp.float32, jnp.bfloat16
    seq_len, model = low.shape
    half, block, step = seq_len // 2, 128, 256
    feeds = gown.shape[0] - EARLY
    count = out.shape[0] - EARLY
    scale = 1.0 / math.sqrt(HEAD_DIM)

    own = gbuf.at[1]

    def acc(k):
        return own.at[k - feeds] if isinstance(k, int) and k >= feeds else ring.at[k % RING]

    reduce = Reduce(acc, out, x_one, y_one, x_two, y_two, from_z, ssem, rsem)
    z, y, x, core = reduce.z, reduce.y, reduce.x, reduce.core
    along, across, down, sibling = reduce.along, reduce.across, reduce.down, reduce.sibling

    def load(k):
        if isinstance(k, int) and k >= feeds:
            return [pltpu.make_async_copy(qrecv.at[k - feeds], theirs_in.at[k % 2], lsem.at[k % 2, 1])]
        return [
            pltpu.make_async_copy(gown.at[EARLY + k], ring.at[k % RING], lsem.at[k % 2, 0]),
            pltpu.make_async_copy(grecv.at[EARLY + k], theirs_in.at[k % 2], lsem.at[k % 2, 1]),
        ]

    def begin(k):
        reduce.wait(load(k))
        _combine(acc(k), theirs_in.at[k % 2])
        reduce.start(reduce.corner(k))

    def tick(k):
        if not isinstance(k, int) or k < count:
            begin(k)
        _if((k >= 1) & (k - 1 < count), lambda: reduce.after_corner(k - 1))
        _if((k >= 2) & (k - 2 < count), lambda: reduce.after_plane(k - 2))
        _if((k >= 3) & (k - 3 < count), lambda: reduce.after_line(k - 3))

    reduce.start(load(0))
    start = [_local(low_in, low, msem.at[0]), _local(normed_in, normed, msem.at[1])]
    _greet(along + [across, down, sibling])
    lines_first = [
        _send(early.at[k, (z + j + 1) % 4], from_e.at[k, j], esend.at[k, j], erecv.at[k, j], along[j])
        for k in range(EARLY)
        for j in range(3)
    ]

    def away(sub, i):
        unit = sub * 2 + i
        return pltpu.make_async_remote_copy(
            src_ref=gbuf.at[0, unit],
            dst_ref=qrecv.at[unit],
            send_sem=qs.at[unit],
            recv_sem=qr.at[unit],
            device_id=sibling,
            device_id_type=MESH,
        )

    def landed(unit):
        away(unit // 2, unit % 2).wait_recv()

    def retreat(heads_in, probs, wblk, dq, dk, dv, dmix):
        def fetch(i):
            turn, sub = i // 2, i % 2
            side = (turn + 1 + core) % 2
            columns = pl.ds(pl.multiple_of(sub * WIDE, WIDE), WIDE)
            slot = i % 2
            copies = [
                pltpu.make_async_copy(qkv.at[n, side, :, columns], heads_in.at[slot, n], bsem.at[slot, n])
                for n in range(3)
            ]
            copies.append(pltpu.make_async_copy(mixed_in.at[side, :, columns], heads_in.at[slot, 3], bsem.at[slot, 3]))
            copies += [
                pltpu.make_async_copy(full.at[3 * sub + n, side], wblk.at[slot, n], bsem.at[slot, 4 + n])
                for n in range(3)
            ]
            copies.append(
                pltpu.make_async_copy(fullo.at[side, :, :, :, :, columns], wblk.at[slot, 3], bsem.at[slot, 7])
            )
            heads = pl.ds((side * 2 + sub) * 2, 2)
            copies.append(pltpu.make_async_copy(probs_in.at[heads], probs.at[slot], bsem.at[slot, 8]))
            return copies

        reduce.start(fetch(0))

        @pl.loop(0, seq_len // block)
        def _(i):
            ingrad[pl.ds(pl.multiple_of(i * block, block), block)] = jnp.zeros((block, model), f32)

        reduce.wait(start)

        @pl.loop(0, 4)
        def _(i):
            turn, sub, slot = i // 2, i % 2, i % 2
            side = (turn + 1 + core) % 2
            reduce.wait(fetch(i))

            @pl.when(i < 3)
            def _():
                reduce.start(fetch(i + 1))

            columns = pl.ds(pl.multiple_of(sub * WIDE, WIDE), WIDE)

            def put(n, value):
                at = slice((n % 2) * WIDE, (n % 2 + 1) * WIDE)
                gbuf[turn, sub * 2 + n // 2, :, :, :, :, at] = value.astype(bf16).reshape(4, 2, 2, model // 16, WIDE)

            def tick_and_load(n):
                k = 2 * i + n

                @pl.when(k < feeds)
                def _():
                    tick(k)

                @pl.when(k + 1 < feeds)
                def _():
                    reduce.start(load(k + 1))

                @pl.when(k == feeds + n)
                def _():
                    if n == 0:
                        for u in range(2):
                            landed(u)
                            reduce.start(load(feeds + u))
                    tick(feeds + n)

            tick_and_load(0)
            wq, wk, wv, wo = (wblk[slot, n].reshape(model, WIDE) for n in range(4))
            dmix[...] = _dot(low[...], wo, NN).astype(bf16)
            put(0, _dot(low[...], heads_in[slot, 3], TN))
            parts = [slice(h * HEAD_DIM, (h + 1) * HEAD_DIM) for h in range(WIDE // HEAD_DIM)]
            spans = _spans(seq_len, LONGEST, step)
            bands = [(0, LONGEST)] + [(first, first + step) for first in range(LONGEST, seq_len, step)]
            for head, part in enumerate(parts):
                for low_key, high_key in bands:
                    dv[low_key:high_key, part] = _dot(
                        probs[slot, head, low_key:high_key, low_key:], dmix[low_key:, part], NN
                    ).astype(bf16)
            for head, part in enumerate(parts):
                for first, stop in spans:
                    block_at = (slot, head, slice(0, stop), slice(first, first + step))
                    weights = probs[block_at].astype(f32)
                    dprobs = _dot(heads_in[slot, 2, :stop, part], dmix[first : first + step, part], NT)
                    inner = jnp.sum(weights * dprobs, axis=0, keepdims=True)
                    probs[block_at] = (weights * (dprobs - inner)).astype(bf16)
            tick_and_load(1)
            for head, part in enumerate(parts):
                for low_key, high_key in bands:
                    dk[low_key:high_key, part] = (
                        _dot(probs[slot, head, low_key:high_key, low_key:], heads_in[slot, 0, low_key:, part], NN)
                        * scale
                    ).astype(bf16)
                for first, last in bands:
                    dq[first:last, part] = (
                        _dot(probs[slot, head, :last, first:last], heads_in[slot, 1, :last, part], TN) * scale
                    ).astype(bf16)
            put(1, _dot(normed[...], dq[...], TN))
            put(2, _dot(normed[...], dk[...], TN))
            put(3, _dot(normed[...], dv[...], TN))
            ingrad[...] += _dot(dq[...], wq, NT) + _dot(dk[...], wk, NT) + _dot(dv[...], wv, NT)

            @pl.when(turn == 0)
            def _():
                for n in range(2):
                    away(sub, n).start()

            at = side * 2 + sub
            bsums[at, 0:1] = jnp.sum(dq[...].astype(f32), axis=0, keepdims=True)
            bsums[at, 1:2] = jnp.sum(dv[...].astype(f32), axis=0, keepdims=True)

        for sub in range(2):
            for n in range(2):
                away(sub, n).wait_send()

    pl.run_scoped(
        retreat,
        pltpu.VMEM((2, 4, seq_len, WIDE), bf16),
        pltpu.VMEM((2, 2, seq_len, seq_len), bf16),
        pltpu.VMEM((2, 4, 4, 2, 2, model // 16, WIDE), bf16),
        pltpu.VMEM((seq_len, WIDE), bf16),
        pltpu.VMEM((seq_len, WIDE), bf16),
        pltpu.VMEM((seq_len, WIDE), bf16),
        pltpu.VMEM((seq_len, WIDE), bf16),
    )

    reduce.wait(lines_first)
    for k in range(EARLY):
        total = early[k, z].astype(f32)
        for j in range(3):
            total = total + from_e[k, j].astype(f32)
        out[count + k] = total

    def finish(xs):
        bring = [_local(x_in, xs, msem.at[1])]
        for unit in (2, 3):
            landed(unit)
            reduce.start(load(feeds + unit))
        begin(feeds + 2)
        begin(feeds + 3)
        reduce.after_corner(feeds + 1)
        reduce.after_plane(feeds)
        reduce.after_line(feeds - 1)
        reduce.after_corner(feeds + 2)
        reduce.after_corner(feeds + 3)
        reduce.wait(bring)
        sums[...] = jnp.zeros_like(sums)

        @pl.loop(0, seq_len // block)
        def _(i):
            rows = pl.ds(pl.multiple_of(i * block, block), block)
            scaled, inverse = _normal(xs[rows].astype(f32))
            grow = ingrad[rows]
            weighted = grow * lines[0:1]
            mean_plain = jnp.mean(weighted, axis=-1, keepdims=True)
            mean_scaled = jnp.mean(weighted * scaled, axis=-1, keepdims=True)
            total = low[rows].astype(f32) + inverse * (weighted - mean_plain - scaled * mean_scaled)
            normed[rows] = total.astype(bf16)
            sums[0:1] += jnp.sum(grow * scaled, axis=0, keepdims=True)
            sums[1:2] += jnp.sum(grow, axis=0, keepdims=True)

    pl.run_scoped(finish, pltpu.VMEM((seq_len, model), bf16))
    mine = pl.ds(pl.multiple_of(core * half, half), half)
    theirs = pl.ds(pl.multiple_of((1 - core) * half, half), half)
    final = [
        _local(normed.at[mine], iout.at[core], msem.at[0]),
        _send(normed.at[theirs], iout.at[core], es.at[0], er.at[0], sibling),
    ]
    for pair in range(4):
        at = slice(pair * WIDE, (pair + 1) * WIDE)
        sums[2:4, at] = bsums[pair, 0:2]
    sums[4:5] = sums_two[2:3]
    sums[5:7] = sums_two[0:2]
    sums[7:8] = sums_two[3:4]
    vacc[...] = jnp.zeros_like(vacc)
    for zi in range(4):
        for yi in range(2):
            at = (zi * 2 + yi) * 128
            for xi in range(2):
                for ci in range(2):
                    i = ((zi * 2 + yi) * 2 + xi) * 2 + ci
                    piece = 2 * ((i % 16) // 4) + i // 16
                    vacc[ci, zi, yi, xi, 0:8] = sums[:, at : at + 128]
                    vacc[ci, zi, yi, xi, 8:9] = gbias[piece, 0:1, (i % 4) * 128 : (i % 4) * 128 + 128]
    vzero = _send(vacc.at[1 - core], v_s, vs.at[0], vr.at[0], sibling)
    reduce.after_plane(feeds + 1)
    reduce.after_line(feeds)
    vzero.wait()
    vmine = vacc.at[core]
    vmine[...] = vmine[...] + v_s[...]
    vone = _send(vmine.at[:, 1 - y, 1 - x], vx_one, vs.at[1], vr.at[1], across)
    reduce.after_plane(feeds + 2)
    vone.wait()
    vmine[:, 1 - y, x] = vmine[:, 1 - y, x] + vx_one[...]
    vtwo = [
        _send(vmine.at[:, y, 1 - x], vx_two, vs.at[2], vr.at[2], across),
        _send(vmine.at[:, 1 - y, x], vy_two, vs.at[3], vr.at[3], down),
    ]
    reduce.after_plane(feeds + 3)
    reduce.after_line(feeds + 1)
    reduce.wait(vtwo)
    vmine[:, y, x] = vmine[:, y, x] + vx_two[...] + vy_two[...]
    vthree = [
        _send(vmine.at[(z + j + 1) % 4, y, x], v_z.at[j], vs.at[4 + j], vr.at[4 + j], along[j]) for j in range(3)
    ]
    reduce.after_line(feeds + 2)
    reduce.after_line(feeds + 3)
    reduce.wait(vthree)
    vout[...] = vmine[z, y, x] + v_z[0] + v_z[1] + v_z[2]
    reduce.wait(final)


def back(lines, sums_two, gbias, early, qkv, mixed, probs, full, fullo, low, normed, x, gown, grecv):
    count = gown.shape[0] - EARLY + 4
    seq_len, model = x.shape
    rows, cols = gown.shape[-2:]
    half = seq_len // 2
    bf16, f32 = jnp.bfloat16, jnp.float32
    hbm = pl.BlockSpec(memory_space=pltpu.HBM)
    vmem = pl.BlockSpec(memory_space=pltpu.VMEM)
    dma = pltpu.SemaphoreType.DMA
    small = (16, 128)
    return pl.pallas_call(
        back_kernel,
        out_shape=(
            jax.ShapeDtypeStruct((count + EARLY, rows, cols), f32),
            jax.ShapeDtypeStruct(small, f32),
            jax.ShapeDtypeStruct((2, half, model), bf16),
            jax.ShapeDtypeStruct((4, 4, 2, 2, rows, cols), bf16),
        ),
        in_specs=[vmem] * 4 + [hbm] * 10,
        out_specs=(vmem, vmem, hbm, hbm),
        scratch_shapes=[
            pltpu.VMEM((RING, 4, 2, 2, rows, cols), bf16),
            pltpu.VMEM((2, 4, 2, 2, rows, cols), bf16),
            pltpu.VMEM((2, 4, 4, 2, 2, rows, cols), bf16),
            pltpu.VMEM((count, 4, rows // 2, cols), bf16),
            pltpu.VMEM((count, 4, rows // 2, cols), bf16),
            pltpu.VMEM((count, 4, rows, cols), bf16),
            pltpu.VMEM((count, 4, rows, cols), bf16),
            pltpu.VMEM((count, 3, rows, cols), bf16),
            pltpu.VMEM((2, 4, 2, 2) + small, f32),
            pltpu.VMEM((4, 2, 2) + small, f32),
            pltpu.VMEM((4,) + small, f32),
            pltpu.VMEM((4,) + small, f32),
            pltpu.VMEM((4,) + small, f32),
            pltpu.VMEM((3,) + small, f32),
            pltpu.VMEM((seq_len, model), bf16),
            pltpu.VMEM((seq_len, model), bf16),
            pltpu.VMEM((seq_len, model), f32),
            pltpu.VMEM((8, model), f32),
            pltpu.VMEM((4, 8, WIDE), f32),
            pltpu.VMEM((EARLY, 3, rows, cols), bf16),
            dma((EARLY, 3)),
            dma((EARLY, 3)),
            dma((count, 7)),
            dma((count, 7)),
            dma((2, 2)),
            dma((4,)),
            dma((4,)),
            dma((7,)),
            dma((7,)),
            dma((2, 9)),
            dma((2,)),
            dma((1,)),
            dma((1,)),
        ],
        compiler_params=pltpu.CompilerParams(
            collective_id=1, has_side_effects=True, vmem_limit_bytes=63 * MIB
        ),
    )(lines, sums_two, gbias, early, qkv, mixed, probs, full, fullo, low, normed, x, gown, grecv)


def finish_kernel(late, layer, ingrad, gq, gk, gv, go, up, down, layer_out, ingrad_out, held, wide, sem):
    moves = []
    parts = held.shape[1]
    for n, (source, target) in enumerate(((layer, layer_out), (ingrad, ingrad_out))):
        for i in range(parts):
            moves.append((_local(source.at[i], held.at[n, i], sem.at[0, n, i]), held.at[n, i], target.at[i], (n, i)))
    stores = []
    for fetch, here, target, (n, i) in moves:
        fetch.wait()
        wide[n, i] = here[...].astype(wide.dtype)
        stores.append(_local(wide.at[n, i], target, sem.at[1, n, i]))
    count = late.shape[0]
    pieces = (count - 4) // 2
    cols = late.shape[2]
    units = [late.at[i % count] for i in range(-EARLY, count - EARLY)]
    for piece in range(pieces):
        at = slice(piece * cols, (piece + 1) * cols)
        up[:, at] = units[2 * piece][...]
        down[:, at] = units[2 * piece + 1][...]
    for sub in range(2):
        at = slice(sub * WIDE, (sub + 1) * WIDE)
        first, second = units[2 * pieces + 2 * sub], units[2 * pieces + 2 * sub + 1]
        go[:, at] = first[:, 0:WIDE]
        gq[:, at] = first[:, WIDE : 2 * WIDE]
        gk[:, at] = second[:, 0:WIDE]
        gv[:, at] = second[:, WIDE : 2 * WIDE]
    for store in stores:
        store.wait()


def finish(late, layer, ingrad):
    rows, cols = late.shape[1:]
    wide = (late.shape[0] - 4) // 2 * cols
    vmem = pl.BlockSpec(memory_space=pltpu.VMEM)
    hbm = pl.BlockSpec(memory_space=pltpu.HBM)
    parts = (8, layer.shape[0] * layer.shape[1] // 8, layer.shape[2])
    whole = jax.ShapeDtypeStruct(parts, late.dtype)
    shapes = ((rows, cols),) * 4 + ((rows, wide),) * 2
    return pl.pallas_call(
        finish_kernel,
        out_shape=tuple(jax.ShapeDtypeStruct(s, late.dtype) for s in shapes) + (whole, whole),
        in_specs=[vmem] + [hbm] * 2,
        out_specs=(vmem,) * 6 + (hbm,) * 2,
        scratch_shapes=[pltpu.VMEM((2,) + parts, layer.dtype), pltpu.VMEM((2,) + parts, late.dtype), pltpu.SemaphoreType.DMA((2, 2, 8))],
        compiler_params=pltpu.CompilerParams(vmem_limit_bytes=63 * MIB),
    )(late, layer.reshape(parts), ingrad.reshape(parts))


def fast_body(
    inputs, prefix, ln1_gain, ln1_bias, query_weight, query_bias, key_weight, value_weight, value_bias,
    out_weight, out_bias, ln2_gain, ln2_bias, up_weight, up_bias, down_weight, down_bias, cotangent,
):
    core = lax.axis_index("tensor")
    half, model = inputs.shape[2], inputs.shape[3]
    rows, cols = query_weight.shape
    pieces = up_weight.shape[1] // cols

    small = jnp.stack([ln1_gain, ln1_bias, query_bias, value_bias, out_bias, ln2_gain, ln2_bias, down_bias])
    place = (lax.axis_index("dp") * 2 + core) % 4
    vec = jnp.pad(up_bias.reshape(1, 128), ((8, 7), (0, 0)))
    vec = lax.dynamic_update_slice(vec, small, (0, place * 32))
    (
        full, fullo, qkv, mixed, probs, normed, x, lines, layer_out, low, sums_two, gown, grecv, gup_bias,
        early,
    ) = front(
        prefix.reshape(-1), query_weight, key_weight, value_weight, out_weight.T, up_weight, down_weight.T, vec,
        inputs[:, 0], cotangent[:, 0],
    )
    out, vout, input_grad, _ = back(
        lines, sums_two, gup_bias, early, qkv, mixed, probs, full, fullo, low, normed, x,
        gown, grecv,
    )
    vectors = lax.dynamic_slice(vout, (0, place * 32), (8, 32))

    gq, gk, gv, gout, gup, gdown, layer_out, input_grad = finish(out, layer_out, input_grad)
    return (
        layer_out.reshape(2, 1, half, model),
        input_grad.reshape(2, 1, half, model),
        vectors[0],
        vectors[1],
        gq,
        vectors[2],
        gk,
        gv,
        vectors[3],
        gout.T,
        vectors[4],
        vectors[5],
        vectors[6],
        gup,
        vout[8],
        gdown.T,
        vectors[7],
    )


def solution(mesh):
    in_specs = (
        P(None, "dp", "tensor", None),
        P(None, "dp"),
        P(("dp", "tensor")),
        P(("dp", "tensor")),
        P("dp", "tensor"),
        P(("dp", "tensor")),
        P("dp", "tensor"),
        P("dp", "tensor"),
        P(("dp", "tensor")),
        P("tensor", "dp"),
        P(("dp", "tensor")),
        P(("dp", "tensor")),
        P(("dp", "tensor")),
        P("dp", "tensor"),
        P(("dp", "tensor")),
        P("tensor", "dp"),
        P(("dp", "tensor")),
        P(None, "dp", "tensor", None),
    )
    out_specs = (
        P(None, "dp", "tensor", None),
        P(None, "dp", "tensor", None),
        P(("dp", "tensor")),
        P(("dp", "tensor")),
        P("dp", "tensor"),
        P(("dp", "tensor")),
        P("dp", "tensor"),
        P("dp", "tensor"),
        P(("dp", "tensor")),
        P("tensor", "dp"),
        P(("dp", "tensor")),
        P(("dp", "tensor")),
        P(("dp", "tensor")),
        P("dp", "tensor"),
        P(("dp", "tensor")),
        P("tensor", "dp"),
        P(("dp", "tensor")),
    )
    sizes = (mesh.shape["dp"], mesh.shape["tensor"])
    chosen = fast_body if sizes == (16, 2) else body
    return jax.shard_map(chosen, mesh=mesh, in_specs=in_specs, out_specs=out_specs, check_vma=False)
```

```python
import math

import jax
import jax.numpy as jnp
from jax import lax
from jax.experimental import pallas as pl
from jax.experimental.pallas import tpu as pltpu
from jax.sharding import PartitionSpec as P

MESH = pl.DeviceIdType.MESH
LONGEST = 512

HEAD_DIM = 128
BLOCK = 512


EPSILON = 1e-05


def norm_forward(values, gain, shift):
    center = values - jnp.mean(values, axis=-1, keepdims=True)
    inverse = lax.rsqrt(jnp.mean(center * center, axis=-1, keepdims=True) + EPSILON)
    scaled = center * inverse
    return (scaled * gain + shift, scaled, inverse)


def norm_backward(grad_out, scaled, inverse, gain):
    weighted = grad_out * gain
    mean_plain = jnp.mean(weighted, axis=-1, keepdims=True)
    mean_scaled = jnp.mean(weighted * scaled, axis=-1, keepdims=True)
    return inverse * (weighted - mean_plain - scaled * mean_scaled)


def smooth_gate(values):
    return jax.nn.gelu(values, approximate=False)


def smooth_slope(values):
    normal_cdf = 0.5 * (1.0 + jax.scipy.special.erf(values / math.sqrt(2.0)))
    density = jnp.exp(-0.5 * values * values) / math.sqrt(2.0 * math.pi)
    return normal_cdf + values * density


def masked_scores(query_block, key_rows, start, prefix_len):
    scale = 1.0 / math.sqrt(key_rows.shape[2])
    scores = (
        jnp.einsum("qhd,khd->hqk", query_block, key_rows, preferred_element_type=jnp.float32)
        * scale
    )
    places = start + jnp.arange(query_block.shape[0], dtype=jnp.int32)
    columns = jnp.arange(key_rows.shape[0], dtype=jnp.int32)
    allowed = (columns[None, :] <= places[:, None]) | (columns[None, :] < prefix_len)
    return jnp.where(allowed[None], scores, -jnp.inf)


def attend_forward(queries, key_rows, value_rows, prefix_len):
    seq_len, heads_local, head_size = queries.shape
    count = seq_len // BLOCK

    def one_block(items):
        query_block, start = items
        scores = masked_scores(query_block, key_rows, start, prefix_len)
        peak = jnp.max(scores, axis=-1, keepdims=True)
        raw_weights = jnp.exp(scores - peak)
        totals = jnp.sum(raw_weights, axis=-1, keepdims=True)
        probs = (raw_weights / totals).astype(jnp.bfloat16)
        mixed = jnp.einsum("hqk,khd->qhd", probs, value_rows, preferred_element_type=jnp.float32)
        return (mixed.astype(jnp.bfloat16), (peak + jnp.log(totals))[..., 0])

    starts = jnp.arange(count, dtype=jnp.int32) * BLOCK
    mixed, log_totals = lax.map(
        one_block, (queries.reshape(count, BLOCK, heads_local, head_size), starts)
    )
    return (mixed.reshape(seq_len, heads_local * head_size), log_totals)


def attend_backward(queries, key_rows, value_rows, grad_mixed, log_totals, prefix_len):
    seq_len, heads_local, head_size = queries.shape
    count = seq_len // BLOCK
    scale = 1.0 / math.sqrt(head_size)

    def one_block(carry, items):
        key_total, value_total = carry
        query_block, grad_block, log_block, start = items
        scores = masked_scores(query_block, key_rows, start, prefix_len)
        probs = jnp.exp(scores - log_block[..., None])
        grad_probs = jnp.einsum(
            "qhd,khd->hqk", grad_block, value_rows, preferred_element_type=jnp.float32
        )
        inner = jnp.sum(probs * grad_probs, axis=-1, keepdims=True)
        grad_scores = (probs * (grad_probs - inner)).astype(jnp.bfloat16)
        grad_query = (
            jnp.einsum("hqk,khd->qhd", grad_scores, key_rows, preferred_element_type=jnp.float32)
            * scale
        )
        key_total = (
            key_total
            + jnp.einsum(
                "hqk,qhd->khd", grad_scores, query_block, preferred_element_type=jnp.float32
            )
            * scale
        )
        value_total = value_total + jnp.einsum(
            "hqk,qhd->khd",
            probs.astype(jnp.bfloat16),
            grad_block,
            preferred_element_type=jnp.float32,
        )
        return ((key_total, value_total), grad_query.astype(jnp.bfloat16))

    empty_total = jnp.zeros(queries.shape, jnp.float32)
    starts = jnp.arange(count, dtype=jnp.int32) * BLOCK
    blocked = (count, BLOCK, heads_local, head_size)
    (key_total, value_total), grad_queries = lax.scan(
        one_block,
        (empty_total, empty_total),
        (queries.reshape(blocked), grad_mixed.reshape(blocked), log_totals, starts),
    )
    width = heads_local * head_size
    return (
        grad_queries.reshape(seq_len, width),
        key_total.astype(jnp.bfloat16).reshape(seq_len, width),
        value_total.astype(jnp.bfloat16).reshape(seq_len, width),
    )


def body(
    inputs,
    prefix,
    ln1_gain,
    ln1_bias,
    query_weight,
    query_bias,
    key_weight,
    value_weight,
    value_bias,
    out_weight,
    out_bias,
    ln2_gain,
    ln2_bias,
    up_weight,
    up_bias,
    down_weight,
    down_bias,
    cotangent,
):
    local_width = query_weight.shape[1]
    local_hidden = up_weight.shape[1]
    shard_rows = inputs.shape[2]
    micro = inputs.shape[0]
    model_width = inputs.shape[3]
    heads_local = local_width // HEAD_DIM
    offset_width = lax.axis_index("tensor") * local_width
    offset_hidden = lax.axis_index("tensor") * local_hidden
    vectors = (
        lax.all_gather(ln1_gain, ("dp", "tensor"), axis=0, tiled=True),
        lax.all_gather(ln1_bias, ("dp", "tensor"), axis=0, tiled=True),
        lax.all_gather(query_bias, ("dp", "tensor"), axis=0, tiled=True),
        lax.all_gather(value_bias, ("dp", "tensor"), axis=0, tiled=True),
        lax.all_gather(out_bias, ("dp", "tensor"), axis=0, tiled=True),
        lax.all_gather(ln2_gain, ("dp", "tensor"), axis=0, tiled=True),
        lax.all_gather(ln2_bias, ("dp", "tensor"), axis=0, tiled=True),
        lax.all_gather(up_bias, ("dp", "tensor"), axis=0, tiled=True),
        lax.all_gather(down_bias, ("dp", "tensor"), axis=0, tiled=True),
    )
    (
        gain_one,
        shift_one,
        query_full_bias,
        value_full_bias,
        out_shift,
        gain_two,
        shift_two,
        up_full_bias,
        down_shift,
    ) = vectors
    query_shift = lax.dynamic_slice_in_dim(query_full_bias, offset_width, local_width)
    value_shift = lax.dynamic_slice_in_dim(value_full_bias, offset_width, local_width)
    up_shift = lax.dynamic_slice_in_dim(up_full_bias, offset_hidden, local_hidden)
    zero_width = jnp.zeros((model_width,), jnp.float32)
    gain_one_grad = zero_width
    shift_one_grad = zero_width
    query_bias_grad = zero_width
    value_bias_grad = zero_width
    out_bias_grad = zero_width
    gain_two_grad = zero_width
    shift_two_grad = zero_width
    up_bias_grad = jnp.zeros((up_full_bias.shape[0],), jnp.float32)
    down_bias_grad = zero_width
    weight_totals = None
    layer_rows = []
    input_rows = []
    for index in range(micro):
        gathered = (
            lax.all_gather(query_weight, "dp", axis=0, tiled=True),
            lax.all_gather(key_weight, "dp", axis=0, tiled=True),
            lax.all_gather(value_weight, "dp", axis=0, tiled=True),
            lax.all_gather(out_weight, "dp", axis=1, tiled=True),
            lax.all_gather(up_weight, "dp", axis=0, tiled=True),
            lax.all_gather(down_weight, "dp", axis=1, tiled=True),
        )
        full_query, full_key, full_value, full_out, full_up, full_down = gathered
        rows_in = inputs[index, 0].astype(jnp.float32)
        prefix_len = prefix[index, 0]
        normed, scaled_one, inverse_one = norm_forward(rows_in, gain_one, shift_one)
        normed_all = lax.all_gather(normed.astype(jnp.bfloat16), "tensor", axis=0, tiled=True)
        seq_len = normed_all.shape[0]
        queries = (
            jnp.dot(normed_all, full_query, preferred_element_type=jnp.float32) + query_shift
        ).astype(jnp.bfloat16)
        key_rows = jnp.dot(normed_all, full_key, preferred_element_type=jnp.float32).astype(
            jnp.bfloat16
        )
        value_rows = (
            jnp.dot(normed_all, full_value, preferred_element_type=jnp.float32) + value_shift
        ).astype(jnp.bfloat16)
        head_shape = (seq_len, heads_local, HEAD_DIM)
        queries_h = queries.reshape(head_shape)
        keys_h = key_rows.reshape(head_shape)
        values_h = value_rows.reshape(head_shape)
        attended, log_totals = attend_forward(queries_h, keys_h, values_h, prefix_len)
        attention_share = lax.psum_scatter(
            jnp.dot(attended, full_out, preferred_element_type=jnp.float32).astype(jnp.bfloat16),
            "tensor",
            scatter_dimension=0,
            tiled=True,
        ).astype(jnp.float32)
        residual = rows_in + attention_share + out_shift
        second, scaled_two, inverse_two = norm_forward(residual, gain_two, shift_two)
        grad_rows = cotangent[index, 0]
        down_bias_grad = down_bias_grad + jnp.sum(grad_rows.astype(jnp.float32), axis=0)
        second_all = lax.all_gather(second.astype(jnp.bfloat16), "tensor", axis=0, tiled=True)
        hidden_pre = jnp.dot(second_all, full_up, preferred_element_type=jnp.float32) + up_shift
        hidden_act = smooth_gate(hidden_pre).astype(jnp.bfloat16)
        feed_share = lax.psum_scatter(
            jnp.dot(hidden_act, full_down, preferred_element_type=jnp.float32).astype(jnp.bfloat16),
            "tensor",
            scatter_dimension=0,
            tiled=True,
        ).astype(jnp.float32)
        layer_rows.append(residual + feed_share + down_shift)
        grad_all = lax.all_gather(grad_rows, "tensor", axis=0, tiled=True)
        down_grad = jnp.dot(hidden_act.T, grad_all, preferred_element_type=jnp.float32)
        grad_act = jnp.dot(grad_all, full_down.T, preferred_element_type=jnp.float32)
        grad_pre = (grad_act * smooth_slope(hidden_pre)).astype(jnp.bfloat16)
        up_grad = jnp.dot(second_all.T, grad_pre, preferred_element_type=jnp.float32)
        up_part = jnp.sum(grad_pre.astype(jnp.float32), axis=0)
        up_bias_grad = up_bias_grad + lax.dynamic_update_slice(
            jnp.zeros_like(up_bias_grad), up_part, (offset_hidden,)
        )
        grad_second = lax.psum_scatter(
            jnp.dot(grad_pre, full_up.T, preferred_element_type=jnp.float32).astype(jnp.bfloat16),
            "tensor",
            scatter_dimension=0,
            tiled=True,
        ).astype(jnp.float32)
        gain_two_grad = gain_two_grad + jnp.sum(grad_second * scaled_two, axis=0)
        shift_two_grad = shift_two_grad + jnp.sum(grad_second, axis=0)
        grad_residual = grad_rows.astype(jnp.float32) + norm_backward(
            grad_second, scaled_two, inverse_two, gain_two
        )
        out_bias_grad = out_bias_grad + jnp.sum(grad_residual, axis=0)
        residual_all = lax.all_gather(
            grad_residual.astype(jnp.bfloat16), "tensor", axis=0, tiled=True
        )
        out_grad = jnp.dot(attended.T, residual_all, preferred_element_type=jnp.float32)
        grad_attended = jnp.dot(
            residual_all, full_out.T, preferred_element_type=jnp.float32
        ).astype(jnp.bfloat16)
        grad_queries, grad_keys, grad_values = attend_backward(
            queries_h, keys_h, values_h, grad_attended, log_totals, prefix_len
        )
        query_grad = jnp.dot(normed_all.T, grad_queries, preferred_element_type=jnp.float32)
        key_grad = jnp.dot(normed_all.T, grad_keys, preferred_element_type=jnp.float32)
        value_grad = jnp.dot(normed_all.T, grad_values, preferred_element_type=jnp.float32)
        query_part = jnp.sum(grad_queries.astype(jnp.float32), axis=0)
        value_part = jnp.sum(grad_values.astype(jnp.float32), axis=0)
        query_bias_grad = query_bias_grad + lax.dynamic_update_slice(
            zero_width, query_part, (offset_width,)
        )
        value_bias_grad = value_bias_grad + lax.dynamic_update_slice(
            zero_width, value_part, (offset_width,)
        )
        partial_sum = jnp.dot(grad_queries, full_query.T, preferred_element_type=jnp.float32)
        partial_sum = partial_sum + jnp.dot(
            grad_keys, full_key.T, preferred_element_type=jnp.float32
        )
        grad_normed = lax.psum_scatter(
            (
                partial_sum + jnp.dot(grad_values, full_value.T, preferred_element_type=jnp.float32)
            ).astype(jnp.bfloat16),
            "tensor",
            scatter_dimension=0,
            tiled=True,
        ).astype(jnp.float32)
        gain_one_grad = gain_one_grad + jnp.sum(grad_normed * scaled_one, axis=0)
        shift_one_grad = shift_one_grad + jnp.sum(grad_normed, axis=0)
        input_rows.append(
            grad_residual + norm_backward(grad_normed, scaled_one, inverse_one, gain_one)
        )
        reduced = (query_grad, key_grad, value_grad, out_grad, up_grad, down_grad)
        if weight_totals is None:
            weight_totals = reduced
        else:
            weight_totals = tuple((left + right for left, right in zip(weight_totals, reduced)))
    query_total, key_total, value_total, out_total, up_total, down_total = weight_totals
    query_total, key_total, value_total, out_total, up_total, down_total = (
        lax.psum_scatter(
            query_total.astype(jnp.bfloat16), "dp", scatter_dimension=0, tiled=True
        ).astype(jnp.float32),
        lax.psum_scatter(
            key_total.astype(jnp.bfloat16), "dp", scatter_dimension=0, tiled=True
        ).astype(jnp.float32),
        lax.psum_scatter(
            value_total.astype(jnp.bfloat16), "dp", scatter_dimension=0, tiled=True
        ).astype(jnp.float32),
        lax.psum_scatter(
            out_total.astype(jnp.bfloat16), "dp", scatter_dimension=1, tiled=True
        ).astype(jnp.float32),
        lax.psum_scatter(
            up_total.astype(jnp.bfloat16), "dp", scatter_dimension=0, tiled=True
        ).astype(jnp.float32),
        lax.psum_scatter(
            down_total.astype(jnp.bfloat16), "dp", scatter_dimension=1, tiled=True
        ).astype(jnp.float32),
    )
    vector_totals = (
        lax.psum_scatter(gain_one_grad, ("dp", "tensor"), scatter_dimension=0, tiled=True),
        lax.psum_scatter(shift_one_grad, ("dp", "tensor"), scatter_dimension=0, tiled=True),
        lax.psum_scatter(query_bias_grad, ("dp", "tensor"), scatter_dimension=0, tiled=True),
        lax.psum_scatter(value_bias_grad, ("dp", "tensor"), scatter_dimension=0, tiled=True),
        lax.psum_scatter(out_bias_grad, ("dp", "tensor"), scatter_dimension=0, tiled=True),
        lax.psum_scatter(gain_two_grad, ("dp", "tensor"), scatter_dimension=0, tiled=True),
        lax.psum_scatter(shift_two_grad, ("dp", "tensor"), scatter_dimension=0, tiled=True),
        lax.psum_scatter(up_bias_grad, ("dp", "tensor"), scatter_dimension=0, tiled=True),
        lax.psum_scatter(down_bias_grad, ("dp", "tensor"), scatter_dimension=0, tiled=True),
    )
    (
        gain_one_out,
        shift_one_out,
        query_bias_out,
        value_bias_out,
        out_bias_out,
        gain_two_out,
        shift_two_out,
        up_bias_out,
        down_bias_out,
    ) = vector_totals
    out_shape = (micro, 1, shard_rows, model_width)
    layer_out = jnp.stack(layer_rows).reshape(out_shape)
    input_grad = jnp.stack(input_rows).reshape(out_shape)
    return (
        layer_out,
        input_grad,
        gain_one_out,
        shift_one_out,
        query_total,
        query_bias_out,
        key_total,
        value_total,
        value_bias_out,
        out_total,
        out_bias_out,
        gain_two_out,
        shift_two_out,
        up_total,
        up_bias_out,
        down_total,
        down_bias_out,
    )


def _place(z, y, x):
    return z * 4 + y * 2 + x


def _coords():
    dp = lax.axis_index("dp")
    core = lax.axis_index("tensor")
    return dp // 4, (dp // 2) % 2, dp % 2, core


def _greet(peers):
    barrier = pltpu.get_barrier_semaphore()
    for peer in peers:
        pl.semaphore_signal(barrier, inc=1, device_id=peer, device_id_type=MESH)
    pl.semaphore_wait(barrier, len(peers))


def _peers():
    z, y, x, core = _coords()
    along = [(_place((z + j) % 4, y, x), core) for j in (1, 2, 3)]
    across = (_place(z, y, 1 - x), core)
    down = (_place(z, 1 - y, x), core)
    sibling = (_place(z, y, x), 1 - core)
    return along, across, down, sibling


def _send(src, dst, send_sem, recv_sem, peer):
    copy = pltpu.make_async_remote_copy(
        src_ref=src,
        dst_ref=dst,
        send_sem=send_sem,
        recv_sem=recv_sem,
        device_id=peer,
        device_id_type=MESH,
    )
    copy.start()
    return copy


def _local(src, dst, sem):
    copy = pltpu.make_async_copy(src, dst, sem)
    copy.start()
    return copy


def _dot(left, right, contract):
    return lax.dot_general(left, right, (contract, ((), ())), preferred_element_type=jnp.float32)


NN = ((1,), (0,))
NT = ((1,), (1,))
TN = ((0,), (0,))
LOG2E = 1.4426950408889634
MIB = 1024 * 1024
WIDE = 256


def _normal(values):
    center = values - jnp.mean(values, axis=-1, keepdims=True)
    inverse = lax.rsqrt(jnp.mean(center * center, axis=-1, keepdims=True) + EPSILON)
    return center * inverse, inverse


def _spans(seq_len, longest, step):
    return [(start, max(longest, start + step)) for start in range(0, seq_len, step)]


class Gather:
    def __init__(self, shards, places, send_sem, recv_sem, local_sem):
        self.z, self.y, self.x, self.core = _coords()
        self.along, self.across, self.down, self.sibling = _peers()
        self.shards, self.places, self.count = shards, places, len(shards)
        self.send_sem, self.recv_sem, self.local_sem = send_sem, recv_sem, local_sem

    def _remote(self, k, slot, src, dst, peer):
        return pltpu.make_async_remote_copy(
            src_ref=src,
            dst_ref=dst,
            send_sem=self.send_sem.at[k, slot],
            recv_sem=self.recv_sem.at[k, slot],
            device_id=peer,
            device_id_type=MESH,
        )

    def line(self, k):
        own = self.places[k].at[self.core, self.z, self.y, self.x]
        here = pltpu.make_async_copy(self.shards[k], own, self.local_sem.at[k])
        return [here] + [self._remote(k, j, self.shards[k], own, self.along[j]) for j in range(3)]

    def plane(self, k):
        block = self.places[k].at[self.core, :, self.y, self.x]
        return [self._remote(k, 3, block, block, self.across), self._remote(k, 4, block, block, self.down)]

    def corner(self, k):
        part = self.shards[k].shape[0] // 2
        one = self.places[k].at[self.core, :, 1 - self.y, self.x, 0:part]
        two = self.places[k].at[self.core, :, self.y, 1 - self.x, part : 2 * part]
        return [self._remote(k, 5, one, one, self.across), self._remote(k, 6, two, two, self.down)]

    def twin(self, k):
        block = self.places[k].at[self.core]
        return [self._remote(k, 7, block, block, self.sibling)]

    def near(self, k):
        own = self.places[k].at[self.core, self.z, self.y, self.x]
        here = pltpu.make_async_copy(self.shards[k], own, self.local_sem.at[k])
        src = self.shards[k]
        return [here, self._remote(k, 3, src, own, self.across), self._remote(k, 4, src, own, self.down)]

    def near_corner(self, k):
        part = self.shards[k].shape[0] // 2
        one = self.places[k].at[self.core, self.z, 1 - self.y, self.x, 0:part]
        two = self.places[k].at[self.core, self.z, self.y, 1 - self.x, part : 2 * part]
        return [self._remote(k, 5, one, one, self.across), self._remote(k, 6, two, two, self.down)]

    def far(self, k, i):
        block = self.places[k].at[self.core, self.z, i // 3]
        return [self._remote(k + i // 3, i % 3, block, block, self.along[i % 3])]

    def start(self, stage, k, *more):
        if 0 <= k < self.count and (more or k != self.count - 1 or stage in self.odd):
            for copy in stage(k, *more):
                copy.start()

    def wait(self, stage, k, *more):
        if 0 <= k < self.count and (more or k != self.count - 1 or stage in self.odd):
            for copy in stage(k, *more):
                copy.wait()

    @property
    def odd(self):
        return (self.near, self.near_corner)

    def last(self, step):
        k = self.count - 1
        if step == 0:
            self.start(self.near, k)
        if step == 1:
            self.wait(self.near, k)
            self.start(self.near_corner, k)
        if step == 2:
            self.wait(self.near_corner, k)
        if 2 <= step < 8:
            self.start(self.far, k, step - 2)
        if step == 9:
            for i in range(6):
                self.wait(self.far, k, i)
            self.twin(k)[0].start()
        if step == 20:
            self.twin(k)[0].wait()

    def tick(self, k, twin=True):
        self.last(k - 3)
        self.wait(self.plane, k)
        self.start(self.corner, k)
        self.wait(self.line, k + 2)
        self.start(self.plane, k + 2)
        self.start(self.line, k + 4)
        if twin:
            self.wait(self.corner, k - 1)
            self.start(self.twin, k - 1)


def _if(condition, action):
    if isinstance(condition, bool):
        if condition:
            action()
    else:
        pl.when(condition)(action)


class Reduce:
    def __init__(self, acc, out, x_one, y_one, x_two, y_two, from_z, send_sem, recv_sem):
        self.z, self.y, self.x, self.core = _coords()
        self.along, self.across, self.down, self.sibling = _peers()
        self.acc, self.out = acc, out
        self.x_one, self.y_one, self.x_two, self.y_two, self.from_z = x_one, y_one, x_two, y_two, from_z
        self.send_sem, self.recv_sem = send_sem, recv_sem

    def _remote(self, k, slot, src, dst, peer):
        return pltpu.make_async_remote_copy(
            src_ref=src,
            dst_ref=dst,
            send_sem=self.send_sem.at[k, slot],
            recv_sem=self.recv_sem.at[k, slot],
            device_id=peer,
            device_id_type=MESH,
        )

    def corner(self, k):
        block = self.acc(k).at[:, 1 - self.y, 1 - self.x]
        part = block.shape[1] // 2
        return [
            self._remote(k, 0, block.at[:, 0:part], self.x_one.at[k], self.across),
            self._remote(k, 1, block.at[:, part : 2 * part], self.y_one.at[k], self.down),
        ]

    def plane(self, k):
        acc = self.acc(k)
        return [
            self._remote(k, 2, acc.at[:, self.y, 1 - self.x], self.x_two.at[k], self.across),
            self._remote(k, 3, acc.at[:, 1 - self.y, self.x], self.y_two.at[k], self.down),
        ]

    def line(self, k):
        acc = self.acc(k)
        return [
            self._remote(k, 4 + j, acc.at[(self.z + j + 1) % 4, self.y, self.x], self.from_z.at[k, j], self.along[j])
            for j in range(3)
        ]

    @staticmethod
    def start(copies):
        for copy in copies:
            copy.start()

    @staticmethod
    def wait(copies):
        for copy in copies:
            copy.wait()

    def after_corner(self, k, go_on=True):
        acc, y, x = self.acc(k), self.y, self.x
        part = acc.shape[3] // 2
        self.wait(self.corner(k))
        one = acc.at[:, 1 - y, x, 0:part]
        two = acc.at[:, y, 1 - x, part : 2 * part]
        one[...] = _add(one[...], self.x_one[k])
        two[...] = _add(two[...], self.y_one[k])
        if go_on:
            self.start(self.plane(k))

    def after_plane(self, k):
        acc = self.acc(k)
        self.wait(self.plane(k))
        here = acc.at[:, self.y, self.x]
        here[...] = _add(here[...], self.x_two[k], self.y_two[k])
        self.start(self.line(k))

    def finish_plane(self, k, target):
        self.wait(self.plane(k))
        target[k] = _add(self.acc(k)[:, self.y, self.x], self.x_two[k], self.y_two[k])

    def after_line(self, k):
        self.wait(self.line(k))
        total = self.acc(k)[self.z, self.y, self.x].astype(self.out.dtype)
        for j in range(3):
            total = total + self.from_z[k, j].astype(self.out.dtype)
        self.out[k] = total


def _add(first, *others):
    if len(others) == 1:
        return first + others[0]
    total = first.astype(jnp.float32)
    for other in others:
        total = total + other.astype(jnp.float32)
    return total.astype(first.dtype)


def _combine(mine, other):
    @pl.loop(0, mine.shape[0])
    def _(i):
        for j in range(2):
            mine[i, j] = _add(mine[i, j], other[i, j])


EARLY = 2
BEGUN = 2
ATTEND_SITES = 3
ATTEND_TICKS = {4: 1, 5: 3, 7: 9}
FEED_TICKS = {9: 0, 10: 1, 11: 2, 12: 3, 13: 4, 14: 6}


def front_kernel(
    prefix, wq_in, wk_in, wv_in, wo_in, up_in, down_in, vec, xin, gin,
    full, fullo, qkv, mixed_out, probs_out, normed_out, x_out, lines, layer_out, low_out, sums, gown, grecv, gbias, early_out,
    vfull, x, grad, second, residual, weights, ubias,
    ssem, rsem, lsem, vs, vr, vl, ws, wr, wl, wsem, osem, fs, fr, fl, es, er, el,
    racc, rtheirs, x_one, y_one, x_two, y_two, rs, rr, rl,
):
    f32, bf16 = jnp.float32, jnp.bfloat16
    seq_len, model = x.shape
    half = seq_len // 2
    block = 128

    cols = wq_in.shape[1]
    shards = [w.at[:, sub * WIDE : (sub + 1) * WIDE] for sub in range(2) for w in (wq_in, wk_in, wv_in)] + [wo_in]
    places = [full.at[k] for k in range(6)] + [fullo]
    for piece in range(weights.shape[0] // 2):
        shards += [w.at[:, piece * cols : (piece + 1) * cols] for w in (up_in, down_in)]
        places += [weights.at[2 * piece], weights.at[2 * piece + 1]]
    early = len(shards) - weights.shape[0]
    gather = Gather(shards, places, ssem, rsem, lsem)
    reduce = Reduce(lambda k: racc.at[k], None, x_one, y_one, x_two, y_two, None, rs, rr)
    z, y, xx, core = gather.z, gather.y, gather.x, gather.core
    along, across, down, sibling = gather.along, gather.across, gather.down, gather.sibling
    _greet(along + [across, down, sibling])

    gather.start(gather.line, 0)
    vown = vfull.at[z, y, xx, core]
    vline = [_local(vec, vown, vl.at[0])] + [_send(vec, vown, vs.at[j], vr.at[j], along[j]) for j in range(3)]
    for k in (1, 2, 3):
        gather.start(gather.line, k)
    mine = pl.ds(pl.multiple_of(core * half, half), half)
    swaps = []
    for i, (part, whole) in enumerate(((xin, x), (gin, grad))):
        swaps.append(_local(part.at[core], whole.at[mine], wl.at[i]))
        swaps.append(_send(part.at[1 - core], whole.at[mine], ws.at[i], wr.at[i], sibling))
    gather.wait(gather.line, 0)
    gather.start(gather.plane, 0)
    for s in vline:
        s.wait()
    vblock = vfull.at[:, y, xx, core]
    vone = [_send(vblock, vblock, vs.at[3], vr.at[3], across), _send(vblock, vblock, vs.at[4], vr.at[4], down)]
    gather.wait(gather.line, 1)
    gather.start(gather.plane, 1)
    gather.tick(0)
    for s in vone:
        s.wait()
    vblock = vfull.at[:, 1 - y, xx, core]
    vtwo = _send(vblock, vblock, vs.at[5], vr.at[5], across)
    gather.tick(1)
    vtwo.wait()
    vblock = vfull.at[:, :, :, core]
    vthree = _send(vblock, vblock, vs.at[6], vr.at[6], sibling)
    for s in swaps:
        s.wait()
    saved = [_local(x, x_out, osem.at[0])]
    gather.tick(2)
    vthree.wait()
    for zi in range(4):
        for yi in range(2):
            at = (zi * 2 + yi) * 128
            group = vfull[zi, yi, 0, 0] + vfull[zi, yi, 0, 1] + vfull[zi, yi, 1, 0] + vfull[zi, yi, 1, 1]
            lines[:, at : at + 128] = group[0:8]
            for xi in range(2):
                for ci in range(2):
                    i = ((zi * 2 + yi) * 2 + xi) * 2 + ci
                    piece = 2 * ((i % 16) // 4) + i // 16
                    ubias[piece, 0:1, (i % 4) * 128 : (i % 4) * 128 + 128] = vfull[zi, yi, xi, ci, 8:9]

    def attention(normed, wblk, stage, mixed, wout, probs):
        @pl.loop(0, seq_len // block)
        def _(i):
            rows = pl.ds(pl.multiple_of(i * block, block), block)
            scaled, _ = _normal(x[rows].astype(f32))
            normed[rows] = (scaled * lines[0:1] + lines[1:2]).astype(bf16)

        gather.wait(gather.corner, 2)
        gather.start(gather.twin, 2)
        gather.tick(3, twin=False)
        keep = _local(normed, normed_out, osem.at[1])

        def side_of(pair):
            return (pair + core) % 2

        def load(pair):
            return [
                pltpu.make_async_copy(full.at[3 * (pair // 2) + i, side_of(pair)], wblk.at[pair % 2, i], wsem.at[pair % 2, i])
                for i in range(3)
            ]

        def store(pair):
            slot = pair % 2
            columns = pl.ds(pl.multiple_of((pair // 2) * WIDE, WIDE), WIDE)
            copies = [
                pltpu.make_async_copy(stage.at[slot, i], qkv.at[i, side_of(pair), :, columns], wsem.at[slot, 3 + i])
                for i in range(3)
            ]
            heads = pl.ds((side_of(pair) * 2 + pair // 2) * 2, 2)
            return copies + [pltpu.make_async_copy(probs.at[slot], probs_out.at[heads], wsem.at[slot, 6])]

        for c in load(0):
            c.start()

        def ticks(site, pair):
            for k, at in ATTEND_TICKS.items():
                if at % ATTEND_SITES == site:

                    @pl.when(pair == at // ATTEND_SITES)
                    def _(k=k):
                        gather.tick(k)

        @pl.loop(0, 4)
        def _(pair):
            slot = pair % 2
            for c in load(pair):
                c.wait()

            @pl.when(pair >= 2)
            def _():
                for c in store(pair - 2):
                    c.wait()

            ticks(0, pair)
            lanes = pl.ds(pl.multiple_of((side_of(pair) * 2 + pair // 2) * WIDE, WIDE), WIDE)
            wq, wk, wv = (wblk[slot, i].reshape(model, WIDE) for i in range(3))
            stage[slot, 0] = (_dot(normed[...], wq, NN) + lines[2:3, lanes]).astype(bf16)
            stage[slot, 1] = _dot(normed[...], wk, NN).astype(bf16)
            stage[slot, 2] = (_dot(normed[...], wv, NN) + lines[3:4, lanes]).astype(bf16)
            ticks(1, pair)
            for sub in range(2):

                @pl.when(pair == 2 * sub)
                def _(sub=sub):
                    for k in range(3 * sub, 3 * sub + 3):
                        gather.wait(gather.twin, k)
                    for c in load(2 * sub + 1):
                        c.start()

            step = 256
            factor = LOG2E / math.sqrt(HEAD_DIM)
            prefix_len = prefix[core]
            parts = [slice(h * HEAD_DIM, (h + 1) * HEAD_DIM) for h in range(WIDE // HEAD_DIM)]
            for head, part in enumerate(parts):
                for start, stop in _spans(seq_len, LONGEST, step):
                    scores = _dot(stage[slot, 1, :stop, part], stage[slot, 0, start : start + step, part], NT)
                    keys = lax.broadcasted_iota(jnp.int32, scores.shape, 0)
                    queries = lax.broadcasted_iota(jnp.int32, (1, step), 1) + start
                    scores = jnp.where(keys < jnp.maximum(queries + 1, prefix_len), scores, -jnp.inf)
                    peak = jnp.max(scores, axis=0, keepdims=True)
                    raw = jnp.exp2((scores - peak) * factor)
                    total = jnp.sum(raw, axis=0, keepdims=True)
                    probs[slot, head, :stop, start : start + step] = (raw * (1.0 / total)).astype(bf16)
            ticks(2, pair)
            bands = [(0, LONGEST)] + [(first, first + step) for first in range(LONGEST, seq_len, step)]
            for head, part in enumerate(parts):
                to = pl.ds(pl.multiple_of((pair // 2) * WIDE + head * HEAD_DIM, HEAD_DIM), HEAD_DIM)
                for first, last in bands:
                    mixed[side_of(pair), first:last, to] = _dot(
                        probs[slot, head, :last, first:last], stage[slot, 2, :last, part], TN
                    ).astype(bf16)
            for c in store(pair):
                c.start()

            @pl.when(pair == 1)
            def _():
                gather.tick(6)
                for c in load(2):
                    c.start()

        gather.tick(8)
        gather.wait(gather.twin, 6)
        fetch = _local(fullo, wout, osem.at[3])
        done = _local(mixed, mixed_out, osem.at[2])
        fetch.wait()
        weight = [wout[c].reshape(model, seq_len // 2) for c in range(2)]
        step = 256

        @pl.loop(0, seq_len // step)
        def _(i):
            rows = pl.ds(pl.multiple_of(i * step, step), step)
            branch = _dot(mixed[0, rows], weight[0], NT) + _dot(mixed[1, rows], weight[1], NT)
            total = x[rows].astype(f32) + branch + lines[4:5]
            residual[rows] = total
            scaled, _ = _normal(total)
            second[rows] = (scaled * lines[5:6] + lines[6:7]).astype(bf16)

        for pair in (2, 3):
            for c in store(pair):
                c.wait()
        done.wait()
        keep.wait()

    pl.run_scoped(
        attention,
        pltpu.VMEM((seq_len, model), bf16),
        pltpu.VMEM((2, 3, 4, 2, 2, 64, WIDE), bf16),
        pltpu.VMEM((2, 3, seq_len, WIDE), bf16),
        pltpu.VMEM((2, seq_len, model // 2), bf16),
        pltpu.VMEM((2, 4, 2, 2, 64, model // 2), bf16),
        pltpu.VMEM((2, 2, seq_len, seq_len), bf16),
    )

    def feed(layer, gres, stage, hid, gpre):
        pieces = weights.shape[0]

        @pl.loop(0, seq_len // block)
        def _(i):
            rows = pl.ds(pl.multiple_of(i * block, block), block)
            layer[rows] = residual[rows] + lines[7:8]
            gres[rows] = jnp.zeros((block, model), f32)

        def away(piece):
            return [
                pltpu.make_async_remote_copy(
                    src_ref=stage.at[1, i],
                    dst_ref=grecv.at[2 * piece + i],
                    send_sem=fs.at[piece, i],
                    recv_sem=fr.at[piece, i],
                    device_id=sibling,
                    device_id_type=MESH,
                )
                for i in range(2)
            ]

        def stay(piece):
            return [pltpu.make_async_copy(stage.at[0, i], gown.at[2 * piece + i], fl.at[i]) for i in range(2)]

        def bring(k):
            return [
                pltpu.make_async_copy(gown.at[k], racc.at[k], rl.at[k % 2, 0]),
                pltpu.make_async_copy(grecv.at[k], rtheirs.at[k % 2], rl.at[k % 2, 1]),
            ]

        @pl.loop(0, pieces)
        def _(t):
            piece, turn = t // 2, t % 2
            side = (t + core) % 2
            for k, at in FEED_TICKS.items():

                @pl.when(t == at)
                def _(k=k):
                    gather.tick(k)

            for p in range(pieces // 2):

                @pl.when(t == 2 * p + 1)
                def _(p=p):
                    gather.wait(gather.twin, early + 2 * p)
                    if p < pieces // 2 - 1:
                        gather.wait(gather.twin, early + 2 * p + 1)
                    else:
                        gather.last(20)

            @pl.when(t == pieces - 3)
            def _():
                for p in range((EARLY + BEGUN) // 2):
                    for c in away(p):
                        c.wait_recv()
                reduce.start(bring(0) + bring(1))

            for at in range(2):

                @pl.when(t == pieces - 2 + at)
                def _(at=at):
                    for k in (2 * at, 2 * at + 1):
                        reduce.wait(bring(k))
                        _combine(racc.at[k], rtheirs.at[k % 2])
                        reduce.start(reduce.corner(k))
                        if at == 0:
                            reduce.start(bring(k + 2))

            @pl.when(t == pieces - 1)
            def _():
                for k in range(EARLY):
                    reduce.after_corner(k)

            @pl.when((t >= 2) & (turn == 1))
            def _():
                for c in away(piece - 1):
                    c.wait_send()

            @pl.when((t >= 2) & (turn == 0))
            def _():
                for c in stay(piece - 1):
                    c.wait()

            up = weights[2 * piece, side].reshape(model, model // 2)
            lower = weights[2 * piece + 1, side].reshape(model, model // 2)
            line = 2 * piece + side
            pre = _dot(second[...], up, NN) + ubias[line]
            phi = 0.5 * (1.0 + lax.erf(pre * (1.0 / math.sqrt(2.0))))
            density = jnp.exp2(pre * pre * (-0.5 * LOG2E)) * (1.0 / math.sqrt(2.0 * math.pi))
            hid[...] = (pre * phi).astype(bf16)
            slope = phi + pre * density
            back = (_dot(grad[...], lower, NN) * slope).astype(bf16)
            gpre[...] = back
            gbias[line] = jnp.sum(back.astype(f32), axis=0, keepdims=True)
            layer[...] += _dot(hid[...], lower, NT)
            gres[...] += _dot(gpre[...], up, NT)
            blocks = stage.shape[2:]
            stage[turn, 0] = _dot(second[...], gpre[...], TN).astype(bf16).reshape(blocks)
            stage[turn, 1] = _dot(grad[...], hid[...], TN).astype(bf16).reshape(blocks)

            @pl.when(turn == 1)
            def _():
                for c in away(piece):
                    c.start()

            @pl.when(turn == 0)
            def _():
                for c in stay(piece):
                    c.start()

        for s in saved:
            s.wait()

        @pl.loop(0, seq_len // block)
        def _(i):
            rows = pl.ds(pl.multiple_of(i * block, block), block)
            x[rows] = layer[rows].astype(bf16)

        theirs = pl.ds(pl.multiple_of((1 - core) * half, half), half)
        final = [
            _local(x.at[mine], layer_out.at[core], el.at[0]),
            _send(x.at[theirs], layer_out.at[core], es.at[0], er.at[0], sibling),
        ]
        sums[...] = jnp.zeros_like(sums)

        @pl.loop(0, seq_len // block)
        def _(i):
            rows = pl.ds(pl.multiple_of(i * block, block), block)
            scaled, inverse = _normal(residual[rows])
            grow = gres[rows]
            upstream = grad[rows].astype(f32)
            weighted = grow * lines[5:6]
            mean_plain = jnp.mean(weighted, axis=-1, keepdims=True)
            mean_scaled = jnp.mean(weighted * scaled, axis=-1, keepdims=True)
            total = upstream + inverse * (weighted - mean_plain - scaled * mean_scaled)
            second[rows] = total.astype(bf16)
            sums[0:1] += jnp.sum(grow * scaled, axis=0, keepdims=True)
            sums[1:2] += jnp.sum(grow, axis=0, keepdims=True)
            sums[2:3] += jnp.sum(total, axis=0, keepdims=True)
            sums[3:4] += jnp.sum(upstream, axis=0, keepdims=True)

        final.append(_local(second, low_out, el.at[2]))
        for k in range(EARLY, EARLY + BEGUN):
            reduce.after_corner(k, go_on=False)
            final.append(_local(racc.at[k], gown.at[k], rl.at[k % 2, 0]))
        for k in range(EARLY):
            reduce.finish_plane(k, early_out)
        last = pieces // 2 - 1
        for c in away(last):
            c.wait_send()
        for c in stay(last):
            c.wait()
        for p in range((EARLY + BEGUN) // 2, pieces // 2):
            for c in away(p):
                c.wait_recv()
        for c in final:
            c.wait()

    pl.run_scoped(
        feed,
        pltpu.VMEM((seq_len, model), f32),
        pltpu.VMEM((seq_len, model), f32),
        pltpu.VMEM((2, 2, 4, 2, 2, model // 16, model // 2), bf16),
        pltpu.VMEM((seq_len, model // 2), bf16),
        pltpu.VMEM((seq_len, model // 2), bf16),
    )


def front(prefix_len, wq, wk, wv, wo, up, down, vec, xin, gin):
    rows, cols = wq.shape
    half, model = xin.shape[1:]
    seq_len = 2 * half
    pieces = 2 * (up.shape[1] // cols)
    chunks = 7 + pieces
    bf16, f32 = jnp.bfloat16, jnp.float32
    hbm = pl.BlockSpec(memory_space=pltpu.HBM)
    vmem = pl.BlockSpec(memory_space=pltpu.VMEM)
    dma = pltpu.SemaphoreType.DMA

    def shape(dims, dtype):
        return jax.ShapeDtypeStruct(dims, dtype)

    heads = model // HEAD_DIM
    return pl.pallas_call(
        front_kernel,
        out_shape=(
            shape((6, 2, 4, 2, 2, rows, WIDE), bf16),
            shape((2, 4, 2, 2, rows, cols), bf16),
            shape((3, 2, seq_len, cols), bf16),
            shape((2, seq_len, cols), bf16),
            shape((heads, seq_len, seq_len), bf16),
            shape((seq_len, model), bf16),
            shape((seq_len, model), bf16),
            shape((8, model), f32),
            shape((2, half, model), bf16),
            shape((seq_len, model), bf16),
            shape((8, model), f32),
            shape((pieces, 4, 2, 2, rows, cols), bf16),
            shape((pieces, 4, 2, 2, rows, cols), bf16),
            shape((pieces, 1, cols), f32),
            shape((EARLY, 4, rows, cols), bf16),
        ),
        in_specs=[pl.BlockSpec(memory_space=pltpu.SMEM)] + [vmem] * 7 + [hbm, hbm],
        out_specs=(hbm, hbm, hbm, hbm, hbm, hbm, hbm, vmem, hbm, hbm, vmem, hbm, hbm, vmem, vmem),
        scratch_shapes=[
            pltpu.VMEM((4, 2, 2, 2) + vec.shape, f32),
            pltpu.VMEM((seq_len, model), bf16),
            pltpu.VMEM((seq_len, model), bf16),
            pltpu.VMEM((seq_len, model), bf16),
            pltpu.VMEM((seq_len, model), f32),
            pltpu.VMEM((pieces, 2, 4, 2, 2, rows, cols), bf16),
            pltpu.VMEM((pieces, 1, cols), f32),
            dma((chunks + 1, 8)),
            dma((chunks + 1, 8)),
            dma((chunks,)),
            dma((7,)),
            dma((7,)),
            dma((1,)),
            dma((2,)),
            dma((2,)),
            dma((2,)),
            dma((2, 7)),
            dma((4,)),
            dma((pieces // 2, 2)),
            dma((pieces // 2, 2)),
            dma((2,)),
            dma((1,)),
            dma((1,)),
            dma((3,)),
            pltpu.VMEM((EARLY + BEGUN, 4, 2, 2, rows, cols), bf16),
            pltpu.VMEM((2, 4, 2, 2, rows, cols), bf16),
            pltpu.VMEM((EARLY + BEGUN, 4, rows // 2, cols), bf16),
            pltpu.VMEM((EARLY + BEGUN, 4, rows // 2, cols), bf16),
            pltpu.VMEM((EARLY, 4, rows, cols), bf16),
            pltpu.VMEM((EARLY, 4, rows, cols), bf16),
            dma((EARLY + BEGUN, 7)),
            dma((EARLY + BEGUN, 7)),
            dma((2, 2)),
        ],
        compiler_params=pltpu.CompilerParams(
            collective_id=0, has_side_effects=True, vmem_limit_bytes=63 * MIB
        ),
    )(prefix_len, wq, wk, wv, wo, up, down, vec, xin, gin)


RING = 6
UNIT_SITES = (
    (("begin", 2),),
    (("begin", 3), ("corner", 2), ("plane", 0)),
    (("begin", 4), ("corner", 3), ("plane", 1), ("line", 0)),
    (("begin", 5), ("corner", 4), ("plane", 2), ("line", 1)),
    (("corner", 5), ("plane", 3), ("line", 2)),
    (("plane", 4), ("line", 3)),
    (("begin", 6), ("plane", 5), ("line", 4)),
    (("begin", 7), ("corner", 6), ("line", 5)),
)


def back_kernel(
    lines, sums_two, gbias, early, qkv, mixed_in, probs_in, full, fullo, low_in, normed_in, x_in, gown, grecv,
    out, vout, iout, qrecv,
    ring, theirs_in, gbuf, x_one, y_one, x_two, y_two, from_z,
    vacc, v_s, vx_one, vx_two, vy_two, v_z,
    low, normed, ingrad, sums, bsums,
    from_e, esend, erecv, ssem, rsem, lsem, qs, qr, vs, vr, bsem, msem, es, er,
):
    f32, bf16 = jnp.float32, jnp.bfloat16
    seq_len, model = low.shape
    half, block, step = seq_len // 2, 128, 256
    feeds = gown.shape[0] - EARLY
    count = out.shape[0] - EARLY
    scale = 1.0 / math.sqrt(HEAD_DIM)

    own = gbuf.at[1]

    def acc(k):
        return own.at[k - feeds] if isinstance(k, int) and k >= feeds else ring.at[k % RING]

    reduce = Reduce(acc, out, x_one, y_one, x_two, y_two, from_z, ssem, rsem)
    z, y, x, core = reduce.z, reduce.y, reduce.x, reduce.core
    along, across, down, sibling = reduce.along, reduce.across, reduce.down, reduce.sibling

    def load(k):
        if isinstance(k, int) and k >= feeds:
            return [pltpu.make_async_copy(qrecv.at[k - feeds], theirs_in.at[k % 2], lsem.at[k % 2, 1])]
        copies = [pltpu.make_async_copy(gown.at[EARLY + k], ring.at[k % RING], lsem.at[k % 2, 0])]
        if k >= BEGUN:
            copies.append(pltpu.make_async_copy(grecv.at[EARLY + k], theirs_in.at[k % 2], lsem.at[k % 2, 1]))
        return copies

    def begin(k):
        reduce.wait(load(k))
        _combine(acc(k), theirs_in.at[k % 2])
        reduce.start(reduce.corner(k))

    for k in range(BEGUN):
        reduce.start(load(k))
    start = [_local(low_in, low, msem.at[0]), _local(normed_in, normed, msem.at[1])]
    _greet(along + [across, down, sibling])
    for k in range(BEGUN):
        reduce.wait(load(k))
        reduce.start(reduce.plane(k))
        reduce.start(load(BEGUN + k))
    lines_first = [
        _send(early.at[k, (z + j + 1) % 4], from_e.at[k, j], esend.at[k, j], erecv.at[k, j], along[j])
        for k in range(EARLY)
        for j in range(3)
    ]

    def away(sub, i):
        unit = sub * 2 + i
        return pltpu.make_async_remote_copy(
            src_ref=gbuf.at[0, unit],
            dst_ref=qrecv.at[unit],
            send_sem=qs.at[unit],
            recv_sem=qr.at[unit],
            device_id=sibling,
            device_id_type=MESH,
        )

    def landed(unit):
        away(unit // 2, unit % 2).wait_recv()

    stages = {
        "begin": begin,
        "corner": reduce.after_corner,
        "plane": reduce.after_plane,
        "line": reduce.after_line,
    }

    def retreat(heads_in, probs, wblk, dq, dk, dv, dmix):
        def fetch(i):
            turn, sub = i // 2, i % 2
            side = (turn + 1 + core) % 2
            columns = pl.ds(pl.multiple_of(sub * WIDE, WIDE), WIDE)
            slot = i % 2
            copies = [
                pltpu.make_async_copy(qkv.at[n, side, :, columns], heads_in.at[slot, n], bsem.at[slot, n])
                for n in range(3)
            ]
            copies.append(pltpu.make_async_copy(mixed_in.at[side, :, columns], heads_in.at[slot, 3], bsem.at[slot, 3]))
            copies += [
                pltpu.make_async_copy(full.at[3 * sub + n, side], wblk.at[slot, n], bsem.at[slot, 4 + n])
                for n in range(3)
            ]
            copies.append(
                pltpu.make_async_copy(fullo.at[side, :, :, :, :, columns], wblk.at[slot, 3], bsem.at[slot, 7])
            )
            heads = pl.ds((side * 2 + sub) * 2, 2)
            copies.append(pltpu.make_async_copy(probs_in.at[heads], probs.at[slot], bsem.at[slot, 8]))
            return copies

        reduce.start(fetch(0))

        @pl.loop(0, seq_len // block)
        def _(i):
            ingrad[pl.ds(pl.multiple_of(i * block, block), block)] = jnp.zeros((block, model), f32)

        reduce.wait(start)

        @pl.loop(0, 4)
        def _(i):
            turn, sub, slot = i // 2, i % 2, i % 2
            side = (turn + 1 + core) % 2
            reduce.wait(fetch(i))

            @pl.when(i < 3)
            def _():
                reduce.start(fetch(i + 1))

            columns = pl.ds(pl.multiple_of(sub * WIDE, WIDE), WIDE)

            def put(n, value):
                at = slice((n % 2) * WIDE, (n % 2 + 1) * WIDE)
                gbuf[turn, sub * 2 + n // 2, :, :, :, :, at] = value.astype(bf16).reshape(4, 2, 2, model // 16, WIDE)

            def site(n):
                for at in range(4):

                    @pl.when(i == at)
                    def _(at=at):
                        if 2 * at + n == feeds:
                            for u in range(2):
                                landed(u)
                                reduce.start(load(feeds + u))
                        for stage, k in UNIT_SITES[2 * at + n]:
                            stages[stage](k)
                            if stage == "begin" and k + 2 < feeds:
                                reduce.start(load(k + 2))

            site(0)
            wq, wk, wv, wo = (wblk[slot, n].reshape(model, WIDE) for n in range(4))
            dmix[...] = _dot(low[...], wo, NN).astype(bf16)
            put(0, _dot(low[...], heads_in[slot, 3], TN))
            parts = [slice(h * HEAD_DIM, (h + 1) * HEAD_DIM) for h in range(WIDE // HEAD_DIM)]
            spans = _spans(seq_len, LONGEST, step)
            bands = [(0, LONGEST)] + [(first, first + step) for first in range(LONGEST, seq_len, step)]
            for head, part in enumerate(parts):
                for low_key, high_key in bands:
                    dv[low_key:high_key, part] = _dot(
                        probs[slot, head, low_key:high_key, low_key:], dmix[low_key:, part], NN
                    ).astype(bf16)
            for head, part in enumerate(parts):
                for first, stop in spans:
                    block_at = (slot, head, slice(0, stop), slice(first, first + step))
                    weights = probs[block_at].astype(f32)
                    dprobs = _dot(heads_in[slot, 2, :stop, part], dmix[first : first + step, part], NT)
                    inner = jnp.sum(weights * dprobs, axis=0, keepdims=True)
                    probs[block_at] = (weights * (dprobs - inner)).astype(bf16)
            site(1)
            for head, part in enumerate(parts):
                for low_key, high_key in bands:
                    dk[low_key:high_key, part] = (
                        _dot(probs[slot, head, low_key:high_key, low_key:], heads_in[slot, 0, low_key:, part], NN)
                        * scale
                    ).astype(bf16)
                for first, last in bands:
                    dq[first:last, part] = (
                        _dot(probs[slot, head, :last, first:last], heads_in[slot, 1, :last, part], TN) * scale
                    ).astype(bf16)
            put(1, _dot(normed[...], dq[...], TN))
            put(2, _dot(normed[...], dk[...], TN))
            put(3, _dot(normed[...], dv[...], TN))
            ingrad[...] += _dot(dq[...], wq, NT) + _dot(dk[...], wk, NT) + _dot(dv[...], wv, NT)

            @pl.when(turn == 0)
            def _():
                for n in range(2):
                    away(sub, n).start()

            at = side * 2 + sub
            bsums[at, 0:1] = jnp.sum(dq[...].astype(f32), axis=0, keepdims=True)
            bsums[at, 1:2] = jnp.sum(dv[...].astype(f32), axis=0, keepdims=True)

        for sub in range(2):
            for n in range(2):
                away(sub, n).wait_send()

    pl.run_scoped(
        retreat,
        pltpu.VMEM((2, 4, seq_len, WIDE), bf16),
        pltpu.VMEM((2, 2, seq_len, seq_len), bf16),
        pltpu.VMEM((2, 4, 4, 2, 2, model // 16, WIDE), bf16),
        pltpu.VMEM((seq_len, WIDE), bf16),
        pltpu.VMEM((seq_len, WIDE), bf16),
        pltpu.VMEM((seq_len, WIDE), bf16),
        pltpu.VMEM((seq_len, WIDE), bf16),
    )

    reduce.wait(lines_first)
    for k in range(EARLY):
        total = early[k, z].astype(f32)
        for j in range(3):
            total = total + from_e[k, j].astype(f32)
        out[count + k] = total

    def finish(xs):
        bring = [_local(x_in, xs, msem.at[1])]
        for unit in (2, 3):
            landed(unit)
            reduce.start(load(feeds + unit))
        begin(feeds + 2)
        begin(feeds + 3)
        reduce.after_corner(feeds + 1)
        reduce.after_plane(feeds)
        reduce.after_corner(feeds + 2)
        reduce.after_corner(feeds + 3)
        reduce.wait(bring)
        sums[...] = jnp.zeros_like(sums)

        @pl.loop(0, seq_len // block)
        def _(i):
            rows = pl.ds(pl.multiple_of(i * block, block), block)
            scaled, inverse = _normal(xs[rows].astype(f32))
            grow = ingrad[rows]
            weighted = grow * lines[0:1]
            mean_plain = jnp.mean(weighted, axis=-1, keepdims=True)
            mean_scaled = jnp.mean(weighted * scaled, axis=-1, keepdims=True)
            total = low[rows].astype(f32) + inverse * (weighted - mean_plain - scaled * mean_scaled)
            normed[rows] = total.astype(bf16)
            sums[0:1] += jnp.sum(grow * scaled, axis=0, keepdims=True)
            sums[1:2] += jnp.sum(grow, axis=0, keepdims=True)

    pl.run_scoped(finish, pltpu.VMEM((seq_len, model), bf16))
    mine = pl.ds(pl.multiple_of(core * half, half), half)
    theirs = pl.ds(pl.multiple_of((1 - core) * half, half), half)
    final = [
        _local(normed.at[mine], iout.at[core], msem.at[0]),
        _send(normed.at[theirs], iout.at[core], es.at[0], er.at[0], sibling),
    ]
    for pair in range(4):
        at = slice(pair * WIDE, (pair + 1) * WIDE)
        sums[2:4, at] = bsums[pair, 0:2]
    sums[4:5] = sums_two[2:3]
    sums[5:7] = sums_two[0:2]
    sums[7:8] = sums_two[3:4]
    vacc[...] = jnp.zeros_like(vacc)
    for zi in range(4):
        for yi in range(2):
            at = (zi * 2 + yi) * 128
            for xi in range(2):
                for ci in range(2):
                    i = ((zi * 2 + yi) * 2 + xi) * 2 + ci
                    piece = 2 * ((i % 16) // 4) + i // 16
                    vacc[ci, zi, yi, xi, 0:8] = sums[:, at : at + 128]
                    vacc[ci, zi, yi, xi, 8:9] = gbias[piece, 0:1, (i % 4) * 128 : (i % 4) * 128 + 128]
    vzero = _send(vacc.at[1 - core], v_s, vs.at[0], vr.at[0], sibling)
    reduce.after_plane(feeds + 1)
    reduce.after_line(feeds)
    vzero.wait()
    vmine = vacc.at[core]
    vmine[...] = vmine[...] + v_s[...]
    vone = _send(vmine.at[:, 1 - y, 1 - x], vx_one, vs.at[1], vr.at[1], across)
    reduce.after_plane(feeds + 2)
    vone.wait()
    vmine[:, 1 - y, x] = vmine[:, 1 - y, x] + vx_one[...]
    vtwo = [
        _send(vmine.at[:, y, 1 - x], vx_two, vs.at[2], vr.at[2], across),
        _send(vmine.at[:, 1 - y, x], vy_two, vs.at[3], vr.at[3], down),
    ]
    reduce.after_plane(feeds + 3)
    reduce.after_line(feeds + 1)
    reduce.wait(vtwo)
    vmine[:, y, x] = vmine[:, y, x] + vx_two[...] + vy_two[...]
    vthree = [
        _send(vmine.at[(z + j + 1) % 4, y, x], v_z.at[j], vs.at[4 + j], vr.at[4 + j], along[j]) for j in range(3)
    ]
    reduce.after_line(feeds + 2)
    reduce.after_line(feeds + 3)
    reduce.wait(vthree)
    vout[...] = vmine[z, y, x] + v_z[0] + v_z[1] + v_z[2]
    reduce.wait(final)


def back(lines, sums_two, gbias, early, qkv, mixed, probs, full, fullo, low, normed, x, gown, grecv):
    count = gown.shape[0] - EARLY + 4
    seq_len, model = x.shape
    rows, cols = gown.shape[-2:]
    half = seq_len // 2
    bf16, f32 = jnp.bfloat16, jnp.float32
    hbm = pl.BlockSpec(memory_space=pltpu.HBM)
    vmem = pl.BlockSpec(memory_space=pltpu.VMEM)
    dma = pltpu.SemaphoreType.DMA
    small = (16, 128)
    return pl.pallas_call(
        back_kernel,
        out_shape=(
            jax.ShapeDtypeStruct((count + EARLY, rows, cols), f32),
            jax.ShapeDtypeStruct(small, f32),
            jax.ShapeDtypeStruct((2, half, model), bf16),
            jax.ShapeDtypeStruct((4, 4, 2, 2, rows, cols), bf16),
        ),
        in_specs=[vmem] * 4 + [hbm] * 10,
        out_specs=(vmem, vmem, hbm, hbm),
        scratch_shapes=[
            pltpu.VMEM((RING, 4, 2, 2, rows, cols), bf16),
            pltpu.VMEM((2, 4, 2, 2, rows, cols), bf16),
            pltpu.VMEM((2, 4, 4, 2, 2, rows, cols), bf16),
            pltpu.VMEM((count, 4, rows // 2, cols), bf16),
            pltpu.VMEM((count, 4, rows // 2, cols), bf16),
            pltpu.VMEM((count, 4, rows, cols), bf16),
            pltpu.VMEM((count, 4, rows, cols), bf16),
            pltpu.VMEM((count, 3, rows, cols), bf16),
            pltpu.VMEM((2, 4, 2, 2) + small, f32),
            pltpu.VMEM((4, 2, 2) + small, f32),
            pltpu.VMEM((4,) + small, f32),
            pltpu.VMEM((4,) + small, f32),
            pltpu.VMEM((4,) + small, f32),
            pltpu.VMEM((3,) + small, f32),
            pltpu.VMEM((seq_len, model), bf16),
            pltpu.VMEM((seq_len, model), bf16),
            pltpu.VMEM((seq_len, model), f32),
            pltpu.VMEM((8, model), f32),
            pltpu.VMEM((4, 8, WIDE), f32),
            pltpu.VMEM((EARLY, 3, rows, cols), bf16),
            dma((EARLY, 3)),
            dma((EARLY, 3)),
            dma((count, 7)),
            dma((count, 7)),
            dma((2, 2)),
            dma((4,)),
            dma((4,)),
            dma((7,)),
            dma((7,)),
            dma((2, 9)),
            dma((2,)),
            dma((1,)),
            dma((1,)),
        ],
        compiler_params=pltpu.CompilerParams(
            collective_id=1, has_side_effects=True, vmem_limit_bytes=63 * MIB
        ),
    )(lines, sums_two, gbias, early, qkv, mixed, probs, full, fullo, low, normed, x, gown, grecv)


def finish_kernel(late, layer, ingrad, gq, gk, gv, go, up, down, layer_out, ingrad_out, held, wide, sem):
    moves = []
    parts = held.shape[1]
    for n, (source, target) in enumerate(((layer, layer_out), (ingrad, ingrad_out))):
        for i in range(parts):
            moves.append((_local(source.at[i], held.at[n, i], sem.at[0, n, i]), held.at[n, i], target.at[i], (n, i)))
    stores = []
    for fetch, here, target, (n, i) in moves:
        fetch.wait()
        wide[n, i] = here[...].astype(wide.dtype)
        stores.append(_local(wide.at[n, i], target, sem.at[1, n, i]))
    count = late.shape[0]
    pieces = (count - 4) // 2
    cols = late.shape[2]
    units = [late.at[i % count] for i in range(-EARLY, count - EARLY)]
    for piece in range(pieces):
        at = slice(piece * cols, (piece + 1) * cols)
        up[:, at] = units[2 * piece][...]
        down[:, at] = units[2 * piece + 1][...]
    for sub in range(2):
        at = slice(sub * WIDE, (sub + 1) * WIDE)
        first, second = units[2 * pieces + 2 * sub], units[2 * pieces + 2 * sub + 1]
        go[:, at] = first[:, 0:WIDE]
        gq[:, at] = first[:, WIDE : 2 * WIDE]
        gk[:, at] = second[:, 0:WIDE]
        gv[:, at] = second[:, WIDE : 2 * WIDE]
    for store in stores:
        store.wait()


def finish(late, layer, ingrad):
    rows, cols = late.shape[1:]
    wide = (late.shape[0] - 4) // 2 * cols
    vmem = pl.BlockSpec(memory_space=pltpu.VMEM)
    hbm = pl.BlockSpec(memory_space=pltpu.HBM)
    parts = (8, layer.shape[0] * layer.shape[1] // 8, layer.shape[2])
    whole = jax.ShapeDtypeStruct(parts, late.dtype)
    shapes = ((rows, cols),) * 4 + ((rows, wide),) * 2
    return pl.pallas_call(
        finish_kernel,
        out_shape=tuple(jax.ShapeDtypeStruct(s, late.dtype) for s in shapes) + (whole, whole),
        in_specs=[vmem] + [hbm] * 2,
        out_specs=(vmem,) * 6 + (hbm,) * 2,
        scratch_shapes=[pltpu.VMEM((2,) + parts, layer.dtype), pltpu.VMEM((2,) + parts, late.dtype), pltpu.SemaphoreType.DMA((2, 2, 8))],
        compiler_params=pltpu.CompilerParams(vmem_limit_bytes=63 * MIB),
    )(late, layer.reshape(parts), ingrad.reshape(parts))


def fast_body(
    inputs, prefix, ln1_gain, ln1_bias, query_weight, query_bias, key_weight, value_weight, value_bias,
    out_weight, out_bias, ln2_gain, ln2_bias, up_weight, up_bias, down_weight, down_bias, cotangent,
):
    core = lax.axis_index("tensor")
    half, model = inputs.shape[2], inputs.shape[3]
    rows, cols = query_weight.shape
    pieces = up_weight.shape[1] // cols

    small = jnp.stack([ln1_gain, ln1_bias, query_bias, value_bias, out_bias, ln2_gain, ln2_bias, down_bias])
    place = (lax.axis_index("dp") * 2 + core) % 4
    vec = jnp.pad(up_bias.reshape(1, 128), ((8, 7), (0, 0)))
    vec = lax.dynamic_update_slice(vec, small, (0, place * 32))
    (
        full, fullo, qkv, mixed, probs, normed, x, lines, layer_out, low, sums_two, gown, grecv, gup_bias,
        early,
    ) = front(
        prefix.reshape(-1), query_weight, key_weight, value_weight, out_weight.T, up_weight, down_weight.T, vec,
        inputs[:, 0], cotangent[:, 0],
    )
    out, vout, input_grad, _ = back(
        lines, sums_two, gup_bias, early, qkv, mixed, probs, full, fullo, low, normed, x,
        gown, grecv,
    )
    vectors = lax.dynamic_slice(vout, (0, place * 32), (8, 32))

    gq, gk, gv, gout, gup, gdown, layer_out, input_grad = finish(out, layer_out, input_grad)
    return (
        layer_out.reshape(2, 1, half, model),
        input_grad.reshape(2, 1, half, model),
        vectors[0],
        vectors[1],
        gq,
        vectors[2],
        gk,
        gv,
        vectors[3],
        gout.T,
        vectors[4],
        vectors[5],
        vectors[6],
        gup,
        vout[8],
        gdown.T,
        vectors[7],
    )


def solution(mesh):
    in_specs = (
        P(None, "dp", "tensor", None),
        P(None, "dp"),
        P(("dp", "tensor")),
        P(("dp", "tensor")),
        P("dp", "tensor"),
        P(("dp", "tensor")),
        P("dp", "tensor"),
        P("dp", "tensor"),
        P(("dp", "tensor")),
        P("tensor", "dp"),
        P(("dp", "tensor")),
        P(("dp", "tensor")),
        P(("dp", "tensor")),
        P("dp", "tensor"),
        P(("dp", "tensor")),
        P("tensor", "dp"),
        P(("dp", "tensor")),
        P(None, "dp", "tensor", None),
    )
    out_specs = (
        P(None, "dp", "tensor", None),
        P(None, "dp", "tensor", None),
        P(("dp", "tensor")),
        P(("dp", "tensor")),
        P("dp", "tensor"),
        P(("dp", "tensor")),
        P("dp", "tensor"),
        P("dp", "tensor"),
        P(("dp", "tensor")),
        P("tensor", "dp"),
        P(("dp", "tensor")),
        P(("dp", "tensor")),
        P(("dp", "tensor")),
        P("dp", "tensor"),
        P(("dp", "tensor")),
        P("tensor", "dp"),
        P(("dp", "tensor")),
    )
    sizes = (mesh.shape["dp"], mesh.shape["tensor"])
    chosen = fast_body if sizes == (16, 2) else body
    return jax.shard_map(chosen, mesh=mesh, in_specs=in_specs, out_specs=out_specs, check_vma=False)
```

```python
import math

import jax
import jax.numpy as jnp
from jax import lax
from jax.experimental import pallas as pl
from jax.experimental.pallas import tpu as pltpu
from jax.sharding import PartitionSpec as P

MESH = pl.DeviceIdType.MESH
LONGEST = 512

HEAD_DIM = 128
BLOCK = 512


EPSILON = 1e-05


def norm_forward(values, gain, shift):
    center = values - jnp.mean(values, axis=-1, keepdims=True)
    inverse = lax.rsqrt(jnp.mean(center * center, axis=-1, keepdims=True) + EPSILON)
    scaled = center * inverse
    return (scaled * gain + shift, scaled, inverse)


def norm_backward(grad_out, scaled, inverse, gain):
    weighted = grad_out * gain
    mean_plain = jnp.mean(weighted, axis=-1, keepdims=True)
    mean_scaled = jnp.mean(weighted * scaled, axis=-1, keepdims=True)
    return inverse * (weighted - mean_plain - scaled * mean_scaled)


def smooth_gate(values):
    return jax.nn.gelu(values, approximate=False)


def smooth_slope(values):
    normal_cdf = 0.5 * (1.0 + jax.scipy.special.erf(values / math.sqrt(2.0)))
    density = jnp.exp(-0.5 * values * values) / math.sqrt(2.0 * math.pi)
    return normal_cdf + values * density


def masked_scores(query_block, key_rows, start, prefix_len):
    scale = 1.0 / math.sqrt(key_rows.shape[2])
    scores = (
        jnp.einsum("qhd,khd->hqk", query_block, key_rows, preferred_element_type=jnp.float32)
        * scale
    )
    places = start + jnp.arange(query_block.shape[0], dtype=jnp.int32)
    columns = jnp.arange(key_rows.shape[0], dtype=jnp.int32)
    allowed = (columns[None, :] <= places[:, None]) | (columns[None, :] < prefix_len)
    return jnp.where(allowed[None], scores, -jnp.inf)


def attend_forward(queries, key_rows, value_rows, prefix_len):
    seq_len, heads_local, head_size = queries.shape
    count = seq_len // BLOCK

    def one_block(items):
        query_block, start = items
        scores = masked_scores(query_block, key_rows, start, prefix_len)
        peak = jnp.max(scores, axis=-1, keepdims=True)
        raw_weights = jnp.exp(scores - peak)
        totals = jnp.sum(raw_weights, axis=-1, keepdims=True)
        probs = (raw_weights / totals).astype(jnp.bfloat16)
        mixed = jnp.einsum("hqk,khd->qhd", probs, value_rows, preferred_element_type=jnp.float32)
        return (mixed.astype(jnp.bfloat16), (peak + jnp.log(totals))[..., 0])

    starts = jnp.arange(count, dtype=jnp.int32) * BLOCK
    mixed, log_totals = lax.map(
        one_block, (queries.reshape(count, BLOCK, heads_local, head_size), starts)
    )
    return (mixed.reshape(seq_len, heads_local * head_size), log_totals)


def attend_backward(queries, key_rows, value_rows, grad_mixed, log_totals, prefix_len):
    seq_len, heads_local, head_size = queries.shape
    count = seq_len // BLOCK
    scale = 1.0 / math.sqrt(head_size)

    def one_block(carry, items):
        key_total, value_total = carry
        query_block, grad_block, log_block, start = items
        scores = masked_scores(query_block, key_rows, start, prefix_len)
        probs = jnp.exp(scores - log_block[..., None])
        grad_probs = jnp.einsum(
            "qhd,khd->hqk", grad_block, value_rows, preferred_element_type=jnp.float32
        )
        inner = jnp.sum(probs * grad_probs, axis=-1, keepdims=True)
        grad_scores = (probs * (grad_probs - inner)).astype(jnp.bfloat16)
        grad_query = (
            jnp.einsum("hqk,khd->qhd", grad_scores, key_rows, preferred_element_type=jnp.float32)
            * scale
        )
        key_total = (
            key_total
            + jnp.einsum(
                "hqk,qhd->khd", grad_scores, query_block, preferred_element_type=jnp.float32
            )
            * scale
        )
        value_total = value_total + jnp.einsum(
            "hqk,qhd->khd",
            probs.astype(jnp.bfloat16),
            grad_block,
            preferred_element_type=jnp.float32,
        )
        return ((key_total, value_total), grad_query.astype(jnp.bfloat16))

    empty_total = jnp.zeros(queries.shape, jnp.float32)
    starts = jnp.arange(count, dtype=jnp.int32) * BLOCK
    blocked = (count, BLOCK, heads_local, head_size)
    (key_total, value_total), grad_queries = lax.scan(
        one_block,
        (empty_total, empty_total),
        (queries.reshape(blocked), grad_mixed.reshape(blocked), log_totals, starts),
    )
    width = heads_local * head_size
    return (
        grad_queries.reshape(seq_len, width),
        key_total.astype(jnp.bfloat16).reshape(seq_len, width),
        value_total.astype(jnp.bfloat16).reshape(seq_len, width),
    )


def body(
    inputs,
    prefix,
    ln1_gain,
    ln1_bias,
    query_weight,
    query_bias,
    key_weight,
    value_weight,
    value_bias,
    out_weight,
    out_bias,
    ln2_gain,
    ln2_bias,
    up_weight,
    up_bias,
    down_weight,
    down_bias,
    cotangent,
):
    local_width = query_weight.shape[1]
    local_hidden = up_weight.shape[1]
    shard_rows = inputs.shape[2]
    micro = inputs.shape[0]
    model_width = inputs.shape[3]
    heads_local = local_width // HEAD_DIM
    offset_width = lax.axis_index("tensor") * local_width
    offset_hidden = lax.axis_index("tensor") * local_hidden
    vectors = (
        lax.all_gather(ln1_gain, ("dp", "tensor"), axis=0, tiled=True),
        lax.all_gather(ln1_bias, ("dp", "tensor"), axis=0, tiled=True),
        lax.all_gather(query_bias, ("dp", "tensor"), axis=0, tiled=True),
        lax.all_gather(value_bias, ("dp", "tensor"), axis=0, tiled=True),
        lax.all_gather(out_bias, ("dp", "tensor"), axis=0, tiled=True),
        lax.all_gather(ln2_gain, ("dp", "tensor"), axis=0, tiled=True),
        lax.all_gather(ln2_bias, ("dp", "tensor"), axis=0, tiled=True),
        lax.all_gather(up_bias, ("dp", "tensor"), axis=0, tiled=True),
        lax.all_gather(down_bias, ("dp", "tensor"), axis=0, tiled=True),
    )
    (
        gain_one,
        shift_one,
        query_full_bias,
        value_full_bias,
        out_shift,
        gain_two,
        shift_two,
        up_full_bias,
        down_shift,
    ) = vectors
    query_shift = lax.dynamic_slice_in_dim(query_full_bias, offset_width, local_width)
    value_shift = lax.dynamic_slice_in_dim(value_full_bias, offset_width, local_width)
    up_shift = lax.dynamic_slice_in_dim(up_full_bias, offset_hidden, local_hidden)
    zero_width = jnp.zeros((model_width,), jnp.float32)
    gain_one_grad = zero_width
    shift_one_grad = zero_width
    query_bias_grad = zero_width
    value_bias_grad = zero_width
    out_bias_grad = zero_width
    gain_two_grad = zero_width
    shift_two_grad = zero_width
    up_bias_grad = jnp.zeros((up_full_bias.shape[0],), jnp.float32)
    down_bias_grad = zero_width
    weight_totals = None
    layer_rows = []
    input_rows = []
    for index in range(micro):
        gathered = (
            lax.all_gather(query_weight, "dp", axis=0, tiled=True),
            lax.all_gather(key_weight, "dp", axis=0, tiled=True),
            lax.all_gather(value_weight, "dp", axis=0, tiled=True),
            lax.all_gather(out_weight, "dp", axis=1, tiled=True),
            lax.all_gather(up_weight, "dp", axis=0, tiled=True),
            lax.all_gather(down_weight, "dp", axis=1, tiled=True),
        )
        full_query, full_key, full_value, full_out, full_up, full_down = gathered
        rows_in = inputs[index, 0].astype(jnp.float32)
        prefix_len = prefix[index, 0]
        normed, scaled_one, inverse_one = norm_forward(rows_in, gain_one, shift_one)
        normed_all = lax.all_gather(normed.astype(jnp.bfloat16), "tensor", axis=0, tiled=True)
        seq_len = normed_all.shape[0]
        queries = (
            jnp.dot(normed_all, full_query, preferred_element_type=jnp.float32) + query_shift
        ).astype(jnp.bfloat16)
        key_rows = jnp.dot(normed_all, full_key, preferred_element_type=jnp.float32).astype(
            jnp.bfloat16
        )
        value_rows = (
            jnp.dot(normed_all, full_value, preferred_element_type=jnp.float32) + value_shift
        ).astype(jnp.bfloat16)
        head_shape = (seq_len, heads_local, HEAD_DIM)
        queries_h = queries.reshape(head_shape)
        keys_h = key_rows.reshape(head_shape)
        values_h = value_rows.reshape(head_shape)
        attended, log_totals = attend_forward(queries_h, keys_h, values_h, prefix_len)
        attention_share = lax.psum_scatter(
            jnp.dot(attended, full_out, preferred_element_type=jnp.float32).astype(jnp.bfloat16),
            "tensor",
            scatter_dimension=0,
            tiled=True,
        ).astype(jnp.float32)
        residual = rows_in + attention_share + out_shift
        second, scaled_two, inverse_two = norm_forward(residual, gain_two, shift_two)
        grad_rows = cotangent[index, 0]
        down_bias_grad = down_bias_grad + jnp.sum(grad_rows.astype(jnp.float32), axis=0)
        second_all = lax.all_gather(second.astype(jnp.bfloat16), "tensor", axis=0, tiled=True)
        hidden_pre = jnp.dot(second_all, full_up, preferred_element_type=jnp.float32) + up_shift
        hidden_act = smooth_gate(hidden_pre).astype(jnp.bfloat16)
        feed_share = lax.psum_scatter(
            jnp.dot(hidden_act, full_down, preferred_element_type=jnp.float32).astype(jnp.bfloat16),
            "tensor",
            scatter_dimension=0,
            tiled=True,
        ).astype(jnp.float32)
        layer_rows.append(residual + feed_share + down_shift)
        grad_all = lax.all_gather(grad_rows, "tensor", axis=0, tiled=True)
        down_grad = jnp.dot(hidden_act.T, grad_all, preferred_element_type=jnp.float32)
        grad_act = jnp.dot(grad_all, full_down.T, preferred_element_type=jnp.float32)
        grad_pre = (grad_act * smooth_slope(hidden_pre)).astype(jnp.bfloat16)
        up_grad = jnp.dot(second_all.T, grad_pre, preferred_element_type=jnp.float32)
        up_part = jnp.sum(grad_pre.astype(jnp.float32), axis=0)
        up_bias_grad = up_bias_grad + lax.dynamic_update_slice(
            jnp.zeros_like(up_bias_grad), up_part, (offset_hidden,)
        )
        grad_second = lax.psum_scatter(
            jnp.dot(grad_pre, full_up.T, preferred_element_type=jnp.float32).astype(jnp.bfloat16),
            "tensor",
            scatter_dimension=0,
            tiled=True,
        ).astype(jnp.float32)
        gain_two_grad = gain_two_grad + jnp.sum(grad_second * scaled_two, axis=0)
        shift_two_grad = shift_two_grad + jnp.sum(grad_second, axis=0)
        grad_residual = grad_rows.astype(jnp.float32) + norm_backward(
            grad_second, scaled_two, inverse_two, gain_two
        )
        out_bias_grad = out_bias_grad + jnp.sum(grad_residual, axis=0)
        residual_all = lax.all_gather(
            grad_residual.astype(jnp.bfloat16), "tensor", axis=0, tiled=True
        )
        out_grad = jnp.dot(attended.T, residual_all, preferred_element_type=jnp.float32)
        grad_attended = jnp.dot(
            residual_all, full_out.T, preferred_element_type=jnp.float32
        ).astype(jnp.bfloat16)
        grad_queries, grad_keys, grad_values = attend_backward(
            queries_h, keys_h, values_h, grad_attended, log_totals, prefix_len
        )
        query_grad = jnp.dot(normed_all.T, grad_queries, preferred_element_type=jnp.float32)
        key_grad = jnp.dot(normed_all.T, grad_keys, preferred_element_type=jnp.float32)
        value_grad = jnp.dot(normed_all.T, grad_values, preferred_element_type=jnp.float32)
        query_part = jnp.sum(grad_queries.astype(jnp.float32), axis=0)
        value_part = jnp.sum(grad_values.astype(jnp.float32), axis=0)
        query_bias_grad = query_bias_grad + lax.dynamic_update_slice(
            zero_width, query_part, (offset_width,)
        )
        value_bias_grad = value_bias_grad + lax.dynamic_update_slice(
            zero_width, value_part, (offset_width,)
        )
        partial_sum = jnp.dot(grad_queries, full_query.T, preferred_element_type=jnp.float32)
        partial_sum = partial_sum + jnp.dot(
            grad_keys, full_key.T, preferred_element_type=jnp.float32
        )
        grad_normed = lax.psum_scatter(
            (
                partial_sum + jnp.dot(grad_values, full_value.T, preferred_element_type=jnp.float32)
            ).astype(jnp.bfloat16),
            "tensor",
            scatter_dimension=0,
            tiled=True,
        ).astype(jnp.float32)
        gain_one_grad = gain_one_grad + jnp.sum(grad_normed * scaled_one, axis=0)
        shift_one_grad = shift_one_grad + jnp.sum(grad_normed, axis=0)
        input_rows.append(
            grad_residual + norm_backward(grad_normed, scaled_one, inverse_one, gain_one)
        )
        reduced = (query_grad, key_grad, value_grad, out_grad, up_grad, down_grad)
        if weight_totals is None:
            weight_totals = reduced
        else:
            weight_totals = tuple((left + right for left, right in zip(weight_totals, reduced)))
    query_total, key_total, value_total, out_total, up_total, down_total = weight_totals
    query_total, key_total, value_total, out_total, up_total, down_total = (
        lax.psum_scatter(
            query_total.astype(jnp.bfloat16), "dp", scatter_dimension=0, tiled=True
        ).astype(jnp.float32),
        lax.psum_scatter(
            key_total.astype(jnp.bfloat16), "dp", scatter_dimension=0, tiled=True
        ).astype(jnp.float32),
        lax.psum_scatter(
            value_total.astype(jnp.bfloat16), "dp", scatter_dimension=0, tiled=True
        ).astype(jnp.float32),
        lax.psum_scatter(
            out_total.astype(jnp.bfloat16), "dp", scatter_dimension=1, tiled=True
        ).astype(jnp.float32),
        lax.psum_scatter(
            up_total.astype(jnp.bfloat16), "dp", scatter_dimension=0, tiled=True
        ).astype(jnp.float32),
        lax.psum_scatter(
            down_total.astype(jnp.bfloat16), "dp", scatter_dimension=1, tiled=True
        ).astype(jnp.float32),
    )
    vector_totals = (
        lax.psum_scatter(gain_one_grad, ("dp", "tensor"), scatter_dimension=0, tiled=True),
        lax.psum_scatter(shift_one_grad, ("dp", "tensor"), scatter_dimension=0, tiled=True),
        lax.psum_scatter(query_bias_grad, ("dp", "tensor"), scatter_dimension=0, tiled=True),
        lax.psum_scatter(value_bias_grad, ("dp", "tensor"), scatter_dimension=0, tiled=True),
        lax.psum_scatter(out_bias_grad, ("dp", "tensor"), scatter_dimension=0, tiled=True),
        lax.psum_scatter(gain_two_grad, ("dp", "tensor"), scatter_dimension=0, tiled=True),
        lax.psum_scatter(shift_two_grad, ("dp", "tensor"), scatter_dimension=0, tiled=True),
        lax.psum_scatter(up_bias_grad, ("dp", "tensor"), scatter_dimension=0, tiled=True),
        lax.psum_scatter(down_bias_grad, ("dp", "tensor"), scatter_dimension=0, tiled=True),
    )
    (
        gain_one_out,
        shift_one_out,
        query_bias_out,
        value_bias_out,
        out_bias_out,
        gain_two_out,
        shift_two_out,
        up_bias_out,
        down_bias_out,
    ) = vector_totals
    out_shape = (micro, 1, shard_rows, model_width)
    layer_out = jnp.stack(layer_rows).reshape(out_shape)
    input_grad = jnp.stack(input_rows).reshape(out_shape)
    return (
        layer_out,
        input_grad,
        gain_one_out,
        shift_one_out,
        query_total,
        query_bias_out,
        key_total,
        value_total,
        value_bias_out,
        out_total,
        out_bias_out,
        gain_two_out,
        shift_two_out,
        up_total,
        up_bias_out,
        down_total,
        down_bias_out,
    )


def _place(z, y, x):
    return z * 4 + y * 2 + x


def _coords():
    dp = lax.axis_index("dp")
    core = lax.axis_index("tensor")
    return dp // 4, (dp // 2) % 2, dp % 2, core


def _greet(peers):
    barrier = pltpu.get_barrier_semaphore()
    for peer in peers:
        pl.semaphore_signal(barrier, inc=1, device_id=peer, device_id_type=MESH)
    pl.semaphore_wait(barrier, len(peers))


def _peers():
    z, y, x, core = _coords()
    along = [(_place((z + j) % 4, y, x), core) for j in (1, 2, 3)]
    across = (_place(z, y, 1 - x), core)
    down = (_place(z, 1 - y, x), core)
    sibling = (_place(z, y, x), 1 - core)
    return along, across, down, sibling


def _send(src, dst, send_sem, recv_sem, peer):
    copy = pltpu.make_async_remote_copy(
        src_ref=src,
        dst_ref=dst,
        send_sem=send_sem,
        recv_sem=recv_sem,
        device_id=peer,
        device_id_type=MESH,
    )
    copy.start()
    return copy


def _local(src, dst, sem):
    copy = pltpu.make_async_copy(src, dst, sem)
    copy.start()
    return copy


def _dot(left, right, contract):
    return lax.dot_general(left, right, (contract, ((), ())), preferred_element_type=jnp.float32)


NN = ((1,), (0,))
NT = ((1,), (1,))
TN = ((0,), (0,))
LOG2E = 1.4426950408889634
MIB = 1024 * 1024
WIDE = 256


def _normal(values):
    center = values - jnp.mean(values, axis=-1, keepdims=True)
    inverse = lax.rsqrt(jnp.mean(center * center, axis=-1, keepdims=True) + EPSILON)
    return center * inverse, inverse


def _spans(seq_len, longest, step):
    return [(start, max(longest, start + step)) for start in range(0, seq_len, step)]


class Gather:
    def __init__(self, shards, places, send_sem, recv_sem, local_sem):
        self.z, self.y, self.x, self.core = _coords()
        self.along, self.across, self.down, self.sibling = _peers()
        self.shards, self.places, self.count = shards, places, len(shards)
        self.send_sem, self.recv_sem, self.local_sem = send_sem, recv_sem, local_sem

    def _remote(self, k, slot, src, dst, peer):
        return pltpu.make_async_remote_copy(
            src_ref=src,
            dst_ref=dst,
            send_sem=self.send_sem.at[k, slot],
            recv_sem=self.recv_sem.at[k, slot],
            device_id=peer,
            device_id_type=MESH,
        )

    def line(self, k):
        own = self.places[k].at[self.core, self.z, self.y, self.x]
        here = pltpu.make_async_copy(self.shards[k], own, self.local_sem.at[k])
        return [here] + [self._remote(k, j, self.shards[k], own, self.along[j]) for j in range(3)]

    def plane(self, k):
        block = self.places[k].at[self.core, :, self.y, self.x]
        return [self._remote(k, 3, block, block, self.across), self._remote(k, 4, block, block, self.down)]

    def corner(self, k):
        part = self.shards[k].shape[0] // 2
        one = self.places[k].at[self.core, :, 1 - self.y, self.x, 0:part]
        two = self.places[k].at[self.core, :, self.y, 1 - self.x, part : 2 * part]
        return [self._remote(k, 5, one, one, self.across), self._remote(k, 6, two, two, self.down)]

    def twin(self, k):
        block = self.places[k].at[self.core]
        return [self._remote(k, 7, block, block, self.sibling)]

    def near(self, k):
        own = self.places[k].at[self.core, self.z, self.y, self.x]
        here = pltpu.make_async_copy(self.shards[k], own, self.local_sem.at[k])
        src = self.shards[k]
        return [here, self._remote(k, 3, src, own, self.across), self._remote(k, 4, src, own, self.down)]

    def near_corner(self, k):
        part = self.shards[k].shape[0] // 2
        one = self.places[k].at[self.core, self.z, 1 - self.y, self.x, 0:part]
        two = self.places[k].at[self.core, self.z, self.y, 1 - self.x, part : 2 * part]
        return [self._remote(k, 5, one, one, self.across), self._remote(k, 6, two, two, self.down)]

    def far(self, k, i):
        block = self.places[k].at[self.core, self.z, i // 3]
        return [self._remote(k + i // 3, i % 3, block, block, self.along[i % 3])]

    def start(self, stage, k, *more):
        if 0 <= k < self.count and (more or k != self.count - 1 or stage in self.odd):
            for copy in stage(k, *more):
                copy.start()

    def wait(self, stage, k, *more):
        if 0 <= k < self.count and (more or k != self.count - 1 or stage in self.odd):
            for copy in stage(k, *more):
                copy.wait()

    @property
    def odd(self):
        return (self.near, self.near_corner)

    def last(self, step):
        k = self.count - 1
        if step == 0:
            self.start(self.near, k)
        if step == 1:
            self.wait(self.near, k)
            self.start(self.near_corner, k)
        if step == 2:
            self.wait(self.near_corner, k)
        if 2 <= step < 8:
            self.start(self.far, k, step - 2)
        if step == 9:
            for i in range(6):
                self.wait(self.far, k, i)
            self.twin(k)[0].start()
        if step == 20:
            self.twin(k)[0].wait()

    def tick(self, k, twin=True):
        self.last(k - 3)
        self.wait(self.plane, k)
        self.start(self.corner, k)
        self.wait(self.line, k + 2)
        self.start(self.plane, k + 2)
        self.start(self.line, k + 4)
        if twin:
            self.wait(self.corner, k - 1)
            self.start(self.twin, k - 1)


def _if(condition, action):
    if isinstance(condition, bool):
        if condition:
            action()
    else:
        pl.when(condition)(action)


class Reduce:
    def __init__(self, acc, out, x_one, y_one, x_two, y_two, from_z, send_sem, recv_sem):
        self.z, self.y, self.x, self.core = _coords()
        self.along, self.across, self.down, self.sibling = _peers()
        self.acc, self.out = acc, out
        self.x_one, self.y_one, self.x_two, self.y_two, self.from_z = x_one, y_one, x_two, y_two, from_z
        self.send_sem, self.recv_sem = send_sem, recv_sem

    def _remote(self, k, slot, src, dst, peer):
        return pltpu.make_async_remote_copy(
            src_ref=src,
            dst_ref=dst,
            send_sem=self.send_sem.at[k, slot],
            recv_sem=self.recv_sem.at[k, slot],
            device_id=peer,
            device_id_type=MESH,
        )

    def corner(self, k):
        block = self.acc(k).at[:, 1 - self.y, 1 - self.x]
        part = block.shape[1] // 2
        return [
            self._remote(k, 0, block.at[:, 0:part], self.x_one.at[k], self.across),
            self._remote(k, 1, block.at[:, part : 2 * part], self.y_one.at[k], self.down),
        ]

    def plane(self, k):
        acc = self.acc(k)
        return [
            self._remote(k, 2, acc.at[:, self.y, 1 - self.x], self.x_two.at[k], self.across),
            self._remote(k, 3, acc.at[:, 1 - self.y, self.x], self.y_two.at[k], self.down),
        ]

    def line(self, k):
        acc = self.acc(k)
        return [
            self._remote(k, 4 + j, acc.at[(self.z + j + 1) % 4, self.y, self.x], self.from_z.at[k, j], self.along[j])
            for j in range(3)
        ]

    @staticmethod
    def start(copies):
        for copy in copies:
            copy.start()

    @staticmethod
    def wait(copies):
        for copy in copies:
            copy.wait()

    def after_corner(self, k, go_on=True):
        acc, y, x = self.acc(k), self.y, self.x
        part = acc.shape[3] // 2
        self.wait(self.corner(k))
        one = acc.at[:, 1 - y, x, 0:part]
        two = acc.at[:, y, 1 - x, part : 2 * part]
        one[...] = _add(one[...], self.x_one[k])
        two[...] = _add(two[...], self.y_one[k])
        if go_on:
            self.start(self.plane(k))

    def after_plane(self, k):
        acc = self.acc(k)
        self.wait(self.plane(k))
        here = acc.at[:, self.y, self.x]
        here[...] = _add(here[...], self.x_two[k], self.y_two[k])
        self.start(self.line(k))

    def finish_plane(self, k, target):
        self.wait(self.plane(k))
        target[k] = _add(self.acc(k)[:, self.y, self.x], self.x_two[k], self.y_two[k])

    def after_line(self, k):
        self.wait(self.line(k))
        total = self.acc(k)[self.z, self.y, self.x].astype(self.out.dtype)
        for j in range(3):
            total = total + self.from_z[k, j].astype(self.out.dtype)
        self.out[k] = total


def _add(first, *others):
    if len(others) == 1:
        return first + others[0]
    total = first.astype(jnp.float32)
    for other in others:
        total = total + other.astype(jnp.float32)
    return total.astype(first.dtype)


def _combine(mine, other):
    @pl.loop(0, mine.shape[0])
    def _(i):
        for j in range(2):
            mine[i, j] = _add(mine[i, j], other[i, j])


EARLY = 2
BEGUN = 2
ATTEND_SITES = 3
ATTEND_TICKS = {4: 1, 5: 3, 7: 9}
FEED_TICKS = {9: 0, 10: 1, 11: 2, 12: 3, 13: 4, 14: 6}


def front_kernel(
    prefix, wq_in, wk_in, wv_in, wo_in, up_in, down_in, vec, xin, gin,
    full, fullo, qkv, mixed_out, probs_out, normed_out, x_out, lines, layer_out, low_out, sums, gown, grecv, gbias, early_out,
    vfull, x, grad, second, residual, weights, ubias,
    ssem, rsem, lsem, vs, vr, vl, ws, wr, wl, wsem, osem, fs, fr, fl, es, er, el,
    racc, rtheirs, x_one, y_one, x_two, y_two, rs, rr, rl,
):
    f32, bf16 = jnp.float32, jnp.bfloat16
    seq_len, model = x.shape
    half = seq_len // 2
    block = 128

    cols = wq_in.shape[1]
    shards = [w.at[:, sub * WIDE : (sub + 1) * WIDE] for sub in range(2) for w in (wq_in, wk_in, wv_in)] + [wo_in]
    places = [full.at[k] for k in range(6)] + [fullo]
    for piece in range(weights.shape[0] // 2):
        shards += [w.at[:, piece * cols : (piece + 1) * cols] for w in (up_in, down_in)]
        places += [weights.at[2 * piece], weights.at[2 * piece + 1]]
    early = len(shards) - weights.shape[0]
    gather = Gather(shards, places, ssem, rsem, lsem)
    reduce = Reduce(lambda k: racc.at[k], None, x_one, y_one, x_two, y_two, None, rs, rr)
    z, y, xx, core = gather.z, gather.y, gather.x, gather.core
    along, across, down, sibling = gather.along, gather.across, gather.down, gather.sibling
    _greet(along + [across, down, sibling])

    gather.start(gather.line, 0)
    vown = vfull.at[z, y, xx, core]
    vline = [_local(vec, vown, vl.at[0])] + [_send(vec, vown, vs.at[j], vr.at[j], along[j]) for j in range(3)]
    for k in (1, 2, 3):
        gather.start(gather.line, k)
    mine = pl.ds(pl.multiple_of(core * half, half), half)
    swaps = []
    for i, (part, whole) in enumerate(((xin, x), (gin, grad))):
        swaps.append(_local(part.at[core], whole.at[mine], wl.at[i]))
        swaps.append(_send(part.at[1 - core], whole.at[mine], ws.at[i], wr.at[i], sibling))
    gather.wait(gather.line, 0)
    gather.start(gather.plane, 0)
    for s in vline:
        s.wait()
    vblock = vfull.at[:, y, xx, core]
    vone = [_send(vblock, vblock, vs.at[3], vr.at[3], across), _send(vblock, vblock, vs.at[4], vr.at[4], down)]
    gather.wait(gather.line, 1)
    gather.start(gather.plane, 1)
    gather.tick(0)
    for s in vone:
        s.wait()
    vblock = vfull.at[:, 1 - y, xx, core]
    vtwo = _send(vblock, vblock, vs.at[5], vr.at[5], across)
    gather.tick(1)
    vtwo.wait()
    vblock = vfull.at[:, :, :, core]
    vthree = _send(vblock, vblock, vs.at[6], vr.at[6], sibling)
    for s in swaps:
        s.wait()
    saved = [_local(x, x_out, osem.at[0])]
    gather.tick(2)
    vthree.wait()
    for zi in range(4):
        for yi in range(2):
            at = (zi * 2 + yi) * 128
            group = vfull[zi, yi, 0, 0] + vfull[zi, yi, 0, 1] + vfull[zi, yi, 1, 0] + vfull[zi, yi, 1, 1]
            lines[:, at : at + 128] = group[0:8]
            for xi in range(2):
                for ci in range(2):
                    i = ((zi * 2 + yi) * 2 + xi) * 2 + ci
                    piece = 2 * ((i % 16) // 4) + i // 16
                    ubias[piece, 0:1, (i % 4) * 128 : (i % 4) * 128 + 128] = vfull[zi, yi, xi, ci, 8:9]

    def attention(normed, wblk, stage, mixed, wout, probs):
        @pl.loop(0, seq_len // block)
        def _(i):
            rows = pl.ds(pl.multiple_of(i * block, block), block)
            scaled, _ = _normal(x[rows].astype(f32))
            normed[rows] = (scaled * lines[0:1] + lines[1:2]).astype(bf16)

        gather.wait(gather.corner, 2)
        gather.start(gather.twin, 2)
        gather.tick(3, twin=False)
        keep = _local(normed, normed_out, osem.at[1])

        def side_of(pair):
            return (pair + core) % 2

        def load(pair):
            return [
                pltpu.make_async_copy(full.at[3 * (pair // 2) + i, side_of(pair)], wblk.at[pair % 2, i], wsem.at[pair % 2, i])
                for i in range(3)
            ]

        def store(pair):
            slot = pair % 2
            columns = pl.ds(pl.multiple_of((pair // 2) * WIDE, WIDE), WIDE)
            copies = [
                pltpu.make_async_copy(stage.at[slot, i], qkv.at[i, side_of(pair), :, columns], wsem.at[slot, 3 + i])
                for i in range(3)
            ]
            heads = pl.ds((side_of(pair) * 2 + pair // 2) * 2, 2)
            return copies + [pltpu.make_async_copy(probs.at[slot], probs_out.at[heads], wsem.at[slot, 6])]

        for c in load(0):
            c.start()

        def ticks(site, pair):
            for k, at in ATTEND_TICKS.items():
                if at % ATTEND_SITES == site:

                    @pl.when(pair == at // ATTEND_SITES)
                    def _(k=k):
                        gather.tick(k)

        @pl.loop(0, 4)
        def _(pair):
            slot = pair % 2
            for c in load(pair):
                c.wait()

            @pl.when(pair >= 2)
            def _():
                for c in store(pair - 2):
                    c.wait()

            ticks(0, pair)
            lanes = pl.ds(pl.multiple_of((side_of(pair) * 2 + pair // 2) * WIDE, WIDE), WIDE)
            wq, wk, wv = (wblk[slot, i].reshape(model, WIDE) for i in range(3))
            stage[slot, 0] = (_dot(normed[...], wq, NN) + lines[2:3, lanes]).astype(bf16)
            stage[slot, 1] = _dot(normed[...], wk, NN).astype(bf16)
            stage[slot, 2] = (_dot(normed[...], wv, NN) + lines[3:4, lanes]).astype(bf16)
            ticks(1, pair)
            for sub in range(2):

                @pl.when(pair == 2 * sub)
                def _(sub=sub):
                    for k in range(3 * sub, 3 * sub + 3):
                        gather.wait(gather.twin, k)
                    for c in load(2 * sub + 1):
                        c.start()

            step = 256
            factor = LOG2E / math.sqrt(HEAD_DIM)
            prefix_len = prefix[core]
            parts = [slice(h * HEAD_DIM, (h + 1) * HEAD_DIM) for h in range(WIDE // HEAD_DIM)]
            for head, part in enumerate(parts):
                for start, stop in _spans(seq_len, LONGEST, step):
                    scores = _dot(stage[slot, 1, :stop, part], stage[slot, 0, start : start + step, part], NT)
                    keys = lax.broadcasted_iota(jnp.int32, scores.shape, 0)
                    queries = lax.broadcasted_iota(jnp.int32, (1, step), 1) + start
                    scores = jnp.where(keys < jnp.maximum(queries + 1, prefix_len), scores, -jnp.inf)
                    peak = jnp.max(scores, axis=0, keepdims=True)
                    raw = jnp.exp2((scores - peak) * factor)
                    total = jnp.sum(raw, axis=0, keepdims=True)
                    probs[slot, head, :stop, start : start + step] = (raw * (1.0 / total)).astype(bf16)
            ticks(2, pair)
            bands = [(0, LONGEST)] + [(first, first + step) for first in range(LONGEST, seq_len, step)]
            for head, part in enumerate(parts):
                to = pl.ds(pl.multiple_of((pair // 2) * WIDE + head * HEAD_DIM, HEAD_DIM), HEAD_DIM)
                for first, last in bands:
                    mixed[side_of(pair), first:last, to] = _dot(
                        probs[slot, head, :last, first:last], stage[slot, 2, :last, part], TN
                    ).astype(bf16)
            for c in store(pair):
                c.start()

            @pl.when(pair == 1)
            def _():
                gather.tick(6)
                for c in load(2):
                    c.start()

        gather.tick(8)
        gather.wait(gather.twin, 6)
        fetch = _local(fullo, wout, osem.at[3])
        done = _local(mixed, mixed_out, osem.at[2])
        fetch.wait()
        weight = [wout[c].reshape(model, seq_len // 2) for c in range(2)]
        step = 256

        @pl.loop(0, seq_len // step)
        def _(i):
            rows = pl.ds(pl.multiple_of(i * step, step), step)
            branch = _dot(mixed[0, rows], weight[0], NT) + _dot(mixed[1, rows], weight[1], NT)
            total = x[rows].astype(f32) + branch + lines[4:5]
            residual[rows] = total
            scaled, _ = _normal(total)
            second[rows] = (scaled * lines[5:6] + lines[6:7]).astype(bf16)

        for pair in (2, 3):
            for c in store(pair):
                c.wait()
        done.wait()
        keep.wait()

    pl.run_scoped(
        attention,
        pltpu.VMEM((seq_len, model), bf16),
        pltpu.VMEM((2, 3, 4, 2, 2, 64, WIDE), bf16),
        pltpu.VMEM((2, 3, seq_len, WIDE), bf16),
        pltpu.VMEM((2, seq_len, model // 2), bf16),
        pltpu.VMEM((2, 4, 2, 2, 64, model // 2), bf16),
        pltpu.VMEM((2, 2, seq_len, seq_len), bf16),
    )

    def feed(layer, gres, stage, hid, gpre):
        pieces = weights.shape[0]

        @pl.loop(0, seq_len // block)
        def _(i):
            rows = pl.ds(pl.multiple_of(i * block, block), block)
            layer[rows] = residual[rows] + lines[7:8]
            gres[rows] = jnp.zeros((block, model), f32)

        def away(piece):
            return [
                pltpu.make_async_remote_copy(
                    src_ref=stage.at[1, i],
                    dst_ref=grecv.at[2 * piece + i],
                    send_sem=fs.at[piece, i],
                    recv_sem=fr.at[piece, i],
                    device_id=sibling,
                    device_id_type=MESH,
                )
                for i in range(2)
            ]

        def stay(piece):
            return [pltpu.make_async_copy(stage.at[0, i], gown.at[2 * piece + i], fl.at[i]) for i in range(2)]

        def bring(k):
            return [
                pltpu.make_async_copy(gown.at[k], racc.at[k], rl.at[k % 2, 0]),
                pltpu.make_async_copy(grecv.at[k], rtheirs.at[k % 2], rl.at[k % 2, 1]),
            ]

        @pl.loop(0, pieces)
        def _(t):
            piece, turn = t // 2, t % 2
            side = (t + core) % 2
            for k, at in FEED_TICKS.items():

                @pl.when(t == at)
                def _(k=k):
                    gather.tick(k)

            for p in range(pieces // 2):

                @pl.when(t == 2 * p + 1)
                def _(p=p):
                    gather.wait(gather.twin, early + 2 * p)
                    if p < pieces // 2 - 1:
                        gather.wait(gather.twin, early + 2 * p + 1)
                    else:
                        gather.last(20)

            @pl.when(t == pieces - 3)
            def _():
                for p in range((EARLY + BEGUN) // 2):
                    for c in away(p):
                        c.wait_recv()
                reduce.start(bring(0) + bring(1))

            for at in range(2):

                @pl.when(t == pieces - 2 + at)
                def _(at=at):
                    for k in (2 * at, 2 * at + 1):
                        reduce.wait(bring(k))
                        _combine(racc.at[k], rtheirs.at[k % 2])
                        reduce.start(reduce.corner(k))
                        if at == 0:
                            reduce.start(bring(k + 2))

            @pl.when(t == pieces - 1)
            def _():
                for k in range(EARLY):
                    reduce.after_corner(k)

            @pl.when((t >= 2) & (turn == 1))
            def _():
                for c in away(piece - 1):
                    c.wait_send()

            @pl.when((t >= 2) & (turn == 0))
            def _():
                for c in stay(piece - 1):
                    c.wait()

            up = weights[2 * piece, side].reshape(model, model // 2)
            lower = weights[2 * piece + 1, side].reshape(model, model // 2)
            line = 2 * piece + side
            pre = _dot(second[...], up, NN) + ubias[line]
            phi = 0.5 * (1.0 + lax.erf(pre * (1.0 / math.sqrt(2.0))))
            density = jnp.exp2(pre * pre * (-0.5 * LOG2E)) * (1.0 / math.sqrt(2.0 * math.pi))
            hid[...] = (pre * phi).astype(bf16)
            slope = phi + pre * density
            back = (_dot(grad[...], lower, NN) * slope).astype(bf16)
            gpre[...] = back
            gbias[line] = jnp.sum(back.astype(f32), axis=0, keepdims=True)
            layer[...] += _dot(hid[...], lower, NT)
            gres[...] += _dot(gpre[...], up, NT)
            blocks = stage.shape[2:]
            stage[turn, 0] = _dot(second[...], gpre[...], TN).astype(bf16).reshape(blocks)
            stage[turn, 1] = _dot(grad[...], hid[...], TN).astype(bf16).reshape(blocks)

            @pl.when(turn == 1)
            def _():
                for c in away(piece):
                    c.start()

            @pl.when(turn == 0)
            def _():
                for c in stay(piece):
                    c.start()

        for s in saved:
            s.wait()

        @pl.loop(0, seq_len // block)
        def _(i):
            rows = pl.ds(pl.multiple_of(i * block, block), block)
            x[rows] = layer[rows].astype(bf16)

        theirs = pl.ds(pl.multiple_of((1 - core) * half, half), half)
        final = [
            _local(x.at[mine], layer_out.at[core], el.at[0]),
            _send(x.at[theirs], layer_out.at[core], es.at[0], er.at[0], sibling),
        ]
        sums[...] = jnp.zeros_like(sums)

        @pl.loop(0, seq_len // block)
        def _(i):
            rows = pl.ds(pl.multiple_of(i * block, block), block)
            scaled, inverse = _normal(residual[rows])
            grow = gres[rows]
            upstream = grad[rows].astype(f32)
            weighted = grow * lines[5:6]
            mean_plain = jnp.mean(weighted, axis=-1, keepdims=True)
            mean_scaled = jnp.mean(weighted * scaled, axis=-1, keepdims=True)
            total = upstream + inverse * (weighted - mean_plain - scaled * mean_scaled)
            second[rows] = total.astype(bf16)
            sums[0:1] += jnp.sum(grow * scaled, axis=0, keepdims=True)
            sums[1:2] += jnp.sum(grow, axis=0, keepdims=True)
            sums[2:3] += jnp.sum(total, axis=0, keepdims=True)
            sums[3:4] += jnp.sum(upstream, axis=0, keepdims=True)

        final.append(_local(second, low_out, el.at[2]))
        for k in range(EARLY, EARLY + BEGUN):
            reduce.after_corner(k, go_on=False)
            final.append(_local(racc.at[k], gown.at[k], rl.at[k % 2, 0]))
        for k in range(EARLY):
            reduce.finish_plane(k, early_out)
        last = pieces // 2 - 1
        for c in away(last):
            c.wait_send()
        for c in stay(last):
            c.wait()
        for p in range((EARLY + BEGUN) // 2, pieces // 2):
            for c in away(p):
                c.wait_recv()
        for c in final:
            c.wait()

    pl.run_scoped(
        feed,
        pltpu.VMEM((seq_len, model), f32),
        pltpu.VMEM((seq_len, model), f32),
        pltpu.VMEM((2, 2, 4, 2, 2, model // 16, model // 2), bf16),
        pltpu.VMEM((seq_len, model // 2), bf16),
        pltpu.VMEM((seq_len, model // 2), bf16),
    )


def front(prefix_len, wq, wk, wv, wo, up, down, vec, xin, gin):
    rows, cols = wq.shape
    half, model = xin.shape[1:]
    seq_len = 2 * half
    pieces = 2 * (up.shape[1] // cols)
    chunks = 7 + pieces
    bf16, f32 = jnp.bfloat16, jnp.float32
    hbm = pl.BlockSpec(memory_space=pltpu.HBM)
    vmem = pl.BlockSpec(memory_space=pltpu.VMEM)
    dma = pltpu.SemaphoreType.DMA

    def shape(dims, dtype):
        return jax.ShapeDtypeStruct(dims, dtype)

    heads = model // HEAD_DIM
    return pl.pallas_call(
        front_kernel,
        out_shape=(
            shape((6, 2, 4, 2, 2, rows, WIDE), bf16),
            shape((2, 4, 2, 2, rows, cols), bf16),
            shape((3, 2, seq_len, cols), bf16),
            shape((2, seq_len, cols), bf16),
            shape((heads, seq_len, seq_len), bf16),
            shape((seq_len, model), bf16),
            shape((seq_len, model), bf16),
            shape((8, model), f32),
            shape((2, half, model), bf16),
            shape((seq_len, model), bf16),
            shape((8, model), f32),
            shape((pieces, 4, 2, 2, rows, cols), bf16),
            shape((pieces, 4, 2, 2, rows, cols), bf16),
            shape((pieces, 1, cols), f32),
            shape((EARLY, 4, rows, cols), bf16),
        ),
        in_specs=[pl.BlockSpec(memory_space=pltpu.SMEM)] + [vmem] * 7 + [hbm, hbm],
        out_specs=(hbm, hbm, hbm, hbm, hbm, hbm, hbm, vmem, hbm, hbm, vmem, hbm, hbm, vmem, vmem),
        scratch_shapes=[
            pltpu.VMEM((4, 2, 2, 2) + vec.shape, f32),
            pltpu.VMEM((seq_len, model), bf16),
            pltpu.VMEM((seq_len, model), bf16),
            pltpu.VMEM((seq_len, model), bf16),
            pltpu.VMEM((seq_len, model), f32),
            pltpu.VMEM((pieces, 2, 4, 2, 2, rows, cols), bf16),
            pltpu.VMEM((pieces, 1, cols), f32),
            dma((chunks + 1, 8)),
            dma((chunks + 1, 8)),
            dma((chunks,)),
            dma((7,)),
            dma((7,)),
            dma((1,)),
            dma((2,)),
            dma((2,)),
            dma((2,)),
            dma((2, 7)),
            dma((4,)),
            dma((pieces // 2, 2)),
            dma((pieces // 2, 2)),
            dma((2,)),
            dma((1,)),
            dma((1,)),
            dma((3,)),
            pltpu.VMEM((EARLY + BEGUN, 4, 2, 2, rows, cols), bf16),
            pltpu.VMEM((2, 4, 2, 2, rows, cols), bf16),
            pltpu.VMEM((EARLY + BEGUN, 4, rows // 2, cols), bf16),
            pltpu.VMEM((EARLY + BEGUN, 4, rows // 2, cols), bf16),
            pltpu.VMEM((EARLY, 4, rows, cols), bf16),
            pltpu.VMEM((EARLY, 4, rows, cols), bf16),
            dma((EARLY + BEGUN, 7)),
            dma((EARLY + BEGUN, 7)),
            dma((2, 2)),
        ],
        compiler_params=pltpu.CompilerParams(
            collective_id=0, has_side_effects=True, vmem_limit_bytes=63 * MIB
        ),
    )(prefix_len, wq, wk, wv, wo, up, down, vec, xin, gin)


RING = 6
UNIT_SITES = (
    (("begin", 2),),
    (("begin", 3), ("corner", 2), ("plane", 0)),
    (("begin", 4), ("corner", 3), ("plane", 1), ("line", 0)),
    (("begin", 5), ("corner", 4), ("plane", 2), ("line", 1)),
    (("corner", 5), ("plane", 3), ("line", 2)),
    (("plane", 4), ("line", 3)),
    (("begin", 6), ("plane", 5), ("line", 4)),
    (("begin", 7), ("corner", 6), ("line", 5)),
)


def back_kernel(
    lines, sums_two, gbias, early, qkv, mixed_in, probs_in, full, fullo, low_in, normed_in, x_in, gown, grecv,
    out, vout, iout, qrecv,
    ring, theirs_in, gbuf, x_one, y_one, x_two, y_two, from_z,
    vacc, v_s, vx_one, vx_two, vy_two, v_z,
    low, normed, ingrad, sums, bsums,
    from_e, esend, erecv, ssem, rsem, lsem, qs, qr, vs, vr, bsem, msem, es, er,
):
    f32, bf16 = jnp.float32, jnp.bfloat16
    seq_len, model = low.shape
    half, block, step = seq_len // 2, 128, 256
    feeds = gown.shape[0] - EARLY
    count = out.shape[0] - EARLY
    scale = 1.0 / math.sqrt(HEAD_DIM)

    own = gbuf.at[1]

    def acc(k):
        return own.at[k - feeds] if isinstance(k, int) and k >= feeds else ring.at[k % RING]

    reduce = Reduce(acc, out, x_one, y_one, x_two, y_two, from_z, ssem, rsem)
    z, y, x, core = reduce.z, reduce.y, reduce.x, reduce.core
    along, across, down, sibling = reduce.along, reduce.across, reduce.down, reduce.sibling

    def load(k):
        if isinstance(k, int) and k >= feeds:
            return [pltpu.make_async_copy(qrecv.at[k - feeds], theirs_in.at[k % 2], lsem.at[k % 2, 1])]
        copies = [pltpu.make_async_copy(gown.at[EARLY + k], ring.at[k % RING], lsem.at[k % 2, 0])]
        if k >= BEGUN:
            copies.append(pltpu.make_async_copy(grecv.at[EARLY + k], theirs_in.at[k % 2], lsem.at[k % 2, 1]))
        return copies

    def begin(k):
        reduce.wait(load(k))
        _combine(acc(k), theirs_in.at[k % 2])
        reduce.start(reduce.corner(k))

    for k in range(BEGUN):
        reduce.start(load(k))
    start = [_local(low_in, low, msem.at[0]), _local(normed_in, normed, msem.at[1])]
    _greet(along + [across, down, sibling])
    for k in range(BEGUN):
        reduce.wait(load(k))
        reduce.start(reduce.plane(k))
        reduce.start(load(BEGUN + k))
    lines_first = [
        _send(early.at[k, (z + j + 1) % 4], from_e.at[k, j], esend.at[k, j], erecv.at[k, j], along[j])
        for k in range(EARLY)
        for j in range(3)
    ]

    def away(sub, i):
        unit = sub * 2 + i
        return pltpu.make_async_remote_copy(
            src_ref=gbuf.at[0, unit],
            dst_ref=qrecv.at[unit],
            send_sem=qs.at[unit],
            recv_sem=qr.at[unit],
            device_id=sibling,
            device_id_type=MESH,
        )

    def landed(unit):
        away(unit // 2, unit % 2).wait_recv()

    stages = {
        "begin": begin,
        "corner": reduce.after_corner,
        "plane": reduce.after_plane,
        "line": reduce.after_line,
    }

    def retreat(heads_in, probs, wblk, dq, dk, dv, dmix):
        def fetch(i):
            turn, sub = i // 2, i % 2
            side = (turn + 1 + core) % 2
            columns = pl.ds(pl.multiple_of(sub * WIDE, WIDE), WIDE)
            slot = i % 2
            copies = [
                pltpu.make_async_copy(qkv.at[n, side, :, columns], heads_in.at[slot, n], bsem.at[slot, n])
                for n in range(3)
            ]
            copies.append(pltpu.make_async_copy(mixed_in.at[side, :, columns], heads_in.at[slot, 3], bsem.at[slot, 3]))
            copies += [
                pltpu.make_async_copy(full.at[3 * sub + n, side], wblk.at[slot, n], bsem.at[slot, 4 + n])
                for n in range(3)
            ]
            copies.append(
                pltpu.make_async_copy(fullo.at[side, :, :, :, :, columns], wblk.at[slot, 3], bsem.at[slot, 7])
            )
            heads = pl.ds((side * 2 + sub) * 2, 2)
            copies.append(pltpu.make_async_copy(probs_in.at[heads], probs.at[slot], bsem.at[slot, 8]))
            return copies

        reduce.start(fetch(0))

        @pl.loop(0, seq_len // block)
        def _(i):
            ingrad[pl.ds(pl.multiple_of(i * block, block), block)] = jnp.zeros((block, model), f32)

        reduce.wait(start)

        @pl.loop(0, 4)
        def _(i):
            turn, sub, slot = i // 2, i % 2, i % 2
            side = (turn + 1 + core) % 2
            reduce.wait(fetch(i))

            @pl.when(i < 3)
            def _():
                reduce.start(fetch(i + 1))

            columns = pl.ds(pl.multiple_of(sub * WIDE, WIDE), WIDE)

            def put(n, value):
                at = slice((n % 2) * WIDE, (n % 2 + 1) * WIDE)
                gbuf[turn, sub * 2 + n // 2, :, :, :, :, at] = value.astype(bf16).reshape(4, 2, 2, model // 16, WIDE)

            def site(n):
                for at in range(4):

                    @pl.when(i == at)
                    def _(at=at):
                        if 2 * at + n == feeds:
                            for u in range(2):
                                landed(u)
                                reduce.start(load(feeds + u))
                        for stage, k in UNIT_SITES[2 * at + n]:
                            stages[stage](k)
                            if stage == "begin" and k + 2 < feeds:
                                reduce.start(load(k + 2))

            site(0)
            wq, wk, wv, wo = (wblk[slot, n].reshape(model, WIDE) for n in range(4))
            dmix[...] = _dot(low[...], wo, NN).astype(bf16)
            put(0, _dot(low[...], heads_in[slot, 3], TN))
            parts = [slice(h * HEAD_DIM, (h + 1) * HEAD_DIM) for h in range(WIDE // HEAD_DIM)]
            spans = _spans(seq_len, LONGEST, step)
            bands = [(0, LONGEST)] + [(first, first + step) for first in range(LONGEST, seq_len, step)]
            for head, part in enumerate(parts):
                for low_key, high_key in bands:
                    dv[low_key:high_key, part] = _dot(
                        probs[slot, head, low_key:high_key, low_key:], dmix[low_key:, part], NN
                    ).astype(bf16)
            for head, part in enumerate(parts):
                for first, stop in spans:
                    block_at = (slot, head, slice(0, stop), slice(first, first + step))
                    weights = probs[block_at].astype(f32)
                    dprobs = _dot(heads_in[slot, 2, :stop, part], dmix[first : first + step, part], NT)
                    inner = jnp.sum(weights * dprobs, axis=0, keepdims=True)
                    probs[block_at] = (weights * (dprobs - inner)).astype(bf16)
            site(1)
            for head, part in enumerate(parts):
                for low_key, high_key in bands:
                    dk[low_key:high_key, part] = (
                        _dot(probs[slot, head, low_key:high_key, low_key:], heads_in[slot, 0, low_key:, part], NN)
                        * scale
                    ).astype(bf16)
                for first, last in bands:
                    dq[first:last, part] = (
                        _dot(probs[slot, head, :last, first:last], heads_in[slot, 1, :last, part], TN) * scale
                    ).astype(bf16)
            put(1, _dot(normed[...], dq[...], TN))
            put(2, _dot(normed[...], dk[...], TN))
            put(3, _dot(normed[...], dv[...], TN))
            ingrad[...] += _dot(dq[...], wq, NT) + _dot(dk[...], wk, NT) + _dot(dv[...], wv, NT)

            @pl.when(turn == 0)
            def _():
                for n in range(2):
                    away(sub, n).start()

            at = side * 2 + sub
            bsums[at, 0:1] = jnp.sum(dq[...].astype(f32), axis=0, keepdims=True)
            bsums[at, 1:2] = jnp.sum(dv[...].astype(f32), axis=0, keepdims=True)

        for sub in range(2):
            for n in range(2):
                away(sub, n).wait_send()

    pl.run_scoped(
        retreat,
        pltpu.VMEM((2, 4, seq_len, WIDE), bf16),
        pltpu.VMEM((2, 2, seq_len, seq_len), bf16),
        pltpu.VMEM((2, 4, 4, 2, 2, model // 16, WIDE), bf16),
        pltpu.VMEM((seq_len, WIDE), bf16),
        pltpu.VMEM((seq_len, WIDE), bf16),
        pltpu.VMEM((seq_len, WIDE), bf16),
        pltpu.VMEM((seq_len, WIDE), bf16),
    )

    reduce.wait(lines_first)
    for k in range(EARLY):
        total = early[k, z].astype(f32)
        for j in range(3):
            total = total + from_e[k, j].astype(f32)
        out[count + k] = total

    def finish(xs):
        bring = [_local(x_in, xs, msem.at[1])]
        for unit in (2, 3):
            landed(unit)
            reduce.start(load(feeds + unit))
        begin(feeds + 2)
        begin(feeds + 3)
        reduce.after_corner(feeds + 1)
        reduce.after_plane(feeds)
        reduce.after_corner(feeds + 2)
        reduce.after_corner(feeds + 3)
        reduce.wait(bring)
        sums[...] = jnp.zeros_like(sums)

        @pl.loop(0, seq_len // block)
        def _(i):
            rows = pl.ds(pl.multiple_of(i * block, block), block)
            scaled, inverse = _normal(xs[rows].astype(f32))
            grow = ingrad[rows]
            weighted = grow * lines[0:1]
            mean_plain = jnp.mean(weighted, axis=-1, keepdims=True)
            mean_scaled = jnp.mean(weighted * scaled, axis=-1, keepdims=True)
            total = low[rows].astype(f32) + inverse * (weighted - mean_plain - scaled * mean_scaled)
            normed[rows] = total.astype(bf16)
            sums[0:1] += jnp.sum(grow * scaled, axis=0, keepdims=True)
            sums[1:2] += jnp.sum(grow, axis=0, keepdims=True)

    pl.run_scoped(finish, pltpu.VMEM((seq_len, model), bf16))
    mine = pl.ds(pl.multiple_of(core * half, half), half)
    theirs = pl.ds(pl.multiple_of((1 - core) * half, half), half)
    final = [
        _local(normed.at[mine], iout.at[core], msem.at[0]),
        _send(normed.at[theirs], iout.at[core], es.at[0], er.at[0], sibling),
    ]
    for pair in range(4):
        at = slice(pair * WIDE, (pair + 1) * WIDE)
        sums[2:4, at] = bsums[pair, 0:2]
    sums[4:5] = sums_two[2:3]
    sums[5:7] = sums_two[0:2]
    sums[7:8] = sums_two[3:4]
    vacc[...] = jnp.zeros_like(vacc)
    for zi in range(4):
        for yi in range(2):
            at = (zi * 2 + yi) * 128
            for xi in range(2):
                for ci in range(2):
                    i = ((zi * 2 + yi) * 2 + xi) * 2 + ci
                    piece = 2 * ((i % 16) // 4) + i // 16
                    vacc[ci, zi, yi, xi, 0:8] = sums[:, at : at + 128]
                    vacc[ci, zi, yi, xi, 8:9] = gbias[piece, 0:1, (i % 4) * 128 : (i % 4) * 128 + 128]
    vzero = _send(vacc.at[1 - core], v_s, vs.at[0], vr.at[0], sibling)
    reduce.after_plane(feeds + 1)
    reduce.after_line(feeds)
    vzero.wait()
    vmine = vacc.at[core]
    vmine[...] = vmine[...] + v_s[...]
    vone = _send(vmine.at[:, 1 - y, 1 - x], vx_one, vs.at[1], vr.at[1], across)
    reduce.after_plane(feeds + 2)
    vone.wait()
    vmine[:, 1 - y, x] = vmine[:, 1 - y, x] + vx_one[...]
    vtwo = [
        _send(vmine.at[:, y, 1 - x], vx_two, vs.at[2], vr.at[2], across),
        _send(vmine.at[:, 1 - y, x], vy_two, vs.at[3], vr.at[3], down),
    ]
    reduce.after_plane(feeds + 3)
    reduce.after_line(feeds + 1)
    reduce.wait(vtwo)
    vmine[:, y, x] = vmine[:, y, x] + vx_two[...] + vy_two[...]
    vthree = [
        _send(vmine.at[(z + j + 1) % 4, y, x], v_z.at[j], vs.at[4 + j], vr.at[4 + j], along[j]) for j in range(3)
    ]
    reduce.after_line(feeds + 2)
    reduce.after_line(feeds + 3)
    reduce.wait(vthree)
    vout[...] = vmine[z, y, x] + v_z[0] + v_z[1] + v_z[2]
    reduce.wait(final)


def back(lines, sums_two, gbias, early, qkv, mixed, probs, full, fullo, low, normed, x, gown, grecv):
    count = gown.shape[0] - EARLY + 4
    seq_len, model = x.shape
    rows, cols = gown.shape[-2:]
    half = seq_len // 2
    bf16, f32 = jnp.bfloat16, jnp.float32
    hbm = pl.BlockSpec(memory_space=pltpu.HBM)
    vmem = pl.BlockSpec(memory_space=pltpu.VMEM)
    dma = pltpu.SemaphoreType.DMA
    small = (16, 128)
    return pl.pallas_call(
        back_kernel,
        out_shape=(
            jax.ShapeDtypeStruct((count + EARLY, rows, cols), f32),
            jax.ShapeDtypeStruct(small, f32),
            jax.ShapeDtypeStruct((2, half, model), bf16),
            jax.ShapeDtypeStruct((4, 4, 2, 2, rows, cols), bf16),
        ),
        in_specs=[vmem] * 4 + [hbm] * 10,
        out_specs=(vmem, vmem, hbm, hbm),
        scratch_shapes=[
            pltpu.VMEM((RING, 4, 2, 2, rows, cols), bf16),
            pltpu.VMEM((2, 4, 2, 2, rows, cols), bf16),
            pltpu.VMEM((2, 4, 4, 2, 2, rows, cols), bf16),
            pltpu.VMEM((count, 4, rows // 2, cols), bf16),
            pltpu.VMEM((count, 4, rows // 2, cols), bf16),
            pltpu.VMEM((count, 4, rows, cols), bf16),
            pltpu.VMEM((count, 4, rows, cols), bf16),
            pltpu.VMEM((count, 3, rows, cols), bf16),
            pltpu.VMEM((2, 4, 2, 2) + small, f32),
            pltpu.VMEM((4, 2, 2) + small, f32),
            pltpu.VMEM((4,) + small, f32),
            pltpu.VMEM((4,) + small, f32),
            pltpu.VMEM((4,) + small, f32),
            pltpu.VMEM((3,) + small, f32),
            pltpu.VMEM((seq_len, model), bf16),
            pltpu.VMEM((seq_len, model), bf16),
            pltpu.VMEM((seq_len, model), f32),
            pltpu.VMEM((8, model), f32),
            pltpu.VMEM((4, 8, WIDE), f32),
            pltpu.VMEM((EARLY, 3, rows, cols), bf16),
            dma((EARLY, 3)),
            dma((EARLY, 3)),
            dma((count, 7)),
            dma((count, 7)),
            dma((2, 2)),
            dma((4,)),
            dma((4,)),
            dma((7,)),
            dma((7,)),
            dma((2, 9)),
            dma((2,)),
            dma((1,)),
            dma((1,)),
        ],
        compiler_params=pltpu.CompilerParams(
            collective_id=1, has_side_effects=True, vmem_limit_bytes=63 * MIB
        ),
    )(lines, sums_two, gbias, early, qkv, mixed, probs, full, fullo, low, normed, x, gown, grecv)


def finish_kernel(
    late, layer, ingrad, gq, gk, gv, go, up, down, layer_out, ingrad_out, held, wide, small, large, sem, usem, osem
):
    count, _, cols = late.shape
    pieces = (count - 4) // 2
    rows = []
    for n, (source, target) in enumerate(((layer, layer_out), (ingrad, ingrad_out))):
        for i in range(held.shape[1]):
            rows.append((_local(source.at[i], held.at[n, i], sem.at[0, n, i]), n, i, target.at[i]))
    units = [late.at[i % count] for i in range(-EARLY, count - EARLY)]
    fetched = []
    for piece in range(pieces):
        at = slice(piece * cols, (piece + 1) * cols)
        for n in range(2):
            fetched.append(_local(units[2 * piece + n], large.at[n, :, at], usem.at[len(fetched)]))
    for sub in range(2):
        at = slice(sub * WIDE, (sub + 1) * WIDE)
        for n in range(4):
            unit = units[2 * pieces + 2 * sub + n // 2].at[:, (n % 2) * WIDE : (n % 2 + 1) * WIDE]
            fetched.append(_local(unit, small.at[n, :, at], usem.at[len(fetched)]))
    stores = []
    for fetch, n, i, target in rows:
        fetch.wait()
        wide[n, i] = held[n, i].astype(wide.dtype)
        stores.append(_local(wide.at[n, i], target, sem.at[1, n, i]))
    for fetch in fetched:
        fetch.wait()
    for n, target in enumerate((go, gq, gk, gv)):
        stores.append(_local(small.at[n], target, osem.at[n]))
    for n, target in enumerate((up, down)):
        stores.append(_local(large.at[n], target, osem.at[4 + n]))
    for store in stores:
        store.wait()


def finish(late, layer, ingrad):
    rows, cols = late.shape[1:]
    wide = (late.shape[0] - 4) // 2 * cols
    hbm = pl.BlockSpec(memory_space=pltpu.HBM)
    parts = (8, layer.shape[0] * layer.shape[1] // 8, layer.shape[2])
    whole = jax.ShapeDtypeStruct(parts, late.dtype)
    shapes = ((rows, cols),) * 4 + ((rows, wide),) * 2
    dma = pltpu.SemaphoreType.DMA
    return pl.pallas_call(
        finish_kernel,
        out_shape=tuple(jax.ShapeDtypeStruct(s, late.dtype) for s in shapes) + (whole, whole),
        in_specs=[hbm] * 3,
        out_specs=(hbm,) * 8,
        scratch_shapes=[
            pltpu.VMEM((2,) + parts, layer.dtype),
            pltpu.VMEM((2,) + parts, late.dtype),
            pltpu.VMEM((4, rows, cols), late.dtype),
            pltpu.VMEM((2, rows, wide), late.dtype),
            dma((2, 2, 8)),
            dma((late.shape[0] + 4,)),
            dma((6,)),
        ],
        compiler_params=pltpu.CompilerParams(vmem_limit_bytes=63 * MIB),
    )(late, layer.reshape(parts), ingrad.reshape(parts))


def fast_body(
    inputs, prefix, ln1_gain, ln1_bias, query_weight, query_bias, key_weight, value_weight, value_bias,
    out_weight, out_bias, ln2_gain, ln2_bias, up_weight, up_bias, down_weight, down_bias, cotangent,
):
    core = lax.axis_index("tensor")
    half, model = inputs.shape[2], inputs.shape[3]
    rows, cols = query_weight.shape
    pieces = up_weight.shape[1] // cols

    small = jnp.stack([ln1_gain, ln1_bias, query_bias, value_bias, out_bias, ln2_gain, ln2_bias, down_bias])
    place = (lax.axis_index("dp") * 2 + core) % 4
    vec = jnp.pad(up_bias.reshape(1, 128), ((8, 7), (0, 0)))
    vec = lax.dynamic_update_slice(vec, small, (0, place * 32))
    (
        full, fullo, qkv, mixed, probs, normed, x, lines, layer_out, low, sums_two, gown, grecv, gup_bias,
        early,
    ) = front(
        prefix.reshape(-1), query_weight, key_weight, value_weight, out_weight.T, up_weight, down_weight.T, vec,
        inputs[:, 0], cotangent[:, 0],
    )
    out, vout, input_grad, _ = back(
        lines, sums_two, gup_bias, early, qkv, mixed, probs, full, fullo, low, normed, x,
        gown, grecv,
    )
    vectors = lax.dynamic_slice(vout, (0, place * 32), (8, 32))

    gq, gk, gv, gout, gup, gdown, layer_out, input_grad = finish(out, layer_out, input_grad)
    return (
        layer_out.reshape(2, 1, half, model),
        input_grad.reshape(2, 1, half, model),
        vectors[0],
        vectors[1],
        gq,
        vectors[2],
        gk,
        gv,
        vectors[3],
        gout.T,
        vectors[4],
        vectors[5],
        vectors[6],
        gup,
        vout[8],
        gdown.T,
        vectors[7],
    )


def solution(mesh):
    in_specs = (
        P(None, "dp", "tensor", None),
        P(None, "dp"),
        P(("dp", "tensor")),
        P(("dp", "tensor")),
        P("dp", "tensor"),
        P(("dp", "tensor")),
        P("dp", "tensor"),
        P("dp", "tensor"),
        P(("dp", "tensor")),
        P("tensor", "dp"),
        P(("dp", "tensor")),
        P(("dp", "tensor")),
        P(("dp", "tensor")),
        P("dp", "tensor"),
        P(("dp", "tensor")),
        P("tensor", "dp"),
        P(("dp", "tensor")),
        P(None, "dp", "tensor", None),
    )
    out_specs = (
        P(None, "dp", "tensor", None),
        P(None, "dp", "tensor", None),
        P(("dp", "tensor")),
        P(("dp", "tensor")),
        P("dp", "tensor"),
        P(("dp", "tensor")),
        P("dp", "tensor"),
        P("dp", "tensor"),
        P(("dp", "tensor")),
        P("tensor", "dp"),
        P(("dp", "tensor")),
        P(("dp", "tensor")),
        P(("dp", "tensor")),
        P("dp", "tensor"),
        P(("dp", "tensor")),
        P("tensor", "dp"),
        P(("dp", "tensor")),
    )
    sizes = (mesh.shape["dp"], mesh.shape["tensor"])
    chosen = fast_body if sizes == (16, 2) else body
    return jax.shard_map(chosen, mesh=mesh, in_specs=in_specs, out_specs=out_specs, check_vma=False)
```
